32 devices in a mesh: dp: 8 (over z, y), mp: 4 (over x, core).
Axes of the slice: x: 2, y: 2, z: 4, core: 2. Of those that a mesh axis runs over, the one named last changes fastest.
Arguments:
- input_stream: bfloat16 [3, 4096, 768], P(None, 'dp'), may hold values from -6 to 6
- teacher: bfloat16 [3, 4096, 768], P(None, 'dp', 'mp'), may hold values from -6 to 6
- timestep: int32 [24], replicated, may hold values from 0 to 999
- lengths: int32 [24], replicated, may hold values from 1 to 512, 9216 in all
- block_perm: int32 [3, 64], replicated, may hold values from 0 to 63, as said below
- table: bfloat16 [1000, 768], P(None, ('dp', 'mp')), may hold values from -3 to 3
- norm_gains: bfloat16 [2, 768], P(None, ('dp', 'mp')), may hold values from 0.5 to 1.5
- shifts: bfloat16 [4, 768], P(None, ('dp', 'mp')), may hold values from -1.796875 to 1.796875
- w_qkv: bfloat16 [768, 2304], P('dp', 'mp'), may hold values from -0.21875 to 0.21875
- qv_bias: bfloat16 [2, 12, 64], P(None, 'mp', 'dp'), may hold values from -1.796875 to 1.796875
- w_out: bfloat16 [768, 768], P('mp', 'dp'), may hold values from -3.5 to 3.5
- w_in: bfloat16 [768, 3072], P('dp', 'mp'), may hold values from -0.21875 to 0.21875
- in_bias: bfloat16 [24, 128], P('mp', 'dp'), may hold values from -1.796875 to 1.796875
- w_back: bfloat16 [3072, 768], P('mp', 'dp'), may hold values from -0.109375 to 0.109375
Outputs:
- y_out: bfloat16 [3, 4096, 768], P(None, 'dp', 'mp')
- loss: float32 [], replicated
- grad_x: bfloat16 [3, 4096, 768], P(None, 'dp', 'mp')
- grad_table: float32 [1000, 768], P(None, ('dp', 'mp'))
- grad_norm_gains: float32 [2, 768], P(None, ('dp', 'mp'))
- grad_shifts: float32 [4, 768], P(None, ('dp', 'mp'))
- grad_qkv: float32 [768, 2304], P('dp', 'mp')
- grad_qv_bias: float32 [2, 12, 64], P(None, 'mp', 'dp')
- grad_out: float32 [768, 768], P('mp', 'dp')
- grad_in: float32 [768, 3072], P('dp', 'mp')
- grad_in_bias: float32 [24, 128], P('mp', 'dp')
- grad_back: float32 [3072, 768], P('mp', 'dp')
The draws below stay inside these ranges and needn't reach their ends.
Inputs may be any that keep to these rules, and one draw needn't show every extreme that they name: Each row block_perm[m] is a permutation of the 64 blocks; with loader block b = s * 8 + k lying on device s, each sequence slot d receives exactly one of its 8 blocks from each loader device s. The lengths sum to 9216 and at least one sequence is full.
All inputs are finite; a program needn't handle non-finite values.
Results may differ from the reference program's by a relative error of at most 0.0055.
The reference program's roundings to bfloat16 on the way count: a program that leaves them out, or rounds other values in their place, can miss the bound.
Values may be sent and summed in bfloat16 or wider, within the bound.
A program may use at most 128 MiB of HBM per device.

```python
import math
import jax
import jax.numpy as jnp
import numpy as np
from jax import lax

D = 768
H = 12
DH = 64
FF = 3072
STEPS = 1000
LEN = 512
MICRO = 3
TOK_MB = 4096
NSEQ = 24
N_DP = 8


def draw_block_perm(key, part):
    base = jax.random.fold_in(key, 7)
    first_key, second_key = jax.random.split(base)
    sources = jax.vmap(lambda single: jax.random.permutation(single, N_DP))(jax.random.split(first_key, MICRO * N_DP))
    sources = sources.reshape(MICRO, N_DP, N_DP).astype(jnp.int32)
    local_maps = jax.vmap(lambda single: jax.random.permutation(single, N_DP))(jax.random.split(second_key, MICRO * N_DP))
    local_maps = jnp.transpose(local_maps.reshape(MICRO, N_DP, N_DP).astype(jnp.int32), (0, 2, 1))
    local_index = jnp.take_along_axis(local_maps, sources, axis=2)
    return (sources * N_DP + local_index).reshape(MICRO, N_DP * N_DP).astype(jnp.int32)


def place_ends(result, key, low, largest):
    dims = result.shape
    index_at = [jax.random.randint(jax.random.fold_in(key, axis), (), 0, dims[axis]) for axis in range(len(dims))]
    result = result.at[tuple(index_at)].set(low)
    longest = dims.index(max(dims))
    index_at[longest] = (index_at[longest] + 1) % dims[longest]
    return result.at[tuple(index_at)].set(largest)


def block_levels(key, dims, cuts, smallest, top_value):
    def one(dim, parts):
        steps = jax.random.uniform(jax.random.fold_in(jax.random.fold_in(key, 6), dim), (parts,), jnp.float32, smallest / len(cuts), top_value / len(cuts))
        return jnp.repeat(jnp.exp(steps), dims[dim] // parts).reshape((-1,) + (1,) * (len(dims) - dim - 1))

    level = one(*cuts[0])
    for cut in cuts[1:]:
        level = level * one(*cut)
    return level


def profile(count, total, most, skew):
    loads = [(1 << 20) // math.isqrt(standing ** skew) + 1 for standing in range(2, count + 1)]
    rest, given = total - most - (count - 1), [1] * (count - 1)
    while rest > 0:
        movable = [i for i in range(count - 1) if given[i] < most]
        mass, left = sum([loads[i] for i in movable]), rest
        for i in movable:
            addition = min(most - given[i], max(1, left * loads[i] // mass), rest)
            given[i] = given[i] + addition
            rest = rest - addition
    return np.array([most] + given)


def ragged_sizes(stream_key, count, total, most, lean):
    if count == 2:
        one = jax.random.randint(stream_key, (), max(1, total - most), min(most, total - 1) + 1)
        return jnp.stack([one, total - one])
    sizes = jnp.asarray(profile(count, total, most, lean), jnp.int32)
    pairs = (count - 1) // 2
    giver, taker = sizes[1:1 + 2 * pairs:2], sizes[2:2 + 2 * pairs:2]
    margin = jnp.minimum(giver - 1, most - taker)
    moved = jax.random.randint(jax.random.fold_in(stream_key, 1), (pairs,), 0, 1 << 20) % (margin + 1)
    sizes = sizes.at[1:1 + 2 * pairs:2].set(giver - moved).at[2:2 + 2 * pairs:2].set(taker + moved)
    return sizes[jax.random.permutation(jax.random.fold_in(stream_key, 2), count)]


def gaussian(own_key, extent, width, bound, cuts=(), dtype=jnp.bfloat16):
    factor_of = block_levels(own_key, extent, cuts, -0.22, 0.18) if cuts else 1.0
    entries = jax.random.normal(own_key, extent, jnp.float32) * width * factor_of
    return jnp.minimum(jnp.maximum(entries, -bound), bound).astype(dtype)


def setup_inputs(seed: int = 0) -> dict:
    seeds = jax.random.split(jax.random.key(seed), 15)
    input_stream = gaussian(seeds[0], (MICRO, TOK_MB, D), 1.0, 6.0, ((1, 8),))
    teacher = gaussian(seeds[1], (MICRO, TOK_MB, D), 1.0, 6.0, ((1, 8), (2, 4)))
    timestep = place_ends(jax.random.randint(seeds[2], (NSEQ,), 0, STEPS), jax.random.fold_in(seeds[2], 1), 0, STEPS - 1).astype(jnp.int32)
    lengths = ragged_sizes(seeds[3], NSEQ, 3 * NSEQ * LEN // 4, LEN, 2).astype(jnp.int32)
    block_perm = draw_block_perm(jax.random.fold_in(seeds[14], 71), 0)
    table = gaussian(seeds[5], (STEPS, D), 0.5, 3.0, ((1, 32),))
    norm_gains = jnp.clip(1.0 + 0.1 * jax.random.normal(seeds[6], (2, D), jnp.float32), 0.5, 1.5).astype(jnp.bfloat16)
    shifts = gaussian(seeds[7], (4, D), 0.3, 1.796875, ((1, 32),))
    w_qkv = gaussian(seeds[8], (D, 3 * D), D ** -0.5, 0.21875, ((0, 8), (1, 4)))
    qv_bias = gaussian(seeds[9], (2, H, DH), 0.3, 1.796875, ((1, 4), (2, 8)))
    w_out = gaussian(seeds[10], (D, D), 3 ** -0.5, 3.5, ((0, 4), (1, 8)))
    w_in = gaussian(seeds[11], (D, FF), D ** -0.5, 0.21875, ((0, 8), (1, 4)))
    in_bias = gaussian(seeds[12], (FF // 128, 128), 0.3, 1.796875, ((0, 4), (1, 8)))
    w_back = gaussian(seeds[13], (FF, D), FF ** -0.5, 0.109375, ((0, 4), (1, 8)))
    return {"input_stream": input_stream, "teacher": teacher, "timestep": timestep, "lengths": lengths, "block_perm": block_perm, "table": table, "norm_gains": norm_gains, "shifts": shifts, "w_qkv": w_qkv, "qv_bias": qv_bias, "w_out": w_out, "w_in": w_in, "in_bias": in_bias, "w_back": w_back}


@jax.custom_vjp
def low(v):
    return lax.optimization_barrier(v.astype(jnp.bfloat16)).astype(jnp.float32)

@jax.custom_vjp
def low_back(v):
    return v

def low_keep(v):
    return (low(v), None)

def low_pass(kept, grad):
    return (grad,)

def back_keep(v):
    return (v, None)

def back_low(kept, grad):
    return (low(grad),)
low.defvjp(low_keep, low_pass)
low_back.defvjp(back_keep, back_low)

def normalize(stream):
    centered = stream - lax.optimization_barrier(jnp.mean(stream, axis=-1, keepdims=True))
    return centered * lax.rsqrt(lax.optimization_barrier(jnp.mean(centered * centered, axis=-1, keepdims=True)) + 1e-05)

def matmul(left, right):
    return jnp.dot(left, right, precision=lax.Precision.HIGHEST, preferred_element_type=jnp.float32)

def encoder_sequence(weights, tokens, table_row, length, target):
    gains, shift_rows, proj_qkv, bias_qv, proj_out, proj_in, bias_in, proj_back = weights
    stream_in = tokens + table_row[None, :]
    normed_in = low(normalize(stream_in) * gains[0] + shift_rows[0])
    projected = matmul(normed_in, proj_qkv).reshape(LEN, H, 3, DH)
    queries = low(low_back(projected[:, :, 0] + bias_qv[0]))
    keys_all = low(low_back(projected[:, :, 1]))
    values = low(low_back(projected[:, :, 2] + bias_qv[1]))
    scores = jnp.einsum('qhe,khe->hqk', queries, keys_all, precision=lax.Precision.HIGHEST)
    scores = low_back(scores * (1.0 / math.sqrt(DH)))
    is_live = jnp.arange(LEN) < length
    scores = jnp.where(is_live[None, None, :], scores, -1e+30)
    probs = low(jax.nn.softmax(scores, axis=-1))
    attended = jnp.einsum('hqk,khe->qhe', probs, values, precision=lax.Precision.HIGHEST).reshape(LEN, D)
    attended = low(low_back(attended))
    branch_attn = low_back(matmul(attended, proj_out) + shift_rows[2])
    stream_mid = stream_in + branch_attn
    normed_mid = low(normalize(stream_mid) * gains[1] + shift_rows[1])
    pre_act = low_back(matmul(normed_mid, proj_in) + bias_in.reshape(FF))
    activation = low(jax.nn.gelu(pre_act, approximate=True))
    branch_mlp = low_back(matmul(activation, proj_back) + shift_rows[3])
    out_rows = stream_mid + branch_mlp
    error_sum = jnp.sum(jnp.where(is_live[:, None], (out_rows - target) ** 2, 0.0))
    return (out_rows, error_sum)

def reference(input_stream, teacher, timestep, lengths, block_perm, table, norm_gains, shifts, w_qkv, qv_bias, w_out, w_in, in_bias, w_back):
    block_rows = LEN // N_DP

    def to_layout(array):
        blocks = array.reshape(MICRO, N_DP * N_DP, block_rows, array.shape[-1])
        moved = jax.vmap(lambda rows, order: rows[order])(blocks, block_perm)
        return moved.reshape(NSEQ, LEN, array.shape[-1])

    def from_layout(array):
        blocks = array.reshape(MICRO, N_DP * N_DP, block_rows, array.shape[-1])
        moved = jax.vmap(lambda rows, order: jnp.zeros_like(rows).at[order].set(rows))(blocks, block_perm)
        return moved.reshape(MICRO, N_DP * LEN, array.shape[-1])
    tokens = to_layout(input_stream).astype(jnp.float32)
    target = to_layout(teacher).astype(jnp.float32)
    valid_count = jnp.sum(lengths).astype(jnp.float32)
    parameters = (table.astype(jnp.float32), norm_gains.astype(jnp.float32), shifts.astype(jnp.float32), w_qkv.astype(jnp.float32), qv_bias.astype(jnp.float32), w_out.astype(jnp.float32), w_in.astype(jnp.float32), in_bias.astype(jnp.float32), w_back.astype(jnp.float32))

    def forward(stream, parameters):
        table_rows = parameters[0][timestep]
        weights = parameters[1:]

        def step_fn(carry, inputs):
            out_rows, error_sum = encoder_sequence(weights, inputs[0], inputs[1], inputs[2], inputs[3])
            return (carry + error_sum, out_rows)
        total_err, outputs = lax.scan(jax.checkpoint(step_fn), jnp.zeros((), jnp.float32), (stream, table_rows, lengths, target))
        return (outputs, total_err / (valid_count * D))
    (outputs, loss), pullback = jax.vjp(forward, tokens, parameters)
    loss_scale = jnp.asarray(NSEQ * LEN * D / 2.0, jnp.float32)
    grad_tokens, gradients = pullback((jnp.zeros_like(outputs), loss_scale))
    return (from_layout(outputs).astype(jnp.bfloat16), loss, from_layout(grad_tokens).astype(jnp.bfloat16), gradients[0], gradients[1], gradients[2], gradients[3], gradients[4], gradients[5], gradients[6], gradients[7], gradients[8])
```

```python
import functools
import math

import jax
import jax.numpy as jnp
from jax import lax
from jax.experimental import pallas as pl
from jax.experimental.pallas import tpu as pltpu
from jax.sharding import PartitionSpec as P

H = 12
DH = 64


epsilon = 1e-05


def normalize_rows(stream):
    centered = stream - jnp.mean(stream, axis=-1, keepdims=True)
    inverse = lax.rsqrt(jnp.mean(centered * centered, axis=-1, keepdims=True) + epsilon)
    return (centered * inverse, inverse)


def column_part(array, start, width):
    return lax.dynamic_slice_in_dim(array, start, width, array.ndim - 1)


def fetch_weights(w_qkv, w_in, w_out, w_back, qv_bias, in_bias):
    return (
        lax.all_gather(w_qkv, "dp", axis=0, tiled=True),
        lax.all_gather(w_in, "dp", axis=0, tiled=True),
        lax.all_gather(w_out, "dp", axis=1, tiled=True),
        lax.all_gather(w_back, "dp", axis=1, tiled=True),
        lax.all_gather(qv_bias, "dp", axis=2, tiled=True),
        lax.all_gather(in_bias, "dp", axis=1, tiled=True),
    )


def invert_map(targets, size):
    ranks = jnp.arange(size, dtype=jnp.int32)
    return jnp.sum(jnp.where(targets[None, :] == ranks[:, None], ranks[None, :], 0), axis=1)


def masked_scores(queries, keys_all, is_live, score_scale):
    scores = (
        jnp.einsum("qhe,khe->hqk", queries, keys_all, preferred_element_type=jnp.float32)
        * score_scale
    )
    return jnp.where(is_live[None, None, :], scores, -1e30)


def attend_rows(keys_all, values, is_live, score_scale, queries):
    scores = masked_scores(queries, keys_all, is_live, score_scale)
    row_top = jnp.max(scores, axis=-1, keepdims=True)
    exponent = jnp.exp(scores - row_top)
    row_total = jnp.sum(exponent, axis=-1, keepdims=True)
    weights_p = (exponent / row_total).astype(jnp.bfloat16)
    mixed = jnp.einsum("hqk,khe->qhe", weights_p, values, preferred_element_type=jnp.float32)
    return (mixed, (row_top + jnp.log(row_total))[..., 0])


def attend_back(keys_all, values, is_live, score_scale, carry, inputs):
    queries, grad_rows, log_total = inputs
    grad_keys, grad_values = carry
    scores = masked_scores(queries, keys_all, is_live, score_scale)
    probabilities = jnp.exp(scores - log_total[..., None])
    grad_probs = jnp.einsum("qhe,khe->hqk", grad_rows, values, preferred_element_type=jnp.float32)
    row_delta = jnp.sum(probabilities * grad_probs, axis=-1, keepdims=True)
    grad_scores = (probabilities * (grad_probs - row_delta)).astype(jnp.bfloat16)
    grad_queries = (
        jnp.einsum("hqk,khe->qhe", grad_scores, keys_all, preferred_element_type=jnp.float32)
        * score_scale
    )
    grad_keys = (
        grad_keys
        + jnp.einsum("hqk,qhe->khe", grad_scores, queries, preferred_element_type=jnp.float32)
        * score_scale
    )
    grad_values = grad_values + jnp.einsum(
        "hqk,qhe->khe",
        probabilities.astype(jnp.bfloat16),
        grad_rows,
        preferred_element_type=jnp.float32,
    )
    return ((grad_keys, grad_values), grad_queries)


def norm_sums(partial_value, normed, gain_full, mp_count):
    weighted = partial_value * gain_full
    sums = jnp.stack([jnp.sum(weighted, axis=1), jnp.sum(weighted * normed, axis=1)], axis=1)
    return jnp.tile(sums, (1, mp_count))


def norm_input_grad(grad_part, gain_part, normed_part, inverse, sums, width):
    scaled = grad_part * gain_part
    return inverse * (scaled - sums[:, 0:1] / width - normed_part * sums[:, 1:2] / width)


def per_device(
    input_stream,
    teacher,
    timestep,
    lengths,
    block_perm,
    table,
    norm_gains,
    shifts,
    w_qkv,
    qv_bias,
    w_out,
    w_in,
    in_bias,
    w_back,
):
    dp_count = lax.axis_size("dp")
    mp_count = lax.axis_size("mp")
    dp_rank = lax.axis_index("dp")
    mp_rank = lax.axis_index("mp")
    micro_count, seq_len, width = input_stream.shape
    part_width = teacher.shape[2]
    block_rows = seq_len // dp_count
    heads_here = H // mp_count
    score_scale = 1.0 / math.sqrt(DH)
    col_start = mp_rank * part_width
    row_block = min(512, seq_len)
    block_count = seq_len // row_block
    valid_count = jnp.sum(lengths).astype(jnp.float32)
    loss_factor = micro_count * dp_count * seq_len / valid_count
    chosen = jnp.take(table, timestep, axis=0)
    gains_full, shifts_full, table_rows = (
        lax.all_gather(norm_gains, ("dp", "mp"), axis=1, tiled=True),
        lax.all_gather(shifts, ("dp", "mp"), axis=1, tiled=True),
        lax.all_gather(chosen, ("dp", "mp"), axis=1, tiled=True),
    )
    gains_full = gains_full.astype(jnp.float32)
    shifts_full = shifts_full.astype(jnp.float32)
    gain_parts = column_part(gains_full, col_start, part_width)
    acc_qkv = jnp.zeros((width, heads_here * 3 * DH), jnp.float32)
    acc_in = jnp.zeros((width, w_in.shape[1]), jnp.float32)
    acc_out = jnp.zeros((heads_here * DH, width), jnp.float32)
    acc_back = jnp.zeros((w_back.shape[0], width), jnp.float32)
    acc_qv = jnp.zeros((2, heads_here, DH), jnp.float32)
    acc_in_bias = jnp.zeros((w_in.shape[1],), jnp.float32)
    acc_gains = jnp.zeros((2, part_width), jnp.float32)
    acc_shifts = jnp.zeros((4, part_width), jnp.float32)
    loss_part = jnp.zeros((), jnp.float32)
    table_sums = []
    outs_y = []
    outs_grad = []
    for micro_index in range(micro_count):
        forward_set = fetch_weights(w_qkv, w_in, w_out, w_back, qv_bias, in_bias)
        proj_qkv, proj_in, proj_out, proj_back, bias_qv, bias_in = forward_set
        bias_qv = bias_qv.astype(jnp.float32)
        bias_in = bias_in.reshape(-1).astype(jnp.float32)
        block_order = block_perm[micro_index].reshape(dp_count, dp_count)
        source = block_order // dp_count
        local_index = block_order % dp_count
        send_index = jnp.sum(jnp.where(source == dp_rank, local_index, 0), axis=1)
        x_blocks = input_stream[micro_index].reshape(dp_count, block_rows, width)
        t_blocks = teacher[micro_index].reshape(dp_count, block_rows, part_width)
        got_x, got_t = (
            lax.all_to_all(
                jnp.take(x_blocks, send_index, axis=0),
                "dp",
                split_axis=0,
                concat_axis=0,
                tiled=True,
            ),
            lax.all_to_all(
                jnp.take(t_blocks, send_index, axis=0),
                "dp",
                split_axis=0,
                concat_axis=0,
                tiled=True,
            ),
        )
        my_source = lax.dynamic_index_in_dim(source, dp_rank, 0, keepdims=False)
        tokens = jnp.take(got_x, my_source, axis=0).reshape(seq_len, width).astype(jnp.float32)
        target = jnp.take(got_t, my_source, axis=0).reshape(seq_len, part_width).astype(jnp.float32)
        seq_index = micro_index * dp_count + dp_rank
        length = lax.dynamic_index_in_dim(lengths, seq_index, 0, keepdims=False)
        table_row = lax.dynamic_index_in_dim(table_rows, seq_index, 0, keepdims=False).astype(
            jnp.float32
        )
        is_live = jnp.arange(seq_len, dtype=jnp.int32) < length
        stream_in = tokens + table_row[None, :]
        normed1, inverse1 = normalize_rows(stream_in)
        normed_in = (normed1 * gains_full[0] + shifts_full[0]).astype(jnp.bfloat16)
        projected = jnp.dot(normed_in, proj_qkv, preferred_element_type=jnp.float32).reshape(
            seq_len, heads_here, 3, DH
        )
        queries = (projected[:, :, 0] + bias_qv[0]).astype(jnp.bfloat16)
        keys_all = projected[:, :, 1].astype(jnp.bfloat16)
        values = (projected[:, :, 2] + bias_qv[1]).astype(jnp.bfloat16)
        query_blocks = queries.reshape(block_count, row_block, heads_here, DH)
        mixed, log_total = lax.map(
            functools.partial(attend_rows, keys_all, values, is_live, score_scale), query_blocks
        )
        attended = mixed.reshape(seq_len, heads_here * DH).astype(jnp.bfloat16)
        attn_part = jnp.dot(attended, proj_out, preferred_element_type=jnp.float32)
        branch_attn = lax.psum_scatter(
            attn_part, "mp", scatter_dimension=1, tiled=True
        ) + column_part(shifts_full[2], col_start, part_width)
        mid_part = column_part(stream_in, col_start, part_width) + branch_attn
        stream_mid = lax.all_gather(mid_part, "mp", axis=1, tiled=True)
        normed2, inverse2 = normalize_rows(stream_mid)
        normed_mid = (normed2 * gains_full[1] + shifts_full[1]).astype(jnp.bfloat16)
        pre_act = jnp.dot(normed_mid, proj_in, preferred_element_type=jnp.float32) + bias_in
        activation = jax.nn.gelu(pre_act, approximate=True).astype(jnp.bfloat16)
        mlp_part = jnp.dot(activation, proj_back, preferred_element_type=jnp.float32)
        mlp_out = lax.psum_scatter(mlp_part, "mp", scatter_dimension=1, tiled=True) + column_part(
            shifts_full[3], col_start, part_width
        )
        out_part = mid_part + mlp_out
        residual_err = jnp.where(is_live[:, None], out_part - target, 0.0)
        loss_part = loss_part + jnp.sum(residual_err * residual_err)
        grad_y = residual_err * loss_factor
        grad_mlp = grad_y.astype(jnp.bfloat16)
        acc_shifts = acc_shifts.at[3].add(jnp.sum(grad_mlp.astype(jnp.float32), axis=0))
        grad_mlp_full = lax.all_gather(grad_mlp, "mp", axis=1, tiled=True)
        back_set = fetch_weights(w_qkv, w_in, w_out, w_back, qv_bias, in_bias)
        back_qkv, back_in, back_out, back_back = (
            back_set[0],
            back_set[1],
            back_set[2],
            back_set[3],
        )
        acc_back = acc_back + jnp.einsum(
            "tf,td->fd", activation, grad_mlp_full, preferred_element_type=jnp.float32
        )
        grad_act = jnp.einsum(
            "td,fd->tf", grad_mlp_full, back_back, preferred_element_type=jnp.float32
        )
        gelu_value, gelu_pull = jax.vjp(lambda inner: jax.nn.gelu(inner, approximate=True), pre_act)
        grad_pre = gelu_pull(grad_act)[0].astype(jnp.bfloat16)
        acc_in_bias = acc_in_bias + jnp.sum(grad_pre.astype(jnp.float32), axis=0)
        acc_in = acc_in + jnp.einsum(
            "td,tf->df", normed_mid, grad_pre, preferred_element_type=jnp.float32
        )
        partial2 = jnp.einsum("tf,df->td", grad_pre, back_in, preferred_element_type=jnp.float32)
        grad_h2, sums2 = (
            lax.psum_scatter(partial2, "mp", scatter_dimension=1, tiled=True),
            lax.psum_scatter(
                norm_sums(partial2, normed2, gains_full[1], mp_count),
                "mp",
                scatter_dimension=1,
                tiled=True,
            ),
        )
        normed2_part = column_part(normed2, col_start, part_width)
        acc_gains = acc_gains.at[1].add(jnp.sum(grad_h2 * normed2_part, axis=0))
        acc_shifts = acc_shifts.at[1].add(jnp.sum(grad_h2, axis=0))
        grad_mid = grad_y + norm_input_grad(
            grad_h2, gain_parts[1], normed2_part, inverse2, sums2, width
        )
        grad_branch = grad_mid.astype(jnp.bfloat16)
        acc_shifts = acc_shifts.at[2].add(jnp.sum(grad_branch.astype(jnp.float32), axis=0))
        grad_branch_full = lax.all_gather(grad_branch, "mp", axis=1, tiled=True)
        acc_out = acc_out + jnp.einsum(
            "tc,td->cd", attended, grad_branch_full, preferred_element_type=jnp.float32
        )
        grad_att = jnp.einsum(
            "td,cd->tc", grad_branch_full, back_out, preferred_element_type=jnp.float32
        ).astype(jnp.bfloat16)
        grad_blocks = grad_att.reshape(block_count, row_block, heads_here, DH)
        zero_heads = jnp.zeros((seq_len, heads_here, DH), jnp.float32)
        (grad_keys, grad_values), grad_queries = lax.scan(
            functools.partial(attend_back, keys_all, values, is_live, score_scale),
            (zero_heads, zero_heads),
            (query_blocks, grad_blocks, log_total),
        )
        grad_queries = grad_queries.reshape(seq_len, heads_here, DH).astype(jnp.bfloat16)
        grad_keys = grad_keys.astype(jnp.bfloat16)
        grad_values = grad_values.astype(jnp.bfloat16)
        acc_qv = acc_qv + jnp.stack(
            [
                jnp.sum(grad_queries.astype(jnp.float32), axis=0),
                jnp.sum(grad_values.astype(jnp.float32), axis=0),
            ]
        )
        grad_qkv_rows = jnp.stack([grad_queries, grad_keys, grad_values], axis=2).reshape(
            seq_len, heads_here * 3 * DH
        )
        acc_qkv = acc_qkv + jnp.einsum(
            "td,tc->dc", normed_in, grad_qkv_rows, preferred_element_type=jnp.float32
        )
        partial1 = jnp.einsum(
            "tc,dc->td", grad_qkv_rows, back_qkv, preferred_element_type=jnp.float32
        )
        grad_h1, sums1 = (
            lax.psum_scatter(partial1, "mp", scatter_dimension=1, tiled=True),
            lax.psum_scatter(
                norm_sums(partial1, normed1, gains_full[0], mp_count),
                "mp",
                scatter_dimension=1,
                tiled=True,
            ),
        )
        normed1_part = column_part(normed1, col_start, part_width)
        acc_gains = acc_gains.at[0].add(jnp.sum(grad_h1 * normed1_part, axis=0))
        acc_shifts = acc_shifts.at[0].add(jnp.sum(grad_h1, axis=0))
        grad_in_stream = grad_mid + norm_input_grad(
            grad_h1, gain_parts[0], normed1_part, inverse1, sums1, width
        )
        table_sums.append(jnp.sum(grad_in_stream, axis=0))
        back_order = invert_map(my_source, dp_count)
        out_blocks = jnp.take(
            out_part.astype(jnp.bfloat16).reshape(dp_count, block_rows, part_width),
            back_order,
            axis=0,
        )
        grad_send = jnp.take(
            grad_in_stream.astype(jnp.bfloat16).reshape(dp_count, block_rows, part_width),
            back_order,
            axis=0,
        )
        home_out, home_grad = (
            lax.all_to_all(out_blocks, "dp", split_axis=0, concat_axis=0, tiled=True),
            lax.all_to_all(grad_send, "dp", split_axis=0, concat_axis=0, tiled=True),
        )
        home_place = invert_map(send_index, dp_count)
        outs_y.append(jnp.take(home_out, home_place, axis=0).reshape(seq_len, part_width))
        outs_grad.append(jnp.take(home_grad, home_place, axis=0).reshape(seq_len, part_width))
    row_sums = jnp.zeros((micro_count, width), jnp.float32)
    row_sums = lax.dynamic_update_slice_in_dim(row_sums, jnp.stack(table_sums), col_start, 1)
    my_steps = jnp.take(timestep, jnp.arange(micro_count, dtype=jnp.int32) * dp_count + dp_rank)
    step_onehot = (
        jnp.arange(table.shape[0], dtype=jnp.int32)[:, None] == my_steps[None, :]
    ).astype(jnp.float32)
    table_grad = jnp.dot(
        step_onehot, row_sums, precision=lax.Precision.HIGHEST, preferred_element_type=jnp.float32
    )
    gains_grad = lax.dynamic_update_slice_in_dim(
        jnp.zeros((2, width), jnp.float32), acc_gains, col_start, 1
    )
    shifts_grad = lax.dynamic_update_slice_in_dim(
        jnp.zeros((4, width), jnp.float32), acc_shifts, col_start, 1
    )
    loss_row = jnp.full((1, dp_count * mp_count), loss_part, jnp.float32)
    grad_table, grad_norm_gains, grad_shifts, loss_cell = (
        lax.psum_scatter(table_grad, ("dp", "mp"), scatter_dimension=1, tiled=True),
        lax.psum_scatter(gains_grad, ("dp", "mp"), scatter_dimension=1, tiled=True),
        lax.psum_scatter(shifts_grad, ("dp", "mp"), scatter_dimension=1, tiled=True),
        lax.psum_scatter(loss_row, ("dp", "mp"), scatter_dimension=1, tiled=True),
    )
    loss = loss_cell[0, 0] / (valid_count * width)
    grad_qkv, grad_in, grad_out, grad_back, grad_qv_bias, grad_in_bias = (
        lax.psum_scatter(acc_qkv, "dp", scatter_dimension=0, tiled=True),
        lax.psum_scatter(acc_in, "dp", scatter_dimension=0, tiled=True),
        lax.psum_scatter(acc_out, "dp", scatter_dimension=1, tiled=True),
        lax.psum_scatter(acc_back, "dp", scatter_dimension=1, tiled=True),
        lax.psum_scatter(acc_qv, "dp", scatter_dimension=2, tiled=True),
        lax.psum_scatter(acc_in_bias.reshape(-1, 128), "dp", scatter_dimension=1, tiled=True),
    )
    y_out = jnp.stack(outs_y)
    grad_x = jnp.stack(outs_grad)
    return (
        y_out,
        loss,
        grad_x,
        grad_table,
        grad_norm_gains,
        grad_shifts,
        grad_qkv,
        grad_qv_bias,
        grad_out,
        grad_in,
        grad_in_bias,
        grad_back,
    )


MESH = pl.DeviceIdType.MESH
BF = jnp.bfloat16
F32 = jnp.float32
VM = pl.BlockSpec(memory_space=pltpu.VMEM)
DP = 8
ROWS = 96
VMEM_LIMIT = 64 * 1024 * 1024 - 65536


def place():
    dp, mp = lax.axis_index("dp"), lax.axis_index("mp")
    x, c = lax.div(mp, 2), lax.rem(mp, 2)
    return dp, mp, x, c


def remote(src, dst, send_sem, recv_sem, dp, mp):
    return pltpu.make_async_remote_copy(
        src_ref=src,
        dst_ref=dst,
        send_sem=send_sem,
        recv_sem=recv_sem,
        device_id=(dp, mp),
        device_id_type=MESH,
    )


def landed(dst, recv_sem, spare, dp, mp):
    remote(dst, dst, spare, recv_sem, dp, mp).wait_recv()


def greet_plane(dp, x, c):
    barrier = pltpu.get_barrier_semaphore()
    pl.semaphore_signal(barrier, inc=1, device_id=(dp, 2 * x + 1 - c), device_id_type=MESH)
    for k in range(DP):
        for xr in range(2):
            if k or xr:
                there = (lax.rem(dp + k, DP), 2 * lax.rem(x + xr, 2) + c)
                pl.semaphore_signal(barrier, inc=1, device_id=there, device_id_type=MESH)
    pl.semaphore_wait(barrier, 2 * DP)


def gather_kernel(
    xs, ts, wsh, small, tok, tea, w, smalls,
    s_tok, r_tok, s_tea, r_tea, s_small, r_small, s_w, r_w, s_core, r_core,
):
    dp, mp, x, c = place()
    z, y = lax.div(dp, 2), lax.rem(dp, 2)
    other = 2 * x + 1 - c
    mine = x * DP + dp
    greet_plane(dp, x, c)
    sent = []

    def go(copy):
        copy.start()
        sent.append(copy)

    pltpu.make_async_copy(xs.at[c, x, dp], tok.at[c, dp], r_tok.at[dp]).start()

    @pl.when(y == x)
    def _():
        pltpu.make_async_copy(xs.at[c, 2, dp], tok.at[c, 8 + z], r_tok.at[8 + z]).start()

    for k in range(1, DP):
        d = lax.rem(dp + k, DP)
        go(remote(xs.at[c, x, d], tok.at[c, dp], s_tok.at[k], r_tok.at[dp], d, mp))

    @pl.when(y == x)
    def _():
        for k in range(1, DP):
            d = lax.rem(dp + k, DP)
            remote(xs.at[c, 2, d], tok.at[c, 8 + z], s_tok.at[8 + k], r_tok.at[8 + z], d, mp).start()

    pltpu.make_async_copy(small, smalls.at[mp, dp], r_small.at[mine]).start()
    for k in range(DP):
        for xr in range(2):
            if k or xr:
                d, m = lax.rem(dp + k, DP), 2 * lax.rem(x + xr, 2) + c
                go(remote(small, smalls.at[mp, dp], s_small.at[2 * k + xr], r_small.at[mine], d, m))

    mx, dy = 2 * (1 - x) + c, 2 * z + 1 - y
    for p in range(3):
        pltpu.make_async_copy(wsh.at[p], w.at[p, mine], r_w.at[p, mine]).start()
        for k in range(1, 4):
            zz = lax.rem(z + k, 4)
            go(remote(wsh.at[p], w.at[p, mine], s_w.at[p, k - 1], r_w.at[p, mine], 2 * zz + y, mp))
        go(remote(wsh.at[p], w.at[p, mine], s_w.at[p, 3], r_w.at[p, mine], dp, mx))
        go(remote(wsh.at[p], w.at[p, mine], s_w.at[p, 4], r_w.at[p, mine], dy, mp))

    def spread(p):
        for k in range(1, 4):
            b = x * DP + 2 * lax.rem(z + k, 4) + y
            landed(w.at[p, b], r_w.at[p, b], s_w.at[p, 0], dp, mp)
            go(remote(w.at[p, b], w.at[p, b], s_w.at[p, 3 + 2 * k], r_w.at[p, b], dp, mx))
            go(remote(w.at[p, b], w.at[p, b], s_w.at[p, 4 + 2 * k], r_w.at[p, b], dy, mp))

    def relay(p):
        for k in range(4):
            bx, by = (1 - x) * DP + 2 * k + y, x * DP + 2 * k + 1 - y
            landed(w.at[p, bx], r_w.at[p, bx], s_w.at[p, 0], dp, mp)
            landed(w.at[p, by], r_w.at[p, by], s_w.at[p, 0], dp, mp)
            if k < 2:
                go(remote(w.at[p, bx], w.at[p, bx], s_w.at[p, 11 + k], r_w.at[p, bx], dy, mp))
            else:
                go(remote(w.at[p, by], w.at[p, by], s_w.at[p, 11 + k], r_w.at[p, by], dp, mx))

    spread(0)

    pltpu.make_async_copy(ts.at[x, dp], tea.at[mp, dp], r_tea.at[x, dp]).start()
    for k in range(DP):
        d = lax.rem(dp + k, DP)
        for xr in range(2):
            if k or xr:
                xx = lax.rem(x + xr, 2)
                go(remote(ts.at[xx, d], tea.at[mp, dp], s_tea.at[2 * k + xr], r_tea.at[x, dp], d, 2 * xx + c))
        if k:
            go(remote(ts.at[2, d], tea.at[mp, 8 + z], s_tea.at[16 + k], r_tea.at[x, 8 + z], d, 2 * y + c))

    @pl.when(y == x)
    def _():
        pltpu.make_async_copy(ts.at[2, dp], tea.at[mp, 8 + z], r_tea.at[x, 8 + z]).start()

    @pl.when(y != x)
    def _():
        copy = remote(ts.at[2, dp], tea.at[mp, 8 + z], s_tea.at[16], r_tea.at[x, 8 + z], dp, 2 * y + c)
        copy.start()
        copy.wait_send()

    spread(1)
    relay(0)
    spread(2)

    for j in range(12):
        landed(tok.at[c, j], r_tok.at[j], s_tok.at[0], dp, mp)
    go(remote(tok.at[c], tok.at[c], s_core.at[0], r_core.at[0], dp, other))
    for j in range(8):
        for xx in range(2):
            m = 2 * xx + c
            landed(smalls.at[m, j], r_small.at[xx * DP + j], s_small.at[0], dp, mp)
    go(remote(smalls.at[c], smalls.at[c], s_core.at[1], r_core.at[1], dp, other))
    go(remote(smalls.at[2 + c], smalls.at[2 + c], s_core.at[2], r_core.at[2], dp, other))

    relay(1)
    relay(2)

    for xx in range(2):
        for j in range(12):
            landed(tea.at[2 * xx + c, j], r_tea.at[xx, j], s_tea.at[0], dp, mp)
    go(remote(tea.at[c], tea.at[c], s_core.at[3], r_core.at[3], dp, other))
    go(remote(tea.at[2 + c], tea.at[2 + c], s_core.at[4], r_core.at[4], dp, other))

    for p in range(3):
        landed(w.at[p, mine], r_w.at[p, mine], s_w.at[p, 0], dp, mp)
        for k in range(4):
            b = (1 - x) * DP + 2 * k + 1 - y
            landed(w.at[p, b], r_w.at[p, b], s_w.at[p, 0], dp, mp)
    o = 1 - c
    landed(tok.at[o], r_core.at[0], s_core.at[0], dp, mp)
    landed(smalls.at[o], r_core.at[1], s_core.at[0], dp, mp)
    landed(smalls.at[2 + o], r_core.at[2], s_core.at[0], dp, mp)
    landed(tea.at[o], r_core.at[3], s_core.at[0], dp, mp)
    landed(tea.at[2 + o], r_core.at[4], s_core.at[0], dp, mp)
    for copy in sent:
        copy.wait_send()

    @pl.when(y == x)
    def _():
        for k in range(1, DP):
            d = lax.rem(dp + k, DP)
            remote(xs.at[c, 2, d], tok.at[c, 8 + z], s_tok.at[8 + k], r_tok.at[8 + z], d, mp).wait_send()


def gather_all(xs, ts, wsh, small):
    dma = pltpu.SemaphoreType.DMA
    return pl.pallas_call(
        gather_kernel,
        name="gather_all",
        out_shape=(
            jax.ShapeDtypeStruct((2, 12, 64, 384), BF),
            jax.ShapeDtypeStruct((4, 12, 64, 192), BF),
            jax.ShapeDtypeStruct((3, 16, ROWS, 768), BF),
            jax.ShapeDtypeStruct((4, DP, 32, 128), BF),
        ),
        in_specs=[VM] * 4,
        out_specs=(VM,) * 4,
        scratch_shapes=[
            dma((16,)), dma((12,)), dma((24,)), dma((2, 12)), dma((16,)), dma((16,)),
            dma((3, 15)), dma((3, 16)), dma((5,)), dma((5,)),
        ],
        compiler_params=pltpu.CompilerParams(
            collective_id=1, has_side_effects=True, vmem_limit_bytes=VMEM_LIMIT
        ),
    )(xs, ts, wsh, small)


def swap_kernel(along_x, a, b, send_sem, recv_sem):
    dp, mp, x, c = place()
    peer = 2 * (1 - x) + c if along_x else 2 * x + 1 - c
    barrier = pltpu.get_barrier_semaphore()
    pl.semaphore_signal(barrier, inc=1, device_id=(dp, peer), device_id_type=MESH)
    pl.semaphore_wait(barrier, 1)
    copy = remote(a, b, send_sem, recv_sem, dp, peer)
    copy.start()
    copy.wait()


def swap(array, along_x, number):
    return pl.pallas_call(
        functools.partial(swap_kernel, along_x),
        name=f"swap_{number}",
        out_shape=jax.ShapeDtypeStruct(array.shape, array.dtype),
        in_specs=[VM],
        out_specs=VM,
        scratch_shapes=[pltpu.SemaphoreType.DMA(()), pltpu.SemaphoreType.DMA(())],
        compiler_params=pltpu.CompilerParams(collective_id=number, has_side_effects=True),
    )(array)


def reduce_kernel(
    g, msg, yg, gs, msgs, back,
    s1, r1, s2, r2, s3, r3,
    s_msg, r_msg, s_yg, r_yg, s_a, r_a, s_b, r_b, s_c, r_c,
):
    dp, mp, x, c = place()
    z, y = lax.div(dp, 2), lax.rem(dp, 2)
    mine = x * DP + dp
    greet_plane(dp, x, c)
    sent = []

    def go(copy):
        copy.start()
        sent.append(copy)

    mx, dy = 2 * (1 - x) + c, 2 * z + 1 - y

    def first(p):
        for k in range(4):
            b = (1 - x) * DP + 2 * k + 1 - y
            s1[p, k] = g[p, b].astype(BF)
            there = (dp, mx) if k < 2 else (dy, mp)
            go(remote(s1.at[p, k], r1.at[p, k], s_a.at[p, k], r_a.at[p, k], *there))

    def second(p):
        for k in range(4):
            bx, by = (1 - x) * DP + 2 * k + y, x * DP + 2 * k + 1 - y
            landed(r1.at[p, k], r_a.at[p, k], s_a.at[p, k], dp, mp)
            extra = r1[p, k].astype(F32)
            gx, gy = g[p, bx], g[p, by]
            if k < 2:
                gy = gy + extra
            else:
                gx = gx + extra
            s2[p, 0, k] = gx.astype(BF)
            s2[p, 1, k] = gy.astype(BF)
            go(remote(s2.at[p, 0, k], r2.at[p, 0, k], s_b.at[p, 0, k], r_b.at[p, 0, k], dp, mx))
            go(remote(s2.at[p, 1, k], r2.at[p, 1, k], s_b.at[p, 1, k], r_b.at[p, 1, k], dy, mp))

    def third(p):
        for k in range(1, 5):
            zz = lax.rem(z + k, 4)
            b = x * DP + 2 * zz + y
            for side in range(2):
                landed(r2.at[p, side, zz], r_b.at[p, side, zz], s_b.at[p, side, 0], dp, mp)
            total = g[p, b] + r2[p, 0, zz].astype(F32) + r2[p, 1, zz].astype(F32)
            if k < 4:
                s3[p, k - 1] = total.astype(BF)
                go(remote(s3.at[p, k - 1], r3.at[p, k - 1], s_c.at[p, k - 1], r_c.at[p, k - 1], 2 * zz + y, mp))
            else:
                gs[p] = total

    def last(p):
        for k in range(3):
            landed(r3.at[p, k], r_c.at[p, k], s_c.at[p, k], dp, mp)
        gs[p] = gs[p] + (r3[p, 0].astype(F32) + r3[p, 1].astype(F32) + r3[p, 2].astype(F32))

    first(2)
    first(1)
    pltpu.make_async_copy(msg.at[mine], msgs.at[mine], r_msg.at[mine]).start()
    for k in range(DP):
        for xr in range(2):
            if k or xr:
                d, xx = lax.rem(dp + k, DP), lax.rem(x + xr, 2)
                go(remote(msg.at[xx * DP + d], msgs.at[mine], s_msg.at[2 * k + xr], r_msg.at[mine], d, 2 * xx + c))
    second(2)
    first(0)
    second(1)
    third(2)

    pltpu.make_async_copy(yg.at[:, mp, dp], back.at[:, x, dp], r_yg.at[x, dp]).start()
    for k in range(DP):
        s = lax.rem(dp + k, DP)
        for xr in range(2):
            if k or xr:
                m = 2 * lax.rem(x + xr, 2) + c
                go(remote(yg.at[:, m, s], back.at[:, x, dp], s_yg.at[2 * k + xr], r_yg.at[x, dp], s, m))
    for k in range(4):
        j = lax.rem(z + k, 4)
        for xr in range(2):
            m = 2 * lax.rem(x + xr, 2) + c
            if k or xr:
                go(remote(yg.at[:, m, 8 + j], back.at[:, 2, dp], s_yg.at[16 + 2 * k + xr], r_yg.at[2, dp], 2 * j + x, m))

    @pl.when(y == x)
    def _():
        pltpu.make_async_copy(yg.at[:, mp, 8 + z], back.at[:, 2, dp], r_yg.at[2, dp]).start()

    @pl.when(y != x)
    def _():
        copy = remote(yg.at[:, mp, 8 + z], back.at[:, 2, dp], s_yg.at[16], r_yg.at[2, dp], 2 * z + x, mp)
        copy.start()
        copy.wait_send()

    second(0)
    third(1)
    third(0)
    last(2)
    last(1)
    last(0)
    for j in range(16):
        landed(msgs.at[j], r_msg.at[j], s_msg.at[0], dp, mp)
    for m in range(3):
        for j in range(DP):
            landed(back.at[:, m, j], r_yg.at[m, j], s_yg.at[0], dp, mp)
    for copy in sent:
        copy.wait_send()


def reduce_all(g, msg, yg):
    dma = pltpu.SemaphoreType.DMA
    block = (ROWS, 768)
    return pl.pallas_call(
        reduce_kernel,
        name="reduce_all",
        out_shape=(
            jax.ShapeDtypeStruct((3, ROWS, 768), F32),
            jax.ShapeDtypeStruct((16, 16, 128), F32),
            jax.ShapeDtypeStruct((2, 3, DP, 64, 192), BF),
        ),
        in_specs=[VM] * 3,
        out_specs=(VM,) * 3,
        scratch_shapes=[
            pltpu.VMEM((3, 4) + block, BF), pltpu.VMEM((3, 4) + block, BF),
            pltpu.VMEM((3, 2, 4) + block, BF), pltpu.VMEM((3, 2, 4) + block, BF),
            pltpu.VMEM((3, 3) + block, BF), pltpu.VMEM((3, 3) + block, BF),
            dma((16,)), dma((16,)), dma((24,)), dma((3, DP)), dma((3, 4)), dma((3, 4)),
            dma((3, 2, 4)), dma((3, 2, 4)), dma((3, 3)), dma((3, 3)),
        ],
        compiler_params=pltpu.CompilerParams(
            collective_id=2, has_side_effects=True, vmem_limit_bytes=VMEM_LIMIT
        ),
    )(g, msg, yg)


def dot(a, b, dims):
    return lax.dot_general(a, b, (dims, ((), ())), preferred_element_type=F32)


def per_device_compact(
    input_stream, teacher, timestep, lengths, block_perm, table, norm_gains, shifts,
    w_qkv, qv_bias, w_out, w_in, in_bias, w_back,
):
    dp, mp, x, c = place()
    seq_len, width, quarter = input_stream.shape[1], input_stream.shape[2], teacher.shape[2]
    score_scale = 1.0 / math.sqrt(DH)
    valid_count = jnp.sum(lengths).astype(F32)
    loss_factor = 3 * DP * seq_len / valid_count

    order = block_perm.reshape(3, DP, DP)
    source, local = order // DP, order % DP
    send_index = jnp.sum(jnp.where(source == dp, local, 0), axis=2)
    my_source = lax.dynamic_index_in_dim(source, dp, 1, keepdims=False)
    ranks = jnp.arange(DP, dtype=jnp.int32)
    where_block = jnp.sum(
        jnp.where(my_source[:, None, :] == ranks[None, :, None], ranks[None, None, :], 0), axis=2
    )
    micro = jnp.arange(3)[:, None]
    x_blocks = input_stream.reshape(3, DP, 64, 2, 384).transpose(3, 0, 1, 2, 4)[:, micro, send_index]
    t_blocks = teacher.reshape(3, DP, 64, quarter)[micro, send_index]
    half_block = lax.dynamic_index_in_dim(where_block[2].reshape(4, 2), x, 1, keepdims=False)
    their_block = lax.dynamic_index_in_dim(where_block[2].reshape(4, 2), 1 - x, 1, keepdims=False)
    first_block = lax.dynamic_index_in_dim(where_block, x, 0, keepdims=False)
    length_a = lax.dynamic_index_in_dim(lengths, x * DP + dp, 0, keepdims=False)
    length_c = lax.dynamic_index_in_dim(lengths, 2 * DP + dp, 0, keepdims=False)
    inside = jnp.arange(64, dtype=jnp.int32)
    live_a = ((first_block[:, None] * 64 + inside[None]) < length_a).reshape(512)
    live_c = ((half_block[:, None] * 64 + inside[None]) < length_c).reshape(256)
    live_d = ((their_block[:, None] * 64 + inside[None]) < length_c).reshape(256)
    live = jnp.concatenate([live_a, live_c])
    keys_live_c = jnp.concatenate([live_c, live_d])

    wsh = jnp.stack([jnp.concatenate([w_qkv, w_out.T], axis=1), w_in, w_back.T])
    chosen = jnp.take(table, timestep, axis=0)
    small = jnp.zeros((32, 128), BF)
    small = small.at[:30, :24].set(jnp.concatenate([norm_gains, shifts, chosen]))
    small = small.at[30, :48].set(qv_bias.reshape(48)).at[31, :96].set(in_bias.reshape(96))

    tok, tea, w, smalls = gather_all(x_blocks, t_blocks, wsh, small)

    tokens = tok.transpose(1, 2, 0, 3).reshape(768, width).astype(F32)
    target = tea.transpose(1, 2, 0, 3).reshape(768, width).astype(F32)
    w = w.reshape(3, 2, width, 768)
    vectors = smalls[:, :, :30, :24].transpose(2, 1, 0, 3).reshape(30, width).astype(F32)
    my_small = jnp.stack(
        [lax.dynamic_index_in_dim(smalls, 2 * k + c, 0, keepdims=False) for k in range(2)]
    ).astype(F32)
    bias_qv = my_small[:, :, 30, :48].reshape(2, DP, 2, 3, 8).transpose(2, 0, 3, 1, 4).reshape(2, 6, DH)
    bias_in = my_small[:, :, 31, :96].reshape(2, DP, 6, 16).transpose(0, 2, 1, 3).reshape(2 * 768)
    gains, shift_rows = vectors[0:2], vectors[2:6]
    row_a = lax.dynamic_index_in_dim(vectors, 6 + x * DP + dp, 0, keepdims=False)
    row_c = lax.dynamic_index_in_dim(vectors, 6 + 2 * DP + dp, 0, keepdims=False)
    is_a = jnp.arange(768)[:, None] < 512
    stream_in = tokens + jnp.where(is_a, row_a[None], row_c[None])
    normed1, inverse1 = normalize_rows(stream_in)
    normed_in = (normed1 * gains[0] + shift_rows[0]).astype(BF)
    proj = w[0].transpose(1, 0, 2)[:, :, :576].reshape(width, 1152)
    out_t = w[0].transpose(1, 0, 2)[:, :, 576:].reshape(width, 384)
    in_w = w[1].transpose(1, 0, 2).reshape(width, 1536)
    back_t = w[2].transpose(1, 0, 2).reshape(width, 1536)
    projected = dot(normed_in, proj, ((1,), (0,))).reshape(768, 6, 3, DH)
    queries = (projected[:, :, 0] + bias_qv[0]).astype(BF)
    keys = projected[:, :, 1].astype(BF)
    values = (projected[:, :, 2] + bias_qv[1]).astype(BF)
    kv = jnp.concatenate([keys[512:].reshape(256, 384), values[512:].reshape(256, 384)], axis=1)
    kv = swap(kv, True, 3)
    keys_c = jnp.concatenate([keys[512:], kv[:, :384].reshape(256, 6, DH)])
    values_c = jnp.concatenate([values[512:], kv[:, 384:].reshape(256, 6, DH)])
    mixed_a, log_a = attend_rows(keys[:512], values[:512], live_a, score_scale, queries[:512])
    mixed_c, log_c = attend_rows(keys_c, values_c, keys_live_c, score_scale, queries[512:])
    attended = jnp.concatenate([mixed_a, mixed_c]).reshape(768, 384).astype(BF)
    part = dot(attended, out_t, ((1,), (1,)))
    stream_mid = stream_in + (part + swap(part, False, 4) + shift_rows[2])
    normed2, inverse2 = normalize_rows(stream_mid)
    normed_mid = (normed2 * gains[1] + shift_rows[1]).astype(BF)
    pre_act = dot(normed_mid, in_w, ((1,), (0,))) + bias_in
    gelu = functools.partial(jax.nn.gelu, approximate=True)
    activation = gelu(pre_act).astype(BF)
    part = dot(activation, back_t, ((1,), (1,)))
    out = stream_mid + (part + swap(part, False, 5) + shift_rows[3])
    residual = jnp.where(live[:, None], out - target, 0.0)
    loss_part = jnp.sum(residual * residual)
    grad_y = residual * loss_factor
    grad_mlp = grad_y.astype(BF)
    g_shift3 = jnp.sum(grad_mlp.astype(F32), axis=0)
    g_back = dot(grad_mlp, activation, ((0,), (0,)))
    grad_act = dot(grad_mlp, back_t, ((1,), (0,)))
    grad_pre = jax.vjp(gelu, pre_act)[1](grad_act)[0].astype(BF)
    g_in_bias = jnp.sum(grad_pre.astype(F32), axis=0)
    g_in = dot(normed_mid, grad_pre, ((0,), (0,)))
    part = dot(grad_pre, in_w, ((1,), (1,)))
    grad_h2 = part + swap(part, False, 6)
    g_gain1, g_shift1 = jnp.sum(grad_h2 * normed2, axis=0), jnp.sum(grad_h2, axis=0)
    g = grad_h2 * gains[1]
    grad_mid = grad_y + inverse2 * (
        g - jnp.mean(g, axis=1, keepdims=True) - normed2 * jnp.mean(g * normed2, axis=1, keepdims=True)
    )
    grad_branch = grad_mid.astype(BF)
    g_shift2 = jnp.sum(grad_branch.astype(F32), axis=0)
    g_out = dot(grad_branch, attended, ((0,), (0,)))
    grad_att = dot(grad_branch, out_t, ((1,), (0,))).astype(BF).reshape(768, 6, DH)
    zero = jnp.zeros((512, 6, DH), F32)
    (gk_a, gv_a), gq_a = attend_back(
        keys[:512], values[:512], live_a, score_scale, (zero, zero), (queries[:512], grad_att[:512], log_a)
    )
    (gk_c, gv_c), gq_c = attend_back(
        keys_c, values_c, keys_live_c, score_scale, (zero, zero), (queries[512:], grad_att[512:], log_c)
    )
    gkv = jnp.concatenate([gk_c[256:].reshape(256, 384), gv_c[256:].reshape(256, 384)], axis=1)
    gkv = swap(gkv.astype(BF), True, 7).astype(F32)
    gk = jnp.concatenate([gk_a, gk_c[:256] + gkv[:, :384].reshape(256, 6, DH)]).astype(BF)
    gv = jnp.concatenate([gv_a, gv_c[:256] + gkv[:, 384:].reshape(256, 6, DH)]).astype(BF)
    gq = jnp.concatenate([gq_a, gq_c]).astype(BF)
    g_qb, g_vb = jnp.sum(gq.astype(F32), axis=0), jnp.sum(gv.astype(F32), axis=0)
    rows = jnp.stack([gq, gk, gv], axis=2).reshape(768, 1152)
    g_qkv = dot(normed_in, rows, ((0,), (0,)))
    part = dot(rows, proj, ((1,), (1,)))
    grad_h1 = part + swap(part, False, 8)
    g_gain0, g_shift0 = jnp.sum(grad_h1 * normed1, axis=0), jnp.sum(grad_h1, axis=0)
    g = grad_h1 * gains[0]
    grad_in = grad_mid + inverse1 * (
        g - jnp.mean(g, axis=1, keepdims=True) - normed1 * jnp.mean(g * normed1, axis=1, keepdims=True)
    )
    table_a, table_c = jnp.sum(grad_in[:512], axis=0), jnp.sum(grad_in[512:], axis=0)

    sums = jnp.stack(
        [g_gain0, g_gain1, g_shift0, g_shift1, g_shift2, g_shift3, table_a, table_c]
    ).reshape(8, DP, 2, 2, 24)
    sums = lax.dynamic_index_in_dim(sums, c, 3, keepdims=False).transpose(2, 1, 0, 3).reshape(16, 8, 24)
    msg = jnp.zeros((16, 16, 128), F32)
    msg = msg.at[:, :8, :24].set(sums).at[:, 8, 0].set(loss_part)
    qvb = jnp.stack([g_qb, g_vb]).reshape(2, 2, 3, DP, 8).transpose(1, 3, 0, 2, 4).reshape(16, 48)
    inb = g_in_bias.reshape(2, 6, DP, 16).transpose(0, 2, 1, 3).reshape(16, 96)
    msg = msg.at[:, 9, :48].set(qvb).at[:, 10, :96].set(inb)
    grads = jnp.stack(
        [
            jnp.concatenate([g_qkv.reshape(width, 2, 576), g_out.reshape(width, 2, 192)], axis=2),
            g_in.reshape(width, 2, 768),
            g_back.reshape(width, 2, 768),
        ]
    ).transpose(0, 2, 1, 3).reshape(3, 16, ROWS, 768)
    yg = jnp.stack([out, grad_in]).astype(BF).reshape(2, 12, 64, 4, quarter).transpose(0, 3, 1, 2, 4)
    gs, msgs, home = reduce_all(grads, msg, yg)

    place_home = jnp.sum(
        jnp.where(send_index[:, None, :] == ranks[None, :, None], ranks[None, None, :], 0), axis=2
    )
    home = home[:, micro, place_home].reshape(2, 3, seq_len, quarter)
    total = jnp.sum(msgs, axis=0)
    loss = total[8, 0] / (valid_count * width)
    rows_a = msgs[:, 6, :24].reshape(16, 24)
    rows_c = msgs[:DP, 7, :24] + msgs[DP:, 7, :24]
    seq_rows = jnp.concatenate([rows_a, rows_c])
    onehot = (jnp.arange(table.shape[0], dtype=jnp.int32)[:, None] == timestep[None, :]).astype(F32)
    grad_table = jnp.dot(onehot, seq_rows, precision=lax.Precision.HIGHEST, preferred_element_type=F32)
    return (
        home[0],
        loss,
        home[1],
        grad_table,
        total[0:2, :24],
        total[2:6, :24],
        gs[0, :, :576],
        total[9, :48].reshape(2, 3, 8),
        gs[0, :, 576:].T,
        gs[1],
        total[10, :96].reshape(6, 16),
        gs[2].T,
    )


def solution(mesh):
    compact = mesh.shape["dp"] == 8 and mesh.shape["mp"] == 4
    return jax.shard_map(
        per_device_compact if compact else per_device,
        mesh=mesh,
        in_specs=(
            P(None, "dp", None),
            P(None, "dp", "mp"),
            P(),
            P(),
            P(),
            P(None, ("dp", "mp")),
            P(None, ("dp", "mp")),
            P(None, ("dp", "mp")),
            P("dp", "mp"),
            P(None, "mp", "dp"),
            P("mp", "dp"),
            P("dp", "mp"),
            P("mp", "dp"),
            P("mp", "dp"),
        ),
        out_specs=(
            P(None, "dp", "mp"),
            P(),
            P(None, "dp", "mp"),
            P(None, ("dp", "mp")),
            P(None, ("dp", "mp")),
            P(None, ("dp", "mp")),
            P("dp", "mp"),
            P(None, "mp", "dp"),
            P("mp", "dp"),
            P("dp", "mp"),
            P("mp", "dp"),
            P("mp", "dp"),
        ),
        check_vma=False,
    )
```

```python
import functools
import math

import jax
import jax.numpy as jnp
from jax import lax
from jax.experimental import pallas as pl
from jax.experimental.pallas import tpu as pltpu
from jax.sharding import PartitionSpec as P

H = 12
DH = 64


epsilon = 1e-05


def normalize_rows(stream):
    centered = stream - jnp.mean(stream, axis=-1, keepdims=True)
    inverse = lax.rsqrt(jnp.mean(centered * centered, axis=-1, keepdims=True) + epsilon)
    return (centered * inverse, inverse)


def column_part(array, start, width):
    return lax.dynamic_slice_in_dim(array, start, width, array.ndim - 1)


def fetch_weights(w_qkv, w_in, w_out, w_back, qv_bias, in_bias):
    return (
        lax.all_gather(w_qkv, "dp", axis=0, tiled=True),
        lax.all_gather(w_in, "dp", axis=0, tiled=True),
        lax.all_gather(w_out, "dp", axis=1, tiled=True),
        lax.all_gather(w_back, "dp", axis=1, tiled=True),
        lax.all_gather(qv_bias, "dp", axis=2, tiled=True),
        lax.all_gather(in_bias, "dp", axis=1, tiled=True),
    )


def invert_map(targets, size):
    ranks = jnp.arange(size, dtype=jnp.int32)
    return jnp.sum(jnp.where(targets[None, :] == ranks[:, None], ranks[None, :], 0), axis=1)


def masked_scores(queries, keys_all, is_live, score_scale):
    scores = (
        jnp.einsum("qhe,khe->hqk", queries, keys_all, preferred_element_type=jnp.float32)
        * score_scale
    )
    return jnp.where(is_live[None, None, :], scores, -1e30)


def attend_rows(keys_all, values, is_live, score_scale, queries):
    scores = masked_scores(queries, keys_all, is_live, score_scale)
    row_top = jnp.max(scores, axis=-1, keepdims=True)
    exponent = jnp.exp(scores - row_top)
    row_total = jnp.sum(exponent, axis=-1, keepdims=True)
    weights_p = (exponent / row_total).astype(jnp.bfloat16)
    mixed = jnp.einsum("hqk,khe->qhe", weights_p, values, preferred_element_type=jnp.float32)
    return (mixed, (row_top + jnp.log(row_total))[..., 0])


def attend_back(keys_all, values, is_live, score_scale, carry, inputs):
    queries, grad_rows, log_total = inputs
    grad_keys, grad_values = carry
    scores = masked_scores(queries, keys_all, is_live, score_scale)
    probabilities = jnp.exp(scores - log_total[..., None])
    grad_probs = jnp.einsum("qhe,khe->hqk", grad_rows, values, preferred_element_type=jnp.float32)
    row_delta = jnp.sum(probabilities * grad_probs, axis=-1, keepdims=True)
    grad_scores = (probabilities * (grad_probs - row_delta)).astype(jnp.bfloat16)
    grad_queries = (
        jnp.einsum("hqk,khe->qhe", grad_scores, keys_all, preferred_element_type=jnp.float32)
        * score_scale
    )
    grad_keys = (
        grad_keys
        + jnp.einsum("hqk,qhe->khe", grad_scores, queries, preferred_element_type=jnp.float32)
        * score_scale
    )
    grad_values = grad_values + jnp.einsum(
        "hqk,qhe->khe",
        probabilities.astype(jnp.bfloat16),
        grad_rows,
        preferred_element_type=jnp.float32,
    )
    return ((grad_keys, grad_values), grad_queries)


def norm_sums(partial_value, normed, gain_full, mp_count):
    weighted = partial_value * gain_full
    sums = jnp.stack([jnp.sum(weighted, axis=1), jnp.sum(weighted * normed, axis=1)], axis=1)
    return jnp.tile(sums, (1, mp_count))


def norm_input_grad(grad_part, gain_part, normed_part, inverse, sums, width):
    scaled = grad_part * gain_part
    return inverse * (scaled - sums[:, 0:1] / width - normed_part * sums[:, 1:2] / width)


def per_device(
    input_stream,
    teacher,
    timestep,
    lengths,
    block_perm,
    table,
    norm_gains,
    shifts,
    w_qkv,
    qv_bias,
    w_out,
    w_in,
    in_bias,
    w_back,
):
    dp_count = lax.axis_size("dp")
    mp_count = lax.axis_size("mp")
    dp_rank = lax.axis_index("dp")
    mp_rank = lax.axis_index("mp")
    micro_count, seq_len, width = input_stream.shape
    part_width = teacher.shape[2]
    block_rows = seq_len // dp_count
    heads_here = H // mp_count
    score_scale = 1.0 / math.sqrt(DH)
    col_start = mp_rank * part_width
    row_block = min(512, seq_len)
    block_count = seq_len // row_block
    valid_count = jnp.sum(lengths).astype(jnp.float32)
    loss_factor = micro_count * dp_count * seq_len / valid_count
    chosen = jnp.take(table, timestep, axis=0)
    gains_full, shifts_full, table_rows = (
        lax.all_gather(norm_gains, ("dp", "mp"), axis=1, tiled=True),
        lax.all_gather(shifts, ("dp", "mp"), axis=1, tiled=True),
        lax.all_gather(chosen, ("dp", "mp"), axis=1, tiled=True),
    )
    gains_full = gains_full.astype(jnp.float32)
    shifts_full = shifts_full.astype(jnp.float32)
    gain_parts = column_part(gains_full, col_start, part_width)
    acc_qkv = jnp.zeros((width, heads_here * 3 * DH), jnp.float32)
    acc_in = jnp.zeros((width, w_in.shape[1]), jnp.float32)
    acc_out = jnp.zeros((heads_here * DH, width), jnp.float32)
    acc_back = jnp.zeros((w_back.shape[0], width), jnp.float32)
    acc_qv = jnp.zeros((2, heads_here, DH), jnp.float32)
    acc_in_bias = jnp.zeros((w_in.shape[1],), jnp.float32)
    acc_gains = jnp.zeros((2, part_width), jnp.float32)
    acc_shifts = jnp.zeros((4, part_width), jnp.float32)
    loss_part = jnp.zeros((), jnp.float32)
    table_sums = []
    outs_y = []
    outs_grad = []
    for micro_index in range(micro_count):
        forward_set = fetch_weights(w_qkv, w_in, w_out, w_back, qv_bias, in_bias)
        proj_qkv, proj_in, proj_out, proj_back, bias_qv, bias_in = forward_set
        bias_qv = bias_qv.astype(jnp.float32)
        bias_in = bias_in.reshape(-1).astype(jnp.float32)
        block_order = block_perm[micro_index].reshape(dp_count, dp_count)
        source = block_order // dp_count
        local_index = block_order % dp_count
        send_index = jnp.sum(jnp.where(source == dp_rank, local_index, 0), axis=1)
        x_blocks = input_stream[micro_index].reshape(dp_count, block_rows, width)
        t_blocks = teacher[micro_index].reshape(dp_count, block_rows, part_width)
        got_x, got_t = (
            lax.all_to_all(
                jnp.take(x_blocks, send_index, axis=0),
                "dp",
                split_axis=0,
                concat_axis=0,
                tiled=True,
            ),
            lax.all_to_all(
                jnp.take(t_blocks, send_index, axis=0),
                "dp",
                split_axis=0,
                concat_axis=0,
                tiled=True,
            ),
        )
        my_source = lax.dynamic_index_in_dim(source, dp_rank, 0, keepdims=False)
        tokens = jnp.take(got_x, my_source, axis=0).reshape(seq_len, width).astype(jnp.float32)
        target = jnp.take(got_t, my_source, axis=0).reshape(seq_len, part_width).astype(jnp.float32)
        seq_index = micro_index * dp_count + dp_rank
        length = lax.dynamic_index_in_dim(lengths, seq_index, 0, keepdims=False)
        table_row = lax.dynamic_index_in_dim(table_rows, seq_index, 0, keepdims=False).astype(
            jnp.float32
        )
        is_live = jnp.arange(seq_len, dtype=jnp.int32) < length
        stream_in = tokens + table_row[None, :]
        normed1, inverse1 = normalize_rows(stream_in)
        normed_in = (normed1 * gains_full[0] + shifts_full[0]).astype(jnp.bfloat16)
        projected = jnp.dot(normed_in, proj_qkv, preferred_element_type=jnp.float32).reshape(
            seq_len, heads_here, 3, DH
        )
        queries = (projected[:, :, 0] + bias_qv[0]).astype(jnp.bfloat16)
        keys_all = projected[:, :, 1].astype(jnp.bfloat16)
        values = (projected[:, :, 2] + bias_qv[1]).astype(jnp.bfloat16)
        query_blocks = queries.reshape(block_count, row_block, heads_here, DH)
        mixed, log_total = lax.map(
            functools.partial(attend_rows, keys_all, values, is_live, score_scale), query_blocks
        )
        attended = mixed.reshape(seq_len, heads_here * DH).astype(jnp.bfloat16)
        attn_part = jnp.dot(attended, proj_out, preferred_element_type=jnp.float32)
        branch_attn = lax.psum_scatter(
            attn_part, "mp", scatter_dimension=1, tiled=True
        ) + column_part(shifts_full[2], col_start, part_width)
        mid_part = column_part(stream_in, col_start, part_width) + branch_attn
        stream_mid = lax.all_gather(mid_part, "mp", axis=1, tiled=True)
        normed2, inverse2 = normalize_rows(stream_mid)
        normed_mid = (normed2 * gains_full[1] + shifts_full[1]).astype(jnp.bfloat16)
        pre_act = jnp.dot(normed_mid, proj_in, preferred_element_type=jnp.float32) + bias_in
        activation = jax.nn.gelu(pre_act, approximate=True).astype(jnp.bfloat16)
        mlp_part = jnp.dot(activation, proj_back, preferred_element_type=jnp.float32)
        mlp_out = lax.psum_scatter(mlp_part, "mp", scatter_dimension=1, tiled=True) + column_part(
            shifts_full[3], col_start, part_width
        )
        out_part = mid_part + mlp_out
        residual_err = jnp.where(is_live[:, None], out_part - target, 0.0)
        loss_part = loss_part + jnp.sum(residual_err * residual_err)
        grad_y = residual_err * loss_factor
        grad_mlp = grad_y.astype(jnp.bfloat16)
        acc_shifts = acc_shifts.at[3].add(jnp.sum(grad_mlp.astype(jnp.float32), axis=0))
        grad_mlp_full = lax.all_gather(grad_mlp, "mp", axis=1, tiled=True)
        back_set = fetch_weights(w_qkv, w_in, w_out, w_back, qv_bias, in_bias)
        back_qkv, back_in, back_out, back_back = (
            back_set[0],
            back_set[1],
            back_set[2],
            back_set[3],
        )
        acc_back = acc_back + jnp.einsum(
            "tf,td->fd", activation, grad_mlp_full, preferred_element_type=jnp.float32
        )
        grad_act = jnp.einsum(
            "td,fd->tf", grad_mlp_full, back_back, preferred_element_type=jnp.float32
        )
        gelu_value, gelu_pull = jax.vjp(lambda inner: jax.nn.gelu(inner, approximate=True), pre_act)
        grad_pre = gelu_pull(grad_act)[0].astype(jnp.bfloat16)
        acc_in_bias = acc_in_bias + jnp.sum(grad_pre.astype(jnp.float32), axis=0)
        acc_in = acc_in + jnp.einsum(
            "td,tf->df", normed_mid, grad_pre, preferred_element_type=jnp.float32
        )
        partial2 = jnp.einsum("tf,df->td", grad_pre, back_in, preferred_element_type=jnp.float32)
        grad_h2, sums2 = (
            lax.psum_scatter(partial2, "mp", scatter_dimension=1, tiled=True),
            lax.psum_scatter(
                norm_sums(partial2, normed2, gains_full[1], mp_count),
                "mp",
                scatter_dimension=1,
                tiled=True,
            ),
        )
        normed2_part = column_part(normed2, col_start, part_width)
        acc_gains = acc_gains.at[1].add(jnp.sum(grad_h2 * normed2_part, axis=0))
        acc_shifts = acc_shifts.at[1].add(jnp.sum(grad_h2, axis=0))
        grad_mid = grad_y + norm_input_grad(
            grad_h2, gain_parts[1], normed2_part, inverse2, sums2, width
        )
        grad_branch = grad_mid.astype(jnp.bfloat16)
        acc_shifts = acc_shifts.at[2].add(jnp.sum(grad_branch.astype(jnp.float32), axis=0))
        grad_branch_full = lax.all_gather(grad_branch, "mp", axis=1, tiled=True)
        acc_out = acc_out + jnp.einsum(
            "tc,td->cd", attended, grad_branch_full, preferred_element_type=jnp.float32
        )
        grad_att = jnp.einsum(
            "td,cd->tc", grad_branch_full, back_out, preferred_element_type=jnp.float32
        ).astype(jnp.bfloat16)
        grad_blocks = grad_att.reshape(block_count, row_block, heads_here, DH)
        zero_heads = jnp.zeros((seq_len, heads_here, DH), jnp.float32)
        (grad_keys, grad_values), grad_queries = lax.scan(
            functools.partial(attend_back, keys_all, values, is_live, score_scale),
            (zero_heads, zero_heads),
            (query_blocks, grad_blocks, log_total),
        )
        grad_queries = grad_queries.reshape(seq_len, heads_here, DH).astype(jnp.bfloat16)
        grad_keys = grad_keys.astype(jnp.bfloat16)
        grad_values = grad_values.astype(jnp.bfloat16)
        acc_qv = acc_qv + jnp.stack(
            [
                jnp.sum(grad_queries.astype(jnp.float32), axis=0),
                jnp.sum(grad_values.astype(jnp.float32), axis=0),
            ]
        )
        grad_qkv_rows = jnp.stack([grad_queries, grad_keys, grad_values], axis=2).reshape(
            seq_len, heads_here * 3 * DH
        )
        acc_qkv = acc_qkv + jnp.einsum(
            "td,tc->dc", normed_in, grad_qkv_rows, preferred_element_type=jnp.float32
        )
        partial1 = jnp.einsum(
            "tc,dc->td", grad_qkv_rows, back_qkv, preferred_element_type=jnp.float32
        )
        grad_h1, sums1 = (
            lax.psum_scatter(partial1, "mp", scatter_dimension=1, tiled=True),
            lax.psum_scatter(
                norm_sums(partial1, normed1, gains_full[0], mp_count),
                "mp",
                scatter_dimension=1,
                tiled=True,
            ),
        )
        normed1_part = column_part(normed1, col_start, part_width)
        acc_gains = acc_gains.at[0].add(jnp.sum(grad_h1 * normed1_part, axis=0))
        acc_shifts = acc_shifts.at[0].add(jnp.sum(grad_h1, axis=0))
        grad_in_stream = grad_mid + norm_input_grad(
            grad_h1, gain_parts[0], normed1_part, inverse1, sums1, width
        )
        table_sums.append(jnp.sum(grad_in_stream, axis=0))
        back_order = invert_map(my_source, dp_count)
        out_blocks = jnp.take(
            out_part.astype(jnp.bfloat16).reshape(dp_count, block_rows, part_width),
            back_order,
            axis=0,
        )
        grad_send = jnp.take(
            grad_in_stream.astype(jnp.bfloat16).reshape(dp_count, block_rows, part_width),
            back_order,
            axis=0,
        )
        home_out, home_grad = (
            lax.all_to_all(out_blocks, "dp", split_axis=0, concat_axis=0, tiled=True),
            lax.all_to_all(grad_send, "dp", split_axis=0, concat_axis=0, tiled=True),
        )
        home_place = invert_map(send_index, dp_count)
        outs_y.append(jnp.take(home_out, home_place, axis=0).reshape(seq_len, part_width))
        outs_grad.append(jnp.take(home_grad, home_place, axis=0).reshape(seq_len, part_width))
    row_sums = jnp.zeros((micro_count, width), jnp.float32)
    row_sums = lax.dynamic_update_slice_in_dim(row_sums, jnp.stack(table_sums), col_start, 1)
    my_steps = jnp.take(timestep, jnp.arange(micro_count, dtype=jnp.int32) * dp_count + dp_rank)
    step_onehot = (
        jnp.arange(table.shape[0], dtype=jnp.int32)[:, None] == my_steps[None, :]
    ).astype(jnp.float32)
    table_grad = jnp.dot(
        step_onehot, row_sums, precision=lax.Precision.HIGHEST, preferred_element_type=jnp.float32
    )
    gains_grad = lax.dynamic_update_slice_in_dim(
        jnp.zeros((2, width), jnp.float32), acc_gains, col_start, 1
    )
    shifts_grad = lax.dynamic_update_slice_in_dim(
        jnp.zeros((4, width), jnp.float32), acc_shifts, col_start, 1
    )
    loss_row = jnp.full((1, dp_count * mp_count), loss_part, jnp.float32)
    grad_table, grad_norm_gains, grad_shifts, loss_cell = (
        lax.psum_scatter(table_grad, ("dp", "mp"), scatter_dimension=1, tiled=True),
        lax.psum_scatter(gains_grad, ("dp", "mp"), scatter_dimension=1, tiled=True),
        lax.psum_scatter(shifts_grad, ("dp", "mp"), scatter_dimension=1, tiled=True),
        lax.psum_scatter(loss_row, ("dp", "mp"), scatter_dimension=1, tiled=True),
    )
    loss = loss_cell[0, 0] / (valid_count * width)
    grad_qkv, grad_in, grad_out, grad_back, grad_qv_bias, grad_in_bias = (
        lax.psum_scatter(acc_qkv, "dp", scatter_dimension=0, tiled=True),
        lax.psum_scatter(acc_in, "dp", scatter_dimension=0, tiled=True),
        lax.psum_scatter(acc_out, "dp", scatter_dimension=1, tiled=True),
        lax.psum_scatter(acc_back, "dp", scatter_dimension=1, tiled=True),
        lax.psum_scatter(acc_qv, "dp", scatter_dimension=2, tiled=True),
        lax.psum_scatter(acc_in_bias.reshape(-1, 128), "dp", scatter_dimension=1, tiled=True),
    )
    y_out = jnp.stack(outs_y)
    grad_x = jnp.stack(outs_grad)
    return (
        y_out,
        loss,
        grad_x,
        grad_table,
        grad_norm_gains,
        grad_shifts,
        grad_qkv,
        grad_qv_bias,
        grad_out,
        grad_in,
        grad_in_bias,
        grad_back,
    )


MESH = pl.DeviceIdType.MESH
BF = jnp.bfloat16
F32 = jnp.float32
VM = pl.BlockSpec(memory_space=pltpu.VMEM)
DP = 8
ROWS = 96
VMEM_LIMIT = 64 * 1024 * 1024 - 65536


def place():
    dp, mp = lax.axis_index("dp"), lax.axis_index("mp")
    x, c = lax.div(mp, 2), lax.rem(mp, 2)
    return dp, mp, x, c


def remote(src, dst, send_sem, recv_sem, dp, mp):
    return pltpu.make_async_remote_copy(
        src_ref=src,
        dst_ref=dst,
        send_sem=send_sem,
        recv_sem=recv_sem,
        device_id=(dp, mp),
        device_id_type=MESH,
    )


def landed(dst, recv_sem, spare, dp, mp):
    remote(dst, dst, spare, recv_sem, dp, mp).wait_recv()


def greet_plane(dp, x, c):
    barrier = pltpu.get_barrier_semaphore()
    pl.semaphore_signal(barrier, inc=1, device_id=(dp, 2 * x + 1 - c), device_id_type=MESH)
    for k in range(DP):
        for xr in range(2):
            if k or xr:
                there = (lax.rem(dp + k, DP), 2 * lax.rem(x + xr, 2) + c)
                pl.semaphore_signal(barrier, inc=1, device_id=there, device_id_type=MESH)
    pl.semaphore_wait(barrier, 2 * DP)


def gather_kernel(
    xs, ts, wsh, small, tok, tea, w, smalls,
    s_tok, r_tok, s_tea, r_tea, s_small, r_small, s_w, r_w, s_core, r_core,
):
    dp, mp, x, c = place()
    z, y = lax.div(dp, 2), lax.rem(dp, 2)
    other = 2 * x + 1 - c
    mine = x * DP + dp
    half = pl.ds(pl.multiple_of(384 * c, 128), 384)
    greet_plane(dp, x, c)
    sent = []

    def go(copy):
        copy.start()
        sent.append(copy)

    pltpu.make_async_copy(xs.at[x, dp, :, half], tok.at[dp, :, half], r_tok.at[dp]).start()

    @pl.when(y == x)
    def _():
        pltpu.make_async_copy(xs.at[2, dp, :, half], tok.at[8 + z, :, half], r_tok.at[8 + z]).start()

    for k in range(1, DP):
        d = lax.rem(dp + k, DP)
        go(remote(xs.at[x, d, :, half], tok.at[dp, :, half], s_tok.at[k], r_tok.at[dp], d, mp))

    @pl.when(y == x)
    def _():
        for k in range(1, DP):
            d = lax.rem(dp + k, DP)
            remote(xs.at[2, d, :, half], tok.at[8 + z, :, half], s_tok.at[8 + k], r_tok.at[8 + z], d, mp).start()

    pltpu.make_async_copy(small, smalls.at[mp, dp], r_small.at[mine]).start()
    for k in range(DP):
        for xr in range(2):
            if k or xr:
                d, m = lax.rem(dp + k, DP), 2 * lax.rem(x + xr, 2) + c
                go(remote(small, smalls.at[mp, dp], s_small.at[2 * k + xr], r_small.at[mine], d, m))

    mx, dy = 2 * (1 - x) + c, 2 * z + 1 - y
    for p in range(3):
        pltpu.make_async_copy(wsh.at[p], w.at[p, mine], r_w.at[p, mine]).start()
        for k in range(1, 4):
            zz = lax.rem(z + k, 4)
            go(remote(wsh.at[p], w.at[p, mine], s_w.at[p, k - 1], r_w.at[p, mine], 2 * zz + y, mp))
        go(remote(wsh.at[p], w.at[p, mine], s_w.at[p, 3], r_w.at[p, mine], dp, mx))
        go(remote(wsh.at[p], w.at[p, mine], s_w.at[p, 4], r_w.at[p, mine], dy, mp))

    def spread(p):
        for k in range(1, 4):
            b = x * DP + 2 * lax.rem(z + k, 4) + y
            landed(w.at[p, b], r_w.at[p, b], s_w.at[p, 0], dp, mp)
            go(remote(w.at[p, b], w.at[p, b], s_w.at[p, 3 + 2 * k], r_w.at[p, b], dp, mx))
            go(remote(w.at[p, b], w.at[p, b], s_w.at[p, 4 + 2 * k], r_w.at[p, b], dy, mp))

    def relay(p):
        for k in range(4):
            bx, by = (1 - x) * DP + 2 * k + y, x * DP + 2 * k + 1 - y
            landed(w.at[p, bx], r_w.at[p, bx], s_w.at[p, 0], dp, mp)
            landed(w.at[p, by], r_w.at[p, by], s_w.at[p, 0], dp, mp)
            if k < 2:
                go(remote(w.at[p, bx], w.at[p, bx], s_w.at[p, 11 + k], r_w.at[p, bx], dy, mp))
            else:
                go(remote(w.at[p, by], w.at[p, by], s_w.at[p, 11 + k], r_w.at[p, by], dp, mx))

    spread(0)

    pltpu.make_async_copy(ts.at[x, dp], tea.at[mp, dp], r_tea.at[x, dp]).start()
    for k in range(DP):
        d = lax.rem(dp + k, DP)
        for xr in range(2):
            if k or xr:
                xx = lax.rem(x + xr, 2)
                go(remote(ts.at[xx, d], tea.at[mp, dp], s_tea.at[2 * k + xr], r_tea.at[x, dp], d, 2 * xx + c))
        if k:
            go(remote(ts.at[2, d], tea.at[mp, 8 + z], s_tea.at[16 + k], r_tea.at[x, 8 + z], d, 2 * y + c))

    @pl.when(y == x)
    def _():
        pltpu.make_async_copy(ts.at[2, dp], tea.at[mp, 8 + z], r_tea.at[x, 8 + z]).start()

    @pl.when(y != x)
    def _():
        copy = remote(ts.at[2, dp], tea.at[mp, 8 + z], s_tea.at[16], r_tea.at[x, 8 + z], dp, 2 * y + c)
        copy.start()
        copy.wait_send()

    spread(1)
    relay(0)
    spread(2)

    for j in range(12):
        landed(tok.at[j, :, half], r_tok.at[j], s_tok.at[0], dp, mp)
    go(remote(tok.at[:, :, half], tok.at[:, :, half], s_core.at[0], r_core.at[0], dp, other))
    for j in range(8):
        for xx in range(2):
            m = 2 * xx + c
            landed(smalls.at[m, j], r_small.at[xx * DP + j], s_small.at[0], dp, mp)
    go(remote(smalls.at[c], smalls.at[c], s_core.at[1], r_core.at[1], dp, other))
    go(remote(smalls.at[2 + c], smalls.at[2 + c], s_core.at[2], r_core.at[2], dp, other))

    relay(1)
    relay(2)

    for xx in range(2):
        for j in range(12):
            landed(tea.at[2 * xx + c, j], r_tea.at[xx, j], s_tea.at[0], dp, mp)
    go(remote(tea.at[c], tea.at[c], s_core.at[3], r_core.at[3], dp, other))
    go(remote(tea.at[2 + c], tea.at[2 + c], s_core.at[4], r_core.at[4], dp, other))

    for p in range(3):
        landed(w.at[p, mine], r_w.at[p, mine], s_w.at[p, 0], dp, mp)
        for k in range(4):
            b = (1 - x) * DP + 2 * k + 1 - y
            landed(w.at[p, b], r_w.at[p, b], s_w.at[p, 0], dp, mp)
    o = 1 - c
    landed(tok.at[:, :, pl.ds(pl.multiple_of(384 * o, 128), 384)], r_core.at[0], s_core.at[0], dp, mp)
    landed(smalls.at[o], r_core.at[1], s_core.at[0], dp, mp)
    landed(smalls.at[2 + o], r_core.at[2], s_core.at[0], dp, mp)
    landed(tea.at[o], r_core.at[3], s_core.at[0], dp, mp)
    landed(tea.at[2 + o], r_core.at[4], s_core.at[0], dp, mp)
    for copy in sent:
        copy.wait_send()

    @pl.when(y == x)
    def _():
        for k in range(1, DP):
            d = lax.rem(dp + k, DP)
            remote(xs.at[2, d, :, half], tok.at[8 + z, :, half], s_tok.at[8 + k], r_tok.at[8 + z], d, mp).wait_send()


def gather_all(xs, ts, wsh, small):
    dma = pltpu.SemaphoreType.DMA
    return pl.pallas_call(
        gather_kernel,
        name="gather_all",
        out_shape=(
            jax.ShapeDtypeStruct((12, 64, 768), BF),
            jax.ShapeDtypeStruct((4, 12, 64, 192), BF),
            jax.ShapeDtypeStruct((3, 16, ROWS, 768), BF),
            jax.ShapeDtypeStruct((4, DP, 32, 128), BF),
        ),
        in_specs=[VM] * 4,
        out_specs=(VM,) * 4,
        scratch_shapes=[
            dma((16,)), dma((12,)), dma((24,)), dma((2, 12)), dma((16,)), dma((16,)),
            dma((3, 15)), dma((3, 16)), dma((5,)), dma((5,)),
        ],
        compiler_params=pltpu.CompilerParams(
            collective_id=1, has_side_effects=True, vmem_limit_bytes=VMEM_LIMIT
        ),
    )(xs, ts, wsh, small)


def reduce_kernel(
    g, msg, yg, gs, msgs, back,
    s1, r1, s2, r2, s3, r3,
    s_msg, r_msg, s_yg, r_yg, s_a, r_a, s_b, r_b, s_c, r_c,
):
    dp, mp, x, c = place()
    z, y = lax.div(dp, 2), lax.rem(dp, 2)
    mine = x * DP + dp
    greet_plane(dp, x, c)
    sent = []

    def go(copy):
        copy.start()
        sent.append(copy)

    mx, dy = 2 * (1 - x) + c, 2 * z + 1 - y

    def first(p):
        for k in range(4):
            b = (1 - x) * DP + 2 * k + 1 - y
            s1[p, k] = g[p, b].astype(BF)
            there = (dp, mx) if k < 2 else (dy, mp)
            go(remote(s1.at[p, k], r1.at[p, k], s_a.at[p, k], r_a.at[p, k], *there))

    def second(p):
        for k in range(4):
            bx, by = (1 - x) * DP + 2 * k + y, x * DP + 2 * k + 1 - y
            landed(r1.at[p, k], r_a.at[p, k], s_a.at[p, k], dp, mp)
            extra = r1[p, k].astype(F32)
            gx, gy = g[p, bx], g[p, by]
            if k < 2:
                gy = gy + extra
            else:
                gx = gx + extra
            s2[p, 0, k] = gx.astype(BF)
            s2[p, 1, k] = gy.astype(BF)
            go(remote(s2.at[p, 0, k], r2.at[p, 0, k], s_b.at[p, 0, k], r_b.at[p, 0, k], dp, mx))
            go(remote(s2.at[p, 1, k], r2.at[p, 1, k], s_b.at[p, 1, k], r_b.at[p, 1, k], dy, mp))

    def third(p):
        for k in range(1, 5):
            zz = lax.rem(z + k, 4)
            b = x * DP + 2 * zz + y
            for side in range(2):
                landed(r2.at[p, side, zz], r_b.at[p, side, zz], s_b.at[p, side, 0], dp, mp)
            total = g[p, b] + r2[p, 0, zz].astype(F32) + r2[p, 1, zz].astype(F32)
            if k < 4:
                s3[p, k - 1] = total.astype(BF)
                go(remote(s3.at[p, k - 1], r3.at[p, k - 1], s_c.at[p, k - 1], r_c.at[p, k - 1], 2 * zz + y, mp))
            else:
                gs[p] = total

    def last(p):
        for k in range(3):
            landed(r3.at[p, k], r_c.at[p, k], s_c.at[p, k], dp, mp)
        gs[p] = gs[p] + (r3[p, 0].astype(F32) + r3[p, 1].astype(F32) + r3[p, 2].astype(F32))

    first(2)
    first(1)
    pltpu.make_async_copy(msg.at[mine], msgs.at[mine], r_msg.at[mine]).start()
    for k in range(DP):
        for xr in range(2):
            if k or xr:
                d, xx = lax.rem(dp + k, DP), lax.rem(x + xr, 2)
                go(remote(msg.at[xx * DP + d], msgs.at[mine], s_msg.at[2 * k + xr], r_msg.at[mine], d, 2 * xx + c))
    second(2)
    first(0)
    second(1)
    third(2)

    pltpu.make_async_copy(yg.at[:, mp, dp], back.at[:, x, dp], r_yg.at[x, dp]).start()
    for k in range(DP):
        s = lax.rem(dp + k, DP)
        for xr in range(2):
            if k or xr:
                m = 2 * lax.rem(x + xr, 2) + c
                go(remote(yg.at[:, m, s], back.at[:, x, dp], s_yg.at[2 * k + xr], r_yg.at[x, dp], s, m))
    for k in range(4):
        j = lax.rem(z + k, 4)
        for xr in range(2):
            m = 2 * lax.rem(x + xr, 2) + c
            if k or xr:
                go(remote(yg.at[:, m, 8 + j], back.at[:, 2, dp], s_yg.at[16 + 2 * k + xr], r_yg.at[2, dp], 2 * j + x, m))

    @pl.when(y == x)
    def _():
        pltpu.make_async_copy(yg.at[:, mp, 8 + z], back.at[:, 2, dp], r_yg.at[2, dp]).start()

    @pl.when(y != x)
    def _():
        copy = remote(yg.at[:, mp, 8 + z], back.at[:, 2, dp], s_yg.at[16], r_yg.at[2, dp], 2 * z + x, mp)
        copy.start()
        copy.wait_send()

    second(0)
    third(1)
    third(0)
    last(2)
    last(1)
    last(0)
    for j in range(16):
        landed(msgs.at[j], r_msg.at[j], s_msg.at[0], dp, mp)
    for m in range(3):
        for j in range(DP):
            landed(back.at[:, m, j], r_yg.at[m, j], s_yg.at[0], dp, mp)
    for copy in sent:
        copy.wait_send()


def reduce_all(g, msg, yg):
    dma = pltpu.SemaphoreType.DMA
    block = (ROWS, 768)
    return pl.pallas_call(
        reduce_kernel,
        name="reduce_all",
        out_shape=(
            jax.ShapeDtypeStruct((3, ROWS, 768), F32),
            jax.ShapeDtypeStruct((16, 16, 128), F32),
            jax.ShapeDtypeStruct((2, 3, DP, 64, 192), BF),
        ),
        in_specs=[VM] * 3,
        out_specs=(VM,) * 3,
        scratch_shapes=[
            pltpu.VMEM((3, 4) + block, BF), pltpu.VMEM((3, 4) + block, BF),
            pltpu.VMEM((3, 2, 4) + block, BF), pltpu.VMEM((3, 2, 4) + block, BF),
            pltpu.VMEM((3, 3) + block, BF), pltpu.VMEM((3, 3) + block, BF),
            dma((16,)), dma((16,)), dma((24,)), dma((3, DP)), dma((3, 4)), dma((3, 4)),
            dma((3, 2, 4)), dma((3, 2, 4)), dma((3, 3)), dma((3, 3)),
        ],
        compiler_params=pltpu.CompilerParams(
            collective_id=2, has_side_effects=True, vmem_limit_bytes=VMEM_LIMIT
        ),
    )(g, msg, yg)


def dot(a, b, dims):
    return lax.dot_general(a, b, (dims, ((), ())), preferred_element_type=F32)


T = 768
R = 256
LOG_SCALE = 0.125


def nn(a, b):
    return dot(a, b, ((1,), (0,)))


def nt(a, b):
    return dot(a, b, ((1,), (1,)))


def chunk(i):
    return pl.ds(pl.multiple_of(i * R, R), R)


def colsum(a):
    return jnp.sum(a, axis=0, keepdims=True)


def wide(column_tile, width):
    return jnp.concatenate([column_tile] * (width // 128), axis=1)


def gelu_pair(v):
    k = 0.7978845608028654
    v2 = v * v
    t = jnp.tanh(k * (v + 0.044715 * (v2 * v)))
    half = 0.5 * (1.0 + t)
    slope = half + 0.5 * v * ((1.0 - t * t) * (k * (1.0 + 0.134145 * v2)))
    return v * half, slope


def norm_back(g, normed, inverse):
    inner = jnp.mean(g * normed, axis=1, keepdims=True)
    return inverse * (g - jnp.mean(g, axis=1, keepdims=True) - normed * inner)


def step_kernel(
    tok, tea, w, vec, mask,
    g, yg, sums,
    nin, q_s, kv, kvt, o_t, att, n2_s, act, gy, gm, gp, x3, recv, tr, ga, dq, dkv, dkx, dkr, lse,
    s_core, r_core, s_x, r_x,
):
    dp, mp, x, c = place()
    other, across = 2 * x + 1 - c, 2 * (1 - x) + c
    barrier = pltpu.get_barrier_semaphore()
    for m in (other, across):
        pl.semaphore_signal(barrier, inc=1, device_id=(dp, m), device_id_type=MESH)
    pl.semaphore_wait(barrier, 2)
    smid = g.at[0, 0]
    sums[...] = jnp.zeros(sums.shape, F32)

    def core(k, buffer, i):
        rows = chunk(i)
        return remote(
            buffer.at[rows], recv.at[k % 2, rows], s_core.at[k, i], r_core.at[k, i], dp, other
        )

    def each(count, body):
        def run(i, carry):
            body(i)
            return carry

        lax.fori_loop(0, count, run, 0)

    def add(row, value):
        width = value.shape[1]
        sums[row : row + 1, 0:width] = sums[row : row + 1, 0:width] + value

    def stream(i):
        return tok[chunk(i)].astype(F32) + jnp.where(i < 2, vec[0:1], vec[1:2])

    def project(i):
        rows = chunk(i)
        normed, _ = normalize_rows(stream(i))
        nb = (normed * vec[2:3] + vec[4:5]).astype(BF)
        nin[rows] = nb
        for xi in range(2):
            pr = (nn(nb, w[0, xi, :, 0:640]) + vec[8 + xi : 9 + xi, 0:640]).astype(BF)
            for j in range(3):
                head, a = 3 * xi + j, 192 * j
                q_s[head, rows] = jnp.concatenate([pr[:, a : a + 64], jnp.zeros((R, 64), BF)], axis=1)
                kv[head, rows] = pr[:, a + 64 : a + 192]

    project(2)
    own, theirs = pl.ds(512, 256), pl.ds(768, 256)
    kv_copy = remote(kv.at[:, own], kv.at[:, theirs], s_x.at[0], r_x.at[0], dp, across)
    kv_copy.start()
    each(2, project)

    def turn(part):
        def body(h):
            kvt[h, :, part * 512 : part * 512 + 512] = kv[h, part * 512 : part * 512 + 512].T

        each(6, body)

    def attend(h, block):
        part = block // 2
        keys, rows = slice(part * 512, part * 512 + 512), slice(block * R, block * R + R)
        st = nt(kv[h, keys], q_s[h, rows]) * LOG_SCALE + wide(mask[keys], R)
        top = jnp.max(st, axis=0, keepdims=True)
        e = jnp.exp(st - top)
        total = colsum(e)
        pt = (e * (1.0 / total)).astype(BF)
        ot = nn(kvt[h, 64:128, keys], pt)
        xi, j = lax.div(h, 3), lax.rem(h, 3)
        o_t[xi, pl.ds(pl.multiple_of(64 + 64 * j, 64), 64), rows] = ot.astype(BF)
        lse[h, :, rows] = top + jnp.log(total)

    o_t[:, 0:64] = jnp.zeros((2, 64, T), BF)
    turn(0)

    def attend_a(h):
        attend(h, 0)
        attend(h, 1)

    each(6, attend_a)
    kv_copy.wait()
    turn(1)
    each(6, lambda h: attend(h, 2))

    def out_project(i):
        rows = chunk(i)
        part = None
        for xi in range(2):
            a = o_t[xi, :, rows].T
            att[xi, rows] = a
            piece = nt(a, w[0, xi, :, 512:768])
            part = piece if part is None else part + piece
        smid[rows] = part
        core(0, smid, i).start()

    each(3, out_project)

    def forward(i):
        rows = chunk(i)
        core(0, smid, i).wait()
        mid = stream(i) + (smid[rows] + recv[0, rows] + vec[6:7])
        smid[rows] = mid
        normed, _ = normalize_rows(mid)
        nb = (normed * vec[3:4] + vec[5:6]).astype(BF)
        n2_s[rows] = nb
        part = None
        for xi in range(2):
            value, slope = gelu_pair(nn(nb, w[1, xi]) + vec[10 + xi : 11 + xi])
            a = value.astype(BF)
            act[xi, rows] = a
            g[1, xi, rows] = slope
            piece = nt(a, w[2, xi])
            part = piece if part is None else part + piece
        gy[rows] = part
        core(1, gy, i).start()

    each(3, forward)

    def turn_back(i):
        rows, blocks = chunk(i), pl.ds(i * 4, 4)
        core(1, gy, i).wait()
        out = smid[rows] + (gy[rows] + recv[1, rows] + vec[7:8])
        out_b = out.astype(BF)
        for m in range(4):
            yg[0, m, blocks] = out_b[:, 192 * m : 192 * m + 192].reshape(4, 64, 192)
        target = jnp.concatenate([tea[m, blocks].reshape(R, 192) for m in range(4)], axis=1)
        residual = jnp.where(wide(mask[rows], T) == 0.0, out - target.astype(F32), 0.0)
        add(8, colsum(residual * residual))
        grad_y = residual * vec[12:13]
        gy[rows] = grad_y
        gb = grad_y.astype(BF)
        gm[rows] = gb
        add(5, colsum(gb.astype(F32)))
        part = None
        for xi in range(2):
            gpre = (nn(gb, w[2, xi]) * g[1, xi, rows]).astype(BF)
            gp[xi, rows] = gpre
            add(11 + xi, colsum(gpre.astype(F32)))
            piece = nt(gpre, w[1, xi])
            part = piece if part is None else part + piece
        x3[rows] = part
        core(2, x3, i).start()

    each(3, turn_back)

    def turn_rows(source):
        def body(i):
            tr[:, chunk(i)] = source[chunk(i)].T

        each(3, body)

    def weight_grad(p, values):
        def body(i):
            for xi in range(2):
                g[p, xi, chunk(i)] = nn(tr[chunk(i)], values[xi])

        each(3, body)

    turn_rows(gm)
    weight_grad(2, act)
    turn_rows(n2_s)
    weight_grad(1, gp)

    def mid_back(i):
        rows = chunk(i)
        core(2, x3, i).wait()
        grad_h = x3[rows] + recv[0, rows]
        normed, inverse = normalize_rows(smid[rows])
        add(1, colsum(grad_h * normed))
        add(3, colsum(grad_h))
        grad_mid = gy[rows] + norm_back(grad_h * vec[3:4], normed, inverse)
        gy[rows] = grad_mid
        gb = grad_mid.astype(BF)
        gm[rows] = gb
        add(4, colsum(gb.astype(F32)))
        for xi in range(2):
            gatt = nn(gb, w[0, xi, :, 512:768]).astype(BF)
            for j in range(3):
                piece = gatt[:, 64 + 64 * j : 128 + 64 * j]
                ga[3 * xi + j, rows] = jnp.concatenate([jnp.zeros((R, 64), BF), piece], axis=1)

    each(3, mid_back)

    def attend_grad(h, block):
        part = block // 2
        keys, rows = slice(part * 512, part * 512 + 512), slice(block * R, block * R + R)
        kvs, q, go = kv[h, keys], q_s[h, rows], ga[h, rows]
        st = nt(kvs, q) * LOG_SCALE + wide(mask[keys], R)
        pt = jnp.exp(st - lse[h, :, rows])
        dpt = nt(kvs, go)
        delta = colsum(pt * dpt)
        dst = (pt * (dpt - delta)).astype(BF)
        dqt = nn(kvt[h, 0:64, keys], dst) * LOG_SCALE
        dq[h, rows] = dqt.T.astype(BF)
        return nn(dst, q) * LOG_SCALE + nn(pt.astype(BF), go)

    def grad_c(h):
        both = attend_grad(h, 2)
        dkv[h, 512:768] = both[0:256]
        dkx[h] = both[256:512].astype(BF)

    def grad_a(h):
        dkv[h, 0:512] = attend_grad(h, 0) + attend_grad(h, 1)

    each(6, grad_c)
    dk_copy = remote(dkx, dkr, s_x.at[1], r_x.at[1], dp, across)
    dk_copy.start()
    each(6, grad_a)
    turn_rows(gm)

    def out_grad(i):
        for xi in range(2):
            g[0, xi, chunk(i), 512:768] = nn(tr[chunk(i)], att[xi])

    each(3, out_grad)
    dk_copy.wait()

    def join(h):
        dkv[h, 512:768] = dkv[h, 512:768] + dkr[h].astype(F32)

    each(6, join)

    def project_back(i):
        rows = chunk(i)
        part = None
        for xi in range(2):
            pieces = []
            for j in range(3):
                pieces += [dq[3 * xi + j, rows], dkv[3 * xi + j, rows].astype(BF)]
            gr = jnp.concatenate(pieces + [jnp.zeros((R, 64), BF)], axis=1)
            gp[xi, rows, 0:640] = gr
            add(9 + xi if xi == 0 else 13, colsum(gr.astype(F32)))
            piece = nt(gr, w[0, xi, :, 0:640])
            part = piece if part is None else part + piece
        x3[rows] = part
        core(3, x3, i).start()

    each(3, project_back)
    turn_rows(nin)

    def qkv_grad(i):
        rows = chunk(i)
        for xi in range(2):
            h = nn(tr[rows], gp[xi, :, 0:640])
            g[0, xi, rows, 0:512] = h[:, 0:512]
            g[0, xi, rows, 512:640] = g[0, xi, rows, 512:640] + h[:, 512:640]

    each(3, qkv_grad)

    def in_back(i):
        rows, blocks = chunk(i), pl.ds(i * 4, 4)
        core(3, x3, i).wait()
        grad_h = x3[rows] + recv[1, rows]
        normed, inverse = normalize_rows(stream(i))
        add(0, colsum(grad_h * normed))
        add(2, colsum(grad_h))
        grad_in = gy[rows] + norm_back(grad_h * vec[2:3], normed, inverse)
        total = colsum(grad_in)
        add(6, jnp.where(i < 2, total, 0.0))
        add(7, jnp.where(i < 2, 0.0, total))
        out_b = grad_in.astype(BF)
        for m in range(4):
            yg[1, m, blocks] = out_b[:, 192 * m : 192 * m + 192].reshape(4, 64, 192)

    each(3, in_back)


def step(tok, tea, w, vec, mask):
    dma = pltpu.SemaphoreType.DMA
    vm = pltpu.VMEM
    return pl.pallas_call(
        step_kernel,
        name="step",
        out_shape=(
            jax.ShapeDtypeStruct((3, 2, T, 768), F32),
            jax.ShapeDtypeStruct((2, 4, 12, 64, 192), BF),
            jax.ShapeDtypeStruct((16, 768), F32),
        ),
        in_specs=[VM] * 5,
        out_specs=(VM,) * 3,
        scratch_shapes=[
            vm((T, 768), BF), vm((6, T, 128), BF), vm((6, 1024, 128), BF), vm((6, 128, 1024), BF),
            vm((2, R, T), BF), vm((2, T, R), BF), vm((T, 768), BF), vm((2, T, 768), BF),
            vm((T, 768), F32), vm((T, 768), BF), vm((2, T, 768), BF), vm((T, 768), F32),
            vm((2, T, 768), F32), vm((768, T), BF), vm((6, T, 128), BF), vm((6, T, 64), BF),
            vm((6, T, 128), F32), vm((6, R, 128), BF), vm((6, R, 128), BF), vm((6, 1, T), F32),
            dma((4, 3)), dma((4, 3)), dma((2,)), dma((2,)),
        ],
        compiler_params=pltpu.CompilerParams(
            collective_id=3, has_side_effects=True, vmem_limit_bytes=VMEM_LIMIT
        ),
    )(tok, tea, w, vec, mask)


def per_device_compact(
    input_stream, teacher, timestep, lengths, block_perm, table, norm_gains, shifts,
    w_qkv, qv_bias, w_out, w_in, in_bias, w_back,
):
    dp, mp, x, c = place()
    seq_len, width, quarter = input_stream.shape[1], input_stream.shape[2], teacher.shape[2]
    valid_count = jnp.sum(lengths).astype(F32)
    loss_factor = 3 * DP * seq_len / valid_count

    order = block_perm.reshape(3, DP, DP)
    source, local = order // DP, order % DP
    send_index = jnp.sum(jnp.where(source == dp, local, 0), axis=2)
    my_source = lax.dynamic_index_in_dim(source, dp, 1, keepdims=False)
    ranks = jnp.arange(DP, dtype=jnp.int32)
    where_block = jnp.sum(
        jnp.where(my_source[:, None, :] == ranks[None, :, None], ranks[None, None, :], 0), axis=2
    )
    micro = jnp.arange(3)[:, None]
    x_blocks = input_stream.reshape(3, DP, 64, width)[micro, send_index]
    t_blocks = teacher.reshape(3, DP, 64, quarter)[micro, send_index]
    half_block = lax.dynamic_index_in_dim(where_block[2].reshape(4, 2), x, 1, keepdims=False)
    their_block = lax.dynamic_index_in_dim(where_block[2].reshape(4, 2), 1 - x, 1, keepdims=False)
    first_block = lax.dynamic_index_in_dim(where_block, x, 0, keepdims=False)
    length_a = lax.dynamic_index_in_dim(lengths, x * DP + dp, 0, keepdims=False)
    length_c = lax.dynamic_index_in_dim(lengths, 2 * DP + dp, 0, keepdims=False)
    inside = jnp.arange(64, dtype=jnp.int32)
    live_a = ((first_block[:, None] * 64 + inside[None]) < length_a).reshape(512)
    live_c = ((half_block[:, None] * 64 + inside[None]) < length_c).reshape(256)
    live_d = ((their_block[:, None] * 64 + inside[None]) < length_c).reshape(256)

    wsh = jnp.stack([jnp.concatenate([w_qkv, w_out.T], axis=1), w_in, w_back.T])
    chosen = jnp.take(table, timestep, axis=0)
    small = jnp.zeros((32, 128), BF)
    small = small.at[:30, :24].set(jnp.concatenate([norm_gains, shifts, chosen]))
    small = small.at[30, :48].set(qv_bias.reshape(48)).at[31, :96].set(in_bias.reshape(96))

    tok, tea, w, smalls = gather_all(x_blocks, t_blocks, wsh, small)

    vectors = smalls[:, :, :30, :24].transpose(2, 1, 0, 3).reshape(30, width).astype(F32)
    my_small = jnp.stack(
        [lax.dynamic_index_in_dim(smalls, 2 * k + c, 0, keepdims=False) for k in range(2)]
    ).astype(F32)
    bias_qv = my_small[:, :, 30, :48].reshape(2, DP, 2, 3, 8).transpose(0, 3, 2, 1, 4).reshape(2, 3, 2, DH)
    bias_in = my_small[:, :, 31, :96].reshape(2, DP, 6, 16).transpose(0, 2, 1, 3).reshape(2, 768)
    bias_qkv = jnp.stack([bias_qv[:, :, 0], jnp.zeros((2, 3, DH), F32), bias_qv[:, :, 1]], axis=2)
    bias_qkv = jnp.pad(bias_qkv.reshape(2, 576), ((0, 0), (0, 192)))
    row_a = lax.dynamic_index_in_dim(vectors, 6 + x * DP + dp, 0)
    row_c = lax.dynamic_index_in_dim(vectors, 6 + 2 * DP + dp, 0)
    factor = jnp.full((4, width), loss_factor, F32)
    vec = jnp.concatenate([row_a, row_c, vectors[0:6], bias_qkv, bias_in, factor])
    live = jnp.concatenate([live_a, live_c, live_d])
    mask = jnp.broadcast_to(jnp.where(live, 0.0, -1e30).astype(F32)[:, None], (1024, 128))
    grads, yg, sums = step(tok.reshape(T, width), tea, w.reshape(3, 2, width, 768), vec, mask)
    loss_part = jnp.sum(sums[8])
    g_qkvb = jnp.stack([sums[9, :576], sums[13, :576]]).reshape(2, 3, 3, DH)
    g_qvb = jnp.stack([g_qkvb[:, :, 0], g_qkvb[:, :, 2]]).reshape(2, 6, DH)

    by_owner = sums[0:8].reshape(8, DP, 2, 2, 24)
    by_owner = lax.dynamic_index_in_dim(by_owner, c, 3, keepdims=False)
    by_owner = by_owner.transpose(2, 1, 0, 3).reshape(16, 8, 24)
    msg = jnp.zeros((16, 16, 128), F32)
    msg = msg.at[:, :8, :24].set(by_owner).at[:, 8, 0].set(loss_part)
    qvb = g_qvb.reshape(2, 2, 3, DP, 8).transpose(1, 3, 0, 2, 4).reshape(16, 48)
    inb = sums[11:13].reshape(2, 6, DP, 16).transpose(0, 2, 1, 3).reshape(16, 96)
    msg = msg.at[:, 9, :48].set(qvb).at[:, 10, :96].set(inb)
    gs, msgs, home = reduce_all(grads.reshape(3, 16, ROWS, 768), msg, yg)

    place_home = jnp.sum(
        jnp.where(send_index[:, None, :] == ranks[None, :, None], ranks[None, None, :], 0), axis=2
    )
    home = home[:, micro, place_home].reshape(2, 3, seq_len, quarter)
    total = jnp.sum(msgs, axis=0)
    loss = total[8, 0] / (valid_count * width)
    rows_a = msgs[:, 6, :24].reshape(16, 24)
    rows_c = msgs[:DP, 7, :24] + msgs[DP:, 7, :24]
    seq_rows = jnp.concatenate([rows_a, rows_c])
    onehot = (jnp.arange(table.shape[0], dtype=jnp.int32)[:, None] == timestep[None, :]).astype(F32)
    grad_table = jnp.dot(onehot, seq_rows, precision=lax.Precision.HIGHEST, preferred_element_type=F32)
    return (
        home[0],
        loss,
        home[1],
        grad_table,
        total[0:2, :24],
        total[2:6, :24],
        gs[0, :, :576],
        total[9, :48].reshape(2, 3, 8),
        gs[0, :, 576:].T,
        gs[1],
        total[10, :96].reshape(6, 16),
        gs[2].T,
    )


def solution(mesh):
    compact = mesh.shape["dp"] == 8 and mesh.shape["mp"] == 4
    return jax.shard_map(
        per_device_compact if compact else per_device,
        mesh=mesh,
        in_specs=(
            P(None, "dp", None),
            P(None, "dp", "mp"),
            P(),
            P(),
            P(),
            P(None, ("dp", "mp")),
            P(None, ("dp", "mp")),
            P(None, ("dp", "mp")),
            P("dp", "mp"),
            P(None, "mp", "dp"),
            P("mp", "dp"),
            P("dp", "mp"),
            P("mp", "dp"),
            P("mp", "dp"),
        ),
        out_specs=(
            P(None, "dp", "mp"),
            P(),
            P(None, "dp", "mp"),
            P(None, ("dp", "mp")),
            P(None, ("dp", "mp")),
            P(None, ("dp", "mp")),
            P("dp", "mp"),
            P(None, "mp", "dp"),
            P("mp", "dp"),
            P("dp", "mp"),
            P("mp", "dp"),
            P("mp", "dp"),
        ),
        check_vma=False,
    )
```

```python
import functools
import math

import jax
import jax.numpy as jnp
from jax import lax
from jax.experimental import pallas as pl
from jax.experimental.pallas import tpu as pltpu
from jax.sharding import PartitionSpec as P

H = 12
DH = 64


epsilon = 1e-05


def normalize_rows(stream):
    centered = stream - jnp.mean(stream, axis=-1, keepdims=True)
    inverse = lax.rsqrt(jnp.mean(centered * centered, axis=-1, keepdims=True) + epsilon)
    return (centered * inverse, inverse)


def column_part(array, start, width):
    return lax.dynamic_slice_in_dim(array, start, width, array.ndim - 1)


def fetch_weights(w_qkv, w_in, w_out, w_back, qv_bias, in_bias):
    return (
        lax.all_gather(w_qkv, "dp", axis=0, tiled=True),
        lax.all_gather(w_in, "dp", axis=0, tiled=True),
        lax.all_gather(w_out, "dp", axis=1, tiled=True),
        lax.all_gather(w_back, "dp", axis=1, tiled=True),
        lax.all_gather(qv_bias, "dp", axis=2, tiled=True),
        lax.all_gather(in_bias, "dp", axis=1, tiled=True),
    )


def invert_map(targets, size):
    ranks = jnp.arange(size, dtype=jnp.int32)
    return jnp.sum(jnp.where(targets[None, :] == ranks[:, None], ranks[None, :], 0), axis=1)


def masked_scores(queries, keys_all, is_live, score_scale):
    scores = (
        jnp.einsum("qhe,khe->hqk", queries, keys_all, preferred_element_type=jnp.float32)
        * score_scale
    )
    return jnp.where(is_live[None, None, :], scores, -1e30)


def attend_rows(keys_all, values, is_live, score_scale, queries):
    scores = masked_scores(queries, keys_all, is_live, score_scale)
    row_top = jnp.max(scores, axis=-1, keepdims=True)
    exponent = jnp.exp(scores - row_top)
    row_total = jnp.sum(exponent, axis=-1, keepdims=True)
    weights_p = (exponent / row_total).astype(jnp.bfloat16)
    mixed = jnp.einsum("hqk,khe->qhe", weights_p, values, preferred_element_type=jnp.float32)
    return (mixed, (row_top + jnp.log(row_total))[..., 0])


def attend_back(keys_all, values, is_live, score_scale, carry, inputs):
    queries, grad_rows, log_total = inputs
    grad_keys, grad_values = carry
    scores = masked_scores(queries, keys_all, is_live, score_scale)
    probabilities = jnp.exp(scores - log_total[..., None])
    grad_probs = jnp.einsum("qhe,khe->hqk", grad_rows, values, preferred_element_type=jnp.float32)
    row_delta = jnp.sum(probabilities * grad_probs, axis=-1, keepdims=True)
    grad_scores = (probabilities * (grad_probs - row_delta)).astype(jnp.bfloat16)
    grad_queries = (
        jnp.einsum("hqk,khe->qhe", grad_scores, keys_all, preferred_element_type=jnp.float32)
        * score_scale
    )
    grad_keys = (
        grad_keys
        + jnp.einsum("hqk,qhe->khe", grad_scores, queries, preferred_element_type=jnp.float32)
        * score_scale
    )
    grad_values = grad_values + jnp.einsum(
        "hqk,qhe->khe",
        probabilities.astype(jnp.bfloat16),
        grad_rows,
        preferred_element_type=jnp.float32,
    )
    return ((grad_keys, grad_values), grad_queries)


def norm_sums(partial_value, normed, gain_full, mp_count):
    weighted = partial_value * gain_full
    sums = jnp.stack([jnp.sum(weighted, axis=1), jnp.sum(weighted * normed, axis=1)], axis=1)
    return jnp.tile(sums, (1, mp_count))


def norm_input_grad(grad_part, gain_part, normed_part, inverse, sums, width):
    scaled = grad_part * gain_part
    return inverse * (scaled - sums[:, 0:1] / width - normed_part * sums[:, 1:2] / width)


def per_device(
    input_stream,
    teacher,
    timestep,
    lengths,
    block_perm,
    table,
    norm_gains,
    shifts,
    w_qkv,
    qv_bias,
    w_out,
    w_in,
    in_bias,
    w_back,
):
    dp_count = lax.axis_size("dp")
    mp_count = lax.axis_size("mp")
    dp_rank = lax.axis_index("dp")
    mp_rank = lax.axis_index("mp")
    micro_count, seq_len, width = input_stream.shape
    part_width = teacher.shape[2]
    block_rows = seq_len // dp_count
    heads_here = H // mp_count
    score_scale = 1.0 / math.sqrt(DH)
    col_start = mp_rank * part_width
    row_block = min(512, seq_len)
    block_count = seq_len // row_block
    valid_count = jnp.sum(lengths).astype(jnp.float32)
    loss_factor = micro_count * dp_count * seq_len / valid_count
    chosen = jnp.take(table, timestep, axis=0)
    gains_full, shifts_full, table_rows = (
        lax.all_gather(norm_gains, ("dp", "mp"), axis=1, tiled=True),
        lax.all_gather(shifts, ("dp", "mp"), axis=1, tiled=True),
        lax.all_gather(chosen, ("dp", "mp"), axis=1, tiled=True),
    )
    gains_full = gains_full.astype(jnp.float32)
    shifts_full = shifts_full.astype(jnp.float32)
    gain_parts = column_part(gains_full, col_start, part_width)
    acc_qkv = jnp.zeros((width, heads_here * 3 * DH), jnp.float32)
    acc_in = jnp.zeros((width, w_in.shape[1]), jnp.float32)
    acc_out = jnp.zeros((heads_here * DH, width), jnp.float32)
    acc_back = jnp.zeros((w_back.shape[0], width), jnp.float32)
    acc_qv = jnp.zeros((2, heads_here, DH), jnp.float32)
    acc_in_bias = jnp.zeros((w_in.shape[1],), jnp.float32)
    acc_gains = jnp.zeros((2, part_width), jnp.float32)
    acc_shifts = jnp.zeros((4, part_width), jnp.float32)
    loss_part = jnp.zeros((), jnp.float32)
    table_sums = []
    outs_y = []
    outs_grad = []
    for micro_index in range(micro_count):
        forward_set = fetch_weights(w_qkv, w_in, w_out, w_back, qv_bias, in_bias)
        proj_qkv, proj_in, proj_out, proj_back, bias_qv, bias_in = forward_set
        bias_qv = bias_qv.astype(jnp.float32)
        bias_in = bias_in.reshape(-1).astype(jnp.float32)
        block_order = block_perm[micro_index].reshape(dp_count, dp_count)
        source = block_order // dp_count
        local_index = block_order % dp_count
        send_index = jnp.sum(jnp.where(source == dp_rank, local_index, 0), axis=1)
        x_blocks = input_stream[micro_index].reshape(dp_count, block_rows, width)
        t_blocks = teacher[micro_index].reshape(dp_count, block_rows, part_width)
        got_x, got_t = (
            lax.all_to_all(
                jnp.take(x_blocks, send_index, axis=0),
                "dp",
                split_axis=0,
                concat_axis=0,
                tiled=True,
            ),
            lax.all_to_all(
                jnp.take(t_blocks, send_index, axis=0),
                "dp",
                split_axis=0,
                concat_axis=0,
                tiled=True,
            ),
        )
        my_source = lax.dynamic_index_in_dim(source, dp_rank, 0, keepdims=False)
        tokens = jnp.take(got_x, my_source, axis=0).reshape(seq_len, width).astype(jnp.float32)
        target = jnp.take(got_t, my_source, axis=0).reshape(seq_len, part_width).astype(jnp.float32)
        seq_index = micro_index * dp_count + dp_rank
        length = lax.dynamic_index_in_dim(lengths, seq_index, 0, keepdims=False)
        table_row = lax.dynamic_index_in_dim(table_rows, seq_index, 0, keepdims=False).astype(
            jnp.float32
        )
        is_live = jnp.arange(seq_len, dtype=jnp.int32) < length
        stream_in = tokens + table_row[None, :]
        normed1, inverse1 = normalize_rows(stream_in)
        normed_in = (normed1 * gains_full[0] + shifts_full[0]).astype(jnp.bfloat16)
        projected = jnp.dot(normed_in, proj_qkv, preferred_element_type=jnp.float32).reshape(
            seq_len, heads_here, 3, DH
        )
        queries = (projected[:, :, 0] + bias_qv[0]).astype(jnp.bfloat16)
        keys_all = projected[:, :, 1].astype(jnp.bfloat16)
        values = (projected[:, :, 2] + bias_qv[1]).astype(jnp.bfloat16)
        query_blocks = queries.reshape(block_count, row_block, heads_here, DH)
        mixed, log_total = lax.map(
            functools.partial(attend_rows, keys_all, values, is_live, score_scale), query_blocks
        )
        attended = mixed.reshape(seq_len, heads_here * DH).astype(jnp.bfloat16)
        attn_part = jnp.dot(attended, proj_out, preferred_element_type=jnp.float32)
        branch_attn = lax.psum_scatter(
            attn_part, "mp", scatter_dimension=1, tiled=True
        ) + column_part(shifts_full[2], col_start, part_width)
        mid_part = column_part(stream_in, col_start, part_width) + branch_attn
        stream_mid = lax.all_gather(mid_part, "mp", axis=1, tiled=True)
        normed2, inverse2 = normalize_rows(stream_mid)
        normed_mid = (normed2 * gains_full[1] + shifts_full[1]).astype(jnp.bfloat16)
        pre_act = jnp.dot(normed_mid, proj_in, preferred_element_type=jnp.float32) + bias_in
        activation = jax.nn.gelu(pre_act, approximate=True).astype(jnp.bfloat16)
        mlp_part = jnp.dot(activation, proj_back, preferred_element_type=jnp.float32)
        mlp_out = lax.psum_scatter(mlp_part, "mp", scatter_dimension=1, tiled=True) + column_part(
            shifts_full[3], col_start, part_width
        )
        out_part = mid_part + mlp_out
        residual_err = jnp.where(is_live[:, None], out_part - target, 0.0)
        loss_part = loss_part + jnp.sum(residual_err * residual_err)
        grad_y = residual_err * loss_factor
        grad_mlp = grad_y.astype(jnp.bfloat16)
        acc_shifts = acc_shifts.at[3].add(jnp.sum(grad_mlp.astype(jnp.float32), axis=0))
        grad_mlp_full = lax.all_gather(grad_mlp, "mp", axis=1, tiled=True)
        back_set = fetch_weights(w_qkv, w_in, w_out, w_back, qv_bias, in_bias)
        back_qkv, back_in, back_out, back_back = (
            back_set[0],
            back_set[1],
            back_set[2],
            back_set[3],
        )
        acc_back = acc_back + jnp.einsum(
            "tf,td->fd", activation, grad_mlp_full, preferred_element_type=jnp.float32
        )
        grad_act = jnp.einsum(
            "td,fd->tf", grad_mlp_full, back_back, preferred_element_type=jnp.float32
        )
        gelu_value, gelu_pull = jax.vjp(lambda inner: jax.nn.gelu(inner, approximate=True), pre_act)
        grad_pre = gelu_pull(grad_act)[0].astype(jnp.bfloat16)
        acc_in_bias = acc_in_bias + jnp.sum(grad_pre.astype(jnp.float32), axis=0)
        acc_in = acc_in + jnp.einsum(
            "td,tf->df", normed_mid, grad_pre, preferred_element_type=jnp.float32
        )
        partial2 = jnp.einsum("tf,df->td", grad_pre, back_in, preferred_element_type=jnp.float32)
        grad_h2, sums2 = (
            lax.psum_scatter(partial2, "mp", scatter_dimension=1, tiled=True),
            lax.psum_scatter(
                norm_sums(partial2, normed2, gains_full[1], mp_count),
                "mp",
                scatter_dimension=1,
                tiled=True,
            ),
        )
        normed2_part = column_part(normed2, col_start, part_width)
        acc_gains = acc_gains.at[1].add(jnp.sum(grad_h2 * normed2_part, axis=0))
        acc_shifts = acc_shifts.at[1].add(jnp.sum(grad_h2, axis=0))
        grad_mid = grad_y + norm_input_grad(
            grad_h2, gain_parts[1], normed2_part, inverse2, sums2, width
        )
        grad_branch = grad_mid.astype(jnp.bfloat16)
        acc_shifts = acc_shifts.at[2].add(jnp.sum(grad_branch.astype(jnp.float32), axis=0))
        grad_branch_full = lax.all_gather(grad_branch, "mp", axis=1, tiled=True)
        acc_out = acc_out + jnp.einsum(
            "tc,td->cd", attended, grad_branch_full, preferred_element_type=jnp.float32
        )
        grad_att = jnp.einsum(
            "td,cd->tc", grad_branch_full, back_out, preferred_element_type=jnp.float32
        ).astype(jnp.bfloat16)
        grad_blocks = grad_att.reshape(block_count, row_block, heads_here, DH)
        zero_heads = jnp.zeros((seq_len, heads_here, DH), jnp.float32)
        (grad_keys, grad_values), grad_queries = lax.scan(
            functools.partial(attend_back, keys_all, values, is_live, score_scale),
            (zero_heads, zero_heads),
            (query_blocks, grad_blocks, log_total),
        )
        grad_queries = grad_queries.reshape(seq_len, heads_here, DH).astype(jnp.bfloat16)
        grad_keys = grad_keys.astype(jnp.bfloat16)
        grad_values = grad_values.astype(jnp.bfloat16)
        acc_qv = acc_qv + jnp.stack(
            [
                jnp.sum(grad_queries.astype(jnp.float32), axis=0),
                jnp.sum(grad_values.astype(jnp.float32), axis=0),
            ]
        )
        grad_qkv_rows = jnp.stack([grad_queries, grad_keys, grad_values], axis=2).reshape(
            seq_len, heads_here * 3 * DH
        )
        acc_qkv = acc_qkv + jnp.einsum(
            "td,tc->dc", normed_in, grad_qkv_rows, preferred_element_type=jnp.float32
        )
        partial1 = jnp.einsum(
            "tc,dc->td", grad_qkv_rows, back_qkv, preferred_element_type=jnp.float32
        )
        grad_h1, sums1 = (
            lax.psum_scatter(partial1, "mp", scatter_dimension=1, tiled=True),
            lax.psum_scatter(
                norm_sums(partial1, normed1, gains_full[0], mp_count),
                "mp",
                scatter_dimension=1,
                tiled=True,
            ),
        )
        normed1_part = column_part(normed1, col_start, part_width)
        acc_gains = acc_gains.at[0].add(jnp.sum(grad_h1 * normed1_part, axis=0))
        acc_shifts = acc_shifts.at[0].add(jnp.sum(grad_h1, axis=0))
        grad_in_stream = grad_mid + norm_input_grad(
            grad_h1, gain_parts[0], normed1_part, inverse1, sums1, width
        )
        table_sums.append(jnp.sum(grad_in_stream, axis=0))
        back_order = invert_map(my_source, dp_count)
        out_blocks = jnp.take(
            out_part.astype(jnp.bfloat16).reshape(dp_count, block_rows, part_width),
            back_order,
            axis=0,
        )
        grad_send = jnp.take(
            grad_in_stream.astype(jnp.bfloat16).reshape(dp_count, block_rows, part_width),
            back_order,
            axis=0,
        )
        home_out, home_grad = (
            lax.all_to_all(out_blocks, "dp", split_axis=0, concat_axis=0, tiled=True),
            lax.all_to_all(grad_send, "dp", split_axis=0, concat_axis=0, tiled=True),
        )
        home_place = invert_map(send_index, dp_count)
        outs_y.append(jnp.take(home_out, home_place, axis=0).reshape(seq_len, part_width))
        outs_grad.append(jnp.take(home_grad, home_place, axis=0).reshape(seq_len, part_width))
    row_sums = jnp.zeros((micro_count, width), jnp.float32)
    row_sums = lax.dynamic_update_slice_in_dim(row_sums, jnp.stack(table_sums), col_start, 1)
    my_steps = jnp.take(timestep, jnp.arange(micro_count, dtype=jnp.int32) * dp_count + dp_rank)
    step_onehot = (
        jnp.arange(table.shape[0], dtype=jnp.int32)[:, None] == my_steps[None, :]
    ).astype(jnp.float32)
    table_grad = jnp.dot(
        step_onehot, row_sums, precision=lax.Precision.HIGHEST, preferred_element_type=jnp.float32
    )
    gains_grad = lax.dynamic_update_slice_in_dim(
        jnp.zeros((2, width), jnp.float32), acc_gains, col_start, 1
    )
    shifts_grad = lax.dynamic_update_slice_in_dim(
        jnp.zeros((4, width), jnp.float32), acc_shifts, col_start, 1
    )
    loss_row = jnp.full((1, dp_count * mp_count), loss_part, jnp.float32)
    grad_table, grad_norm_gains, grad_shifts, loss_cell = (
        lax.psum_scatter(table_grad, ("dp", "mp"), scatter_dimension=1, tiled=True),
        lax.psum_scatter(gains_grad, ("dp", "mp"), scatter_dimension=1, tiled=True),
        lax.psum_scatter(shifts_grad, ("dp", "mp"), scatter_dimension=1, tiled=True),
        lax.psum_scatter(loss_row, ("dp", "mp"), scatter_dimension=1, tiled=True),
    )
    loss = loss_cell[0, 0] / (valid_count * width)
    grad_qkv, grad_in, grad_out, grad_back, grad_qv_bias, grad_in_bias = (
        lax.psum_scatter(acc_qkv, "dp", scatter_dimension=0, tiled=True),
        lax.psum_scatter(acc_in, "dp", scatter_dimension=0, tiled=True),
        lax.psum_scatter(acc_out, "dp", scatter_dimension=1, tiled=True),
        lax.psum_scatter(acc_back, "dp", scatter_dimension=1, tiled=True),
        lax.psum_scatter(acc_qv, "dp", scatter_dimension=2, tiled=True),
        lax.psum_scatter(acc_in_bias.reshape(-1, 128), "dp", scatter_dimension=1, tiled=True),
    )
    y_out = jnp.stack(outs_y)
    grad_x = jnp.stack(outs_grad)
    return (
        y_out,
        loss,
        grad_x,
        grad_table,
        grad_norm_gains,
        grad_shifts,
        grad_qkv,
        grad_qv_bias,
        grad_out,
        grad_in,
        grad_in_bias,
        grad_back,
    )


MESH = pl.DeviceIdType.MESH
BF = jnp.bfloat16
F32 = jnp.float32
VM = pl.BlockSpec(memory_space=pltpu.VMEM)
DP = 8
ROWS = 96
VMEM_LIMIT = 64 * 1024 * 1024 - 65536


def place():
    dp, mp = lax.axis_index("dp"), lax.axis_index("mp")
    x, c = lax.div(mp, 2), lax.rem(mp, 2)
    return dp, mp, x, c


def remote(src, dst, send_sem, recv_sem, dp, mp):
    return pltpu.make_async_remote_copy(
        src_ref=src,
        dst_ref=dst,
        send_sem=send_sem,
        recv_sem=recv_sem,
        device_id=(dp, mp),
        device_id_type=MESH,
    )


def landed(dst, recv_sem, spare, dp, mp):
    remote(dst, dst, spare, recv_sem, dp, mp).wait_recv()


def greet_plane(dp, x, c):
    barrier = pltpu.get_barrier_semaphore()
    pl.semaphore_signal(barrier, inc=1, device_id=(dp, 2 * x + 1 - c), device_id_type=MESH)
    for k in range(DP):
        for xr in range(2):
            if k or xr:
                there = (lax.rem(dp + k, DP), 2 * lax.rem(x + xr, 2) + c)
                pl.semaphore_signal(barrier, inc=1, device_id=there, device_id_type=MESH)
    pl.semaphore_wait(barrier, 2 * DP)


def reduce_kernel(
    g, msg, yg, gs, msgs, back,
    s1, r1, s2, r2, s3, r3,
    s_msg, r_msg, s_yg, r_yg, s_a, r_a, s_b, r_b, s_c, r_c,
):
    dp, mp, x, c = place()
    z, y = lax.div(dp, 2), lax.rem(dp, 2)
    mine = x * DP + dp
    greet_plane(dp, x, c)
    sent = []

    def go(copy):
        copy.start()
        sent.append(copy)

    mx, dy = 2 * (1 - x) + c, 2 * z + 1 - y

    def first(p):
        for k in range(4):
            b = (1 - x) * DP + 2 * k + 1 - y
            s1[p, k] = g[p, b].astype(BF)
            there = (dp, mx) if k < 2 else (dy, mp)
            go(remote(s1.at[p, k], r1.at[p, k], s_a.at[p, k], r_a.at[p, k], *there))

    def second(p):
        for k in range(4):
            bx, by = (1 - x) * DP + 2 * k + y, x * DP + 2 * k + 1 - y
            landed(r1.at[p, k], r_a.at[p, k], s_a.at[p, k], dp, mp)
            extra = r1[p, k].astype(F32)
            gx, gy = g[p, bx], g[p, by]
            if k < 2:
                gy = gy + extra
            else:
                gx = gx + extra
            s2[p, 0, k] = gx.astype(BF)
            s2[p, 1, k] = gy.astype(BF)
            go(remote(s2.at[p, 0, k], r2.at[p, 0, k], s_b.at[p, 0, k], r_b.at[p, 0, k], dp, mx))
            go(remote(s2.at[p, 1, k], r2.at[p, 1, k], s_b.at[p, 1, k], r_b.at[p, 1, k], dy, mp))

    def third(p):
        for k in range(1, 5):
            zz = lax.rem(z + k, 4)
            b = x * DP + 2 * zz + y
            for side in range(2):
                landed(r2.at[p, side, zz], r_b.at[p, side, zz], s_b.at[p, side, 0], dp, mp)
            total = g[p, b] + r2[p, 0, zz].astype(F32) + r2[p, 1, zz].astype(F32)
            if k < 4:
                s3[p, k - 1] = total.astype(BF)
                go(remote(s3.at[p, k - 1], r3.at[p, k - 1], s_c.at[p, k - 1], r_c.at[p, k - 1], 2 * zz + y, mp))
            else:
                gs[p] = total

    def last(p):
        for k in range(3):
            landed(r3.at[p, k], r_c.at[p, k], s_c.at[p, k], dp, mp)
        gs[p] = gs[p] + (r3[p, 0].astype(F32) + r3[p, 1].astype(F32) + r3[p, 2].astype(F32))

    first(2)
    first(1)
    pltpu.make_async_copy(msg.at[mine], msgs.at[mine], r_msg.at[mine]).start()
    for k in range(DP):
        for xr in range(2):
            if k or xr:
                d, xx = lax.rem(dp + k, DP), lax.rem(x + xr, 2)
                go(remote(msg.at[xx * DP + d], msgs.at[mine], s_msg.at[2 * k + xr], r_msg.at[mine], d, 2 * xx + c))
    second(2)
    first(0)
    second(1)
    third(2)

    pltpu.make_async_copy(yg.at[:, mp, dp], back.at[:, x, dp], r_yg.at[x, dp]).start()
    for k in range(DP):
        s = lax.rem(dp + k, DP)
        for xr in range(2):
            if k or xr:
                m = 2 * lax.rem(x + xr, 2) + c
                go(remote(yg.at[:, m, s], back.at[:, x, dp], s_yg.at[2 * k + xr], r_yg.at[x, dp], s, m))
    for k in range(4):
        j = lax.rem(z + k, 4)
        for xr in range(2):
            m = 2 * lax.rem(x + xr, 2) + c
            if k or xr:
                go(remote(yg.at[:, m, 8 + j], back.at[:, 2, dp], s_yg.at[16 + 2 * k + xr], r_yg.at[2, dp], 2 * j + x, m))

    @pl.when(y == x)
    def _():
        pltpu.make_async_copy(yg.at[:, mp, 8 + z], back.at[:, 2, dp], r_yg.at[2, dp]).start()

    @pl.when(y != x)
    def _():
        copy = remote(yg.at[:, mp, 8 + z], back.at[:, 2, dp], s_yg.at[16], r_yg.at[2, dp], 2 * z + x, mp)
        copy.start()
        copy.wait_send()

    second(0)
    third(1)
    third(0)
    last(2)
    last(1)
    last(0)
    for j in range(16):
        landed(msgs.at[j], r_msg.at[j], s_msg.at[0], dp, mp)
    for m in range(3):
        for j in range(DP):
            landed(back.at[:, m, j], r_yg.at[m, j], s_yg.at[0], dp, mp)
    for copy in sent:
        copy.wait_send()


def reduce_all(g, msg, yg):
    dma = pltpu.SemaphoreType.DMA
    block = (ROWS, 768)
    return pl.pallas_call(
        reduce_kernel,
        name="reduce_all",
        out_shape=(
            jax.ShapeDtypeStruct((3, ROWS, 768), F32),
            jax.ShapeDtypeStruct((16, 16, 128), F32),
            jax.ShapeDtypeStruct((2, 3, DP, 64, 192), BF),
        ),
        in_specs=[VM] * 3,
        out_specs=(VM,) * 3,
        scratch_shapes=[
            pltpu.VMEM((3, 4) + block, BF), pltpu.VMEM((3, 4) + block, BF),
            pltpu.VMEM((3, 2, 4) + block, BF), pltpu.VMEM((3, 2, 4) + block, BF),
            pltpu.VMEM((3, 3) + block, BF), pltpu.VMEM((3, 3) + block, BF),
            dma((16,)), dma((16,)), dma((24,)), dma((3, DP)), dma((3, 4)), dma((3, 4)),
            dma((3, 2, 4)), dma((3, 2, 4)), dma((3, 3)), dma((3, 3)),
        ],
        compiler_params=pltpu.CompilerParams(
            collective_id=2, has_side_effects=True, vmem_limit_bytes=VMEM_LIMIT
        ),
    )(g, msg, yg)


def dot(a, b, dims):
    return lax.dot_general(a, b, (dims, ((), ())), preferred_element_type=F32)


T = 768
R = 256
LOG_SCALE = 0.125


def nn(a, b):
    return dot(a, b, ((1,), (0,)))


def nt(a, b):
    return dot(a, b, ((1,), (1,)))


def chunk(i):
    return pl.ds(pl.multiple_of(i * R, R), R)


def colsum(a):
    return jnp.sum(a, axis=0, keepdims=True)


def wide(column_tile, width):
    return jnp.concatenate([column_tile] * (width // 128), axis=1)


def gelu_pair(v):
    k = 0.7978845608028654
    v2 = v * v
    t = jnp.tanh(k * (v + 0.044715 * (v2 * v)))
    half = 0.5 * (1.0 + t)
    slope = half + 0.5 * v * ((1.0 - t * t) * (k * (1.0 + 0.134145 * v2)))
    return v * half, slope


def norm_back(g, normed, inverse):
    inner = jnp.mean(g * normed, axis=1, keepdims=True)
    return inverse * (g - jnp.mean(g, axis=1, keepdims=True) - normed * inner)


def step_kernel(
    xs, ts, wsh, small, mask, factor,
    g, yg, sums,
    tok, tea, w, smalls, vecs, vec, nin, q_s, kv, kvt, o_t, att, n2_s, act, gy, gm, gp, x3, recv, tr, ga, dq, dkv, dkx, dkr, lse,
    s_core, r_core, s_x, r_x,
    s_tok, r_tok, s_tea, r_tea, s_small, r_small, s_w, r_w, s_pair, r_pair,
):
    dp, mp, x, c = place()
    other, across = 2 * x + 1 - c, 2 * (1 - x) + c
    z, y = lax.div(dp, 2), lax.rem(dp, 2)
    mine = x * DP + dp
    half = pl.ds(pl.multiple_of(384 * c, 128), 384)
    beside = 2 * z + 1 - y
    greet_plane(dp, x, c)
    sent = []

    def go(copy):
        copy.start()
        sent.append(copy)

    def rows64(j):
        return pl.ds(pl.multiple_of(64 * j, 64), 64)

    def weights_z(p):
        pltpu.make_async_copy(wsh.at[p], w.at[p, mine], r_w.at[p, mine]).start()
        for k in range(1, 4):
            zz = lax.rem(z + k, 4)
            go(remote(wsh.at[p], w.at[p, mine], s_w.at[p, k - 1], r_w.at[p, mine], 2 * zz + y, mp))

    def weights_xy(p):
        go(remote(wsh.at[p], w.at[p, mine], s_w.at[p, 3], r_w.at[p, mine], dp, across))
        go(remote(wsh.at[p], w.at[p, mine], s_w.at[p, 4], r_w.at[p, mine], beside, mp))

    def spread(p):
        for k in range(1, 4):
            b = x * DP + 2 * lax.rem(z + k, 4) + y
            landed(w.at[p, b], r_w.at[p, b], s_w.at[p, 0], dp, mp)
            go(remote(w.at[p, b], w.at[p, b], s_w.at[p, 3 + 2 * k], r_w.at[p, b], dp, across))
            go(remote(w.at[p, b], w.at[p, b], s_w.at[p, 4 + 2 * k], r_w.at[p, b], beside, mp))

    def relay(p):
        for k in range(4):
            bx, by = (1 - x) * DP + 2 * k + y, x * DP + 2 * k + 1 - y
            landed(w.at[p, bx], r_w.at[p, bx], s_w.at[p, 0], dp, mp)
            landed(w.at[p, by], r_w.at[p, by], s_w.at[p, 0], dp, mp)
            if k < 2:
                go(remote(w.at[p, bx], w.at[p, bx], s_w.at[p, 11 + k], r_w.at[p, bx], beside, mp))
            else:
                go(remote(w.at[p, by], w.at[p, by], s_w.at[p, 11 + k], r_w.at[p, by], dp, across))

    def complete(p):
        landed(w.at[p, mine], r_w.at[p, mine], s_w.at[p, 0], dp, mp)
        for k in range(4):
            b = (1 - x) * DP + 2 * k + 1 - y
            landed(w.at[p, b], r_w.at[p, b], s_w.at[p, 0], dp, mp)

    pltpu.make_async_copy(small, smalls.at[mp, dp], r_small.at[mine]).start()
    for k in range(DP):
        for xr in range(2):
            if k or xr:
                d, m = lax.rem(dp + k, DP), 2 * lax.rem(x + xr, 2) + c
                go(remote(small, smalls.at[mp, dp], s_small.at[2 * k + xr], r_small.at[mine], d, m))

    def token_copy(k, d, m_from, j):
        return remote(
            xs.at[m_from, d, :, half], tok.at[rows64(j), half], s_tok.at[k], r_tok.at[j], d, mp
        )

    weights_xy(0)
    pltpu.make_async_copy(xs.at[x, dp, :, half], tok.at[rows64(dp), half], r_tok.at[dp]).start()
    for k in range(1, DP):
        go(token_copy(k, lax.rem(dp + k, DP), x, dp))

    @pl.when(y == x)
    def _():
        pltpu.make_async_copy(
            xs.at[2, dp, :, half], tok.at[rows64(8 + z), half], r_tok.at[8 + z]
        ).start()
        for k in range(1, DP):
            token_copy(8 + k, lax.rem(dp + k, DP), 2, 8 + z).start()

    weights_z(0)
    weights_z(1)
    spread(0)

    for j in range(12):
        landed(tok.at[rows64(j), half], r_tok.at[j], s_tok.at[0], dp, mp)
    go(remote(tok.at[:, half], tok.at[:, half], s_pair.at[0], r_pair.at[0], dp, other))
    for j in range(8):
        for xx in range(2):
            m = 2 * xx + c
            landed(smalls.at[m, j], r_small.at[xx * DP + j], s_small.at[0], dp, mp)
    go(remote(smalls.at[c], smalls.at[c], s_pair.at[1], r_pair.at[1], dp, other))
    go(remote(smalls.at[2 + c], smalls.at[2 + c], s_pair.at[2], r_pair.at[2], dp, other))
    relay(0)
    weights_xy(1)
    weights_z(2)

    pltpu.make_async_copy(ts.at[x, dp], tea.at[mp, dp], r_tea.at[x, dp]).start()
    for k in range(DP):
        d = lax.rem(dp + k, DP)
        for xr in range(2):
            if k or xr:
                xx = lax.rem(x + xr, 2)
                go(remote(ts.at[xx, d], tea.at[mp, dp], s_tea.at[2 * k + xr], r_tea.at[x, dp], d, 2 * xx + c))
        if k:
            go(remote(ts.at[2, d], tea.at[mp, 8 + z], s_tea.at[16 + k], r_tea.at[x, 8 + z], d, 2 * y + c))

    @pl.when(y == x)
    def _():
        pltpu.make_async_copy(ts.at[2, dp], tea.at[mp, 8 + z], r_tea.at[x, 8 + z]).start()

    @pl.when(y != x)
    def _():
        remote(ts.at[2, dp], tea.at[mp, 8 + z], s_tea.at[16], r_tea.at[x, 8 + z], dp, 2 * y + c).start()

    o = 1 - c
    their_half = pl.ds(pl.multiple_of(384 * o, 128), 384)
    landed(tok.at[:, their_half], r_pair.at[0], s_pair.at[0], dp, mp)
    landed(smalls.at[o], r_pair.at[1], s_pair.at[0], dp, mp)
    landed(smalls.at[2 + o], r_pair.at[2], s_pair.at[0], dp, mp)

    low, high = lax.broadcasted_iota(jnp.int32, (512, 128), 0), lax.broadcasted_iota(jnp.int32, (512, 128), 1)
    lane, quarter = low & 127, lax.shift_right_logical(low, 7)
    pick = jnp.where((high == 24 * quarter + lane) & (lane < 24), 1.0, 0.0).astype(BF)
    stacked = jnp.concatenate(
        [jnp.concatenate([smalls[m, d, 0:32] for m in range(4)], axis=1) for d in range(DP)], axis=0
    )
    picked = nn(stacked, pick)
    vecs[...] = jnp.concatenate([picked[32 * d : 32 * d + 32, 0:96] for d in range(DP)], axis=1)
    vec[0:1] = vecs[pl.ds(6 + x * DP + dp, 1)]
    vec[1:2] = vecs[pl.ds(6 + 2 * DP + dp, 1)]
    vec[2:8] = vecs[0:6]
    blank = jnp.zeros((1, 64), F32)
    for xi in range(2):
        biases = smalls[2 * xi + c, 0, 32:48].astype(F32)
        for d in range(1, DP):
            biases = biases + smalls[2 * xi + c, d, 32:48].astype(F32)
        vec[10 + xi : 11 + xi] = jnp.concatenate([biases[k : k + 1] for k in range(6)], axis=1)
        pieces = []
        for j in range(3):
            pieces += [biases[8 + j : 9 + j, 0:64], blank, biases[11 + j : 12 + j, 0:64]]
        vec[8 + xi : 9 + xi] = jnp.concatenate(pieces + [blank] * 3, axis=1)
    complete(0)
    smid = g.at[0, 0]

    def half_of(p, xi, low, high):
        return w[p, DP * xi : DP * xi + DP, :, low:high].reshape(768, high - low)

    sums[...] = jnp.zeros(sums.shape, F32)

    def core(k, buffer, i):
        rows = chunk(i)
        return remote(
            buffer.at[rows], recv.at[k % 2, rows], s_core.at[k, i], r_core.at[k, i], dp, other
        )

    def each(count, body):
        def run(i, carry):
            body(i)
            return carry

        lax.fori_loop(0, count, run, 0)

    def add(row, value):
        width = value.shape[1]
        sums[row : row + 1, 0:width] = sums[row : row + 1, 0:width] + value

    def stream(i):
        return tok[chunk(i)].astype(F32) + jnp.where(i < 2, vec[0:1], vec[1:2])

    def project(i):
        rows = chunk(i)
        normed, _ = normalize_rows(stream(i))
        nb = (normed * vec[2:3] + vec[4:5]).astype(BF)
        nin[rows] = nb
        for xi in range(2):
            pr = (nn(nb, half_of(0, xi, 0, 640)) + vec[8 + xi : 9 + xi, 0:640]).astype(BF)
            for j in range(3):
                head, a = 3 * xi + j, 192 * j
                q_s[head, rows] = jnp.concatenate([pr[:, a : a + 64], jnp.zeros((R, 64), BF)], axis=1)
                kv[head, rows] = pr[:, a + 64 : a + 192]

    project(2)
    own, theirs = pl.ds(512, 256), pl.ds(768, 256)
    kv_copy = remote(kv.at[:, own], kv.at[:, theirs], s_x.at[0], r_x.at[0], dp, across)
    kv_copy.start()
    each(2, project)
    spread(1)

    def turn(part):
        def body(h):
            kvt[h, :, part * 512 : part * 512 + 512] = kv[h, part * 512 : part * 512 + 512].T

        each(6, body)

    def attend(h, block):
        part = block // 2
        keys, rows = slice(part * 512, part * 512 + 512), slice(block * R, block * R + R)
        st = nt(kv[h, keys], q_s[h, rows]) * LOG_SCALE + wide(mask[keys], R)
        top = jnp.max(st, axis=0, keepdims=True)
        e = jnp.exp(st - top)
        total = colsum(e)
        pt = (e * (1.0 / total)).astype(BF)
        ot = nn(kvt[h, 64:128, keys], pt)
        xi, j = lax.div(h, 3), lax.rem(h, 3)
        o_t[xi, pl.ds(pl.multiple_of(64 + 64 * j, 64), 64), rows] = ot.astype(BF)
        lse[h, :, rows] = top + jnp.log(total)

    o_t[:, 0:64] = jnp.zeros((2, 64, T), BF)
    turn(0)

    def attend_a(h):
        attend(h, 0)
        attend(h, 1)

    each(6, attend_a)
    kv_copy.wait()
    relay(1)
    weights_xy(2)
    turn(1)
    each(6, lambda h: attend(h, 2))
    spread(2)

    def out_project(i):
        rows = chunk(i)
        part = None
        for xi in range(2):
            a = o_t[xi, :, rows].T
            att[xi, rows] = a
            piece = nt(a, half_of(0, xi, 512, 768))
            part = piece if part is None else part + piece
        smid[rows] = part
        core(0, smid, i).start()

    each(3, out_project)
    complete(1)

    def forward(i):
        rows = chunk(i)
        core(0, smid, i).wait()
        mid = stream(i) + (smid[rows] + recv[0, rows] + vec[6:7])
        smid[rows] = mid
        normed, _ = normalize_rows(mid)
        nb = (normed * vec[3:4] + vec[5:6]).astype(BF)
        n2_s[rows] = nb
        for xi in range(2):
            value, slope = gelu_pair(nn(nb, half_of(1, xi, 0, 768)) + vec[10 + xi : 11 + xi])
            act[xi, rows] = value.astype(BF)
            g[1, xi, rows] = slope

    each(3, forward)
    relay(2)
    for xx in range(2):
        for j in range(12):
            landed(tea.at[2 * xx + c, j], r_tea.at[xx, j], s_tea.at[0], dp, mp)
    go(remote(tea.at[c], tea.at[c], s_pair.at[3], r_pair.at[3], dp, other))
    go(remote(tea.at[2 + c], tea.at[2 + c], s_pair.at[4], r_pair.at[4], dp, other))
    complete(2)

    def forward_out(i):
        rows = chunk(i)
        gy[rows] = nt(act[0, rows], half_of(2, 0, 0, 768)) + nt(act[1, rows], half_of(2, 1, 0, 768))
        core(1, gy, i).start()

    each(3, forward_out)
    landed(tea.at[o], r_pair.at[3], s_pair.at[0], dp, mp)
    landed(tea.at[2 + o], r_pair.at[4], s_pair.at[0], dp, mp)

    def turn_back(i):
        rows, blocks = chunk(i), pl.ds(i * 4, 4)
        core(1, gy, i).wait()
        out = smid[rows] + (gy[rows] + recv[1, rows] + vec[7:8])
        out_b = out.astype(BF)
        for m in range(4):
            yg[0, m, blocks] = out_b[:, 192 * m : 192 * m + 192].reshape(4, 64, 192)
        target = jnp.concatenate([tea[m, blocks].reshape(R, 192) for m in range(4)], axis=1)
        residual = jnp.where(wide(mask[rows], T) == 0.0, out - target.astype(F32), 0.0)
        add(8, colsum(residual * residual))
        grad_y = residual * factor[0:1, 0:1]
        gy[rows] = grad_y
        gb = grad_y.astype(BF)
        gm[rows] = gb
        add(5, colsum(gb.astype(F32)))
        part = None
        for xi in range(2):
            gpre = (nn(gb, half_of(2, xi, 0, 768)) * g[1, xi, rows]).astype(BF)
            gp[xi, rows] = gpre
            add(11 + xi, colsum(gpre.astype(F32)))
            piece = nt(gpre, half_of(1, xi, 0, 768))
            part = piece if part is None else part + piece
        x3[rows] = part
        core(2, x3, i).start()

    each(3, turn_back)

    def turn_rows(source):
        def body(i):
            tr[:, chunk(i)] = source[chunk(i)].T

        each(3, body)

    def weight_grad(p, values):
        def body(i):
            for xi in range(2):
                g[p, xi, chunk(i)] = nn(tr[chunk(i)], values[xi])

        each(3, body)

    turn_rows(gm)
    weight_grad(2, act)
    turn_rows(n2_s)
    weight_grad(1, gp)

    def mid_back(i):
        rows = chunk(i)
        core(2, x3, i).wait()
        grad_h = x3[rows] + recv[0, rows]
        normed, inverse = normalize_rows(smid[rows])
        add(1, colsum(grad_h * normed))
        add(3, colsum(grad_h))
        grad_mid = gy[rows] + norm_back(grad_h * vec[3:4], normed, inverse)
        gy[rows] = grad_mid
        gb = grad_mid.astype(BF)
        gm[rows] = gb
        add(4, colsum(gb.astype(F32)))
        for xi in range(2):
            gatt = nn(gb, half_of(0, xi, 512, 768)).astype(BF)
            for j in range(3):
                piece = gatt[:, 64 + 64 * j : 128 + 64 * j]
                ga[3 * xi + j, rows] = jnp.concatenate([jnp.zeros((R, 64), BF), piece], axis=1)

    each(3, mid_back)

    def attend_grad(h, block):
        part = block // 2
        keys, rows = slice(part * 512, part * 512 + 512), slice(block * R, block * R + R)
        kvs, q, go = kv[h, keys], q_s[h, rows], ga[h, rows]
        st = nt(kvs, q) * LOG_SCALE + wide(mask[keys], R)
        pt = jnp.exp(st - lse[h, :, rows])
        dpt = nt(kvs, go)
        delta = colsum(pt * dpt)
        dst = (pt * (dpt - delta)).astype(BF)
        dqt = nn(kvt[h, 0:64, keys], dst) * LOG_SCALE
        dq[h, rows] = dqt.T.astype(BF)
        return nn(dst, q) * LOG_SCALE + nn(pt.astype(BF), go)

    def grad_c(h):
        both = attend_grad(h, 2)
        dkv[h, 512:768] = both[0:256]
        dkx[h] = both[256:512].astype(BF)

    def grad_a(h):
        dkv[h, 0:512] = attend_grad(h, 0) + attend_grad(h, 1)

    each(6, grad_c)
    dk_copy = remote(dkx, dkr, s_x.at[1], r_x.at[1], dp, across)
    dk_copy.start()
    each(6, grad_a)
    turn_rows(gm)

    def out_grad(i):
        for xi in range(2):
            g[0, xi, chunk(i), 512:768] = nn(tr[chunk(i)], att[xi])

    each(3, out_grad)
    dk_copy.wait()

    def join(h):
        dkv[h, 512:768] = dkv[h, 512:768] + dkr[h].astype(F32)

    each(6, join)

    def project_back(i):
        rows = chunk(i)
        part = None
        for xi in range(2):
            pieces = []
            for j in range(3):
                pieces += [dq[3 * xi + j, rows], dkv[3 * xi + j, rows].astype(BF)]
            gr = jnp.concatenate(pieces + [jnp.zeros((R, 64), BF)], axis=1)
            gp[xi, rows, 0:640] = gr
            add(9 + xi if xi == 0 else 13, colsum(gr.astype(F32)))
            piece = nt(gr, half_of(0, xi, 0, 640))
            part = piece if part is None else part + piece
        x3[rows] = part
        core(3, x3, i).start()

    each(3, project_back)
    turn_rows(nin)

    def qkv_grad(i):
        rows = chunk(i)
        for xi in range(2):
            h = nn(tr[rows], gp[xi, :, 0:640])
            g[0, xi, rows, 0:512] = h[:, 0:512]
            g[0, xi, rows, 512:640] = g[0, xi, rows, 512:640] + h[:, 512:640]

    each(3, qkv_grad)

    def in_back(i):
        rows, blocks = chunk(i), pl.ds(i * 4, 4)
        core(3, x3, i).wait()
        grad_h = x3[rows] + recv[1, rows]
        normed, inverse = normalize_rows(stream(i))
        add(0, colsum(grad_h * normed))
        add(2, colsum(grad_h))
        grad_in = gy[rows] + norm_back(grad_h * vec[2:3], normed, inverse)
        total = colsum(grad_in)
        add(6, jnp.where(i < 2, total, 0.0))
        add(7, jnp.where(i < 2, 0.0, total))
        out_b = grad_in.astype(BF)
        for m in range(4):
            yg[1, m, blocks] = out_b[:, 192 * m : 192 * m + 192].reshape(4, 64, 192)

    each(3, in_back)
    for copy in sent:
        copy.wait_send()

    @pl.when(y == x)
    def _():
        for k in range(1, DP):
            token_copy(8 + k, lax.rem(dp + k, DP), 2, 8 + z).wait_send()

    @pl.when(y != x)
    def _():
        remote(ts.at[2, dp], tea.at[mp, 8 + z], s_tea.at[16], r_tea.at[x, 8 + z], dp, 2 * y + c).wait_send()


def step(xs, ts, wsh, small, mask, factor):
    dma = pltpu.SemaphoreType.DMA
    vm = pltpu.VMEM
    return pl.pallas_call(
        step_kernel,
        name="step",
        out_shape=(
            jax.ShapeDtypeStruct((3, 2, T, 768), F32),
            jax.ShapeDtypeStruct((2, 4, 12, 64, 192), BF),
            jax.ShapeDtypeStruct((16, 768), F32),
        ),
        in_specs=[pl.BlockSpec(memory_space=pl.ANY)] * 4 + [VM] * 2,
        out_specs=(VM,) * 3,
        scratch_shapes=[
            vm((T, 768), BF), vm((4, 12, 64, 192), BF), vm((3, 16, ROWS, 768), BF),
            vm((4, DP, 48, 128), BF), vm((32, 768), F32), vm((16, 768), F32),
            vm((T, 768), BF), vm((6, T, 128), BF), vm((6, 1024, 128), BF), vm((6, 128, 1024), BF),
            vm((2, R, T), BF), vm((2, T, R), BF), vm((T, 768), BF), vm((2, T, 768), BF),
            vm((T, 768), F32), vm((T, 768), BF), vm((2, T, 768), BF), vm((T, 768), F32),
            vm((2, T, 768), F32), vm((768, T), BF), vm((6, T, 128), BF), vm((6, T, 64), BF),
            vm((6, T, 128), F32), vm((6, R, 128), BF), vm((6, R, 128), BF), vm((6, 1, T), F32),
            dma((4, 3)), dma((4, 3)), dma((2,)), dma((2,)),
            dma((16,)), dma((12,)), dma((24,)), dma((2, 12)), dma((16,)), dma((16,)),
            dma((3, 15)), dma((3, 16)), dma((5,)), dma((5,)),
        ],
        compiler_params=pltpu.CompilerParams(
            collective_id=3, has_side_effects=True, vmem_limit_bytes=VMEM_LIMIT
        ),
    )(xs, ts, wsh, small, mask, factor)


def per_device_compact(
    input_stream, teacher, timestep, lengths, block_perm, table, norm_gains, shifts,
    w_qkv, qv_bias, w_out, w_in, in_bias, w_back,
):
    dp, mp, x, c = place()
    seq_len, width, quarter = input_stream.shape[1], input_stream.shape[2], teacher.shape[2]
    valid_count = jnp.sum(lengths).astype(F32)
    loss_factor = 3 * DP * seq_len / valid_count

    order = block_perm.reshape(3, DP, DP)
    source, local = order // DP, order % DP
    send_index = jnp.sum(jnp.where(source == dp, local, 0), axis=2)
    my_source = lax.dynamic_index_in_dim(source, dp, 1, keepdims=False)
    ranks = jnp.arange(DP, dtype=jnp.int32)
    where_block = jnp.sum(
        jnp.where(my_source[:, None, :] == ranks[None, :, None], ranks[None, None, :], 0), axis=2
    )
    micro = jnp.arange(3)[:, None]
    x_blocks = input_stream.reshape(3, DP, 64, width)[micro, send_index]
    t_blocks = teacher.reshape(3, DP, 64, quarter)[micro, send_index]
    half_block = lax.dynamic_index_in_dim(where_block[2].reshape(4, 2), x, 1, keepdims=False)
    their_block = lax.dynamic_index_in_dim(where_block[2].reshape(4, 2), 1 - x, 1, keepdims=False)
    first_block = lax.dynamic_index_in_dim(where_block, x, 0, keepdims=False)
    length_a = lax.dynamic_index_in_dim(lengths, x * DP + dp, 0, keepdims=False)
    length_c = lax.dynamic_index_in_dim(lengths, 2 * DP + dp, 0, keepdims=False)
    inside = jnp.arange(64, dtype=jnp.int32)
    live_a = ((first_block[:, None] * 64 + inside[None]) < length_a).reshape(512)
    live_c = ((half_block[:, None] * 64 + inside[None]) < length_c).reshape(256)
    live_d = ((their_block[:, None] * 64 + inside[None]) < length_c).reshape(256)

    wsh = jnp.stack([jnp.concatenate([w_qkv, w_out.T], axis=1), w_in, w_back.T])
    chosen = jnp.take(table, timestep, axis=0)
    rows = jnp.concatenate([norm_gains, shifts, chosen])
    lanes = jnp.arange(128)
    spread_in = jnp.where(lanes // 16 == dp, jnp.tile(in_bias, (1, 8)), 0)
    spread_qv = jnp.where((lanes // 8 == dp)[:64], jnp.tile(qv_bias.reshape(6, 8), (1, 8)), 0)
    small = jnp.concatenate(
        [
            jnp.pad(rows, ((0, 2), (0, 104))),
            jnp.pad(spread_in, ((0, 2), (0, 0))),
            jnp.pad(spread_qv, ((0, 2), (0, 64))),
        ]
    ).astype(BF)
    live = jnp.concatenate([live_a, live_c, live_d])
    mask = jnp.broadcast_to(jnp.where(live, 0.0, -1e30).astype(F32)[:, None], (1024, 128))
    factor = jnp.full((8, 128), loss_factor, F32)
    grads, yg, sums = step(x_blocks, t_blocks, wsh, small, mask, factor)
    loss_part = jnp.sum(sums[8])
    g_qkvb = jnp.stack([sums[9, :576], sums[13, :576]]).reshape(2, 3, 3, DH)
    g_qvb = jnp.stack([g_qkvb[:, :, 0], g_qkvb[:, :, 2]]).reshape(2, 6, DH)

    by_owner = sums[0:8].reshape(8, DP, 2, 2, 24)
    by_owner = lax.dynamic_index_in_dim(by_owner, c, 3, keepdims=False)
    by_owner = by_owner.transpose(2, 1, 0, 3).reshape(16, 8, 24)
    msg = jnp.zeros((16, 16, 128), F32)
    msg = msg.at[:, :8, :24].set(by_owner).at[:, 8, 0].set(loss_part)
    qvb = g_qvb.reshape(2, 2, 3, DP, 8).transpose(1, 3, 0, 2, 4).reshape(16, 48)
    inb = sums[11:13].reshape(2, 6, DP, 16).transpose(0, 2, 1, 3).reshape(16, 96)
    msg = msg.at[:, 9, :48].set(qvb).at[:, 10, :96].set(inb)
    gs, msgs, home = reduce_all(grads.reshape(3, 16, ROWS, 768), msg, yg)

    place_home = jnp.sum(
        jnp.where(send_index[:, None, :] == ranks[None, :, None], ranks[None, None, :], 0), axis=2
    )
    home = home[:, micro, place_home].reshape(2, 3, seq_len, quarter)
    total = jnp.sum(msgs, axis=0)
    loss = total[8, 0] / (valid_count * width)
    rows_a = msgs[:, 6, :24].reshape(16, 24)
    rows_c = msgs[:DP, 7, :24] + msgs[DP:, 7, :24]
    seq_rows = jnp.concatenate([rows_a, rows_c])
    onehot = (jnp.arange(table.shape[0], dtype=jnp.int32)[:, None] == timestep[None, :]).astype(F32)
    grad_table = jnp.dot(onehot, seq_rows, precision=lax.Precision.HIGHEST, preferred_element_type=F32)
    return (
        home[0],
        loss,
        home[1],
        grad_table,
        total[0:2, :24],
        total[2:6, :24],
        gs[0, :, :576],
        total[9, :48].reshape(2, 3, 8),
        gs[0, :, 576:].T,
        gs[1],
        total[10, :96].reshape(6, 16),
        gs[2].T,
    )


def solution(mesh):
    compact = mesh.shape["dp"] == 8 and mesh.shape["mp"] == 4
    return jax.shard_map(
        per_device_compact if compact else per_device,
        mesh=mesh,
        in_specs=(
            P(None, "dp", None),
            P(None, "dp", "mp"),
            P(),
            P(),
            P(),
            P(None, ("dp", "mp")),
            P(None, ("dp", "mp")),
            P(None, ("dp", "mp")),
            P("dp", "mp"),
            P(None, "mp", "dp"),
            P("mp", "dp"),
            P("dp", "mp"),
            P("mp", "dp"),
            P("mp", "dp"),
        ),
        out_specs=(
            P(None, "dp", "mp"),
            P(),
            P(None, "dp", "mp"),
            P(None, ("dp", "mp")),
            P(None, ("dp", "mp")),
            P(None, ("dp", "mp")),
            P("dp", "mp"),
            P(None, "mp", "dp"),
            P("mp", "dp"),
            P("dp", "mp"),
            P("mp", "dp"),
            P("mp", "dp"),
        ),
        check_vma=False,
    )
```

```python
import functools
import math

import jax
import jax.numpy as jnp
from jax import lax
from jax.experimental import pallas as pl
from jax.experimental.pallas import tpu as pltpu
from jax.sharding import PartitionSpec as P

H = 12
DH = 64


epsilon = 1e-05


def normalize_rows(stream):
    centered = stream - jnp.mean(stream, axis=-1, keepdims=True)
    inverse = lax.rsqrt(jnp.mean(centered * centered, axis=-1, keepdims=True) + epsilon)
    return (centered * inverse, inverse)


def column_part(array, start, width):
    return lax.dynamic_slice_in_dim(array, start, width, array.ndim - 1)


def fetch_weights(w_qkv, w_in, w_out, w_back, qv_bias, in_bias):
    return (
        lax.all_gather(w_qkv, "dp", axis=0, tiled=True),
        lax.all_gather(w_in, "dp", axis=0, tiled=True),
        lax.all_gather(w_out, "dp", axis=1, tiled=True),
        lax.all_gather(w_back, "dp", axis=1, tiled=True),
        lax.all_gather(qv_bias, "dp", axis=2, tiled=True),
        lax.all_gather(in_bias, "dp", axis=1, tiled=True),
    )


def invert_map(targets, size):
    ranks = jnp.arange(size, dtype=jnp.int32)
    return jnp.sum(jnp.where(targets[None, :] == ranks[:, None], ranks[None, :], 0), axis=1)


def masked_scores(queries, keys_all, is_live, score_scale):
    scores = (
        jnp.einsum("qhe,khe->hqk", queries, keys_all, preferred_element_type=jnp.float32)
        * score_scale
    )
    return jnp.where(is_live[None, None, :], scores, -1e30)


def attend_rows(keys_all, values, is_live, score_scale, queries):
    scores = masked_scores(queries, keys_all, is_live, score_scale)
    row_top = jnp.max(scores, axis=-1, keepdims=True)
    exponent = jnp.exp(scores - row_top)
    row_total = jnp.sum(exponent, axis=-1, keepdims=True)
    weights_p = (exponent / row_total).astype(jnp.bfloat16)
    mixed = jnp.einsum("hqk,khe->qhe", weights_p, values, preferred_element_type=jnp.float32)
    return (mixed, (row_top + jnp.log(row_total))[..., 0])


def attend_back(keys_all, values, is_live, score_scale, carry, inputs):
    queries, grad_rows, log_total = inputs
    grad_keys, grad_values = carry
    scores = masked_scores(queries, keys_all, is_live, score_scale)
    probabilities = jnp.exp(scores - log_total[..., None])
    grad_probs = jnp.einsum("qhe,khe->hqk", grad_rows, values, preferred_element_type=jnp.float32)
    row_delta = jnp.sum(probabilities * grad_probs, axis=-1, keepdims=True)
    grad_scores = (probabilities * (grad_probs - row_delta)).astype(jnp.bfloat16)
    grad_queries = (
        jnp.einsum("hqk,khe->qhe", grad_scores, keys_all, preferred_element_type=jnp.float32)
        * score_scale
    )
    grad_keys = (
        grad_keys
        + jnp.einsum("hqk,qhe->khe", grad_scores, queries, preferred_element_type=jnp.float32)
        * score_scale
    )
    grad_values = grad_values + jnp.einsum(
        "hqk,qhe->khe",
        probabilities.astype(jnp.bfloat16),
        grad_rows,
        preferred_element_type=jnp.float32,
    )
    return ((grad_keys, grad_values), grad_queries)


def norm_sums(partial_value, normed, gain_full, mp_count):
    weighted = partial_value * gain_full
    sums = jnp.stack([jnp.sum(weighted, axis=1), jnp.sum(weighted * normed, axis=1)], axis=1)
    return jnp.tile(sums, (1, mp_count))


def norm_input_grad(grad_part, gain_part, normed_part, inverse, sums, width):
    scaled = grad_part * gain_part
    return inverse * (scaled - sums[:, 0:1] / width - normed_part * sums[:, 1:2] / width)


def per_device(
    input_stream,
    teacher,
    timestep,
    lengths,
    block_perm,
    table,
    norm_gains,
    shifts,
    w_qkv,
    qv_bias,
    w_out,
    w_in,
    in_bias,
    w_back,
):
    dp_count = lax.axis_size("dp")
    mp_count = lax.axis_size("mp")
    dp_rank = lax.axis_index("dp")
    mp_rank = lax.axis_index("mp")
    micro_count, seq_len, width = input_stream.shape
    part_width = teacher.shape[2]
    block_rows = seq_len // dp_count
    heads_here = H // mp_count
    score_scale = 1.0 / math.sqrt(DH)
    col_start = mp_rank * part_width
    row_block = min(512, seq_len)
    block_count = seq_len // row_block
    valid_count = jnp.sum(lengths).astype(jnp.float32)
    loss_factor = micro_count * dp_count * seq_len / valid_count
    chosen = jnp.take(table, timestep, axis=0)
    gains_full, shifts_full, table_rows = (
        lax.all_gather(norm_gains, ("dp", "mp"), axis=1, tiled=True),
        lax.all_gather(shifts, ("dp", "mp"), axis=1, tiled=True),
        lax.all_gather(chosen, ("dp", "mp"), axis=1, tiled=True),
    )
    gains_full = gains_full.astype(jnp.float32)
    shifts_full = shifts_full.astype(jnp.float32)
    gain_parts = column_part(gains_full, col_start, part_width)
    acc_qkv = jnp.zeros((width, heads_here * 3 * DH), jnp.float32)
    acc_in = jnp.zeros((width, w_in.shape[1]), jnp.float32)
    acc_out = jnp.zeros((heads_here * DH, width), jnp.float32)
    acc_back = jnp.zeros((w_back.shape[0], width), jnp.float32)
    acc_qv = jnp.zeros((2, heads_here, DH), jnp.float32)
    acc_in_bias = jnp.zeros((w_in.shape[1],), jnp.float32)
    acc_gains = jnp.zeros((2, part_width), jnp.float32)
    acc_shifts = jnp.zeros((4, part_width), jnp.float32)
    loss_part = jnp.zeros((), jnp.float32)
    table_sums = []
    outs_y = []
    outs_grad = []
    for micro_index in range(micro_count):
        forward_set = fetch_weights(w_qkv, w_in, w_out, w_back, qv_bias, in_bias)
        proj_qkv, proj_in, proj_out, proj_back, bias_qv, bias_in = forward_set
        bias_qv = bias_qv.astype(jnp.float32)
        bias_in = bias_in.reshape(-1).astype(jnp.float32)
        block_order = block_perm[micro_index].reshape(dp_count, dp_count)
        source = block_order // dp_count
        local_index = block_order % dp_count
        send_index = jnp.sum(jnp.where(source == dp_rank, local_index, 0), axis=1)
        x_blocks = input_stream[micro_index].reshape(dp_count, block_rows, width)
        t_blocks = teacher[micro_index].reshape(dp_count, block_rows, part_width)
        got_x, got_t = (
            lax.all_to_all(
                jnp.take(x_blocks, send_index, axis=0),
                "dp",
                split_axis=0,
                concat_axis=0,
                tiled=True,
            ),
            lax.all_to_all(
                jnp.take(t_blocks, send_index, axis=0),
                "dp",
                split_axis=0,
                concat_axis=0,
                tiled=True,
            ),
        )
        my_source = lax.dynamic_index_in_dim(source, dp_rank, 0, keepdims=False)
        tokens = jnp.take(got_x, my_source, axis=0).reshape(seq_len, width).astype(jnp.float32)
        target = jnp.take(got_t, my_source, axis=0).reshape(seq_len, part_width).astype(jnp.float32)
        seq_index = micro_index * dp_count + dp_rank
        length = lax.dynamic_index_in_dim(lengths, seq_index, 0, keepdims=False)
        table_row = lax.dynamic_index_in_dim(table_rows, seq_index, 0, keepdims=False).astype(
            jnp.float32
        )
        is_live = jnp.arange(seq_len, dtype=jnp.int32) < length
        stream_in = tokens + table_row[None, :]
        normed1, inverse1 = normalize_rows(stream_in)
        normed_in = (normed1 * gains_full[0] + shifts_full[0]).astype(jnp.bfloat16)
        projected = jnp.dot(normed_in, proj_qkv, preferred_element_type=jnp.float32).reshape(
            seq_len, heads_here, 3, DH
        )
        queries = (projected[:, :, 0] + bias_qv[0]).astype(jnp.bfloat16)
        keys_all = projected[:, :, 1].astype(jnp.bfloat16)
        values = (projected[:, :, 2] + bias_qv[1]).astype(jnp.bfloat16)
        query_blocks = queries.reshape(block_count, row_block, heads_here, DH)
        mixed, log_total = lax.map(
            functools.partial(attend_rows, keys_all, values, is_live, score_scale), query_blocks
        )
        attended = mixed.reshape(seq_len, heads_here * DH).astype(jnp.bfloat16)
        attn_part = jnp.dot(attended, proj_out, preferred_element_type=jnp.float32)
        branch_attn = lax.psum_scatter(
            attn_part, "mp", scatter_dimension=1, tiled=True
        ) + column_part(shifts_full[2], col_start, part_width)
        mid_part = column_part(stream_in, col_start, part_width) + branch_attn
        stream_mid = lax.all_gather(mid_part, "mp", axis=1, tiled=True)
        normed2, inverse2 = normalize_rows(stream_mid)
        normed_mid = (normed2 * gains_full[1] + shifts_full[1]).astype(jnp.bfloat16)
        pre_act = jnp.dot(normed_mid, proj_in, preferred_element_type=jnp.float32) + bias_in
        activation = jax.nn.gelu(pre_act, approximate=True).astype(jnp.bfloat16)
        mlp_part = jnp.dot(activation, proj_back, preferred_element_type=jnp.float32)
        mlp_out = lax.psum_scatter(mlp_part, "mp", scatter_dimension=1, tiled=True) + column_part(
            shifts_full[3], col_start, part_width
        )
        out_part = mid_part + mlp_out
        residual_err = jnp.where(is_live[:, None], out_part - target, 0.0)
        loss_part = loss_part + jnp.sum(residual_err * residual_err)
        grad_y = residual_err * loss_factor
        grad_mlp = grad_y.astype(jnp.bfloat16)
        acc_shifts = acc_shifts.at[3].add(jnp.sum(grad_mlp.astype(jnp.float32), axis=0))
        grad_mlp_full = lax.all_gather(grad_mlp, "mp", axis=1, tiled=True)
        back_set = fetch_weights(w_qkv, w_in, w_out, w_back, qv_bias, in_bias)
        back_qkv, back_in, back_out, back_back = (
            back_set[0],
            back_set[1],
            back_set[2],
            back_set[3],
        )
        acc_back = acc_back + jnp.einsum(
            "tf,td->fd", activation, grad_mlp_full, preferred_element_type=jnp.float32
        )
        grad_act = jnp.einsum(
            "td,fd->tf", grad_mlp_full, back_back, preferred_element_type=jnp.float32
        )
        gelu_value, gelu_pull = jax.vjp(lambda inner: jax.nn.gelu(inner, approximate=True), pre_act)
        grad_pre = gelu_pull(grad_act)[0].astype(jnp.bfloat16)
        acc_in_bias = acc_in_bias + jnp.sum(grad_pre.astype(jnp.float32), axis=0)
        acc_in = acc_in + jnp.einsum(
            "td,tf->df", normed_mid, grad_pre, preferred_element_type=jnp.float32
        )
        partial2 = jnp.einsum("tf,df->td", grad_pre, back_in, preferred_element_type=jnp.float32)
        grad_h2, sums2 = (
            lax.psum_scatter(partial2, "mp", scatter_dimension=1, tiled=True),
            lax.psum_scatter(
                norm_sums(partial2, normed2, gains_full[1], mp_count),
                "mp",
                scatter_dimension=1,
                tiled=True,
            ),
        )
        normed2_part = column_part(normed2, col_start, part_width)
        acc_gains = acc_gains.at[1].add(jnp.sum(grad_h2 * normed2_part, axis=0))
        acc_shifts = acc_shifts.at[1].add(jnp.sum(grad_h2, axis=0))
        grad_mid = grad_y + norm_input_grad(
            grad_h2, gain_parts[1], normed2_part, inverse2, sums2, width
        )
        grad_branch = grad_mid.astype(jnp.bfloat16)
        acc_shifts = acc_shifts.at[2].add(jnp.sum(grad_branch.astype(jnp.float32), axis=0))
        grad_branch_full = lax.all_gather(grad_branch, "mp", axis=1, tiled=True)
        acc_out = acc_out + jnp.einsum(
            "tc,td->cd", attended, grad_branch_full, preferred_element_type=jnp.float32
        )
        grad_att = jnp.einsum(
            "td,cd->tc", grad_branch_full, back_out, preferred_element_type=jnp.float32
        ).astype(jnp.bfloat16)
        grad_blocks = grad_att.reshape(block_count, row_block, heads_here, DH)
        zero_heads = jnp.zeros((seq_len, heads_here, DH), jnp.float32)
        (grad_keys, grad_values), grad_queries = lax.scan(
            functools.partial(attend_back, keys_all, values, is_live, score_scale),
            (zero_heads, zero_heads),
            (query_blocks, grad_blocks, log_total),
        )
        grad_queries = grad_queries.reshape(seq_len, heads_here, DH).astype(jnp.bfloat16)
        grad_keys = grad_keys.astype(jnp.bfloat16)
        grad_values = grad_values.astype(jnp.bfloat16)
        acc_qv = acc_qv + jnp.stack(
            [
                jnp.sum(grad_queries.astype(jnp.float32), axis=0),
                jnp.sum(grad_values.astype(jnp.float32), axis=0),
            ]
        )
        grad_qkv_rows = jnp.stack([grad_queries, grad_keys, grad_values], axis=2).reshape(
            seq_len, heads_here * 3 * DH
        )
        acc_qkv = acc_qkv + jnp.einsum(
            "td,tc->dc", normed_in, grad_qkv_rows, preferred_element_type=jnp.float32
        )
        partial1 = jnp.einsum(
            "tc,dc->td", grad_qkv_rows, back_qkv, preferred_element_type=jnp.float32
        )
        grad_h1, sums1 = (
            lax.psum_scatter(partial1, "mp", scatter_dimension=1, tiled=True),
            lax.psum_scatter(
                norm_sums(partial1, normed1, gains_full[0], mp_count),
                "mp",
                scatter_dimension=1,
                tiled=True,
            ),
        )
        normed1_part = column_part(normed1, col_start, part_width)
        acc_gains = acc_gains.at[0].add(jnp.sum(grad_h1 * normed1_part, axis=0))
        acc_shifts = acc_shifts.at[0].add(jnp.sum(grad_h1, axis=0))
        grad_in_stream = grad_mid + norm_input_grad(
            grad_h1, gain_parts[0], normed1_part, inverse1, sums1, width
        )
        table_sums.append(jnp.sum(grad_in_stream, axis=0))
        back_order = invert_map(my_source, dp_count)
        out_blocks = jnp.take(
            out_part.astype(jnp.bfloat16).reshape(dp_count, block_rows, part_width),
            back_order,
            axis=0,
        )
        grad_send = jnp.take(
            grad_in_stream.astype(jnp.bfloat16).reshape(dp_count, block_rows, part_width),
            back_order,
            axis=0,
        )
        home_out, home_grad = (
            lax.all_to_all(out_blocks, "dp", split_axis=0, concat_axis=0, tiled=True),
            lax.all_to_all(grad_send, "dp", split_axis=0, concat_axis=0, tiled=True),
        )
        home_place = invert_map(send_index, dp_count)
        outs_y.append(jnp.take(home_out, home_place, axis=0).reshape(seq_len, part_width))
        outs_grad.append(jnp.take(home_grad, home_place, axis=0).reshape(seq_len, part_width))
    row_sums = jnp.zeros((micro_count, width), jnp.float32)
    row_sums = lax.dynamic_update_slice_in_dim(row_sums, jnp.stack(table_sums), col_start, 1)
    my_steps = jnp.take(timestep, jnp.arange(micro_count, dtype=jnp.int32) * dp_count + dp_rank)
    step_onehot = (
        jnp.arange(table.shape[0], dtype=jnp.int32)[:, None] == my_steps[None, :]
    ).astype(jnp.float32)
    table_grad = jnp.dot(
        step_onehot, row_sums, precision=lax.Precision.HIGHEST, preferred_element_type=jnp.float32
    )
    gains_grad = lax.dynamic_update_slice_in_dim(
        jnp.zeros((2, width), jnp.float32), acc_gains, col_start, 1
    )
    shifts_grad = lax.dynamic_update_slice_in_dim(
        jnp.zeros((4, width), jnp.float32), acc_shifts, col_start, 1
    )
    loss_row = jnp.full((1, dp_count * mp_count), loss_part, jnp.float32)
    grad_table, grad_norm_gains, grad_shifts, loss_cell = (
        lax.psum_scatter(table_grad, ("dp", "mp"), scatter_dimension=1, tiled=True),
        lax.psum_scatter(gains_grad, ("dp", "mp"), scatter_dimension=1, tiled=True),
        lax.psum_scatter(shifts_grad, ("dp", "mp"), scatter_dimension=1, tiled=True),
        lax.psum_scatter(loss_row, ("dp", "mp"), scatter_dimension=1, tiled=True),
    )
    loss = loss_cell[0, 0] / (valid_count * width)
    grad_qkv, grad_in, grad_out, grad_back, grad_qv_bias, grad_in_bias = (
        lax.psum_scatter(acc_qkv, "dp", scatter_dimension=0, tiled=True),
        lax.psum_scatter(acc_in, "dp", scatter_dimension=0, tiled=True),
        lax.psum_scatter(acc_out, "dp", scatter_dimension=1, tiled=True),
        lax.psum_scatter(acc_back, "dp", scatter_dimension=1, tiled=True),
        lax.psum_scatter(acc_qv, "dp", scatter_dimension=2, tiled=True),
        lax.psum_scatter(acc_in_bias.reshape(-1, 128), "dp", scatter_dimension=1, tiled=True),
    )
    y_out = jnp.stack(outs_y)
    grad_x = jnp.stack(outs_grad)
    return (
        y_out,
        loss,
        grad_x,
        grad_table,
        grad_norm_gains,
        grad_shifts,
        grad_qkv,
        grad_qv_bias,
        grad_out,
        grad_in,
        grad_in_bias,
        grad_back,
    )


MESH = pl.DeviceIdType.MESH
BF = jnp.bfloat16
F32 = jnp.float32
VM = pl.BlockSpec(memory_space=pltpu.VMEM)
DP = 8
ROWS = 96
VMEM_LIMIT = 64 * 1024 * 1024 - 65536


def place():
    dp, mp = lax.axis_index("dp"), lax.axis_index("mp")
    x, c = lax.div(mp, 2), lax.rem(mp, 2)
    return dp, mp, x, c


def remote(src, dst, send_sem, recv_sem, dp, mp):
    return pltpu.make_async_remote_copy(
        src_ref=src,
        dst_ref=dst,
        send_sem=send_sem,
        recv_sem=recv_sem,
        device_id=(dp, mp),
        device_id_type=MESH,
    )


def landed(dst, recv_sem, spare, dp, mp):
    remote(dst, dst, spare, recv_sem, dp, mp).wait_recv()


def greet_plane(dp, x, c):
    barrier = pltpu.get_barrier_semaphore()
    pl.semaphore_signal(barrier, inc=1, device_id=(dp, 2 * x + 1 - c), device_id_type=MESH)
    for k in range(DP):
        for xr in range(2):
            if k or xr:
                there = (lax.rem(dp + k, DP), 2 * lax.rem(x + xr, 2) + c)
                pl.semaphore_signal(barrier, inc=1, device_id=there, device_id_type=MESH)
    pl.semaphore_wait(barrier, 2 * DP)


def dot(a, b, dims):
    return lax.dot_general(a, b, (dims, ((), ())), preferred_element_type=F32)


T = 768
R = 256
LOG_SCALE = 0.125


def nn(a, b):
    return dot(a, b, ((1,), (0,)))


def nt(a, b):
    return dot(a, b, ((1,), (1,)))


def chunk(i):
    return pl.ds(pl.multiple_of(i * R, R), R)


def colsum(a):
    return jnp.sum(a, axis=0, keepdims=True)


def wide(column_tile, width):
    return jnp.concatenate([column_tile] * (width // 128), axis=1)


def gelu_pair(v):
    k = 0.7978845608028654
    v2 = v * v
    t = jnp.tanh(k * (v + 0.044715 * (v2 * v)))
    half = 0.5 * (1.0 + t)
    slope = half + 0.5 * v * ((1.0 - t * t) * (k * (1.0 + 0.134145 * v2)))
    return v * half, slope


def norm_back(g, normed, inverse):
    inner = jnp.mean(g * normed, axis=1, keepdims=True)
    return inverse * (g - jnp.mean(g, axis=1, keepdims=True) - normed * inner)


def step_kernel(
    xs, ts, wsh, small, mask, factor,
    gs, msgs, back,
    g, yg, sums, msg, r1, r2, r3,
    tok, tea, w, smalls, vecs, vec, nin, q_s, kv, kvt, o_t, att, n2_s, act, gy, gm, gp, x3, recv, tr, dkx, dkr, lse,
    s_core, r_core, s_x, r_x,
    s_tok, r_tok, s_tea, r_tea, s_small, r_small, s_w, r_w, s_pair, r_pair,
    s_msg, r_msg, s_yg, r_yg, s_a, r_a, s_b, r_b, s_c, r_c,
):
    dp, mp, x, c = place()
    other, across = 2 * x + 1 - c, 2 * (1 - x) + c
    z, y = lax.div(dp, 2), lax.rem(dp, 2)
    mine = x * DP + dp
    half = pl.ds(pl.multiple_of(384 * c, 128), 384)
    beside = 2 * z + 1 - y
    greet_plane(dp, x, c)
    sent = []

    def go(copy):
        copy.start()
        sent.append(copy)

    def rows64(j):
        return pl.ds(pl.multiple_of(64 * j, 64), 64)

    def weights_z(p):
        pltpu.make_async_copy(wsh.at[p], w.at[p, mine], r_w.at[p, mine]).start()
        for k in range(1, 4):
            zz = lax.rem(z + k, 4)
            go(remote(wsh.at[p], w.at[p, mine], s_w.at[p, k - 1], r_w.at[p, mine], 2 * zz + y, mp))

    def weights_xy(p):
        go(remote(wsh.at[p], w.at[p, mine], s_w.at[p, 3], r_w.at[p, mine], dp, across))
        go(remote(wsh.at[p], w.at[p, mine], s_w.at[p, 4], r_w.at[p, mine], beside, mp))

    def spread(p):
        for k in range(1, 4):
            b = x * DP + 2 * lax.rem(z + k, 4) + y
            landed(w.at[p, b], r_w.at[p, b], s_w.at[p, 0], dp, mp)
            go(remote(w.at[p, b], w.at[p, b], s_w.at[p, 3 + 2 * k], r_w.at[p, b], dp, across))
            go(remote(w.at[p, b], w.at[p, b], s_w.at[p, 4 + 2 * k], r_w.at[p, b], beside, mp))

    def relay(p):
        for k in range(4):
            bx, by = (1 - x) * DP + 2 * k + y, x * DP + 2 * k + 1 - y
            landed(w.at[p, bx], r_w.at[p, bx], s_w.at[p, 0], dp, mp)
            landed(w.at[p, by], r_w.at[p, by], s_w.at[p, 0], dp, mp)
            if k < 2:
                go(remote(w.at[p, bx], w.at[p, bx], s_w.at[p, 11 + k], r_w.at[p, bx], beside, mp))
            else:
                go(remote(w.at[p, by], w.at[p, by], s_w.at[p, 11 + k], r_w.at[p, by], dp, across))

    def complete(p):
        landed(w.at[p, mine], r_w.at[p, mine], s_w.at[p, 0], dp, mp)
        for k in range(4):
            b = (1 - x) * DP + 2 * k + 1 - y
            landed(w.at[p, b], r_w.at[p, b], s_w.at[p, 0], dp, mp)

    weights_z(0)
    weights_xy(0)

    pltpu.make_async_copy(small, smalls.at[mp, dp], r_small.at[mine]).start()
    for k in range(DP):
        for xr in range(2):
            if k or xr:
                d, m = lax.rem(dp + k, DP), 2 * lax.rem(x + xr, 2) + c
                go(remote(small, smalls.at[mp, dp], s_small.at[2 * k + xr], r_small.at[mine], d, m))

    def token_copy(k, d, m_from, j):
        return remote(
            xs.at[m_from, d, :, half], tok.at[rows64(j), half], s_tok.at[k], r_tok.at[j], d, mp
        )

    weights_xy(1)
    weights_xy(2)
    pltpu.make_async_copy(xs.at[x, dp, :, half], tok.at[rows64(dp), half], r_tok.at[dp]).start()
    for k in range(1, DP):
        go(token_copy(k, lax.rem(dp + k, DP), x, dp))

    @pl.when(y == x)
    def _():
        pltpu.make_async_copy(
            xs.at[2, dp, :, half], tok.at[rows64(8 + z), half], r_tok.at[8 + z]
        ).start()
        for k in range(1, DP):
            token_copy(8 + k, lax.rem(dp + k, DP), 2, 8 + z).start()

    weights_z(1)
    weights_z(2)
    spread(0)

    for j in range(12):
        landed(tok.at[rows64(j), half], r_tok.at[j], s_tok.at[0], dp, mp)
    go(remote(tok.at[:, half], tok.at[:, half], s_pair.at[0], r_pair.at[0], dp, other))
    for j in range(8):
        for xx in range(2):
            m = 2 * xx + c
            landed(smalls.at[m, j], r_small.at[xx * DP + j], s_small.at[0], dp, mp)
    go(remote(smalls.at[c], smalls.at[c], s_pair.at[1], r_pair.at[1], dp, other))
    go(remote(smalls.at[2 + c], smalls.at[2 + c], s_pair.at[2], r_pair.at[2], dp, other))
    relay(0)

    pltpu.make_async_copy(ts.at[x, dp], tea.at[mp, dp], r_tea.at[x, dp]).start()
    for k in range(DP):
        d = lax.rem(dp + k, DP)
        for xr in range(2):
            if k or xr:
                xx = lax.rem(x + xr, 2)
                go(remote(ts.at[xx, d], tea.at[mp, dp], s_tea.at[2 * k + xr], r_tea.at[x, dp], d, 2 * xx + c))
        if k:
            go(remote(ts.at[2, d], tea.at[mp, 8 + z], s_tea.at[16 + k], r_tea.at[x, 8 + z], d, 2 * y + c))

    @pl.when(y == x)
    def _():
        pltpu.make_async_copy(ts.at[2, dp], tea.at[mp, 8 + z], r_tea.at[x, 8 + z]).start()

    @pl.when(y != x)
    def _():
        remote(ts.at[2, dp], tea.at[mp, 8 + z], s_tea.at[16], r_tea.at[x, 8 + z], dp, 2 * y + c).start()

    o = 1 - c
    their_half = pl.ds(pl.multiple_of(384 * o, 128), 384)
    landed(tok.at[:, their_half], r_pair.at[0], s_pair.at[0], dp, mp)
    landed(smalls.at[o], r_pair.at[1], s_pair.at[0], dp, mp)
    landed(smalls.at[2 + o], r_pair.at[2], s_pair.at[0], dp, mp)

    low, high = lax.broadcasted_iota(jnp.int32, (512, 128), 0), lax.broadcasted_iota(jnp.int32, (512, 128), 1)
    lane, quarter = low & 127, lax.shift_right_logical(low, 7)
    pick = jnp.where((high == 24 * quarter + lane) & (lane < 24), 1.0, 0.0).astype(BF)
    stacked = jnp.concatenate(
        [jnp.concatenate([smalls[m, d, 0:32] for m in range(4)], axis=1) for d in range(DP)], axis=0
    )
    picked = nn(stacked, pick)
    vecs[...] = jnp.concatenate([picked[32 * d : 32 * d + 32, 0:96] for d in range(DP)], axis=1)
    vec[0:1] = vecs[pl.ds(6 + x * DP + dp, 1)]
    vec[1:2] = vecs[pl.ds(6 + 2 * DP + dp, 1)]
    vec[2:8] = vecs[0:6]
    blank = jnp.zeros((1, 64), F32)
    for xi in range(2):
        biases = smalls[2 * xi + c, 0, 32:48].astype(F32)
        for d in range(1, DP):
            biases = biases + smalls[2 * xi + c, d, 32:48].astype(F32)
        vec[10 + xi : 11 + xi] = jnp.concatenate([biases[k : k + 1] for k in range(6)], axis=1)
        pieces = []
        for j in range(3):
            pieces += [biases[8 + j : 9 + j, 0:64], blank, biases[11 + j : 12 + j, 0:64]]
        vec[8 + xi : 9 + xi] = jnp.concatenate(pieces + [blank] * 3, axis=1)
    complete(0)
    smid = g.at[0, 0]

    def half_of(p, xi, low, high):
        return w[p, DP * xi : DP * xi + DP, :, low:high].reshape(768, high - low)

    sums[...] = jnp.zeros(sums.shape, F32)

    def core(k, buffer, i):
        rows = chunk(i)
        return remote(
            buffer.at[rows], recv.at[k % 2, rows], s_core.at[k, i], r_core.at[k, i], dp, other
        )

    def each(count, body):
        def run(i, carry):
            body(i)
            return carry

        lax.fori_loop(0, count, run, 0)

    def lanes(h):
        return pl.ds(pl.multiple_of(128 * h, 128), 128)

    def add(row, value):
        width = value.shape[1]
        sums[row : row + 1, 0:width] = sums[row : row + 1, 0:width] + value

    def stream(i):
        return tok[chunk(i)].astype(F32) + jnp.where(i < 2, vec[0:1], vec[1:2])

    def block(p, xi, d):
        return g.at[p, xi, pl.ds(pl.multiple_of(ROWS * d, ROWS), ROWS)]

    def first(p):
        for k in range(4):
            w[p, k] = block(p, 1 - x, 2 * k + 1 - y)[...].astype(BF)
            there = (dp, across) if k < 2 else (beside, mp)
            go(remote(w.at[p, k], r1.at[p, k], s_a.at[p, k], r_a.at[p, k], *there))

    def second(p):
        for k in range(4):
            landed(r1.at[p, k], r_a.at[p, k], s_a.at[p, k], dp, mp)
            extra = r1[p, k].astype(F32)
            gx, gy_ = block(p, 1 - x, 2 * k + y)[...], block(p, x, 2 * k + 1 - y)[...]
            if k < 2:
                gy_ = gy_ + extra
            else:
                gx = gx + extra
            w[p, 4 + k] = gx.astype(BF)
            w[p, 8 + k] = gy_.astype(BF)
            go(remote(w.at[p, 4 + k], r2.at[p, 0, k], s_b.at[p, 0, k], r_b.at[p, 0, k], dp, across))
            go(remote(w.at[p, 8 + k], r2.at[p, 1, k], s_b.at[p, 1, k], r_b.at[p, 1, k], beside, mp))

    def third(p):
        for k in range(1, 5):
            zz = lax.rem(z + k, 4)
            for side in range(2):
                landed(r2.at[p, side, zz], r_b.at[p, side, zz], s_b.at[p, side, 0], dp, mp)
            total = block(p, x, 2 * zz + y)[...] + r2[p, 0, zz].astype(F32) + r2[p, 1, zz].astype(F32)
            if k < 4:
                w[p, 11 + k] = total.astype(BF)
                go(remote(w.at[p, 11 + k], r3.at[p, k - 1], s_c.at[p, k - 1], r_c.at[p, k - 1], 2 * zz + y, mp))
            else:
                gs[p] = total

    def last(p):
        for k in range(3):
            landed(r3.at[p, k], r_c.at[p, k], s_c.at[p, k], dp, mp)
        gs[p] = gs[p] + (r3[p, 0].astype(F32) + r3[p, 1].astype(F32) + r3[p, 2].astype(F32))

    def home_copy(n):
        return remote(
            yg.at[n, mp, 8 + z], back.at[n, 2, dp], s_yg.at[n, 16], r_yg.at[n, 2, dp], 2 * z + x, mp
        )

    def go_home(n):
        pltpu.make_async_copy(yg.at[n, mp, dp], back.at[n, x, dp], r_yg.at[n, x, dp]).start()
        for k in range(DP):
            s = lax.rem(dp + k, DP)
            for xr in range(2):
                if k or xr:
                    m = 2 * lax.rem(x + xr, 2) + c
                    go(remote(yg.at[n, m, s], back.at[n, x, dp], s_yg.at[n, 2 * k + xr], r_yg.at[n, x, dp], s, m))
        for k in range(4):
            j = lax.rem(z + k, 4)
            for xr in range(2):
                m = 2 * lax.rem(x + xr, 2) + c
                if k or xr:
                    go(remote(yg.at[n, m, 8 + j], back.at[n, 2, dp], s_yg.at[n, 16 + 2 * k + xr], r_yg.at[n, 2, dp], 2 * j + x, m))

        @pl.when(y == x)
        def _():
            pltpu.make_async_copy(yg.at[n, mp, 8 + z], back.at[n, 2, dp], r_yg.at[n, 2, dp]).start()

        @pl.when(y != x)
        def _():
            home_copy(n).start()

    def project(i):
        rows = chunk(i)
        normed, _ = normalize_rows(stream(i))
        nb = (normed * vec[2:3] + vec[4:5]).astype(BF)
        nin[rows] = nb
        for xi in range(2):
            pr = (nn(nb, half_of(0, xi, 0, 640)) + vec[8 + xi : 9 + xi, 0:640]).astype(BF)
            for j in range(3):
                head, a = 3 * xi + j, 192 * j
                q_s[head, rows] = jnp.concatenate([pr[:, a : a + 64], jnp.zeros((R, 64), BF)], axis=1)
                kv[head, rows] = pr[:, a + 64 : a + 192]

    project(2)
    own, theirs = pl.ds(512, 256), pl.ds(768, 256)
    kv_copy = remote(kv.at[:, own], kv.at[:, theirs], s_x.at[0], r_x.at[0], dp, across)
    kv_copy.start()
    each(2, project)
    spread(1)

    def turn(part):
        def body(h):
            kvt[h, :, part * 512 : part * 512 + 512] = kv[h, part * 512 : part * 512 + 512].T

        each(6, body)

    def attend(h, block):
        part = block // 2
        keys, rows = slice(part * 512, part * 512 + 512), slice(block * R, block * R + R)
        st = nt(kv[h, keys], q_s[h, rows]) * LOG_SCALE + wide(mask[keys], R)
        top = jnp.max(st, axis=0, keepdims=True)
        e = jnp.exp(st - top)
        total = colsum(e)
        pt = (e * (1.0 / total)).astype(BF)
        ot = nn(kvt[h, 64:128, keys], pt)
        xi, j = lax.div(h, 3), lax.rem(h, 3)
        o_t[xi, pl.ds(pl.multiple_of(64 + 64 * j, 64), 64), rows] = ot.astype(BF)
        lse[h, :, rows] = top + jnp.log(total)

    o_t[:, 0:64] = jnp.zeros((2, 64, T), BF)
    turn(0)

    def attend_a(h):
        attend(h, 0)
        attend(h, 1)

    each(6, attend_a)
    kv_copy.wait()
    relay(1)
    turn(1)
    each(6, lambda h: attend(h, 2))
    spread(2)

    def out_project(i):
        rows = chunk(i)
        part = None
        for xi in range(2):
            a = o_t[xi, :, rows].T
            att[xi, rows] = a
            piece = nt(a, half_of(0, xi, 512, 768))
            part = piece if part is None else part + piece
        smid[rows] = part
        core(0, smid, i).start()

    each(3, out_project)
    complete(1)

    def forward(i):
        rows = chunk(i)
        core(0, smid, i).wait()
        mid = stream(i) + (smid[rows] + recv[0, rows] + vec[6:7])
        smid[rows] = mid
        normed, _ = normalize_rows(mid)
        nb = (normed * vec[3:4] + vec[5:6]).astype(BF)
        n2_s[rows] = nb
        for xi in range(2):
            value, slope = gelu_pair(nn(nb, half_of(1, xi, 0, 768)) + vec[10 + xi : 11 + xi])
            act[xi, rows] = value.astype(BF)
            g[1, xi, rows] = slope

    each(3, forward)
    relay(2)
    for xx in range(2):
        for j in range(12):
            landed(tea.at[2 * xx + c, j], r_tea.at[xx, j], s_tea.at[0], dp, mp)
    go(remote(tea.at[c], tea.at[c], s_pair.at[3], r_pair.at[3], dp, other))
    go(remote(tea.at[2 + c], tea.at[2 + c], s_pair.at[4], r_pair.at[4], dp, other))
    complete(2)

    def forward_out(i):
        rows = chunk(i)
        gy[rows] = nt(act[0, rows], half_of(2, 0, 0, 768)) + nt(act[1, rows], half_of(2, 1, 0, 768))
        core(1, gy, i).start()

    each(3, forward_out)
    landed(tea.at[o], r_pair.at[3], s_pair.at[0], dp, mp)
    landed(tea.at[2 + o], r_pair.at[4], s_pair.at[0], dp, mp)

    def turn_back(i):
        rows, blocks = chunk(i), pl.ds(i * 4, 4)
        core(1, gy, i).wait()
        out = smid[rows] + (gy[rows] + recv[1, rows] + vec[7:8])
        out_b = out.astype(BF)
        for m in range(4):
            yg[0, m, blocks] = out_b[:, 192 * m : 192 * m + 192].reshape(4, 64, 192)
        target = jnp.concatenate([tea[m, blocks].reshape(R, 192) for m in range(4)], axis=1)
        residual = jnp.where(wide(mask[rows], T) == 0.0, out - target.astype(F32), 0.0)
        add(8, colsum(residual * residual))
        grad_y = residual * factor[0:1, 0:1]
        gy[rows] = grad_y
        gb = grad_y.astype(BF)
        gm[rows] = gb
        add(5, colsum(gb.astype(F32)))
        part = None
        for xi in range(2):
            gpre = (nn(gb, half_of(2, xi, 0, 768)) * g[1, xi, rows]).astype(BF)
            gp[xi, rows] = gpre
            add(11 + xi, colsum(gpre.astype(F32)))
            piece = nt(gpre, half_of(1, xi, 0, 768))
            part = piece if part is None else part + piece
        x3[rows] = part
        core(2, x3, i).start()

    each(3, turn_back)

    def turn_rows(source):
        def body(i):
            tr[:, chunk(i)] = source[chunk(i)].T

        each(3, body)

    def weight_grad(p, values):
        def body(i):
            for xi in range(2):
                g[p, xi, chunk(i)] = nn(tr[chunk(i)], values[xi])

        each(3, body)

    turn_rows(gm)
    weight_grad(2, act)
    for copy in sent:
        copy.wait_send()
    sent.clear()
    first(2)
    turn_rows(n2_s)
    weight_grad(1, gp)
    first(1)
    second(2)

    def mid_back(i):
        rows = chunk(i)
        core(2, x3, i).wait()
        grad_h = x3[rows] + recv[0, rows]
        normed, inverse = normalize_rows(smid[rows])
        add(1, colsum(grad_h * normed))
        add(3, colsum(grad_h))
        grad_mid = gy[rows] + norm_back(grad_h * vec[3:4], normed, inverse)
        gy[rows] = grad_mid
        gb = grad_mid.astype(BF)
        gm[rows] = gb
        add(4, colsum(gb.astype(F32)))
        for xi in range(2):
            gatt = nn(gb, half_of(0, xi, 512, 768)).astype(BF)
            for j in range(3):
                piece = gatt[:, 64 + 64 * j : 128 + 64 * j]
                n2_s[rows, 384 * xi + 128 * j : 384 * xi + 128 * j + 128] = jnp.concatenate([jnp.zeros((R, 64), BF), piece], axis=1)

    each(3, mid_back)
    go_home(0)

    def attend_grad(h, block):
        part = block // 2
        keys, rows = slice(part * 512, part * 512 + 512), slice(block * R, block * R + R)
        kvs, q, go = kv[h, keys], q_s[h, rows], n2_s[rows, lanes(h)]
        st = nt(kvs, q) * LOG_SCALE + wide(mask[keys], R)
        pt = jnp.exp(st - lse[h, :, rows])
        dpt = nt(kvs, go)
        delta = colsum(pt * dpt)
        dst = (pt * (dpt - delta)).astype(BF)
        dqt = nn(kvt[h, 0:64, keys], dst) * LOG_SCALE
        q_s[h, rows, 0:64] = dqt.T.astype(BF)
        return nn(dst, q) * LOG_SCALE + nn(pt.astype(BF), go)

    def grad_c(h):
        both = attend_grad(h, 2)
        recv[0, 512:768, lanes(h)] = both[0:256]
        dkx[h] = both[256:512].astype(BF)

    def grad_a(h):
        recv[0, 0:512, lanes(h)] = attend_grad(h, 0) + attend_grad(h, 1)

    each(6, grad_c)
    dk_copy = remote(dkx, dkr, s_x.at[1], r_x.at[1], dp, across)
    dk_copy.start()
    second(1)
    third(2)
    each(6, grad_a)
    turn_rows(gm)

    def out_grad(i):
        for xi in range(2):
            g[0, xi, chunk(i), 512:768] = nn(tr[chunk(i)], att[xi])

    each(3, out_grad)
    third(1)
    dk_copy.wait()

    def join(h):
        recv[0, 512:768, lanes(h)] = recv[0, 512:768, lanes(h)] + dkr[h].astype(F32)

    each(6, join)

    def project_back(i):
        rows = chunk(i)
        part = None
        for xi in range(2):
            pieces = []
            for j in range(3):
                at = 384 * xi + 128 * j
                pieces += [q_s[3 * xi + j, rows, 0:64], recv[0, rows, at : at + 128].astype(BF)]
            gr = jnp.concatenate(pieces + [jnp.zeros((R, 64), BF)], axis=1)
            gp[xi, rows, 0:640] = gr
            add(9 + xi if xi == 0 else 13, colsum(gr.astype(F32)))
            piece = nt(gr, half_of(0, xi, 0, 640))
            part = piece if part is None else part + piece
        x3[rows] = part
        core(3, x3, i).start()

    each(3, project_back)
    turn_rows(nin)

    def qkv_grad(i):
        rows = chunk(i)
        for xi in range(2):
            h = nn(tr[rows], gp[xi, :, 0:640])
            g[0, xi, rows, 0:512] = h[:, 0:512]
            g[0, xi, rows, 512:640] = g[0, xi, rows, 512:640] + h[:, 512:640]

    each(3, qkv_grad)
    first(0)

    def in_back(i):
        rows, blocks = chunk(i), pl.ds(i * 4, 4)
        core(3, x3, i).wait()
        grad_h = x3[rows] + recv[1, rows]
        normed, inverse = normalize_rows(stream(i))
        add(0, colsum(grad_h * normed))
        add(2, colsum(grad_h))
        grad_in = gy[rows] + norm_back(grad_h * vec[2:3], normed, inverse)
        total = colsum(grad_in)
        add(6, jnp.where(i < 2, total, 0.0))
        add(7, jnp.where(i < 2, 0.0, total))
        out_b = grad_in.astype(BF)
        for m in range(4):
            yg[1, m, blocks] = out_b[:, 192 * m : 192 * m + 192].reshape(4, 64, 192)

    each(3, in_back)
    second(0)

    msg[...] = jnp.zeros(msg.shape, F32)
    loss_row = sums[8:9, 0:128]
    for k in range(1, 6):
        loss_row = loss_row + sums[8:9, 128 * k : 128 * k + 128]
    for xi in range(2):
        bias_sums = sums[9:10] if xi == 0 else sums[13:14]
        hidden = sums[11 + xi : 12 + xi]
        for d in range(DP):
            at, owner = 96 * d + 48 * xi, 8 * xi + d
            msg[owner, 0:8, 0:24] = jnp.where(c == 0, sums[0:8, at : at + 24], sums[0:8, at + 24 : at + 48])
            msg[owner, 8:9] = loss_row
            for j in range(3):
                for kind in range(2):
                    low = 192 * j + 128 * kind
                    msg[owner, 9 + 3 * kind + j : 10 + 3 * kind + j, 0:64] = bias_sums[:, low : low + 64]
            for k in range(6):
                msg[owner, 16 + k : 17 + k] = hidden[:, 128 * k : 128 * k + 128]
    pltpu.make_async_copy(msg.at[mine], msgs.at[mine], r_msg.at[mine]).start()
    for k in range(DP):
        for xr in range(2):
            if k or xr:
                d, xx = lax.rem(dp + k, DP), lax.rem(x + xr, 2)
                go(remote(msg.at[xx * DP + d], msgs.at[mine], s_msg.at[2 * k + xr], r_msg.at[mine], d, 2 * xx + c))
    go_home(1)
    third(0)
    last(2)
    last(1)
    last(0)
    for j in range(16):
        landed(msgs.at[j], r_msg.at[j], s_msg.at[0], dp, mp)
    for n in range(2):
        for m in range(3):
            for j in range(DP):
                landed(back.at[n, m, j], r_yg.at[n, m, j], s_yg.at[n, 0], dp, mp)
    for copy in sent:
        copy.wait_send()

    @pl.when(y == x)
    def _():
        for k in range(1, DP):
            token_copy(8 + k, lax.rem(dp + k, DP), 2, 8 + z).wait_send()

    @pl.when(y != x)
    def _():
        remote(ts.at[2, dp], tea.at[mp, 8 + z], s_tea.at[16], r_tea.at[x, 8 + z], dp, 2 * y + c).wait_send()
        home_copy(0).wait_send()
        home_copy(1).wait_send()


def step(xs, ts, wsh, small, mask, factor):
    dma = pltpu.SemaphoreType.DMA
    vm = pltpu.VMEM
    block = (ROWS, 768)
    return pl.pallas_call(
        step_kernel,
        name="step",
        out_shape=(
            jax.ShapeDtypeStruct((3, ROWS, 768), F32),
            jax.ShapeDtypeStruct((16, 24, 128), F32),
            jax.ShapeDtypeStruct((2, 3, DP, 64, 192), BF),
        ),
        in_specs=[pl.BlockSpec(memory_space=pl.ANY)] * 4 + [VM] * 2,
        out_specs=(VM, VM, pl.BlockSpec(memory_space=pl.ANY)),
        scratch_shapes=[
            vm((3, 2, T, 768), F32), vm((2, 4, 12, 64, 192), BF), vm((16, 768), F32), vm((16, 24, 128), F32),
            vm((3, 4) + block, BF), vm((3, 2, 4) + block, BF), vm((3, 3) + block, BF),
            vm((T, 768), BF), vm((4, 12, 64, 192), BF), vm((3, 16) + block, BF),
            vm((4, DP, 48, 128), BF), vm((32, 768), F32), vm((16, 768), F32),
            vm((T, 768), BF), vm((6, T, 128), BF), vm((6, 1024, 128), BF), vm((6, 128, 1024), BF),
            vm((2, R, T), BF), vm((2, T, R), BF), vm((T, 768), BF), vm((2, T, 768), BF),
            vm((T, 768), F32), vm((T, 768), BF), vm((2, T, 768), BF), vm((T, 768), F32),
            vm((2, T, 768), F32), vm((768, T), BF), vm((6, R, 128), BF), vm((6, R, 128), BF),
            vm((6, 1, T), F32),
            dma((4, 3)), dma((4, 3)), dma((2,)), dma((2,)),
            dma((16,)), dma((12,)), dma((24,)), dma((2, 12)), dma((16,)), dma((16,)),
            dma((3, 15)), dma((3, 16)), dma((5,)), dma((5,)),
            dma((16,)), dma((16,)), dma((2, 24)), dma((2, 3, DP)), dma((3, 4)), dma((3, 4)),
            dma((3, 2, 4)), dma((3, 2, 4)), dma((3, 3)), dma((3, 3)),
        ],
        compiler_params=pltpu.CompilerParams(
            collective_id=3, has_side_effects=True, vmem_limit_bytes=VMEM_LIMIT
        ),
    )(xs, ts, wsh, small, mask, factor)


def per_device_compact(
    input_stream, teacher, timestep, lengths, block_perm, table, norm_gains, shifts,
    w_qkv, qv_bias, w_out, w_in, in_bias, w_back,
):
    dp, mp, x, c = place()
    seq_len, width, quarter = input_stream.shape[1], input_stream.shape[2], teacher.shape[2]
    valid_count = jnp.sum(lengths).astype(F32)
    loss_factor = 3 * DP * seq_len / valid_count

    order = block_perm.reshape(3, DP, DP)
    source, local = order // DP, order % DP
    send_index = jnp.sum(jnp.where(source == dp, local, 0), axis=2)
    my_source = lax.dynamic_index_in_dim(source, dp, 1, keepdims=False)
    ranks = jnp.arange(DP, dtype=jnp.int32)
    where_block = jnp.sum(
        jnp.where(my_source[:, None, :] == ranks[None, :, None], ranks[None, None, :], 0), axis=2
    )
    micro = jnp.arange(3)[:, None]
    x_blocks = input_stream.reshape(3, DP, 64, width)[micro, send_index]
    t_blocks = teacher.reshape(3, DP, 64, quarter)[micro, send_index]
    half_block = lax.dynamic_index_in_dim(where_block[2].reshape(4, 2), x, 1, keepdims=False)
    their_block = lax.dynamic_index_in_dim(where_block[2].reshape(4, 2), 1 - x, 1, keepdims=False)
    first_block = lax.dynamic_index_in_dim(where_block, x, 0, keepdims=False)
    length_a = lax.dynamic_index_in_dim(lengths, x * DP + dp, 0, keepdims=False)
    length_c = lax.dynamic_index_in_dim(lengths, 2 * DP + dp, 0, keepdims=False)
    inside = jnp.arange(64, dtype=jnp.int32)
    live_a = ((first_block[:, None] * 64 + inside[None]) < length_a).reshape(512)
    live_c = ((half_block[:, None] * 64 + inside[None]) < length_c).reshape(256)
    live_d = ((their_block[:, None] * 64 + inside[None]) < length_c).reshape(256)

    wsh = jnp.stack([jnp.concatenate([w_qkv, w_out.T], axis=1), w_in, w_back.T])
    chosen = jnp.take(table, timestep, axis=0)
    rows = jnp.concatenate([norm_gains, shifts, chosen])
    lanes = jnp.arange(128)
    spread_in = jnp.where(lanes // 16 == dp, jnp.tile(in_bias, (1, 8)), 0)
    spread_qv = jnp.where((lanes // 8 == dp)[:64], jnp.tile(qv_bias.reshape(6, 8), (1, 8)), 0)
    small = jnp.concatenate(
        [
            jnp.pad(rows, ((0, 2), (0, 104))),
            jnp.pad(spread_in, ((0, 2), (0, 0))),
            jnp.pad(spread_qv, ((0, 2), (0, 64))),
        ]
    ).astype(BF)
    live = jnp.concatenate([live_a, live_c, live_d])
    mask = jnp.broadcast_to(jnp.where(live, 0.0, -1e30).astype(F32)[:, None], (1024, 128))
    factor = jnp.full((8, 128), loss_factor, F32)
    gs, msgs, home = step(x_blocks, t_blocks, wsh, small, mask, factor)

    place_home = jnp.sum(
        jnp.where(send_index[:, None, :] == ranks[None, :, None], ranks[None, None, :], 0), axis=2
    )
    home = home[:, micro, place_home].reshape(2, 3, seq_len, quarter)
    total = jnp.sum(msgs, axis=0)
    loss = jnp.sum(total[8]) / (valid_count * width)
    rows_a = msgs[:, 6, :24].reshape(16, 24)
    rows_c = msgs[:DP, 7, :24] + msgs[DP:, 7, :24]
    seq_rows = jnp.concatenate([rows_a, rows_c])
    onehot = (jnp.arange(table.shape[0], dtype=jnp.int32)[:, None] == timestep[None, :]).astype(F32)
    grad_table = jnp.dot(onehot, seq_rows, precision=lax.Precision.HIGHEST, preferred_element_type=F32)
    return (
        home[0],
        loss,
        home[1],
        grad_table,
        total[0:2, :24],
        total[2:6, :24],
        gs[0, :, :576],
        lax.dynamic_slice(total, (9, 8 * dp), (6, 8)).reshape(2, 3, 8),
        gs[0, :, 576:].T,
        gs[1],
        lax.dynamic_slice(total, (16, 16 * dp), (6, 16)),
        gs[2].T,
    )


def solution(mesh):
    compact = mesh.shape["dp"] == 8 and mesh.shape["mp"] == 4
    return jax.shard_map(
        per_device_compact if compact else per_device,
        mesh=mesh,
        in_specs=(
            P(None, "dp", None),
            P(None, "dp", "mp"),
            P(),
            P(),
            P(),
            P(None, ("dp", "mp")),
            P(None, ("dp", "mp")),
            P(None, ("dp", "mp")),
            P("dp", "mp"),
            P(None, "mp", "dp"),
            P("mp", "dp"),
            P("dp", "mp"),
            P("mp", "dp"),
            P("mp", "dp"),
        ),
        out_specs=(
            P(None, "dp", "mp"),
            P(),
            P(None, "dp", "mp"),
            P(None, ("dp", "mp")),
            P(None, ("dp", "mp")),
            P(None, ("dp", "mp")),
            P("dp", "mp"),
            P(None, "mp", "dp"),
            P("mp", "dp"),
            P("dp", "mp"),
            P("mp", "dp"),
            P("mp", "dp"),
        ),
        check_vma=False,
    )
```

```python
import functools
import math

import jax
import jax.numpy as jnp
from jax import lax
from jax.experimental import pallas as pl
from jax.experimental.pallas import tpu as pltpu
from jax.sharding import PartitionSpec as P

H = 12
DH = 64


epsilon = 1e-05


def normalize_rows(stream):
    centered = stream - jnp.mean(stream, axis=-1, keepdims=True)
    inverse = lax.rsqrt(jnp.mean(centered * centered, axis=-1, keepdims=True) + epsilon)
    return (centered * inverse, inverse)


def column_part(array, start, width):
    return lax.dynamic_slice_in_dim(array, start, width, array.ndim - 1)


def fetch_weights(w_qkv, w_in, w_out, w_back, qv_bias, in_bias):
    return (
        lax.all_gather(w_qkv, "dp", axis=0, tiled=True),
        lax.all_gather(w_in, "dp", axis=0, tiled=True),
        lax.all_gather(w_out, "dp", axis=1, tiled=True),
        lax.all_gather(w_back, "dp", axis=1, tiled=True),
        lax.all_gather(qv_bias, "dp", axis=2, tiled=True),
        lax.all_gather(in_bias, "dp", axis=1, tiled=True),
    )


def invert_map(targets, size):
    ranks = jnp.arange(size, dtype=jnp.int32)
    return jnp.sum(jnp.where(targets[None, :] == ranks[:, None], ranks[None, :], 0), axis=1)


def masked_scores(queries, keys_all, is_live, score_scale):
    scores = (
        jnp.einsum("qhe,khe->hqk", queries, keys_all, preferred_element_type=jnp.float32)
        * score_scale
    )
    return jnp.where(is_live[None, None, :], scores, -1e30)


def attend_rows(keys_all, values, is_live, score_scale, queries):
    scores = masked_scores(queries, keys_all, is_live, score_scale)
    row_top = jnp.max(scores, axis=-1, keepdims=True)
    exponent = jnp.exp(scores - row_top)
    row_total = jnp.sum(exponent, axis=-1, keepdims=True)
    weights_p = (exponent / row_total).astype(jnp.bfloat16)
    mixed = jnp.einsum("hqk,khe->qhe", weights_p, values, preferred_element_type=jnp.float32)
    return (mixed, (row_top + jnp.log(row_total))[..., 0])


def attend_back(keys_all, values, is_live, score_scale, carry, inputs):
    queries, grad_rows, log_total = inputs
    grad_keys, grad_values = carry
    scores = masked_scores(queries, keys_all, is_live, score_scale)
    probabilities = jnp.exp(scores - log_total[..., None])
    grad_probs = jnp.einsum("qhe,khe->hqk", grad_rows, values, preferred_element_type=jnp.float32)
    row_delta = jnp.sum(probabilities * grad_probs, axis=-1, keepdims=True)
    grad_scores = (probabilities * (grad_probs - row_delta)).astype(jnp.bfloat16)
    grad_queries = (
        jnp.einsum("hqk,khe->qhe", grad_scores, keys_all, preferred_element_type=jnp.float32)
        * score_scale
    )
    grad_keys = (
        grad_keys
        + jnp.einsum("hqk,qhe->khe", grad_scores, queries, preferred_element_type=jnp.float32)
        * score_scale
    )
    grad_values = grad_values + jnp.einsum(
        "hqk,qhe->khe",
        probabilities.astype(jnp.bfloat16),
        grad_rows,
        preferred_element_type=jnp.float32,
    )
    return ((grad_keys, grad_values), grad_queries)


def norm_sums(partial_value, normed, gain_full, mp_count):
    weighted = partial_value * gain_full
    sums = jnp.stack([jnp.sum(weighted, axis=1), jnp.sum(weighted * normed, axis=1)], axis=1)
    return jnp.tile(sums, (1, mp_count))


def norm_input_grad(grad_part, gain_part, normed_part, inverse, sums, width):
    scaled = grad_part * gain_part
    return inverse * (scaled - sums[:, 0:1] / width - normed_part * sums[:, 1:2] / width)


def per_device(
    input_stream,
    teacher,
    timestep,
    lengths,
    block_perm,
    table,
    norm_gains,
    shifts,
    w_qkv,
    qv_bias,
    w_out,
    w_in,
    in_bias,
    w_back,
):
    dp_count = lax.axis_size("dp")
    mp_count = lax.axis_size("mp")
    dp_rank = lax.axis_index("dp")
    mp_rank = lax.axis_index("mp")
    micro_count, seq_len, width = input_stream.shape
    part_width = teacher.shape[2]
    block_rows = seq_len // dp_count
    heads_here = H // mp_count
    score_scale = 1.0 / math.sqrt(DH)
    col_start = mp_rank * part_width
    row_block = min(512, seq_len)
    block_count = seq_len // row_block
    valid_count = jnp.sum(lengths).astype(jnp.float32)
    loss_factor = micro_count * dp_count * seq_len / valid_count
    chosen = jnp.take(table, timestep, axis=0)
    gains_full, shifts_full, table_rows = (
        lax.all_gather(norm_gains, ("dp", "mp"), axis=1, tiled=True),
        lax.all_gather(shifts, ("dp", "mp"), axis=1, tiled=True),
        lax.all_gather(chosen, ("dp", "mp"), axis=1, tiled=True),
    )
    gains_full = gains_full.astype(jnp.float32)
    shifts_full = shifts_full.astype(jnp.float32)
    gain_parts = column_part(gains_full, col_start, part_width)
    acc_qkv = jnp.zeros((width, heads_here * 3 * DH), jnp.float32)
    acc_in = jnp.zeros((width, w_in.shape[1]), jnp.float32)
    acc_out = jnp.zeros((heads_here * DH, width), jnp.float32)
    acc_back = jnp.zeros((w_back.shape[0], width), jnp.float32)
    acc_qv = jnp.zeros((2, heads_here, DH), jnp.float32)
    acc_in_bias = jnp.zeros((w_in.shape[1],), jnp.float32)
    acc_gains = jnp.zeros((2, part_width), jnp.float32)
    acc_shifts = jnp.zeros((4, part_width), jnp.float32)
    loss_part = jnp.zeros((), jnp.float32)
    table_sums = []
    outs_y = []
    outs_grad = []
    for micro_index in range(micro_count):
        forward_set = fetch_weights(w_qkv, w_in, w_out, w_back, qv_bias, in_bias)
        proj_qkv, proj_in, proj_out, proj_back, bias_qv, bias_in = forward_set
        bias_qv = bias_qv.astype(jnp.float32)
        bias_in = bias_in.reshape(-1).astype(jnp.float32)
        block_order = block_perm[micro_index].reshape(dp_count, dp_count)
        source = block_order // dp_count
        local_index = block_order % dp_count
        send_index = jnp.sum(jnp.where(source == dp_rank, local_index, 0), axis=1)
        x_blocks = input_stream[micro_index].reshape(dp_count, block_rows, width)
        t_blocks = teacher[micro_index].reshape(dp_count, block_rows, part_width)
        got_x, got_t = (
            lax.all_to_all(
                jnp.take(x_blocks, send_index, axis=0),
                "dp",
                split_axis=0,
                concat_axis=0,
                tiled=True,
            ),
            lax.all_to_all(
                jnp.take(t_blocks, send_index, axis=0),
                "dp",
                split_axis=0,
                concat_axis=0,
                tiled=True,
            ),
        )
        my_source = lax.dynamic_index_in_dim(source, dp_rank, 0, keepdims=False)
        tokens = jnp.take(got_x, my_source, axis=0).reshape(seq_len, width).astype(jnp.float32)
        target = jnp.take(got_t, my_source, axis=0).reshape(seq_len, part_width).astype(jnp.float32)
        seq_index = micro_index * dp_count + dp_rank
        length = lax.dynamic_index_in_dim(lengths, seq_index, 0, keepdims=False)
        table_row = lax.dynamic_index_in_dim(table_rows, seq_index, 0, keepdims=False).astype(
            jnp.float32
        )
        is_live = jnp.arange(seq_len, dtype=jnp.int32) < length
        stream_in = tokens + table_row[None, :]
        normed1, inverse1 = normalize_rows(stream_in)
        normed_in = (normed1 * gains_full[0] + shifts_full[0]).astype(jnp.bfloat16)
        projected = jnp.dot(normed_in, proj_qkv, preferred_element_type=jnp.float32).reshape(
            seq_len, heads_here, 3, DH
        )
        queries = (projected[:, :, 0] + bias_qv[0]).astype(jnp.bfloat16)
        keys_all = projected[:, :, 1].astype(jnp.bfloat16)
        values = (projected[:, :, 2] + bias_qv[1]).astype(jnp.bfloat16)
        query_blocks = queries.reshape(block_count, row_block, heads_here, DH)
        mixed, log_total = lax.map(
            functools.partial(attend_rows, keys_all, values, is_live, score_scale), query_blocks
        )
        attended = mixed.reshape(seq_len, heads_here * DH).astype(jnp.bfloat16)
        attn_part = jnp.dot(attended, proj_out, preferred_element_type=jnp.float32)
        branch_attn = lax.psum_scatter(
            attn_part, "mp", scatter_dimension=1, tiled=True
        ) + column_part(shifts_full[2], col_start, part_width)
        mid_part = column_part(stream_in, col_start, part_width) + branch_attn
        stream_mid = lax.all_gather(mid_part, "mp", axis=1, tiled=True)
        normed2, inverse2 = normalize_rows(stream_mid)
        normed_mid = (normed2 * gains_full[1] + shifts_full[1]).astype(jnp.bfloat16)
        pre_act = jnp.dot(normed_mid, proj_in, preferred_element_type=jnp.float32) + bias_in
        activation = jax.nn.gelu(pre_act, approximate=True).astype(jnp.bfloat16)
        mlp_part = jnp.dot(activation, proj_back, preferred_element_type=jnp.float32)
        mlp_out = lax.psum_scatter(mlp_part, "mp", scatter_dimension=1, tiled=True) + column_part(
            shifts_full[3], col_start, part_width
        )
        out_part = mid_part + mlp_out
        residual_err = jnp.where(is_live[:, None], out_part - target, 0.0)
        loss_part = loss_part + jnp.sum(residual_err * residual_err)
        grad_y = residual_err * loss_factor
        grad_mlp = grad_y.astype(jnp.bfloat16)
        acc_shifts = acc_shifts.at[3].add(jnp.sum(grad_mlp.astype(jnp.float32), axis=0))
        grad_mlp_full = lax.all_gather(grad_mlp, "mp", axis=1, tiled=True)
        back_set = fetch_weights(w_qkv, w_in, w_out, w_back, qv_bias, in_bias)
        back_qkv, back_in, back_out, back_back = (
            back_set[0],
            back_set[1],
            back_set[2],
            back_set[3],
        )
        acc_back = acc_back + jnp.einsum(
            "tf,td->fd", activation, grad_mlp_full, preferred_element_type=jnp.float32
        )
        grad_act = jnp.einsum(
            "td,fd->tf", grad_mlp_full, back_back, preferred_element_type=jnp.float32
        )
        gelu_value, gelu_pull = jax.vjp(lambda inner: jax.nn.gelu(inner, approximate=True), pre_act)
        grad_pre = gelu_pull(grad_act)[0].astype(jnp.bfloat16)
        acc_in_bias = acc_in_bias + jnp.sum(grad_pre.astype(jnp.float32), axis=0)
        acc_in = acc_in + jnp.einsum(
            "td,tf->df", normed_mid, grad_pre, preferred_element_type=jnp.float32
        )
        partial2 = jnp.einsum("tf,df->td", grad_pre, back_in, preferred_element_type=jnp.float32)
        grad_h2, sums2 = (
            lax.psum_scatter(partial2, "mp", scatter_dimension=1, tiled=True),
            lax.psum_scatter(
                norm_sums(partial2, normed2, gains_full[1], mp_count),
                "mp",
                scatter_dimension=1,
                tiled=True,
            ),
        )
        normed2_part = column_part(normed2, col_start, part_width)
        acc_gains = acc_gains.at[1].add(jnp.sum(grad_h2 * normed2_part, axis=0))
        acc_shifts = acc_shifts.at[1].add(jnp.sum(grad_h2, axis=0))
        grad_mid = grad_y + norm_input_grad(
            grad_h2, gain_parts[1], normed2_part, inverse2, sums2, width
        )
        grad_branch = grad_mid.astype(jnp.bfloat16)
        acc_shifts = acc_shifts.at[2].add(jnp.sum(grad_branch.astype(jnp.float32), axis=0))
        grad_branch_full = lax.all_gather(grad_branch, "mp", axis=1, tiled=True)
        acc_out = acc_out + jnp.einsum(
            "tc,td->cd", attended, grad_branch_full, preferred_element_type=jnp.float32
        )
        grad_att = jnp.einsum(
            "td,cd->tc", grad_branch_full, back_out, preferred_element_type=jnp.float32
        ).astype(jnp.bfloat16)
        grad_blocks = grad_att.reshape(block_count, row_block, heads_here, DH)
        zero_heads = jnp.zeros((seq_len, heads_here, DH), jnp.float32)
        (grad_keys, grad_values), grad_queries = lax.scan(
            functools.partial(attend_back, keys_all, values, is_live, score_scale),
            (zero_heads, zero_heads),
            (query_blocks, grad_blocks, log_total),
        )
        grad_queries = grad_queries.reshape(seq_len, heads_here, DH).astype(jnp.bfloat16)
        grad_keys = grad_keys.astype(jnp.bfloat16)
        grad_values = grad_values.astype(jnp.bfloat16)
        acc_qv = acc_qv + jnp.stack(
            [
                jnp.sum(grad_queries.astype(jnp.float32), axis=0),
                jnp.sum(grad_values.astype(jnp.float32), axis=0),
            ]
        )
        grad_qkv_rows = jnp.stack([grad_queries, grad_keys, grad_values], axis=2).reshape(
            seq_len, heads_here * 3 * DH
        )
        acc_qkv = acc_qkv + jnp.einsum(
            "td,tc->dc", normed_in, grad_qkv_rows, preferred_element_type=jnp.float32
        )
        partial1 = jnp.einsum(
            "tc,dc->td", grad_qkv_rows, back_qkv, preferred_element_type=jnp.float32
        )
        grad_h1, sums1 = (
            lax.psum_scatter(partial1, "mp", scatter_dimension=1, tiled=True),
            lax.psum_scatter(
                norm_sums(partial1, normed1, gains_full[0], mp_count),
                "mp",
                scatter_dimension=1,
                tiled=True,
            ),
        )
        normed1_part = column_part(normed1, col_start, part_width)
        acc_gains = acc_gains.at[0].add(jnp.sum(grad_h1 * normed1_part, axis=0))
        acc_shifts = acc_shifts.at[0].add(jnp.sum(grad_h1, axis=0))
        grad_in_stream = grad_mid + norm_input_grad(
            grad_h1, gain_parts[0], normed1_part, inverse1, sums1, width
        )
        table_sums.append(jnp.sum(grad_in_stream, axis=0))
        back_order = invert_map(my_source, dp_count)
        out_blocks = jnp.take(
            out_part.astype(jnp.bfloat16).reshape(dp_count, block_rows, part_width),
            back_order,
            axis=0,
        )
        grad_send = jnp.take(
            grad_in_stream.astype(jnp.bfloat16).reshape(dp_count, block_rows, part_width),
            back_order,
            axis=0,
        )
        home_out, home_grad = (
            lax.all_to_all(out_blocks, "dp", split_axis=0, concat_axis=0, tiled=True),
            lax.all_to_all(grad_send, "dp", split_axis=0, concat_axis=0, tiled=True),
        )
        home_place = invert_map(send_index, dp_count)
        outs_y.append(jnp.take(home_out, home_place, axis=0).reshape(seq_len, part_width))
        outs_grad.append(jnp.take(home_grad, home_place, axis=0).reshape(seq_len, part_width))
    row_sums = jnp.zeros((micro_count, width), jnp.float32)
    row_sums = lax.dynamic_update_slice_in_dim(row_sums, jnp.stack(table_sums), col_start, 1)
    my_steps = jnp.take(timestep, jnp.arange(micro_count, dtype=jnp.int32) * dp_count + dp_rank)
    step_onehot = (
        jnp.arange(table.shape[0], dtype=jnp.int32)[:, None] == my_steps[None, :]
    ).astype(jnp.float32)
    table_grad = jnp.dot(
        step_onehot, row_sums, precision=lax.Precision.HIGHEST, preferred_element_type=jnp.float32
    )
    gains_grad = lax.dynamic_update_slice_in_dim(
        jnp.zeros((2, width), jnp.float32), acc_gains, col_start, 1
    )
    shifts_grad = lax.dynamic_update_slice_in_dim(
        jnp.zeros((4, width), jnp.float32), acc_shifts, col_start, 1
    )
    loss_row = jnp.full((1, dp_count * mp_count), loss_part, jnp.float32)
    grad_table, grad_norm_gains, grad_shifts, loss_cell = (
        lax.psum_scatter(table_grad, ("dp", "mp"), scatter_dimension=1, tiled=True),
        lax.psum_scatter(gains_grad, ("dp", "mp"), scatter_dimension=1, tiled=True),
        lax.psum_scatter(shifts_grad, ("dp", "mp"), scatter_dimension=1, tiled=True),
        lax.psum_scatter(loss_row, ("dp", "mp"), scatter_dimension=1, tiled=True),
    )
    loss = loss_cell[0, 0] / (valid_count * width)
    grad_qkv, grad_in, grad_out, grad_back, grad_qv_bias, grad_in_bias = (
        lax.psum_scatter(acc_qkv, "dp", scatter_dimension=0, tiled=True),
        lax.psum_scatter(acc_in, "dp", scatter_dimension=0, tiled=True),
        lax.psum_scatter(acc_out, "dp", scatter_dimension=1, tiled=True),
        lax.psum_scatter(acc_back, "dp", scatter_dimension=1, tiled=True),
        lax.psum_scatter(acc_qv, "dp", scatter_dimension=2, tiled=True),
        lax.psum_scatter(acc_in_bias.reshape(-1, 128), "dp", scatter_dimension=1, tiled=True),
    )
    y_out = jnp.stack(outs_y)
    grad_x = jnp.stack(outs_grad)
    return (
        y_out,
        loss,
        grad_x,
        grad_table,
        grad_norm_gains,
        grad_shifts,
        grad_qkv,
        grad_qv_bias,
        grad_out,
        grad_in,
        grad_in_bias,
        grad_back,
    )


MESH = pl.DeviceIdType.MESH
BF = jnp.bfloat16
F32 = jnp.float32
VM = pl.BlockSpec(memory_space=pltpu.VMEM)
DP = 8
ROWS = 96
VMEM_LIMIT = 64 * 1024 * 1024 - 65536


def place():
    dp, mp = lax.axis_index("dp"), lax.axis_index("mp")
    x, c = lax.div(mp, 2), lax.rem(mp, 2)
    return dp, mp, x, c


def remote(src, dst, send_sem, recv_sem, dp, mp):
    return pltpu.make_async_remote_copy(
        src_ref=src,
        dst_ref=dst,
        send_sem=send_sem,
        recv_sem=recv_sem,
        device_id=(dp, mp),
        device_id_type=MESH,
    )


def landed(dst, recv_sem, spare, dp, mp):
    remote(dst, dst, spare, recv_sem, dp, mp).wait_recv()


def greet_plane(dp, x, c):
    barrier = pltpu.get_barrier_semaphore()
    pl.semaphore_signal(barrier, inc=1, device_id=(dp, 2 * x + 1 - c), device_id_type=MESH)
    for k in range(DP):
        for xr in range(2):
            if k or xr:
                there = (lax.rem(dp + k, DP), 2 * lax.rem(x + xr, 2) + c)
                pl.semaphore_signal(barrier, inc=1, device_id=there, device_id_type=MESH)
    pl.semaphore_wait(barrier, 2 * DP)


def dot(a, b, dims):
    return lax.dot_general(a, b, (dims, ((), ())), preferred_element_type=F32)


T = 768
R = 256
LOG_SCALE = 0.125


def nn(a, b):
    return dot(a, b, ((1,), (0,)))


def nt(a, b):
    return dot(a, b, ((1,), (1,)))


def chunk(i):
    return pl.ds(pl.multiple_of(i * R, R), R)


def colsum(a):
    return jnp.sum(a, axis=0, keepdims=True)


def wide(column_tile, width):
    return jnp.concatenate([column_tile] * (width // 128), axis=1)


def gelu_pair(v):
    k = 0.7978845608028654
    v2 = v * v
    t = jnp.tanh(k * (v + 0.044715 * (v2 * v)))
    half = 0.5 * (1.0 + t)
    slope = half + 0.5 * v * ((1.0 - t * t) * (k * (1.0 + 0.134145 * v2)))
    return v * half, slope


def norm_back(g, normed, inverse):
    inner = jnp.mean(g * normed, axis=1, keepdims=True)
    return inverse * (g - jnp.mean(g, axis=1, keepdims=True) - normed * inner)


def step_kernel(
    xs, ts, wsh, small, mask, factor,
    gs, msgs, back,
    g, yg, sums, msg, r1, r2, r3,
    tok, tea, w, smalls, vecs, vec, nin, q_s, kv, kvt, o_t, att, n2_s, act, gy, gm, gp, x3, recv, tr, dkx, dkr, lse,
    s_core, r_core, s_x, r_x,
    s_tok, r_tok, s_tea, r_tea, s_small, r_small, s_w, r_w, s_pair, r_pair,
    s_msg, r_msg, s_yg, r_yg, s_a, r_a, s_b, r_b, s_c, r_c,
):
    dp, mp, x, c = place()
    other, across = 2 * x + 1 - c, 2 * (1 - x) + c
    z, y = lax.div(dp, 2), lax.rem(dp, 2)
    mine = x * DP + dp
    half = pl.ds(pl.multiple_of(384 * c, 128), 384)
    beside = 2 * z + 1 - y
    greet_plane(dp, x, c)
    sent = []

    def go(copy):
        copy.start()
        sent.append(copy)

    def rows64(j):
        return pl.ds(pl.multiple_of(64 * j, 64), 64)

    def weights_z(p):
        pltpu.make_async_copy(wsh.at[p], w.at[p, mine], r_w.at[p, mine]).start()
        for k in range(1, 4):
            zz = lax.rem(z + k, 4)
            go(remote(wsh.at[p], w.at[p, mine], s_w.at[p, k - 1], r_w.at[p, mine], 2 * zz + y, mp))

    def weights_xy(p):
        go(remote(wsh.at[p], w.at[p, mine], s_w.at[p, 3], r_w.at[p, mine], dp, across))
        go(remote(wsh.at[p], w.at[p, mine], s_w.at[p, 4], r_w.at[p, mine], beside, mp))

    def spread(p):
        for k in (3, 2, 1):
            b = x * DP + 2 * lax.rem(z + k, 4) + y
            landed(w.at[p, b], r_w.at[p, b], s_w.at[p, 0], dp, mp)
            go(remote(w.at[p, b], w.at[p, b], s_w.at[p, 3 + 2 * k], r_w.at[p, b], dp, across))
            go(remote(w.at[p, b], w.at[p, b], s_w.at[p, 4 + 2 * k], r_w.at[p, b], beside, mp))

    def relay(p):
        for n in (0, 3, 2, 1):
            k = lax.rem(z + n, 4)
            bx, by = (1 - x) * DP + 2 * k + y, x * DP + 2 * k + 1 - y
            landed(w.at[p, bx], r_w.at[p, bx], s_w.at[p, 0], dp, mp)
            landed(w.at[p, by], r_w.at[p, by], s_w.at[p, 0], dp, mp)
            b = jnp.where(k < 2, bx, by)
            there = jnp.where(k < 2, beside, dp), jnp.where(k < 2, mp, across)
            go(remote(w.at[p, b], w.at[p, b], s_w.at[p, 11 + n], r_w.at[p, b], *there))

    def complete(p):
        landed(w.at[p, mine], r_w.at[p, mine], s_w.at[p, 0], dp, mp)
        for k in range(4):
            b = (1 - x) * DP + 2 * k + 1 - y
            landed(w.at[p, b], r_w.at[p, b], s_w.at[p, 0], dp, mp)

    weights_z(0)
    weights_xy(0)

    pltpu.make_async_copy(small, smalls.at[mp, dp], r_small.at[mine]).start()
    for k in range(DP):
        for xr in range(2):
            if k or xr:
                d, m = lax.rem(dp + k, DP), 2 * lax.rem(x + xr, 2) + c
                go(remote(small, smalls.at[mp, dp], s_small.at[2 * k + xr], r_small.at[mine], d, m))

    def token_copy(k, d, m_from, j):
        return remote(
            xs.at[m_from, d, :, half], tok.at[rows64(j), half], s_tok.at[k], r_tok.at[j], d, mp
        )

    weights_xy(1)
    weights_xy(2)
    pltpu.make_async_copy(xs.at[x, dp, :, half], tok.at[rows64(dp), half], r_tok.at[dp]).start()
    for k in range(1, DP):
        go(token_copy(k, lax.rem(dp + k, DP), x, dp))

    @pl.when(y == x)
    def _():
        pltpu.make_async_copy(
            xs.at[2, dp, :, half], tok.at[rows64(8 + z), half], r_tok.at[8 + z]
        ).start()
        for k in range(1, DP):
            token_copy(8 + k, lax.rem(dp + k, DP), 2, 8 + z).start()

    weights_z(1)
    weights_z(2)
    spread(0)

    for j in range(12):
        landed(tok.at[rows64(j), half], r_tok.at[j], s_tok.at[0], dp, mp)
    go(remote(tok.at[:, half], tok.at[:, half], s_pair.at[0], r_pair.at[0], dp, other))
    for j in range(8):
        for xx in range(2):
            m = 2 * xx + c
            landed(smalls.at[m, j], r_small.at[xx * DP + j], s_small.at[0], dp, mp)
    go(remote(smalls.at[c], smalls.at[c], s_pair.at[1], r_pair.at[1], dp, other))
    go(remote(smalls.at[2 + c], smalls.at[2 + c], s_pair.at[2], r_pair.at[2], dp, other))
    relay(0)

    pltpu.make_async_copy(ts.at[x, dp], tea.at[mp, dp], r_tea.at[x, dp]).start()
    for k in range(DP):
        d = lax.rem(dp + k, DP)
        for xr in range(2):
            if k or xr:
                xx = lax.rem(x + xr, 2)
                go(remote(ts.at[xx, d], tea.at[mp, dp], s_tea.at[2 * k + xr], r_tea.at[x, dp], d, 2 * xx + c))
        if k:
            go(remote(ts.at[2, d], tea.at[mp, 8 + z], s_tea.at[16 + k], r_tea.at[x, 8 + z], d, 2 * y + c))

    @pl.when(y == x)
    def _():
        pltpu.make_async_copy(ts.at[2, dp], tea.at[mp, 8 + z], r_tea.at[x, 8 + z]).start()

    @pl.when(y != x)
    def _():
        remote(ts.at[2, dp], tea.at[mp, 8 + z], s_tea.at[16], r_tea.at[x, 8 + z], dp, 2 * y + c).start()

    o = 1 - c
    their_half = pl.ds(pl.multiple_of(384 * o, 128), 384)
    landed(tok.at[:, their_half], r_pair.at[0], s_pair.at[0], dp, mp)
    landed(smalls.at[o], r_pair.at[1], s_pair.at[0], dp, mp)
    landed(smalls.at[2 + o], r_pair.at[2], s_pair.at[0], dp, mp)

    low, high = lax.broadcasted_iota(jnp.int32, (512, 128), 0), lax.broadcasted_iota(jnp.int32, (512, 128), 1)
    lane, quarter = low & 127, lax.shift_right_logical(low, 7)
    pick = jnp.where((high == 24 * quarter + lane) & (lane < 24), 1.0, 0.0).astype(BF)
    stacked = jnp.concatenate(
        [jnp.concatenate([smalls[m, d, 0:32] for m in range(4)], axis=1) for d in range(DP)], axis=0
    )
    picked = nn(stacked, pick)
    vecs[...] = jnp.concatenate([picked[32 * d : 32 * d + 32, 0:96] for d in range(DP)], axis=1)
    vec[0:1] = vecs[pl.ds(6 + x * DP + dp, 1)]
    vec[1:2] = vecs[pl.ds(6 + 2 * DP + dp, 1)]
    vec[2:8] = vecs[0:6]
    blank = jnp.zeros((1, 64), F32)
    for xi in range(2):
        biases = smalls[2 * xi + c, 0, 32:48].astype(F32)
        for d in range(1, DP):
            biases = biases + smalls[2 * xi + c, d, 32:48].astype(F32)
        vec[10 + xi : 11 + xi] = jnp.concatenate([biases[k : k + 1] for k in range(6)], axis=1)
        pieces = []
        for j in range(3):
            pieces += [biases[8 + j : 9 + j, 0:64], blank, biases[11 + j : 12 + j, 0:64]]
        vec[8 + xi : 9 + xi] = jnp.concatenate(pieces + [blank] * 3, axis=1)
    complete(0)
    smid = g.at[0, 0]

    def half_of(p, xi, low, high):
        return w[p, DP * xi : DP * xi + DP, :, low:high].reshape(768, high - low)

    sums[...] = jnp.zeros(sums.shape, F32)

    def core(k, buffer, i):
        rows = chunk(i)
        return remote(
            buffer.at[rows], recv.at[k % 2, rows], s_core.at[k, i], r_core.at[k, i], dp, other
        )

    def each(count, body):
        def run(i, carry):
            body(i)
            return carry

        lax.fori_loop(0, count, run, 0)

    def lanes(h):
        return pl.ds(pl.multiple_of(128 * h, 128), 128)

    def add(row, value):
        width = value.shape[1]
        sums[row : row + 1, 0:width] = sums[row : row + 1, 0:width] + value

    def stream(i):
        return tok[chunk(i)].astype(F32) + jnp.where(i < 2, vec[0:1], vec[1:2])

    def block(p, xi, d):
        return g.at[p, xi, pl.ds(pl.multiple_of(ROWS * d, ROWS), ROWS)]

    def first(p):
        for n in range(1, 5):
            k = lax.rem(z + n, 4)
            w[p, k] = block(p, 1 - x, 2 * k + 1 - y)[...].astype(BF)
            there = jnp.where(k < 2, dp, beside), jnp.where(k < 2, across, mp)
            go(remote(w.at[p, k], r1.at[p, k], s_a.at[p, k], r_a.at[p, k], *there))

    def second(p):
        for n in range(1, 5):
            k = lax.rem(z + n, 4)
            landed(r1.at[p, k], r_a.at[p, k], s_a.at[p, k], dp, mp)
            extra = r1[p, k].astype(F32)
            gx, gy_ = block(p, 1 - x, 2 * k + y)[...], block(p, x, 2 * k + 1 - y)[...]
            w[p, 4 + k] = (gx + jnp.where(k < 2, 0.0, extra)).astype(BF)
            w[p, 8 + k] = (gy_ + jnp.where(k < 2, extra, 0.0)).astype(BF)
            go(remote(w.at[p, 4 + k], r2.at[p, 0, k], s_b.at[p, 0, k], r_b.at[p, 0, k], dp, across))
            go(remote(w.at[p, 8 + k], r2.at[p, 1, k], s_b.at[p, 1, k], r_b.at[p, 1, k], beside, mp))

    def third(p):
        for k in range(1, 5):
            zz = lax.rem(z + k, 4)
            for side in range(2):
                landed(r2.at[p, side, zz], r_b.at[p, side, zz], s_b.at[p, side, 0], dp, mp)
            total = block(p, x, 2 * zz + y)[...] + r2[p, 0, zz].astype(F32) + r2[p, 1, zz].astype(F32)
            if k < 4:
                w[p, 11 + k] = total.astype(BF)
                go(remote(w.at[p, 11 + k], r3.at[p, k - 1], s_c.at[p, k - 1], r_c.at[p, k - 1], 2 * zz + y, mp))
            else:
                gs[p] = total

    def last(p):
        for k in range(3):
            landed(r3.at[p, k], r_c.at[p, k], s_c.at[p, k], dp, mp)
        gs[p] = gs[p] + (r3[p, 0].astype(F32) + r3[p, 1].astype(F32) + r3[p, 2].astype(F32))

    def home_copy(n):
        return remote(
            yg.at[n, mp, 8 + z], back.at[n, 2, dp], s_yg.at[n, 16], r_yg.at[n, 2, dp], 2 * z + x, mp
        )

    def go_home(n):
        pltpu.make_async_copy(yg.at[n, mp, dp], back.at[n, x, dp], r_yg.at[n, x, dp]).start()
        for k in range(DP):
            s = lax.rem(dp + k, DP)
            for xr in range(2):
                if k or xr:
                    m = 2 * lax.rem(x + xr, 2) + c
                    go(remote(yg.at[n, m, s], back.at[n, x, dp], s_yg.at[n, 2 * k + xr], r_yg.at[n, x, dp], s, m))
        for k in range(4):
            j = lax.rem(z + k, 4)
            for xr in range(2):
                m = 2 * lax.rem(x + xr, 2) + c
                if k or xr:
                    go(remote(yg.at[n, m, 8 + j], back.at[n, 2, dp], s_yg.at[n, 16 + 2 * k + xr], r_yg.at[n, 2, dp], 2 * j + x, m))

        @pl.when(y == x)
        def _():
            pltpu.make_async_copy(yg.at[n, mp, 8 + z], back.at[n, 2, dp], r_yg.at[n, 2, dp]).start()

        @pl.when(y != x)
        def _():
            home_copy(n).start()

    def project(i):
        rows = chunk(i)
        normed, _ = normalize_rows(stream(i))
        nb = (normed * vec[2:3] + vec[4:5]).astype(BF)
        nin[rows] = nb
        for xi in range(2):
            pr = (nn(nb, half_of(0, xi, 0, 640)) + vec[8 + xi : 9 + xi, 0:640]).astype(BF)
            for j in range(3):
                head, a = 3 * xi + j, 192 * j
                q_s[head, rows] = jnp.concatenate([pr[:, a : a + 64], jnp.zeros((R, 64), BF)], axis=1)
                kv[head, rows] = pr[:, a + 64 : a + 192]

    project(2)
    own, theirs = pl.ds(512, 256), pl.ds(768, 256)
    kv_copy = remote(kv.at[:, own], kv.at[:, theirs], s_x.at[0], r_x.at[0], dp, across)
    kv_copy.start()
    each(2, project)
    spread(1)

    def turn(part):
        def body(h):
            kvt[h, :, part * 512 : part * 512 + 512] = kv[h, part * 512 : part * 512 + 512].T

        each(6, body)

    def attend(h, block):
        part = block // 2
        keys, rows = slice(part * 512, part * 512 + 512), slice(block * R, block * R + R)
        st = nt(kv[h, keys], q_s[h, rows]) * LOG_SCALE + wide(mask[keys], R)
        top = jnp.max(st, axis=0, keepdims=True)
        e = jnp.exp(st - top)
        total = colsum(e)
        pt = (e * (1.0 / total)).astype(BF)
        ot = nn(kvt[h, 64:128, keys], pt)
        xi, j = lax.div(h, 3), lax.rem(h, 3)
        o_t[xi, pl.ds(pl.multiple_of(64 + 64 * j, 64), 64), rows] = ot.astype(BF)
        lse[h, :, rows] = top + jnp.log(total)

    o_t[:, 0:64] = jnp.zeros((2, 64, T), BF)
    turn(0)

    def attend_a(h):
        attend(h, 0)
        attend(h, 1)

    each(6, attend_a)
    kv_copy.wait()
    relay(1)
    turn(1)
    each(6, lambda h: attend(h, 2))
    spread(2)

    def out_project(i):
        rows = chunk(i)
        part = None
        for xi in range(2):
            a = o_t[xi, :, rows].T
            att[xi, rows] = a
            piece = nt(a, half_of(0, xi, 512, 768))
            part = piece if part is None else part + piece
        smid[rows] = part
        core(0, smid, i).start()

    each(3, out_project)
    complete(1)

    def forward(i):
        rows = chunk(i)
        core(0, smid, i).wait()
        mid = stream(i) + (smid[rows] + recv[0, rows] + vec[6:7])
        smid[rows] = mid
        normed, _ = normalize_rows(mid)
        nb = (normed * vec[3:4] + vec[5:6]).astype(BF)
        n2_s[rows] = nb
        for xi in range(2):
            value, slope = gelu_pair(nn(nb, half_of(1, xi, 0, 768)) + vec[10 + xi : 11 + xi])
            act[xi, rows] = value.astype(BF)
            g[1, xi, rows] = slope

    each(3, forward)
    relay(2)
    for xx in range(2):
        for j in range(12):
            landed(tea.at[2 * xx + c, j], r_tea.at[xx, j], s_tea.at[0], dp, mp)
    go(remote(tea.at[c], tea.at[c], s_pair.at[3], r_pair.at[3], dp, other))
    go(remote(tea.at[2 + c], tea.at[2 + c], s_pair.at[4], r_pair.at[4], dp, other))
    complete(2)

    def forward_out(i):
        rows = chunk(i)
        gy[rows] = nt(act[0, rows], half_of(2, 0, 0, 768)) + nt(act[1, rows], half_of(2, 1, 0, 768))
        core(1, gy, i).start()

    each(3, forward_out)
    landed(tea.at[o], r_pair.at[3], s_pair.at[0], dp, mp)
    landed(tea.at[2 + o], r_pair.at[4], s_pair.at[0], dp, mp)

    def teacher_rows(j):
        pieces = []
        for m in range(4):
            low = tea[m, j, 64:96]
            pieces += [tea[m, j, 0:64], jnp.concatenate([low[:, 0:64], low[:, 64:128]], axis=0)]
        return jnp.concatenate(pieces, axis=1)

    def pack_out(n, i, value):
        for q in range(4):
            a = 64 * q
            for m in range(4):
                b = 192 * m
                yg[n, m, 4 * i + q, 0:64] = value[a : a + 64, b : b + 128]
                yg[n, m, 4 * i + q, 64:96] = jnp.concatenate(
                    [value[a : a + 32, b + 128 : b + 192], value[a + 32 : a + 64, b + 128 : b + 192]], axis=1
                )

    def turn_back(i):
        rows = chunk(i)
        core(1, gy, i).wait()
        out = smid[rows] + (gy[rows] + recv[1, rows] + vec[7:8])
        out_b = out.astype(BF)
        pack_out(0, i, out_b)
        target = jnp.concatenate([teacher_rows(4 * i + q) for q in range(4)], axis=0)
        residual = jnp.where(wide(mask[rows], T) == 0.0, out - target.astype(F32), 0.0)
        add(8, colsum(residual * residual))
        grad_y = residual * factor[0:1, 0:1]
        gy[rows] = grad_y
        gb = grad_y.astype(BF)
        gm[rows] = gb
        add(5, colsum(gb.astype(F32)))
        part = None
        for xi in range(2):
            gpre = (nn(gb, half_of(2, xi, 0, 768)) * g[1, xi, rows]).astype(BF)
            gp[xi, rows] = gpre
            add(11 + xi, colsum(gpre.astype(F32)))
            piece = nt(gpre, half_of(1, xi, 0, 768))
            part = piece if part is None else part + piece
        x3[rows] = part
        core(2, x3, i).start()

    each(3, turn_back)

    def turn_rows(source):
        def body(i):
            tr[:, chunk(i)] = source[chunk(i)].T

        each(3, body)

    def weight_grad(p, values):
        def body(i):
            for xi in range(2):
                g[p, xi, chunk(i)] = nn(tr[chunk(i)], values[xi])

        each(3, body)

    turn_rows(gm)
    weight_grad(2, act)
    for copy in sent:
        copy.wait_send()
    sent.clear()
    first(2)
    turn_rows(n2_s)
    weight_grad(1, gp)
    first(1)
    second(2)

    def mid_back(i):
        rows = chunk(i)
        core(2, x3, i).wait()
        grad_h = x3[rows] + recv[0, rows]
        normed, inverse = normalize_rows(smid[rows])
        add(1, colsum(grad_h * normed))
        add(3, colsum(grad_h))
        grad_mid = gy[rows] + norm_back(grad_h * vec[3:4], normed, inverse)
        gy[rows] = grad_mid
        gb = grad_mid.astype(BF)
        gm[rows] = gb
        add(4, colsum(gb.astype(F32)))
        for xi in range(2):
            gatt = nn(gb, half_of(0, xi, 512, 768)).astype(BF)
            for j in range(3):
                piece = gatt[:, 64 + 64 * j : 128 + 64 * j]
                n2_s[rows, 384 * xi + 128 * j : 384 * xi + 128 * j + 128] = jnp.concatenate([jnp.zeros((R, 64), BF), piece], axis=1)

    each(3, mid_back)
    go_home(0)

    def attend_grad(h, block):
        part = block // 2
        keys, rows = slice(part * 512, part * 512 + 512), slice(block * R, block * R + R)
        kvs, q, go = kv[h, keys], q_s[h, rows], n2_s[rows, lanes(h)]
        st = nt(kvs, q) * LOG_SCALE + wide(mask[keys], R)
        pt = jnp.exp(st - lse[h, :, rows])
        dpt = nt(kvs, go)
        delta = colsum(pt * dpt)
        dst = (pt * (dpt - delta)).astype(BF)
        dqt = nn(kvt[h, 0:64, keys], dst) * LOG_SCALE
        q_s[h, rows, 0:64] = dqt.T.astype(BF)
        return nn(dst, q) * LOG_SCALE + nn(pt.astype(BF), go)

    def grad_c(h):
        both = attend_grad(h, 2)
        recv[0, 512:768, lanes(h)] = both[0:256]
        dkx[h] = both[256:512].astype(BF)

    def grad_a(h):
        recv[0, 0:512, lanes(h)] = attend_grad(h, 0) + attend_grad(h, 1)

    each(6, grad_c)
    dk_copy = remote(dkx, dkr, s_x.at[1], r_x.at[1], dp, across)
    dk_copy.start()
    second(1)
    third(2)
    each(6, grad_a)
    turn_rows(gm)

    def out_grad(i):
        for xi in range(2):
            g[0, xi, chunk(i), 512:768] = nn(tr[chunk(i)], att[xi])

    each(3, out_grad)
    third(1)
    dk_copy.wait()

    def join(h):
        recv[0, 512:768, lanes(h)] = recv[0, 512:768, lanes(h)] + dkr[h].astype(F32)

    each(6, join)

    def project_back(i):
        rows = chunk(i)
        part = None
        for xi in range(2):
            pieces = []
            for j in range(3):
                at = 384 * xi + 128 * j
                pieces += [q_s[3 * xi + j, rows, 0:64], recv[0, rows, at : at + 128].astype(BF)]
            gr = jnp.concatenate(pieces + [jnp.zeros((R, 64), BF)], axis=1)
            gp[xi, rows, 0:640] = gr
            add(9 + xi if xi == 0 else 13, colsum(gr.astype(F32)))
            piece = nt(gr, half_of(0, xi, 0, 640))
            part = piece if part is None else part + piece
        x3[rows] = part
        core(3, x3, i).start()

    each(3, project_back)
    turn_rows(nin)

    def qkv_grad(i):
        rows = chunk(i)
        for xi in range(2):
            h = nn(tr[rows], gp[xi, :, 0:640])
            g[0, xi, rows, 0:512] = h[:, 0:512]
            g[0, xi, rows, 512:640] = g[0, xi, rows, 512:640] + h[:, 512:640]

    each(3, qkv_grad)
    first(0)

    def in_back(i):
        rows = chunk(i)
        core(3, x3, i).wait()
        grad_h = x3[rows] + recv[1, rows]
        normed, inverse = normalize_rows(stream(i))
        add(0, colsum(grad_h * normed))
        add(2, colsum(grad_h))
        grad_in = gy[rows] + norm_back(grad_h * vec[2:3], normed, inverse)
        total = colsum(grad_in)
        add(6, jnp.where(i < 2, total, 0.0))
        add(7, jnp.where(i < 2, 0.0, total))
        out_b = grad_in.astype(BF)
        pack_out(1, i, out_b)

    each(3, in_back)
    second(0)

    msg[...] = jnp.zeros(msg.shape, F32)
    loss_row = sums[8:9, 0:128]
    for k in range(1, 6):
        loss_row = loss_row + sums[8:9, 128 * k : 128 * k + 128]
    for xi in range(2):
        bias_sums = sums[9:10] if xi == 0 else sums[13:14]
        hidden = sums[11 + xi : 12 + xi]
        for d in range(DP):
            at, owner = 96 * d + 48 * xi, 8 * xi + d
            msg[owner, 0:8, 0:24] = jnp.where(c == 0, sums[0:8, at : at + 24], sums[0:8, at + 24 : at + 48])
            msg[owner, 8:9] = loss_row
            for j in range(3):
                for kind in range(2):
                    low = 192 * j + 128 * kind
                    msg[owner, 9 + 3 * kind + j : 10 + 3 * kind + j, 0:64] = bias_sums[:, low : low + 64]
            for k in range(6):
                msg[owner, 16 + k : 17 + k] = hidden[:, 128 * k : 128 * k + 128]
    pltpu.make_async_copy(msg.at[mine], msgs.at[mine], r_msg.at[mine]).start()
    for k in range(DP):
        for xr in range(2):
            if k or xr:
                d, xx = lax.rem(dp + k, DP), lax.rem(x + xr, 2)
                go(remote(msg.at[xx * DP + d], msgs.at[mine], s_msg.at[2 * k + xr], r_msg.at[mine], d, 2 * xx + c))
    go_home(1)
    third(0)
    last(2)
    last(1)
    last(0)
    for j in range(16):
        landed(msgs.at[j], r_msg.at[j], s_msg.at[0], dp, mp)
    for n in range(2):
        for m in range(3):
            for j in range(DP):
                landed(back.at[n, m, j], r_yg.at[n, m, j], s_yg.at[n, 0], dp, mp)
    for copy in sent:
        copy.wait_send()

    @pl.when(y == x)
    def _():
        for k in range(1, DP):
            token_copy(8 + k, lax.rem(dp + k, DP), 2, 8 + z).wait_send()

    @pl.when(y != x)
    def _():
        remote(ts.at[2, dp], tea.at[mp, 8 + z], s_tea.at[16], r_tea.at[x, 8 + z], dp, 2 * y + c).wait_send()
        home_copy(0).wait_send()
        home_copy(1).wait_send()


def step(xs, ts, wsh, small, mask, factor):
    dma = pltpu.SemaphoreType.DMA
    vm = pltpu.VMEM
    block = (ROWS, 768)
    return pl.pallas_call(
        step_kernel,
        name="step",
        out_shape=(
            jax.ShapeDtypeStruct((3, ROWS, 768), F32),
            jax.ShapeDtypeStruct((16, 24, 128), F32),
            jax.ShapeDtypeStruct((2, 3, DP, 96, 128), BF),
        ),
        in_specs=[pl.BlockSpec(memory_space=pl.ANY)] * 4 + [VM] * 2,
        out_specs=(VM, VM, pl.BlockSpec(memory_space=pl.ANY)),
        scratch_shapes=[
            vm((3, 2, T, 768), F32), vm((2, 4, 12, 96, 128), BF), vm((16, 768), F32), vm((16, 24, 128), F32),
            vm((3, 4) + block, BF), vm((3, 2, 4) + block, BF), vm((3, 3) + block, BF),
            vm((T, 768), BF), vm((4, 12, 96, 128), BF), vm((3, 16) + block, BF),
            vm((4, DP, 48, 128), BF), vm((32, 768), F32), vm((16, 768), F32),
            vm((T, 768), BF), vm((6, T, 128), BF), vm((6, 1024, 128), BF), vm((6, 128, 1024), BF),
            vm((2, R, T), BF), vm((2, T, R), BF), vm((T, 768), BF), vm((2, T, 768), BF),
            vm((T, 768), F32), vm((T, 768), BF), vm((2, T, 768), BF), vm((T, 768), F32),
            vm((2, T, 768), F32), vm((768, T), BF), vm((6, R, 128), BF), vm((6, R, 128), BF),
            vm((6, 1, T), F32),
            dma((4, 3)), dma((4, 3)), dma((2,)), dma((2,)),
            dma((16,)), dma((12,)), dma((24,)), dma((2, 12)), dma((16,)), dma((16,)),
            dma((3, 15)), dma((3, 16)), dma((5,)), dma((5,)),
            dma((16,)), dma((16,)), dma((2, 24)), dma((2, 3, DP)), dma((3, 4)), dma((3, 4)),
            dma((3, 2, 4)), dma((3, 2, 4)), dma((3, 3)), dma((3, 3)),
        ],
        compiler_params=pltpu.CompilerParams(
            collective_id=3, has_side_effects=True, vmem_limit_bytes=VMEM_LIMIT
        ),
    )(xs, ts, wsh, small, mask, factor)


def per_device_compact(
    input_stream, teacher, timestep, lengths, block_perm, table, norm_gains, shifts,
    w_qkv, qv_bias, w_out, w_in, in_bias, w_back,
):
    dp, mp, x, c = place()
    seq_len, width, quarter = input_stream.shape[1], input_stream.shape[2], teacher.shape[2]
    valid_count = jnp.sum(lengths).astype(F32)
    loss_factor = 3 * DP * seq_len / valid_count

    order = block_perm.reshape(3, DP, DP)
    source, local = order // DP, order % DP
    send_index = jnp.sum(jnp.where(source == dp, local, 0), axis=2)
    my_source = lax.dynamic_index_in_dim(source, dp, 1, keepdims=False)
    ranks = jnp.arange(DP, dtype=jnp.int32)
    where_block = jnp.sum(
        jnp.where(my_source[:, None, :] == ranks[None, :, None], ranks[None, None, :], 0), axis=2
    )
    micro = jnp.arange(3)[:, None]
    x_blocks = input_stream.reshape(3, DP, 64, width)[micro, send_index]
    low = teacher.reshape(3, DP, 64, quarter)
    low = jnp.concatenate(
        [low[..., :128], jnp.concatenate([low[:, :, :32, 128:], low[:, :, 32:, 128:]], axis=3)], axis=2
    )
    t_blocks = low[micro, send_index]
    half_block = lax.dynamic_index_in_dim(where_block[2].reshape(4, 2), x, 1, keepdims=False)
    their_block = lax.dynamic_index_in_dim(where_block[2].reshape(4, 2), 1 - x, 1, keepdims=False)
    first_block = lax.dynamic_index_in_dim(where_block, x, 0, keepdims=False)
    length_a = lax.dynamic_index_in_dim(lengths, x * DP + dp, 0, keepdims=False)
    length_c = lax.dynamic_index_in_dim(lengths, 2 * DP + dp, 0, keepdims=False)
    inside = jnp.arange(64, dtype=jnp.int32)
    live_a = ((first_block[:, None] * 64 + inside[None]) < length_a).reshape(512)
    live_c = ((half_block[:, None] * 64 + inside[None]) < length_c).reshape(256)
    live_d = ((their_block[:, None] * 64 + inside[None]) < length_c).reshape(256)

    wsh = jnp.stack([jnp.concatenate([w_qkv, w_out.T], axis=1), w_in, w_back.T])
    chosen = jnp.take(table, timestep, axis=0)
    rows = jnp.concatenate([norm_gains, shifts, chosen])
    lanes = jnp.arange(128)
    spread_in = jnp.where(lanes // 16 == dp, jnp.tile(in_bias, (1, 8)), 0)
    spread_qv = jnp.where((lanes // 8 == dp)[:64], jnp.tile(qv_bias.reshape(6, 8), (1, 8)), 0)
    small = jnp.concatenate(
        [
            jnp.pad(rows, ((0, 2), (0, 104))),
            jnp.pad(spread_in, ((0, 2), (0, 0))),
            jnp.pad(spread_qv, ((0, 2), (0, 64))),
        ]
    ).astype(BF)
    live = jnp.concatenate([live_a, live_c, live_d])
    mask = jnp.broadcast_to(jnp.where(live, 0.0, -1e30).astype(F32)[:, None], (1024, 128))
    factor = jnp.full((8, 128), loss_factor, F32)
    gs, msgs, home = step(x_blocks, t_blocks, wsh, small, mask, factor)

    place_home = jnp.sum(
        jnp.where(send_index[:, None, :] == ranks[None, :, None], ranks[None, None, :], 0), axis=2
    )
    home = [home[n][micro, place_home] for n in range(2)]
    home = [
        jnp.concatenate(
            [h[:, :, :64], jnp.concatenate([h[:, :, 64:, :64], h[:, :, 64:, 64:]], axis=2)], axis=3
        ).reshape(3, seq_len, quarter)
        for h in home
    ]
    total = jnp.sum(msgs, axis=0)
    loss = jnp.sum(total[8]) / (valid_count * width)
    rows_a = msgs[:, 6, :24].reshape(16, 24)
    rows_c = msgs[:DP, 7, :24] + msgs[DP:, 7, :24]
    seq_rows = jnp.concatenate([rows_a, rows_c])
    onehot = (jnp.arange(table.shape[0], dtype=jnp.int32)[:, None] == timestep[None, :]).astype(F32)
    grad_table = jnp.dot(onehot, seq_rows, precision=lax.Precision.HIGHEST, preferred_element_type=F32)
    return (
        home[0],
        loss,
        home[1],
        grad_table,
        total[0:2, :24],
        total[2:6, :24],
        gs[0, :, :576],
        lax.dynamic_slice(total, (9, 8 * dp), (6, 8)).reshape(2, 3, 8),
        gs[0, :, 576:].T,
        gs[1],
        lax.dynamic_slice(total, (16, 16 * dp), (6, 16)),
        gs[2].T,
    )


def solution(mesh):
    compact = mesh.shape["dp"] == 8 and mesh.shape["mp"] == 4
    return jax.shard_map(
        per_device_compact if compact else per_device,
        mesh=mesh,
        in_specs=(
            P(None, "dp", None),
            P(None, "dp", "mp"),
            P(),
            P(),
            P(),
            P(None, ("dp", "mp")),
            P(None, ("dp", "mp")),
            P(None, ("dp", "mp")),
            P("dp", "mp"),
            P(None, "mp", "dp"),
            P("mp", "dp"),
            P("dp", "mp"),
            P("mp", "dp"),
            P("mp", "dp"),
        ),
        out_specs=(
            P(None, "dp", "mp"),
            P(),
            P(None, "dp", "mp"),
            P(None, ("dp", "mp")),
            P(None, ("dp", "mp")),
            P(None, ("dp", "mp")),
            P("dp", "mp"),
            P(None, "mp", "dp"),
            P("mp", "dp"),
            P("dp", "mp"),
            P("mp", "dp"),
            P("mp", "dp"),
        ),
        check_vma=False,
    )
```

```python
import functools
import math

import jax
import jax.numpy as jnp
from jax import lax
from jax.experimental import pallas as pl
from jax.experimental.pallas import tpu as pltpu
from jax.sharding import PartitionSpec as P

H = 12
DH = 64


epsilon = 1e-05


def normalize_rows(stream):
    centered = stream - jnp.mean(stream, axis=-1, keepdims=True)
    inverse = lax.rsqrt(jnp.mean(centered * centered, axis=-1, keepdims=True) + epsilon)
    return (centered * inverse, inverse)


def column_part(array, start, width):
    return lax.dynamic_slice_in_dim(array, start, width, array.ndim - 1)


def fetch_weights(w_qkv, w_in, w_out, w_back, qv_bias, in_bias):
    return (
        lax.all_gather(w_qkv, "dp", axis=0, tiled=True),
        lax.all_gather(w_in, "dp", axis=0, tiled=True),
        lax.all_gather(w_out, "dp", axis=1, tiled=True),
        lax.all_gather(w_back, "dp", axis=1, tiled=True),
        lax.all_gather(qv_bias, "dp", axis=2, tiled=True),
        lax.all_gather(in_bias, "dp", axis=1, tiled=True),
    )


def invert_map(targets, size):
    ranks = jnp.arange(size, dtype=jnp.int32)
    return jnp.sum(jnp.where(targets[None, :] == ranks[:, None], ranks[None, :], 0), axis=1)


def masked_scores(queries, keys_all, is_live, score_scale):
    scores = (
        jnp.einsum("qhe,khe->hqk", queries, keys_all, preferred_element_type=jnp.float32)
        * score_scale
    )
    return jnp.where(is_live[None, None, :], scores, -1e30)


def attend_rows(keys_all, values, is_live, score_scale, queries):
    scores = masked_scores(queries, keys_all, is_live, score_scale)
    row_top = jnp.max(scores, axis=-1, keepdims=True)
    exponent = jnp.exp(scores - row_top)
    row_total = jnp.sum(exponent, axis=-1, keepdims=True)
    weights_p = (exponent / row_total).astype(jnp.bfloat16)
    mixed = jnp.einsum("hqk,khe->qhe", weights_p, values, preferred_element_type=jnp.float32)
    return (mixed, (row_top + jnp.log(row_total))[..., 0])


def attend_back(keys_all, values, is_live, score_scale, carry, inputs):
    queries, grad_rows, log_total = inputs
    grad_keys, grad_values = carry
    scores = masked_scores(queries, keys_all, is_live, score_scale)
    probabilities = jnp.exp(scores - log_total[..., None])
    grad_probs = jnp.einsum("qhe,khe->hqk", grad_rows, values, preferred_element_type=jnp.float32)
    row_delta = jnp.sum(probabilities * grad_probs, axis=-1, keepdims=True)
    grad_scores = (probabilities * (grad_probs - row_delta)).astype(jnp.bfloat16)
    grad_queries = (
        jnp.einsum("hqk,khe->qhe", grad_scores, keys_all, preferred_element_type=jnp.float32)
        * score_scale
    )
    grad_keys = (
        grad_keys
        + jnp.einsum("hqk,qhe->khe", grad_scores, queries, preferred_element_type=jnp.float32)
        * score_scale
    )
    grad_values = grad_values + jnp.einsum(
        "hqk,qhe->khe",
        probabilities.astype(jnp.bfloat16),
        grad_rows,
        preferred_element_type=jnp.float32,
    )
    return ((grad_keys, grad_values), grad_queries)


def norm_sums(partial_value, normed, gain_full, mp_count):
    weighted = partial_value * gain_full
    sums = jnp.stack([jnp.sum(weighted, axis=1), jnp.sum(weighted * normed, axis=1)], axis=1)
    return jnp.tile(sums, (1, mp_count))


def norm_input_grad(grad_part, gain_part, normed_part, inverse, sums, width):
    scaled = grad_part * gain_part
    return inverse * (scaled - sums[:, 0:1] / width - normed_part * sums[:, 1:2] / width)


def per_device(
    input_stream,
    teacher,
    timestep,
    lengths,
    block_perm,
    table,
    norm_gains,
    shifts,
    w_qkv,
    qv_bias,
    w_out,
    w_in,
    in_bias,
    w_back,
):
    dp_count = lax.axis_size("dp")
    mp_count = lax.axis_size("mp")
    dp_rank = lax.axis_index("dp")
    mp_rank = lax.axis_index("mp")
    micro_count, seq_len, width = input_stream.shape
    part_width = teacher.shape[2]
    block_rows = seq_len // dp_count
    heads_here = H // mp_count
    score_scale = 1.0 / math.sqrt(DH)
    col_start = mp_rank * part_width
    row_block = min(512, seq_len)
    block_count = seq_len // row_block
    valid_count = jnp.sum(lengths).astype(jnp.float32)
    loss_factor = micro_count * dp_count * seq_len / valid_count
    chosen = jnp.take(table, timestep, axis=0)
    gains_full, shifts_full, table_rows = (
        lax.all_gather(norm_gains, ("dp", "mp"), axis=1, tiled=True),
        lax.all_gather(shifts, ("dp", "mp"), axis=1, tiled=True),
        lax.all_gather(chosen, ("dp", "mp"), axis=1, tiled=True),
    )
    gains_full = gains_full.astype(jnp.float32)
    shifts_full = shifts_full.astype(jnp.float32)
    gain_parts = column_part(gains_full, col_start, part_width)
    acc_qkv = jnp.zeros((width, heads_here * 3 * DH), jnp.float32)
    acc_in = jnp.zeros((width, w_in.shape[1]), jnp.float32)
    acc_out = jnp.zeros((heads_here * DH, width), jnp.float32)
    acc_back = jnp.zeros((w_back.shape[0], width), jnp.float32)
    acc_qv = jnp.zeros((2, heads_here, DH), jnp.float32)
    acc_in_bias = jnp.zeros((w_in.shape[1],), jnp.float32)
    acc_gains = jnp.zeros((2, part_width), jnp.float32)
    acc_shifts = jnp.zeros((4, part_width), jnp.float32)
    loss_part = jnp.zeros((), jnp.float32)
    table_sums = []
    outs_y = []
    outs_grad = []
    for micro_index in range(micro_count):
        forward_set = fetch_weights(w_qkv, w_in, w_out, w_back, qv_bias, in_bias)
        proj_qkv, proj_in, proj_out, proj_back, bias_qv, bias_in = forward_set
        bias_qv = bias_qv.astype(jnp.float32)
        bias_in = bias_in.reshape(-1).astype(jnp.float32)
        block_order = block_perm[micro_index].reshape(dp_count, dp_count)
        source = block_order // dp_count
        local_index = block_order % dp_count
        send_index = jnp.sum(jnp.where(source == dp_rank, local_index, 0), axis=1)
        x_blocks = input_stream[micro_index].reshape(dp_count, block_rows, width)
        t_blocks = teacher[micro_index].reshape(dp_count, block_rows, part_width)
        got_x, got_t = (
            lax.all_to_all(
                jnp.take(x_blocks, send_index, axis=0),
                "dp",
                split_axis=0,
                concat_axis=0,
                tiled=True,
            ),
            lax.all_to_all(
                jnp.take(t_blocks, send_index, axis=0),
                "dp",
                split_axis=0,
                concat_axis=0,
                tiled=True,
            ),
        )
        my_source = lax.dynamic_index_in_dim(source, dp_rank, 0, keepdims=False)
        tokens = jnp.take(got_x, my_source, axis=0).reshape(seq_len, width).astype(jnp.float32)
        target = jnp.take(got_t, my_source, axis=0).reshape(seq_len, part_width).astype(jnp.float32)
        seq_index = micro_index * dp_count + dp_rank
        length = lax.dynamic_index_in_dim(lengths, seq_index, 0, keepdims=False)
        table_row = lax.dynamic_index_in_dim(table_rows, seq_index, 0, keepdims=False).astype(
            jnp.float32
        )
        is_live = jnp.arange(seq_len, dtype=jnp.int32) < length
        stream_in = tokens + table_row[None, :]
        normed1, inverse1 = normalize_rows(stream_in)
        normed_in = (normed1 * gains_full[0] + shifts_full[0]).astype(jnp.bfloat16)
        projected = jnp.dot(normed_in, proj_qkv, preferred_element_type=jnp.float32).reshape(
            seq_len, heads_here, 3, DH
        )
        queries = (projected[:, :, 0] + bias_qv[0]).astype(jnp.bfloat16)
        keys_all = projected[:, :, 1].astype(jnp.bfloat16)
        values = (projected[:, :, 2] + bias_qv[1]).astype(jnp.bfloat16)
        query_blocks = queries.reshape(block_count, row_block, heads_here, DH)
        mixed, log_total = lax.map(
            functools.partial(attend_rows, keys_all, values, is_live, score_scale), query_blocks
        )
        attended = mixed.reshape(seq_len, heads_here * DH).astype(jnp.bfloat16)
        attn_part = jnp.dot(attended, proj_out, preferred_element_type=jnp.float32)
        branch_attn = lax.psum_scatter(
            attn_part, "mp", scatter_dimension=1, tiled=True
        ) + column_part(shifts_full[2], col_start, part_width)
        mid_part = column_part(stream_in, col_start, part_width) + branch_attn
        stream_mid = lax.all_gather(mid_part, "mp", axis=1, tiled=True)
        normed2, inverse2 = normalize_rows(stream_mid)
        normed_mid = (normed2 * gains_full[1] + shifts_full[1]).astype(jnp.bfloat16)
        pre_act = jnp.dot(normed_mid, proj_in, preferred_element_type=jnp.float32) + bias_in
        activation = jax.nn.gelu(pre_act, approximate=True).astype(jnp.bfloat16)
        mlp_part = jnp.dot(activation, proj_back, preferred_element_type=jnp.float32)
        mlp_out = lax.psum_scatter(mlp_part, "mp", scatter_dimension=1, tiled=True) + column_part(
            shifts_full[3], col_start, part_width
        )
        out_part = mid_part + mlp_out
        residual_err = jnp.where(is_live[:, None], out_part - target, 0.0)
        loss_part = loss_part + jnp.sum(residual_err * residual_err)
        grad_y = residual_err * loss_factor
        grad_mlp = grad_y.astype(jnp.bfloat16)
        acc_shifts = acc_shifts.at[3].add(jnp.sum(grad_mlp.astype(jnp.float32), axis=0))
        grad_mlp_full = lax.all_gather(grad_mlp, "mp", axis=1, tiled=True)
        back_set = fetch_weights(w_qkv, w_in, w_out, w_back, qv_bias, in_bias)
        back_qkv, back_in, back_out, back_back = (
            back_set[0],
            back_set[1],
            back_set[2],
            back_set[3],
        )
        acc_back = acc_back + jnp.einsum(
            "tf,td->fd", activation, grad_mlp_full, preferred_element_type=jnp.float32
        )
        grad_act = jnp.einsum(
            "td,fd->tf", grad_mlp_full, back_back, preferred_element_type=jnp.float32
        )
        gelu_value, gelu_pull = jax.vjp(lambda inner: jax.nn.gelu(inner, approximate=True), pre_act)
        grad_pre = gelu_pull(grad_act)[0].astype(jnp.bfloat16)
        acc_in_bias = acc_in_bias + jnp.sum(grad_pre.astype(jnp.float32), axis=0)
        acc_in = acc_in + jnp.einsum(
            "td,tf->df", normed_mid, grad_pre, preferred_element_type=jnp.float32
        )
        partial2 = jnp.einsum("tf,df->td", grad_pre, back_in, preferred_element_type=jnp.float32)
        grad_h2, sums2 = (
            lax.psum_scatter(partial2, "mp", scatter_dimension=1, tiled=True),
            lax.psum_scatter(
                norm_sums(partial2, normed2, gains_full[1], mp_count),
                "mp",
                scatter_dimension=1,
                tiled=True,
            ),
        )
        normed2_part = column_part(normed2, col_start, part_width)
        acc_gains = acc_gains.at[1].add(jnp.sum(grad_h2 * normed2_part, axis=0))
        acc_shifts = acc_shifts.at[1].add(jnp.sum(grad_h2, axis=0))
        grad_mid = grad_y + norm_input_grad(
            grad_h2, gain_parts[1], normed2_part, inverse2, sums2, width
        )
        grad_branch = grad_mid.astype(jnp.bfloat16)
        acc_shifts = acc_shifts.at[2].add(jnp.sum(grad_branch.astype(jnp.float32), axis=0))
        grad_branch_full = lax.all_gather(grad_branch, "mp", axis=1, tiled=True)
        acc_out = acc_out + jnp.einsum(
            "tc,td->cd", attended, grad_branch_full, preferred_element_type=jnp.float32
        )
        grad_att = jnp.einsum(
            "td,cd->tc", grad_branch_full, back_out, preferred_element_type=jnp.float32
        ).astype(jnp.bfloat16)
        grad_blocks = grad_att.reshape(block_count, row_block, heads_here, DH)
        zero_heads = jnp.zeros((seq_len, heads_here, DH), jnp.float32)
        (grad_keys, grad_values), grad_queries = lax.scan(
            functools.partial(attend_back, keys_all, values, is_live, score_scale),
            (zero_heads, zero_heads),
            (query_blocks, grad_blocks, log_total),
        )
        grad_queries = grad_queries.reshape(seq_len, heads_here, DH).astype(jnp.bfloat16)
        grad_keys = grad_keys.astype(jnp.bfloat16)
        grad_values = grad_values.astype(jnp.bfloat16)
        acc_qv = acc_qv + jnp.stack(
            [
                jnp.sum(grad_queries.astype(jnp.float32), axis=0),
                jnp.sum(grad_values.astype(jnp.float32), axis=0),
            ]
        )
        grad_qkv_rows = jnp.stack([grad_queries, grad_keys, grad_values], axis=2).reshape(
            seq_len, heads_here * 3 * DH
        )
        acc_qkv = acc_qkv + jnp.einsum(
            "td,tc->dc", normed_in, grad_qkv_rows, preferred_element_type=jnp.float32
        )
        partial1 = jnp.einsum(
            "tc,dc->td", grad_qkv_rows, back_qkv, preferred_element_type=jnp.float32
        )
        grad_h1, sums1 = (
            lax.psum_scatter(partial1, "mp", scatter_dimension=1, tiled=True),
            lax.psum_scatter(
                norm_sums(partial1, normed1, gains_full[0], mp_count),
                "mp",
                scatter_dimension=1,
                tiled=True,
            ),
        )
        normed1_part = column_part(normed1, col_start, part_width)
        acc_gains = acc_gains.at[0].add(jnp.sum(grad_h1 * normed1_part, axis=0))
        acc_shifts = acc_shifts.at[0].add(jnp.sum(grad_h1, axis=0))
        grad_in_stream = grad_mid + norm_input_grad(
            grad_h1, gain_parts[0], normed1_part, inverse1, sums1, width
        )
        table_sums.append(jnp.sum(grad_in_stream, axis=0))
        back_order = invert_map(my_source, dp_count)
        out_blocks = jnp.take(
            out_part.astype(jnp.bfloat16).reshape(dp_count, block_rows, part_width),
            back_order,
            axis=0,
        )
        grad_send = jnp.take(
            grad_in_stream.astype(jnp.bfloat16).reshape(dp_count, block_rows, part_width),
            back_order,
            axis=0,
        )
        home_out, home_grad = (
            lax.all_to_all(out_blocks, "dp", split_axis=0, concat_axis=0, tiled=True),
            lax.all_to_all(grad_send, "dp", split_axis=0, concat_axis=0, tiled=True),
        )
        home_place = invert_map(send_index, dp_count)
        outs_y.append(jnp.take(home_out, home_place, axis=0).reshape(seq_len, part_width))
        outs_grad.append(jnp.take(home_grad, home_place, axis=0).reshape(seq_len, part_width))
    row_sums = jnp.zeros((micro_count, width), jnp.float32)
    row_sums = lax.dynamic_update_slice_in_dim(row_sums, jnp.stack(table_sums), col_start, 1)
    my_steps = jnp.take(timestep, jnp.arange(micro_count, dtype=jnp.int32) * dp_count + dp_rank)
    step_onehot = (
        jnp.arange(table.shape[0], dtype=jnp.int32)[:, None] == my_steps[None, :]
    ).astype(jnp.float32)
    table_grad = jnp.dot(
        step_onehot, row_sums, precision=lax.Precision.HIGHEST, preferred_element_type=jnp.float32
    )
    gains_grad = lax.dynamic_update_slice_in_dim(
        jnp.zeros((2, width), jnp.float32), acc_gains, col_start, 1
    )
    shifts_grad = lax.dynamic_update_slice_in_dim(
        jnp.zeros((4, width), jnp.float32), acc_shifts, col_start, 1
    )
    loss_row = jnp.full((1, dp_count * mp_count), loss_part, jnp.float32)
    grad_table, grad_norm_gains, grad_shifts, loss_cell = (
        lax.psum_scatter(table_grad, ("dp", "mp"), scatter_dimension=1, tiled=True),
        lax.psum_scatter(gains_grad, ("dp", "mp"), scatter_dimension=1, tiled=True),
        lax.psum_scatter(shifts_grad, ("dp", "mp"), scatter_dimension=1, tiled=True),
        lax.psum_scatter(loss_row, ("dp", "mp"), scatter_dimension=1, tiled=True),
    )
    loss = loss_cell[0, 0] / (valid_count * width)
    grad_qkv, grad_in, grad_out, grad_back, grad_qv_bias, grad_in_bias = (
        lax.psum_scatter(acc_qkv, "dp", scatter_dimension=0, tiled=True),
        lax.psum_scatter(acc_in, "dp", scatter_dimension=0, tiled=True),
        lax.psum_scatter(acc_out, "dp", scatter_dimension=1, tiled=True),
        lax.psum_scatter(acc_back, "dp", scatter_dimension=1, tiled=True),
        lax.psum_scatter(acc_qv, "dp", scatter_dimension=2, tiled=True),
        lax.psum_scatter(acc_in_bias.reshape(-1, 128), "dp", scatter_dimension=1, tiled=True),
    )
    y_out = jnp.stack(outs_y)
    grad_x = jnp.stack(outs_grad)
    return (
        y_out,
        loss,
        grad_x,
        grad_table,
        grad_norm_gains,
        grad_shifts,
        grad_qkv,
        grad_qv_bias,
        grad_out,
        grad_in,
        grad_in_bias,
        grad_back,
    )


MESH = pl.DeviceIdType.MESH
BF = jnp.bfloat16
F32 = jnp.float32
VM = pl.BlockSpec(memory_space=pltpu.VMEM)
DP = 8
ROWS = 96
VMEM_LIMIT = 64 * 1024 * 1024 - 65536


def place():
    dp, mp = lax.axis_index("dp"), lax.axis_index("mp")
    x, c = lax.div(mp, 2), lax.rem(mp, 2)
    return dp, mp, x, c


def remote(src, dst, send_sem, recv_sem, dp, mp):
    return pltpu.make_async_remote_copy(
        src_ref=src,
        dst_ref=dst,
        send_sem=send_sem,
        recv_sem=recv_sem,
        device_id=(dp, mp),
        device_id_type=MESH,
    )


def landed(dst, recv_sem, spare, dp, mp):
    remote(dst, dst, spare, recv_sem, dp, mp).wait_recv()


def greet_plane(dp, x, c):
    barrier = pltpu.get_barrier_semaphore()
    pl.semaphore_signal(barrier, inc=1, device_id=(dp, 2 * x + 1 - c), device_id_type=MESH)
    for k in range(DP):
        for xr in range(2):
            if k or xr:
                there = (lax.rem(dp + k, DP), 2 * lax.rem(x + xr, 2) + c)
                pl.semaphore_signal(barrier, inc=1, device_id=there, device_id_type=MESH)
    pl.semaphore_wait(barrier, 2 * DP)


def dot(a, b, dims):
    return lax.dot_general(a, b, (dims, ((), ())), preferred_element_type=F32)


T = 768
R = 256
LOG_SCALE = 0.125


def nn(a, b):
    return dot(a, b, ((1,), (0,)))


def nt(a, b):
    return dot(a, b, ((1,), (1,)))


def chunk(i):
    return pl.ds(pl.multiple_of(i * R, R), R)


def colsum(a):
    return jnp.sum(a, axis=0, keepdims=True)


def wide(column_tile, width):
    return jnp.concatenate([column_tile] * (width // 128), axis=1)


def gelu_pair(v):
    k = 0.7978845608028654
    v2 = v * v
    t = jnp.tanh(k * (v + 0.044715 * (v2 * v)))
    half = 0.5 * (1.0 + t)
    slope = half + 0.5 * v * ((1.0 - t * t) * (k * (1.0 + 0.134145 * v2)))
    return v * half, slope


def norm_back(g, normed, inverse):
    inner = jnp.mean(g * normed, axis=1, keepdims=True)
    return inverse * (g - jnp.mean(g, axis=1, keepdims=True) - normed * inner)


def step_kernel(
    xs, ts, wsh, small, mask, factor,
    gs, msgs, back,
    g, yg, sums, msg, r1, r2, r3,
    tok, tea, w, smalls, vecs, vec, nin, q_s, kv, kvt, o_t, att, n2_s, act, gy, gm, gp, x3, recv, tr, dkx, dkr, lse,
    s_core, r_core, s_x, r_x,
    s_tok, r_tok, s_tea, r_tea, s_small, r_small, s_w, r_w, s_pair, r_pair,
    s_msg, r_msg, s_yg, r_yg, s_a, r_a, s_b, r_b, s_c, r_c,
):
    dp, mp, x, c = place()
    other, across = 2 * x + 1 - c, 2 * (1 - x) + c
    z, y = lax.div(dp, 2), lax.rem(dp, 2)
    mine = x * DP + dp
    half = pl.ds(pl.multiple_of(384 * c, 128), 384)
    beside = 2 * z + 1 - y
    greet_plane(dp, x, c)
    sent = []

    def go(copy):
        copy.start()
        sent.append(copy)

    def rows64(j):
        return pl.ds(pl.multiple_of(64 * j, 64), 64)

    def weights_z(p):
        pltpu.make_async_copy(wsh.at[p], w.at[p, mine], r_w.at[p, mine]).start()
        for k in range(1, 4):
            zz = lax.rem(z + k, 4)
            go(remote(wsh.at[p], w.at[p, mine], s_w.at[p, k - 1], r_w.at[p, mine], 2 * zz + y, mp))

    def weights_xy(p):
        go(remote(wsh.at[p], w.at[p, mine], s_w.at[p, 3], r_w.at[p, mine], dp, across))
        go(remote(wsh.at[p], w.at[p, mine], s_w.at[p, 4], r_w.at[p, mine], beside, mp))

    def spread(p):
        for k in (3, 2, 1):
            b = x * DP + 2 * lax.rem(z + k, 4) + y
            landed(w.at[p, b], r_w.at[p, b], s_w.at[p, 0], dp, mp)
            go(remote(w.at[p, b], w.at[p, b], s_w.at[p, 3 + 2 * k], r_w.at[p, b], dp, across))
            go(remote(w.at[p, b], w.at[p, b], s_w.at[p, 4 + 2 * k], r_w.at[p, b], beside, mp))

    def relay(p):
        for n in (0, 3, 2, 1):
            k = lax.rem(z + n, 4)
            bx, by = (1 - x) * DP + 2 * k + y, x * DP + 2 * k + 1 - y
            landed(w.at[p, bx], r_w.at[p, bx], s_w.at[p, 0], dp, mp)
            landed(w.at[p, by], r_w.at[p, by], s_w.at[p, 0], dp, mp)
            b = jnp.where(k < 2, bx, by)
            there = jnp.where(k < 2, beside, dp), jnp.where(k < 2, mp, across)
            go(remote(w.at[p, b], w.at[p, b], s_w.at[p, 11 + n], r_w.at[p, b], *there))

    def complete(p):
        landed(w.at[p, mine], r_w.at[p, mine], s_w.at[p, 0], dp, mp)
        for k in range(4):
            b = (1 - x) * DP + 2 * k + 1 - y
            landed(w.at[p, b], r_w.at[p, b], s_w.at[p, 0], dp, mp)

    weights_z(0)
    weights_xy(0)

    pltpu.make_async_copy(small, smalls.at[mp, dp], r_small.at[mine]).start()
    for k in range(DP):
        for xr in range(2):
            if k or xr:
                d, m = lax.rem(dp + k, DP), 2 * lax.rem(x + xr, 2) + c
                go(remote(small, smalls.at[mp, dp], s_small.at[2 * k + xr], r_small.at[mine], d, m))

    def token_copy(k, d, m_from, j):
        return remote(
            xs.at[m_from, d, :, half], tok.at[rows64(j), half], s_tok.at[k], r_tok.at[j], d, mp
        )

    weights_xy(1)
    weights_xy(2)
    pltpu.make_async_copy(xs.at[x, dp, :, half], tok.at[rows64(dp), half], r_tok.at[dp]).start()
    for k in range(1, DP):
        go(token_copy(k, lax.rem(dp + k, DP), x, dp))

    @pl.when(y == x)
    def _():
        pltpu.make_async_copy(
            xs.at[2, dp, :, half], tok.at[rows64(8 + z), half], r_tok.at[8 + z]
        ).start()
        for k in range(1, DP):
            token_copy(8 + k, lax.rem(dp + k, DP), 2, 8 + z).start()

    weights_z(1)
    weights_z(2)
    spread(0)

    for j in range(12):
        landed(tok.at[rows64(j), half], r_tok.at[j], s_tok.at[0], dp, mp)
    go(remote(tok.at[:, half], tok.at[:, half], s_pair.at[0], r_pair.at[0], dp, other))
    for j in range(8):
        for xx in range(2):
            m = 2 * xx + c
            landed(smalls.at[m, j], r_small.at[xx * DP + j], s_small.at[0], dp, mp)
    go(remote(smalls.at[c], smalls.at[c], s_pair.at[1], r_pair.at[1], dp, other))
    go(remote(smalls.at[2 + c], smalls.at[2 + c], s_pair.at[2], r_pair.at[2], dp, other))
    relay(0)

    pltpu.make_async_copy(ts.at[x, dp], tea.at[mp, dp], r_tea.at[x, dp]).start()
    for k in range(DP):
        d = lax.rem(dp + k, DP)
        for xr in range(2):
            if k or xr:
                xx = lax.rem(x + xr, 2)
                go(remote(ts.at[xx, d], tea.at[mp, dp], s_tea.at[2 * k + xr], r_tea.at[x, dp], d, 2 * xx + c))
        if k:
            go(remote(ts.at[2, d], tea.at[mp, 8 + z], s_tea.at[16 + k], r_tea.at[x, 8 + z], d, 2 * y + c))

    @pl.when(y == x)
    def _():
        pltpu.make_async_copy(ts.at[2, dp], tea.at[mp, 8 + z], r_tea.at[x, 8 + z]).start()

    @pl.when(y != x)
    def _():
        remote(ts.at[2, dp], tea.at[mp, 8 + z], s_tea.at[16], r_tea.at[x, 8 + z], dp, 2 * y + c).start()

    o = 1 - c
    their_half = pl.ds(pl.multiple_of(384 * o, 128), 384)
    landed(tok.at[:, their_half], r_pair.at[0], s_pair.at[0], dp, mp)
    landed(smalls.at[o], r_pair.at[1], s_pair.at[0], dp, mp)
    landed(smalls.at[2 + o], r_pair.at[2], s_pair.at[0], dp, mp)

    low, high = lax.broadcasted_iota(jnp.int32, (512, 128), 0), lax.broadcasted_iota(jnp.int32, (512, 128), 1)
    lane, quarter = low & 127, lax.shift_right_logical(low, 7)
    pick = jnp.where((high == 24 * quarter + lane) & (lane < 24), 1.0, 0.0).astype(BF)
    stacked = jnp.concatenate(
        [jnp.concatenate([smalls[m, d, 0:32] for m in range(4)], axis=1) for d in range(DP)], axis=0
    )
    picked = nn(stacked, pick)
    vecs[...] = jnp.concatenate([picked[32 * d : 32 * d + 32, 0:96] for d in range(DP)], axis=1)
    vec[0:1] = vecs[pl.ds(6 + x * DP + dp, 1)]
    vec[1:2] = vecs[pl.ds(6 + 2 * DP + dp, 1)]
    vec[2:8] = vecs[0:6]
    blank = jnp.zeros((1, 64), F32)
    for xi in range(2):
        biases = smalls[2 * xi + c, 0, 32:48].astype(F32)
        for d in range(1, DP):
            biases = biases + smalls[2 * xi + c, d, 32:48].astype(F32)
        vec[10 + xi : 11 + xi] = jnp.concatenate([biases[k : k + 1] for k in range(6)], axis=1)
        pieces = []
        for j in range(3):
            pieces += [biases[8 + j : 9 + j, 0:64], blank, biases[11 + j : 12 + j, 0:64]]
        vec[8 + xi : 9 + xi] = jnp.concatenate(pieces + [blank] * 3, axis=1)
    complete(0)
    smid = g.at[0, 0]

    def half_of(p, xi, low, high):
        return w[p, DP * xi : DP * xi + DP, :, low:high].reshape(768, high - low)

    sums[...] = jnp.zeros(sums.shape, F32)

    def core(k, buffer, i):
        rows = chunk(i)
        return remote(
            buffer.at[rows], recv.at[k % 2, rows], s_core.at[k, i], r_core.at[k, i], dp, other
        )

    def each(count, body):
        def run(i, carry):
            body(i)
            return carry

        lax.fori_loop(0, count, run, 0)

    def lanes(h):
        return pl.ds(pl.multiple_of(128 * h, 128), 128)

    def add(row, value):
        width = value.shape[1]
        sums[row : row + 1, 0:width] = sums[row : row + 1, 0:width] + value

    def stream(i):
        return tok[chunk(i)].astype(F32) + jnp.where(i < 2, vec[0:1], vec[1:2])

    def block(p, xi, d):
        return g.at[p, xi, pl.ds(pl.multiple_of(ROWS * d, ROWS), ROWS)]

    def first(p):
        for n in range(1, 5):
            k = lax.rem(z + n, 4)
            w[p, k] = block(p, 1 - x, 2 * k + 1 - y)[...].astype(BF)
            there = jnp.where(k < 2, dp, beside), jnp.where(k < 2, across, mp)
            go(remote(w.at[p, k], r1.at[p, k], s_a.at[p, k], r_a.at[p, k], *there))

    def second(p):
        for n in range(1, 5):
            k = lax.rem(z + n, 4)
            landed(r1.at[p, k], r_a.at[p, k], s_a.at[p, k], dp, mp)
            extra = r1[p, k].astype(F32)
            gx, gy_ = block(p, 1 - x, 2 * k + y)[...], block(p, x, 2 * k + 1 - y)[...]
            w[p, 4 + k] = (gx + jnp.where(k < 2, 0.0, extra)).astype(BF)
            w[p, 8 + k] = (gy_ + jnp.where(k < 2, extra, 0.0)).astype(BF)
            go(remote(w.at[p, 4 + k], r2.at[p, 0, k], s_b.at[p, 0, k], r_b.at[p, 0, k], dp, across))
            go(remote(w.at[p, 8 + k], r2.at[p, 1, k], s_b.at[p, 1, k], r_b.at[p, 1, k], beside, mp))

    def third(p):
        for k in range(1, 5):
            zz = lax.rem(z + k, 4)
            for side in range(2):
                landed(r2.at[p, side, zz], r_b.at[p, side, zz], s_b.at[p, side, 0], dp, mp)
            total = block(p, x, 2 * zz + y)[...] + r2[p, 0, zz].astype(F32) + r2[p, 1, zz].astype(F32)
            if k < 4:
                w[p, 11 + k] = total.astype(BF)
                go(remote(w.at[p, 11 + k], r3.at[p, k - 1], s_c.at[p, k - 1], r_c.at[p, k - 1], 2 * zz + y, mp))
            else:
                gs[p] = total

    def last(p):
        for k in range(3):
            landed(r3.at[p, k], r_c.at[p, k], s_c.at[p, k], dp, mp)
        gs[p] = gs[p] + (r3[p, 0].astype(F32) + r3[p, 1].astype(F32) + r3[p, 2].astype(F32))

    def home_copy(n):
        return remote(
            yg.at[n, mp, 8 + z], back.at[n, 2, dp], s_yg.at[n, 16], r_yg.at[n, 2, dp], 2 * z + x, mp
        )

    def go_home(n):
        pltpu.make_async_copy(yg.at[n, mp, dp], back.at[n, x, dp], r_yg.at[n, x, dp]).start()
        for k in range(DP):
            s = lax.rem(dp + k, DP)
            for xr in range(2):
                if k or xr:
                    m = 2 * lax.rem(x + xr, 2) + c
                    go(remote(yg.at[n, m, s], back.at[n, x, dp], s_yg.at[n, 2 * k + xr], r_yg.at[n, x, dp], s, m))
        for k in range(4):
            j = lax.rem(z + k, 4)
            for xr in range(2):
                m = 2 * lax.rem(x + xr, 2) + c
                if k or xr:
                    go(remote(yg.at[n, m, 8 + j], back.at[n, 2, dp], s_yg.at[n, 16 + 2 * k + xr], r_yg.at[n, 2, dp], 2 * j + x, m))

        @pl.when(y == x)
        def _():
            pltpu.make_async_copy(yg.at[n, mp, 8 + z], back.at[n, 2, dp], r_yg.at[n, 2, dp]).start()

        @pl.when(y != x)
        def _():
            home_copy(n).start()

    def project(i):
        rows = chunk(i)
        normed, _ = normalize_rows(stream(i))
        nb = (normed * vec[2:3] + vec[4:5]).astype(BF)
        nin[rows] = nb
        for xi in range(2):
            pr = (nn(nb, half_of(0, xi, 0, 640)) + vec[8 + xi : 9 + xi, 0:640]).astype(BF)
            for j in range(3):
                head, a = 3 * xi + j, 192 * j
                q_s[head, rows] = jnp.concatenate([pr[:, a : a + 64], jnp.zeros((R, 64), BF)], axis=1)
                kv[head, rows] = pr[:, a + 64 : a + 192]

    project(2)
    own, theirs = pl.ds(512, 256), pl.ds(768, 256)
    kv_copy = remote(kv.at[:, own], kv.at[:, theirs], s_x.at[0], r_x.at[0], dp, across)
    kv_copy.start()
    each(2, project)
    spread(1)

    def turn(part):
        def body(h):
            kvt[h, :, part * 512 : part * 512 + 512] = kv[h, part * 512 : part * 512 + 512].T

        each(6, body)

    def attend(h, block):
        part = block // 2
        keys, rows = slice(part * 512, part * 512 + 512), slice(block * R, block * R + R)
        st = nt(kv[h, keys], q_s[h, rows]) * LOG_SCALE + wide(mask[keys], R)
        top = jnp.max(st, axis=0, keepdims=True)
        e = jnp.exp(st - top)
        total = colsum(e)
        pt = (e * (1.0 / total)).astype(BF)
        ot = nn(kvt[h, 64:128, keys], pt)
        xi, j = lax.div(h, 3), lax.rem(h, 3)
        o_t[xi, pl.ds(pl.multiple_of(64 + 64 * j, 64), 64), rows] = ot.astype(BF)
        lse[h, :, rows] = top + jnp.log(total)

    o_t[:, 0:64] = jnp.zeros((2, 64, T), BF)
    turn(0)

    def attend_a(h):
        attend(h, 0)
        attend(h, 1)

    each(6, attend_a)
    kv_copy.wait()
    relay(1)
    turn(1)
    each(6, lambda h: attend(h, 2))
    spread(2)

    def out_project(i):
        rows = chunk(i)
        part = None
        for xi in range(2):
            a = o_t[xi, :, rows].T
            att[xi, rows] = a
            piece = nt(a, half_of(0, xi, 512, 768))
            part = piece if part is None else part + piece
        smid[rows] = part
        core(0, smid, i).start()

    each(3, out_project)
    complete(1)

    def forward(i):
        rows = chunk(i)
        core(0, smid, i).wait()
        mid = stream(i) + (smid[rows] + recv[0, rows] + vec[6:7])
        smid[rows] = mid
        normed, _ = normalize_rows(mid)
        nb = (normed * vec[3:4] + vec[5:6]).astype(BF)
        n2_s[rows] = nb
        for xi in range(2):
            value, slope = gelu_pair(nn(nb, half_of(1, xi, 0, 768)) + vec[10 + xi : 11 + xi])
            act[xi, rows] = value.astype(BF)
            g[1, xi, rows] = slope

    each(3, forward)
    relay(2)
    for xx in range(2):
        for j in range(12):
            landed(tea.at[2 * xx + c, j], r_tea.at[xx, j], s_tea.at[0], dp, mp)
    go(remote(tea.at[c], tea.at[c], s_pair.at[3], r_pair.at[3], dp, other))
    go(remote(tea.at[2 + c], tea.at[2 + c], s_pair.at[4], r_pair.at[4], dp, other))
    complete(2)

    def forward_out(i):
        rows = chunk(i)
        gy[rows] = nt(act[0, rows], half_of(2, 0, 0, 768)) + nt(act[1, rows], half_of(2, 1, 0, 768))
        core(1, gy, i).start()

    each(3, forward_out)
    landed(tea.at[o], r_pair.at[3], s_pair.at[0], dp, mp)
    landed(tea.at[2 + o], r_pair.at[4], s_pair.at[0], dp, mp)

    def teacher_rows(j):
        pieces = []
        for m in range(4):
            low = tea[m, j, 64:96]
            pieces += [tea[m, j, 0:64], jnp.concatenate([low[:, 0:64], low[:, 64:128]], axis=0)]
        return jnp.concatenate(pieces, axis=1)

    def pack_out(n, i, value):
        for q in range(4):
            a = 64 * q
            for m in range(4):
                b = 192 * m
                yg[n, m, 4 * i + q, 0:64] = value[a : a + 64, b : b + 128]
                yg[n, m, 4 * i + q, 64:96] = jnp.concatenate(
                    [value[a : a + 32, b + 128 : b + 192], value[a + 32 : a + 64, b + 128 : b + 192]], axis=1
                )

    def turn_back(i):
        rows = chunk(i)
        core(1, gy, i).wait()
        out = smid[rows] + (gy[rows] + recv[1, rows] + vec[7:8])
        out_b = out.astype(BF)
        pack_out(0, i, out_b)
        target = jnp.concatenate([teacher_rows(4 * i + q) for q in range(4)], axis=0)
        residual = jnp.where(wide(mask[rows], T) == 0.0, out - target.astype(F32), 0.0)
        add(8, colsum(residual * residual))
        grad_y = residual * factor[0:1, 0:1]
        gy[rows] = grad_y
        gb = grad_y.astype(BF)
        gm[rows] = gb
        add(5, colsum(gb.astype(F32)))
        part = None
        for xi in range(2):
            gpre = (nn(gb, half_of(2, xi, 0, 768)) * g[1, xi, rows]).astype(BF)
            gp[xi, rows] = gpre
            add(11 + xi, colsum(gpre.astype(F32)))
            piece = nt(gpre, half_of(1, xi, 0, 768))
            part = piece if part is None else part + piece
        x3[rows] = part
        core(2, x3, i).start()

    each(3, turn_back)

    def turn_rows(source):
        def body(i):
            tr[:, chunk(i)] = source[chunk(i)].T

        each(3, body)

    def weight_grad(p, values):
        def body(i):
            for xi in range(2):
                g[p, xi, chunk(i)] = nn(tr[chunk(i)], values[xi])

        each(3, body)

    turn_rows(gm)
    weight_grad(2, act)
    for copy in sent:
        copy.wait_send()
    sent.clear()
    first(2)
    turn_rows(n2_s)
    weight_grad(1, gp)
    first(1)
    second(2)

    def mid_back(i):
        rows = chunk(i)
        core(2, x3, i).wait()
        grad_h = x3[rows] + recv[0, rows]
        normed, inverse = normalize_rows(smid[rows])
        add(1, colsum(grad_h * normed))
        add(3, colsum(grad_h))
        grad_mid = gy[rows] + norm_back(grad_h * vec[3:4], normed, inverse)
        gy[rows] = grad_mid
        gb = grad_mid.astype(BF)
        gm[rows] = gb
        add(4, colsum(gb.astype(F32)))
        for xi in range(2):
            gatt = nn(gb, half_of(0, xi, 512, 768)).astype(BF)
            for j in range(3):
                piece = gatt[:, 64 + 64 * j : 128 + 64 * j]
                n2_s[rows, 384 * xi + 128 * j : 384 * xi + 128 * j + 128] = jnp.concatenate([jnp.zeros((R, 64), BF), piece], axis=1)

    each(3, mid_back)
    go_home(0)

    def attend_grad(h, block):
        part = block // 2
        keys, rows = slice(part * 512, part * 512 + 512), slice(block * R, block * R + R)
        kvs, q, go = kv[h, keys], q_s[h, rows], n2_s[rows, lanes(h)]
        st = nt(kvs, q) * LOG_SCALE + wide(mask[keys], R)
        pt = jnp.exp(st - lse[h, :, rows])
        dpt = nt(kvs, go)
        delta = colsum(pt * dpt)
        dst = (pt * (dpt - delta)).astype(BF)
        dqt = nn(kvt[h, 0:64, keys], dst) * LOG_SCALE
        q_s[h, rows, 0:64] = dqt.T.astype(BF)
        return nn(dst, q) * LOG_SCALE + nn(pt.astype(BF), go)

    def grad_c(h):
        both = attend_grad(h, 2)
        recv[0, 512:768, lanes(h)] = both[0:256]
        dkx[h] = both[256:512].astype(BF)

    def grad_a(h):
        recv[0, 0:512, lanes(h)] = attend_grad(h, 0) + attend_grad(h, 1)

    each(6, grad_c)
    dk_copy = remote(dkx, dkr, s_x.at[1], r_x.at[1], dp, across)
    dk_copy.start()
    second(1)
    third(2)
    each(6, grad_a)
    turn_rows(gm)

    def out_grad(i):
        for xi in range(2):
            g[0, xi, chunk(i), 512:768] = nn(tr[chunk(i)], att[xi])

    each(3, out_grad)
    third(1)
    dk_copy.wait()

    def join(h):
        recv[0, 512:768, lanes(h)] = recv[0, 512:768, lanes(h)] + dkr[h].astype(F32)

    each(6, join)

    def project_back(i):
        rows = chunk(i)
        part = None
        for xi in range(2):
            pieces = []
            for j in range(3):
                at = 384 * xi + 128 * j
                pieces += [q_s[3 * xi + j, rows, 0:64], recv[0, rows, at : at + 128].astype(BF)]
            gr = jnp.concatenate(pieces + [jnp.zeros((R, 64), BF)], axis=1)
            gp[xi, rows, 0:640] = gr
            add(9 + xi if xi == 0 else 13, colsum(gr.astype(F32)))
            piece = nt(gr, half_of(0, xi, 0, 640))
            part = piece if part is None else part + piece
        x3[rows] = part
        core(3, x3, i).start()

    each(3, project_back)
    turn_rows(nin)

    def qkv_grad(i):
        rows = chunk(i)
        for xi in range(2):
            h = nn(tr[rows], gp[xi, :, 0:640])
            g[0, xi, rows, 0:512] = h[:, 0:512]
            g[0, xi, rows, 512:640] = g[0, xi, rows, 512:640] + h[:, 512:640]

    each(3, qkv_grad)
    first(0)

    def in_back(i):
        rows = chunk(i)
        core(3, x3, i).wait()
        grad_h = x3[rows] + recv[1, rows]
        normed, inverse = normalize_rows(stream(i))
        add(0, colsum(grad_h * normed))
        add(2, colsum(grad_h))
        grad_in = gy[rows] + norm_back(grad_h * vec[2:3], normed, inverse)
        total = colsum(grad_in)
        add(6, jnp.where(i < 2, total, 0.0))
        add(7, jnp.where(i < 2, 0.0, total))
        out_b = grad_in.astype(BF)
        pack_out(1, i, out_b)

    each(3, in_back)
    second(0)

    msg[...] = jnp.zeros(msg.shape, F32)
    loss_row = sums[8:9, 0:128]
    for k in range(1, 6):
        loss_row = loss_row + sums[8:9, 128 * k : 128 * k + 128]
    for xi in range(2):
        bias_sums = sums[9:10] if xi == 0 else sums[13:14]
        hidden = sums[11 + xi : 12 + xi]
        for d in range(DP):
            at, owner = 96 * d + 48 * xi, 8 * xi + d
            msg[owner, 0:8, 0:24] = jnp.where(c == 0, sums[0:8, at : at + 24], sums[0:8, at + 24 : at + 48])
            msg[owner, 8:9] = loss_row
            for j in range(3):
                for kind in range(2):
                    low = 192 * j + 128 * kind
                    msg[owner, 9 + 3 * kind + j : 10 + 3 * kind + j, 0:64] = bias_sums[:, low : low + 64]
            for k in range(6):
                msg[owner, 16 + k : 17 + k] = hidden[:, 128 * k : 128 * k + 128]
    pltpu.make_async_copy(msg.at[mine], msgs.at[mine], r_msg.at[mine]).start()
    for k in range(DP):
        for xr in range(2):
            if k or xr:
                d, xx = lax.rem(dp + k, DP), lax.rem(x + xr, 2)
                go(remote(msg.at[xx * DP + d], msgs.at[mine], s_msg.at[2 * k + xr], r_msg.at[mine], d, 2 * xx + c))
    go_home(1)
    third(0)
    last(2)
    last(1)
    last(0)
    for j in range(16):
        landed(msgs.at[j], r_msg.at[j], s_msg.at[0], dp, mp)
    for n in range(2):
        for m in range(3):
            for j in range(DP):
                landed(back.at[n, m, j], r_yg.at[n, m, j], s_yg.at[n, 0], dp, mp)
    for copy in sent:
        copy.wait_send()

    @pl.when(y == x)
    def _():
        for k in range(1, DP):
            token_copy(8 + k, lax.rem(dp + k, DP), 2, 8 + z).wait_send()

    @pl.when(y != x)
    def _():
        remote(ts.at[2, dp], tea.at[mp, 8 + z], s_tea.at[16], r_tea.at[x, 8 + z], dp, 2 * y + c).wait_send()
        home_copy(0).wait_send()
        home_copy(1).wait_send()


def step(xs, ts, wsh, small, mask, factor):
    dma = pltpu.SemaphoreType.DMA
    vm = pltpu.VMEM
    block = (ROWS, 768)
    return pl.pallas_call(
        step_kernel,
        name="step",
        out_shape=(
            jax.ShapeDtypeStruct((3, ROWS, 768), F32),
            jax.ShapeDtypeStruct((16, 24, 128), F32),
            jax.ShapeDtypeStruct((2, 3, DP, 96, 128), BF),
        ),
        in_specs=[pl.BlockSpec(memory_space=pl.ANY)] * 4 + [VM] * 2,
        out_specs=(VM, VM, pl.BlockSpec(memory_space=pl.ANY)),
        scratch_shapes=[
            vm((3, 2, T, 768), F32), vm((2, 4, 12, 96, 128), BF), vm((16, 768), F32), vm((16, 24, 128), F32),
            vm((3, 4) + block, BF), vm((3, 2, 4) + block, BF), vm((3, 3) + block, BF),
            vm((T, 768), BF), vm((4, 12, 96, 128), BF), vm((3, 16) + block, BF),
            vm((4, DP, 48, 128), BF), vm((32, 768), F32), vm((16, 768), F32),
            vm((T, 768), BF), vm((6, T, 128), BF), vm((6, 1024, 128), BF), vm((6, 128, 1024), BF),
            vm((2, R, T), BF), vm((2, T, R), BF), vm((T, 768), BF), vm((2, T, 768), BF),
            vm((T, 768), F32), vm((T, 768), BF), vm((2, T, 768), BF), vm((T, 768), F32),
            vm((2, T, 768), F32), vm((768, T), BF), vm((6, R, 128), BF), vm((6, R, 128), BF),
            vm((6, 1, T), F32),
            dma((4, 3)), dma((4, 3)), dma((2,)), dma((2,)),
            dma((16,)), dma((12,)), dma((24,)), dma((2, 12)), dma((16,)), dma((16,)),
            dma((3, 15)), dma((3, 16)), dma((5,)), dma((5,)),
            dma((16,)), dma((16,)), dma((2, 24)), dma((2, 3, DP)), dma((3, 4)), dma((3, 4)),
            dma((3, 2, 4)), dma((3, 2, 4)), dma((3, 3)), dma((3, 3)),
        ],
        compiler_params=pltpu.CompilerParams(
            collective_id=3, has_side_effects=True, vmem_limit_bytes=VMEM_LIMIT
        ),
    )(xs, ts, wsh, small, mask, factor)


def send_slot(perm, m, d, dp):
    index = 0
    for k in range(DP):
        v = perm[m, DP * d + k]
        index = index + jnp.where(lax.shift_right_logical(v, 3) == dp, v & 7, 0)
    return index


def one_hot(timestep):
    steps = lax.broadcasted_iota(jnp.int32, (1, 1000), 1)
    return jnp.concatenate(
        [jnp.where(steps == timestep[n], 1.0, 0.0).astype(F32) for n in range(24)], axis=0
    )


def valid_count(lengths):
    count = lengths[0]
    for n in range(1, 24):
        count = count + lengths[n]
    return count


def pack_kernel(
    perm, lengths, timestep, xin, tin, table, gains, shifts, qvb, inb, w_qkv, w_out, w_in, w_back,
    xs, ts, wsh, small, mask, factor,
    rows, lines, sem,
):
    dp, mp, x, c = place()
    slots = [[send_slot(perm, m, d, dp) for d in range(DP)] for m in range(3)]
    copies = []
    for m in range(3):
        for d in range(DP):
            source = xin.at[m, pl.ds(pl.multiple_of(64 * slots[m][d], 64), 64)]
            copies.append(pltpu.make_async_copy(source, xs.at[m, d], sem.at[m, d]))
            copies[-1].start()
    for m in range(3):
        rows[m] = tin[m].T
    for m in range(3):
        for d in range(DP):
            v = rows[m, pl.ds(pl.multiple_of(64 * slots[m][d], 64), 64)]
            ts[m, d, 0:64] = v[:, 0:128]
            ts[m, d, 64:96] = jnp.concatenate([v[0:32, 128:192], v[32:64, 128:192]], axis=1)
    wsh[0, :, 0:576] = w_qkv[...]
    wsh[0, :, 576:768] = w_out[...].T
    wsh[1] = w_in[...]
    wsh[2] = w_back[...]

    lane = lax.broadcasted_iota(jnp.int32, (8, 128), 1)
    lines[...] = jnp.zeros(lines.shape, F32)
    lines[0:2, 0:24] = gains[...].astype(F32)
    lines[2:6, 0:24] = shifts[...].astype(F32)
    lines[6:30, 0:24] = nt(one_hot(timestep).astype(BF), table[...])
    spread = jnp.concatenate([inb[...].astype(F32)] * 8, axis=1)
    lines[32:38] = jnp.where(lax.shift_right_logical(lane[0:6], 4) == dp, spread, 0.0)
    for j in range(3):
        both = jnp.concatenate([qvb[j].astype(F32)] * 8, axis=1)
        both = jnp.where(lax.shift_right_logical(lane[0:2, 0:64], 3) == dp, both, 0.0)
        lines[40 + j : 41 + j, 0:64] = both[0:1]
        lines[43 + j : 44 + j, 0:64] = both[1:2]
    small[...] = lines[...].astype(BF)

    inside = lax.broadcasted_iota(jnp.int32, (64, 128), 0)
    micro_lengths = lengths[x * DP + dp], lengths[2 * DP + dp]
    for j in range(16):
        own = j < 8
        m = x if own else 2
        wanted = j if own else 2 * (j % 4) + (x if j < 12 else 1 - x)
        at = 0
        for p in range(DP):
            v = perm[m, DP * dp + p]
            at = at + jnp.where(lax.shift_right_logical(v, 3) == wanted, p, 0)
        live = inside + 64 * at < micro_lengths[0 if own else 1]
        mask[64 * j : 64 * j + 64] = jnp.where(live, 0.0, -1e30).astype(F32)
    count = jnp.full((8, 128), valid_count(lengths), jnp.int32).astype(F32)
    factor[...] = (3.0 * DP * 512) / count
    for copy in copies:
        copy.wait()


def pack(*arguments):
    vm = pltpu.VMEM
    smem = pl.BlockSpec(memory_space=pltpu.SMEM)
    return pl.pallas_call(
        pack_kernel,
        name="pack",
        out_shape=(
            jax.ShapeDtypeStruct((3, DP, 64, 768), BF),
            jax.ShapeDtypeStruct((3, DP, 96, 128), BF),
            jax.ShapeDtypeStruct((3, ROWS, 768), BF),
            jax.ShapeDtypeStruct((48, 128), BF),
            jax.ShapeDtypeStruct((1024, 128), F32),
            jax.ShapeDtypeStruct((8, 128), F32),
        ),
        in_specs=[smem] * 3 + [pl.BlockSpec(memory_space=pl.ANY)] + [VM] * 10,
        out_specs=(VM,) * 6,
        scratch_shapes=[vm((3, 512, 192), BF), vm((48, 128), F32), pltpu.SemaphoreType.DMA((3, DP))],
        compiler_params=pltpu.CompilerParams(vmem_limit_bytes=32 * 1024 * 1024),
    )(*arguments)


def unpack_kernel(
    perm, lengths, timestep, gs, msgs, home,
    y_out, loss, grad_x, table, gains, shifts, g_qkv, g_qvb, g_out, g_in, g_inb, g_back,
    rows,
):
    dp, mp, x, c = place()
    for m in range(3):
        slots = [send_slot(perm, m, d, dp) for d in range(DP)]
        for n, target in ((0, y_out), (1, grad_x)):
            for d in range(DP):
                low = home[n, m, d, 64:96]
                value = jnp.concatenate(
                    [home[n, m, d, 0:64], jnp.concatenate([low[:, 0:64], low[:, 64:128]], axis=0)], axis=1
                )
                rows[n, pl.ds(pl.multiple_of(64 * slots[d], 64), 64)] = value
            target[m] = rows[n].T
    total = msgs[0]
    for j in range(1, 16):
        total = total + msgs[j]
    count = jnp.full((1, 1), valid_count(lengths), jnp.int32).astype(F32)
    loss[...] = jnp.sum(total[8:9], axis=1, keepdims=True) / (count * 768.0)
    gains[...] = total[0:2, 0:24]
    shifts[...] = total[2:6, 0:24]
    turned = pltpu.roll(total, lax.rem(128 - 8 * dp, 128), 1)
    for j in range(3):
        for kind in range(2):
            at = 9 + 3 * kind + j
            g_qvb[j, kind : kind + 1] = turned[at : at + 1, 0:8]
    g_inb[...] = pltpu.roll(total, lax.rem(128 - 16 * dp, 128), 1)[16:22, 0:16]
    lines = [msgs[j, 6:7] for j in range(16)] + [msgs[d, 7:8] + msgs[DP + d, 7:8] for d in range(DP)]
    columns = jnp.concatenate(lines, axis=0).T[0:24]
    chosen = one_hot(timestep)
    result = columns[:, 0:1] * chosen[0:1]
    for n in range(1, 24):
        result = result + columns[:, n : n + 1] * chosen[n : n + 1]
    table[...] = result
    g_qkv[...] = gs[0, :, 0:576]
    g_out[...] = gs[0, :, 576:768].T
    g_in[...] = gs[1]
    g_back[...] = gs[2]


def unpack(*arguments):
    smem = pl.BlockSpec(memory_space=pltpu.SMEM)
    shapes = [
        ((3, 192, 512), BF), ((1, 1), F32), ((3, 192, 512), BF), ((24, 1000), F32), ((2, 24), F32),
        ((4, 24), F32), ((96, 576), F32), ((3, 2, 8), F32), ((192, 96), F32), ((96, 768), F32),
        ((6, 16), F32), ((96, 768), F32),
    ]
    return pl.pallas_call(
        unpack_kernel,
        name="unpack",
        out_shape=tuple(jax.ShapeDtypeStruct(*shape) for shape in shapes),
        in_specs=[smem] * 3 + [VM] * 3,
        out_specs=(VM,) * 12,
        scratch_shapes=[pltpu.VMEM((2, 512, 192), BF)],
        compiler_params=pltpu.CompilerParams(vmem_limit_bytes=32 * 1024 * 1024),
    )(*arguments)


def per_device_compact(
    input_stream, teacher, timestep, lengths, block_perm, table, norm_gains, shifts,
    w_qkv, qv_bias, w_out, w_in, in_bias, w_back,
):
    packed = pack(
        block_perm, lengths, timestep, input_stream, teacher.transpose(0, 2, 1), table.T, norm_gains, shifts,
        qv_bias.transpose(1, 0, 2), in_bias, w_qkv, w_out, w_in, w_back.T,
    )
    outs = list(unpack(block_perm, lengths, timestep, *step(*packed)))
    outs[0], outs[2] = outs[0].transpose(0, 2, 1), outs[2].transpose(0, 2, 1)
    outs[1], outs[3] = outs[1].reshape(()), outs[3].T
    outs[7], outs[11] = outs[7].transpose(1, 0, 2), outs[11].T
    return tuple(outs)


def solution(mesh):
    compact = mesh.shape["dp"] == 8 and mesh.shape["mp"] == 4
    return jax.shard_map(
        per_device_compact if compact else per_device,
        mesh=mesh,
        in_specs=(
            P(None, "dp", None),
            P(None, "dp", "mp"),
            P(),
            P(),
            P(),
            P(None, ("dp", "mp")),
            P(None, ("dp", "mp")),
            P(None, ("dp", "mp")),
            P("dp", "mp"),
            P(None, "mp", "dp"),
            P("mp", "dp"),
            P("dp", "mp"),
            P("mp", "dp"),
            P("mp", "dp"),
        ),
        out_specs=(
            P(None, "dp", "mp"),
            P(),
            P(None, "dp", "mp"),
            P(None, ("dp", "mp")),
            P(None, ("dp", "mp")),
            P(None, ("dp", "mp")),
            P("dp", "mp"),
            P(None, "mp", "dp"),
            P("mp", "dp"),
            P("dp", "mp"),
            P("mp", "dp"),
            P("mp", "dp"),
        ),
        check_vma=False,
    )
```

```python
import functools
import math

import jax
import jax.numpy as jnp
from jax import lax
from jax.experimental import pallas as pl
from jax.experimental.pallas import tpu as pltpu
from jax.sharding import PartitionSpec as P

H = 12
DH = 64


epsilon = 1e-05


def normalize_rows(stream):
    centered = stream - jnp.mean(stream, axis=-1, keepdims=True)
    inverse = lax.rsqrt(jnp.mean(centered * centered, axis=-1, keepdims=True) + epsilon)
    return (centered * inverse, inverse)


def column_part(array, start, width):
    return lax.dynamic_slice_in_dim(array, start, width, array.ndim - 1)


def fetch_weights(w_qkv, w_in, w_out, w_back, qv_bias, in_bias):
    return (
        lax.all_gather(w_qkv, "dp", axis=0, tiled=True),
        lax.all_gather(w_in, "dp", axis=0, tiled=True),
        lax.all_gather(w_out, "dp", axis=1, tiled=True),
        lax.all_gather(w_back, "dp", axis=1, tiled=True),
        lax.all_gather(qv_bias, "dp", axis=2, tiled=True),
        lax.all_gather(in_bias, "dp", axis=1, tiled=True),
    )


def invert_map(targets, size):
    ranks = jnp.arange(size, dtype=jnp.int32)
    return jnp.sum(jnp.where(targets[None, :] == ranks[:, None], ranks[None, :], 0), axis=1)


def masked_scores(queries, keys_all, is_live, score_scale):
    scores = (
        jnp.einsum("qhe,khe->hqk", queries, keys_all, preferred_element_type=jnp.float32)
        * score_scale
    )
    return jnp.where(is_live[None, None, :], scores, -1e30)


def attend_rows(keys_all, values, is_live, score_scale, queries):
    scores = masked_scores(queries, keys_all, is_live, score_scale)
    row_top = jnp.max(scores, axis=-1, keepdims=True)
    exponent = jnp.exp(scores - row_top)
    row_total = jnp.sum(exponent, axis=-1, keepdims=True)
    weights_p = (exponent / row_total).astype(jnp.bfloat16)
    mixed = jnp.einsum("hqk,khe->qhe", weights_p, values, preferred_element_type=jnp.float32)
    return (mixed, (row_top + jnp.log(row_total))[..., 0])


def attend_back(keys_all, values, is_live, score_scale, carry, inputs):
    queries, grad_rows, log_total = inputs
    grad_keys, grad_values = carry
    scores = masked_scores(queries, keys_all, is_live, score_scale)
    probabilities = jnp.exp(scores - log_total[..., None])
    grad_probs = jnp.einsum("qhe,khe->hqk", grad_rows, values, preferred_element_type=jnp.float32)
    row_delta = jnp.sum(probabilities * grad_probs, axis=-1, keepdims=True)
    grad_scores = (probabilities * (grad_probs - row_delta)).astype(jnp.bfloat16)
    grad_queries = (
        jnp.einsum("hqk,khe->qhe", grad_scores, keys_all, preferred_element_type=jnp.float32)
        * score_scale
    )
    grad_keys = (
        grad_keys
        + jnp.einsum("hqk,qhe->khe", grad_scores, queries, preferred_element_type=jnp.float32)
        * score_scale
    )
    grad_values = grad_values + jnp.einsum(
        "hqk,qhe->khe",
        probabilities.astype(jnp.bfloat16),
        grad_rows,
        preferred_element_type=jnp.float32,
    )
    return ((grad_keys, grad_values), grad_queries)


def norm_sums(partial_value, normed, gain_full, mp_count):
    weighted = partial_value * gain_full
    sums = jnp.stack([jnp.sum(weighted, axis=1), jnp.sum(weighted * normed, axis=1)], axis=1)
    return jnp.tile(sums, (1, mp_count))


def norm_input_grad(grad_part, gain_part, normed_part, inverse, sums, width):
    scaled = grad_part * gain_part
    return inverse * (scaled - sums[:, 0:1] / width - normed_part * sums[:, 1:2] / width)


def per_device(
    input_stream,
    teacher,
    timestep,
    lengths,
    block_perm,
    table,
    norm_gains,
    shifts,
    w_qkv,
    qv_bias,
    w_out,
    w_in,
    in_bias,
    w_back,
):
    dp_count = lax.axis_size("dp")
    mp_count = lax.axis_size("mp")
    dp_rank = lax.axis_index("dp")
    mp_rank = lax.axis_index("mp")
    micro_count, seq_len, width = input_stream.shape
    part_width = teacher.shape[2]
    block_rows = seq_len // dp_count
    heads_here = H // mp_count
    score_scale = 1.0 / math.sqrt(DH)
    col_start = mp_rank * part_width
    row_block = min(512, seq_len)
    block_count = seq_len // row_block
    valid_count = jnp.sum(lengths).astype(jnp.float32)
    loss_factor = micro_count * dp_count * seq_len / valid_count
    chosen = jnp.take(table, timestep, axis=0)
    gains_full, shifts_full, table_rows = (
        lax.all_gather(norm_gains, ("dp", "mp"), axis=1, tiled=True),
        lax.all_gather(shifts, ("dp", "mp"), axis=1, tiled=True),
        lax.all_gather(chosen, ("dp", "mp"), axis=1, tiled=True),
    )
    gains_full = gains_full.astype(jnp.float32)
    shifts_full = shifts_full.astype(jnp.float32)
    gain_parts = column_part(gains_full, col_start, part_width)
    acc_qkv = jnp.zeros((width, heads_here * 3 * DH), jnp.float32)
    acc_in = jnp.zeros((width, w_in.shape[1]), jnp.float32)
    acc_out = jnp.zeros((heads_here * DH, width), jnp.float32)
    acc_back = jnp.zeros((w_back.shape[0], width), jnp.float32)
    acc_qv = jnp.zeros((2, heads_here, DH), jnp.float32)
    acc_in_bias = jnp.zeros((w_in.shape[1],), jnp.float32)
    acc_gains = jnp.zeros((2, part_width), jnp.float32)
    acc_shifts = jnp.zeros((4, part_width), jnp.float32)
    loss_part = jnp.zeros((), jnp.float32)
    table_sums = []
    outs_y = []
    outs_grad = []
    for micro_index in range(micro_count):
        forward_set = fetch_weights(w_qkv, w_in, w_out, w_back, qv_bias, in_bias)
        proj_qkv, proj_in, proj_out, proj_back, bias_qv, bias_in = forward_set
        bias_qv = bias_qv.astype(jnp.float32)
        bias_in = bias_in.reshape(-1).astype(jnp.float32)
        block_order = block_perm[micro_index].reshape(dp_count, dp_count)
        source = block_order // dp_count
        local_index = block_order % dp_count
        send_index = jnp.sum(jnp.where(source == dp_rank, local_index, 0), axis=1)
        x_blocks = input_stream[micro_index].reshape(dp_count, block_rows, width)
        t_blocks = teacher[micro_index].reshape(dp_count, block_rows, part_width)
        got_x, got_t = (
            lax.all_to_all(
                jnp.take(x_blocks, send_index, axis=0),
                "dp",
                split_axis=0,
                concat_axis=0,
                tiled=True,
            ),
            lax.all_to_all(
                jnp.take(t_blocks, send_index, axis=0),
                "dp",
                split_axis=0,
                concat_axis=0,
                tiled=True,
            ),
        )
        my_source = lax.dynamic_index_in_dim(source, dp_rank, 0, keepdims=False)
        tokens = jnp.take(got_x, my_source, axis=0).reshape(seq_len, width).astype(jnp.float32)
        target = jnp.take(got_t, my_source, axis=0).reshape(seq_len, part_width).astype(jnp.float32)
        seq_index = micro_index * dp_count + dp_rank
        length = lax.dynamic_index_in_dim(lengths, seq_index, 0, keepdims=False)
        table_row = lax.dynamic_index_in_dim(table_rows, seq_index, 0, keepdims=False).astype(
            jnp.float32
        )
        is_live = jnp.arange(seq_len, dtype=jnp.int32) < length
        stream_in = tokens + table_row[None, :]
        normed1, inverse1 = normalize_rows(stream_in)
        normed_in = (normed1 * gains_full[0] + shifts_full[0]).astype(jnp.bfloat16)
        projected = jnp.dot(normed_in, proj_qkv, preferred_element_type=jnp.float32).reshape(
            seq_len, heads_here, 3, DH
        )
        queries = (projected[:, :, 0] + bias_qv[0]).astype(jnp.bfloat16)
        keys_all = projected[:, :, 1].astype(jnp.bfloat16)
        values = (projected[:, :, 2] + bias_qv[1]).astype(jnp.bfloat16)
        query_blocks = queries.reshape(block_count, row_block, heads_here, DH)
        mixed, log_total = lax.map(
            functools.partial(attend_rows, keys_all, values, is_live, score_scale), query_blocks
        )
        attended = mixed.reshape(seq_len, heads_here * DH).astype(jnp.bfloat16)
        attn_part = jnp.dot(attended, proj_out, preferred_element_type=jnp.float32)
        branch_attn = lax.psum_scatter(
            attn_part, "mp", scatter_dimension=1, tiled=True
        ) + column_part(shifts_full[2], col_start, part_width)
        mid_part = column_part(stream_in, col_start, part_width) + branch_attn
        stream_mid = lax.all_gather(mid_part, "mp", axis=1, tiled=True)
        normed2, inverse2 = normalize_rows(stream_mid)
        normed_mid = (normed2 * gains_full[1] + shifts_full[1]).astype(jnp.bfloat16)
        pre_act = jnp.dot(normed_mid, proj_in, preferred_element_type=jnp.float32) + bias_in
        activation = jax.nn.gelu(pre_act, approximate=True).astype(jnp.bfloat16)
        mlp_part = jnp.dot(activation, proj_back, preferred_element_type=jnp.float32)
        mlp_out = lax.psum_scatter(mlp_part, "mp", scatter_dimension=1, tiled=True) + column_part(
            shifts_full[3], col_start, part_width
        )
        out_part = mid_part + mlp_out
        residual_err = jnp.where(is_live[:, None], out_part - target, 0.0)
        loss_part = loss_part + jnp.sum(residual_err * residual_err)
        grad_y = residual_err * loss_factor
        grad_mlp = grad_y.astype(jnp.bfloat16)
        acc_shifts = acc_shifts.at[3].add(jnp.sum(grad_mlp.astype(jnp.float32), axis=0))
        grad_mlp_full = lax.all_gather(grad_mlp, "mp", axis=1, tiled=True)
        back_set = fetch_weights(w_qkv, w_in, w_out, w_back, qv_bias, in_bias)
        back_qkv, back_in, back_out, back_back = (
            back_set[0],
            back_set[1],
            back_set[2],
            back_set[3],
        )
        acc_back = acc_back + jnp.einsum(
            "tf,td->fd", activation, grad_mlp_full, preferred_element_type=jnp.float32
        )
        grad_act = jnp.einsum(
            "td,fd->tf", grad_mlp_full, back_back, preferred_element_type=jnp.float32
        )
        gelu_value, gelu_pull = jax.vjp(lambda inner: jax.nn.gelu(inner, approximate=True), pre_act)
        grad_pre = gelu_pull(grad_act)[0].astype(jnp.bfloat16)
        acc_in_bias = acc_in_bias + jnp.sum(grad_pre.astype(jnp.float32), axis=0)
        acc_in = acc_in + jnp.einsum(
            "td,tf->df", normed_mid, grad_pre, preferred_element_type=jnp.float32
        )
        partial2 = jnp.einsum("tf,df->td", grad_pre, back_in, preferred_element_type=jnp.float32)
        grad_h2, sums2 = (
            lax.psum_scatter(partial2, "mp", scatter_dimension=1, tiled=True),
            lax.psum_scatter(
                norm_sums(partial2, normed2, gains_full[1], mp_count),
                "mp",
                scatter_dimension=1,
                tiled=True,
            ),
        )
        normed2_part = column_part(normed2, col_start, part_width)
        acc_gains = acc_gains.at[1].add(jnp.sum(grad_h2 * normed2_part, axis=0))
        acc_shifts = acc_shifts.at[1].add(jnp.sum(grad_h2, axis=0))
        grad_mid = grad_y + norm_input_grad(
            grad_h2, gain_parts[1], normed2_part, inverse2, sums2, width
        )
        grad_branch = grad_mid.astype(jnp.bfloat16)
        acc_shifts = acc_shifts.at[2].add(jnp.sum(grad_branch.astype(jnp.float32), axis=0))
        grad_branch_full = lax.all_gather(grad_branch, "mp", axis=1, tiled=True)
        acc_out = acc_out + jnp.einsum(
            "tc,td->cd", attended, grad_branch_full, preferred_element_type=jnp.float32
        )
        grad_att = jnp.einsum(
            "td,cd->tc", grad_branch_full, back_out, preferred_element_type=jnp.float32
        ).astype(jnp.bfloat16)
        grad_blocks = grad_att.reshape(block_count, row_block, heads_here, DH)
        zero_heads = jnp.zeros((seq_len, heads_here, DH), jnp.float32)
        (grad_keys, grad_values), grad_queries = lax.scan(
            functools.partial(attend_back, keys_all, values, is_live, score_scale),
            (zero_heads, zero_heads),
            (query_blocks, grad_blocks, log_total),
        )
        grad_queries = grad_queries.reshape(seq_len, heads_here, DH).astype(jnp.bfloat16)
        grad_keys = grad_keys.astype(jnp.bfloat16)
        grad_values = grad_values.astype(jnp.bfloat16)
        acc_qv = acc_qv + jnp.stack(
            [
                jnp.sum(grad_queries.astype(jnp.float32), axis=0),
                jnp.sum(grad_values.astype(jnp.float32), axis=0),
            ]
        )
        grad_qkv_rows = jnp.stack([grad_queries, grad_keys, grad_values], axis=2).reshape(
            seq_len, heads_here * 3 * DH
        )
        acc_qkv = acc_qkv + jnp.einsum(
            "td,tc->dc", normed_in, grad_qkv_rows, preferred_element_type=jnp.float32
        )
        partial1 = jnp.einsum(
            "tc,dc->td", grad_qkv_rows, back_qkv, preferred_element_type=jnp.float32
        )
        grad_h1, sums1 = (
            lax.psum_scatter(partial1, "mp", scatter_dimension=1, tiled=True),
            lax.psum_scatter(
                norm_sums(partial1, normed1, gains_full[0], mp_count),
                "mp",
                scatter_dimension=1,
                tiled=True,
            ),
        )
        normed1_part = column_part(normed1, col_start, part_width)
        acc_gains = acc_gains.at[0].add(jnp.sum(grad_h1 * normed1_part, axis=0))
        acc_shifts = acc_shifts.at[0].add(jnp.sum(grad_h1, axis=0))
        grad_in_stream = grad_mid + norm_input_grad(
            grad_h1, gain_parts[0], normed1_part, inverse1, sums1, width
        )
        table_sums.append(jnp.sum(grad_in_stream, axis=0))
        back_order = invert_map(my_source, dp_count)
        out_blocks = jnp.take(
            out_part.astype(jnp.bfloat16).reshape(dp_count, block_rows, part_width),
            back_order,
            axis=0,
        )
        grad_send = jnp.take(
            grad_in_stream.astype(jnp.bfloat16).reshape(dp_count, block_rows, part_width),
            back_order,
            axis=0,
        )
        home_out, home_grad = (
            lax.all_to_all(out_blocks, "dp", split_axis=0, concat_axis=0, tiled=True),
            lax.all_to_all(grad_send, "dp", split_axis=0, concat_axis=0, tiled=True),
        )
        home_place = invert_map(send_index, dp_count)
        outs_y.append(jnp.take(home_out, home_place, axis=0).reshape(seq_len, part_width))
        outs_grad.append(jnp.take(home_grad, home_place, axis=0).reshape(seq_len, part_width))
    row_sums = jnp.zeros((micro_count, width), jnp.float32)
    row_sums = lax.dynamic_update_slice_in_dim(row_sums, jnp.stack(table_sums), col_start, 1)
    my_steps = jnp.take(timestep, jnp.arange(micro_count, dtype=jnp.int32) * dp_count + dp_rank)
    step_onehot = (
        jnp.arange(table.shape[0], dtype=jnp.int32)[:, None] == my_steps[None, :]
    ).astype(jnp.float32)
    table_grad = jnp.dot(
        step_onehot, row_sums, precision=lax.Precision.HIGHEST, preferred_element_type=jnp.float32
    )
    gains_grad = lax.dynamic_update_slice_in_dim(
        jnp.zeros((2, width), jnp.float32), acc_gains, col_start, 1
    )
    shifts_grad = lax.dynamic_update_slice_in_dim(
        jnp.zeros((4, width), jnp.float32), acc_shifts, col_start, 1
    )
    loss_row = jnp.full((1, dp_count * mp_count), loss_part, jnp.float32)
    grad_table, grad_norm_gains, grad_shifts, loss_cell = (
        lax.psum_scatter(table_grad, ("dp", "mp"), scatter_dimension=1, tiled=True),
        lax.psum_scatter(gains_grad, ("dp", "mp"), scatter_dimension=1, tiled=True),
        lax.psum_scatter(shifts_grad, ("dp", "mp"), scatter_dimension=1, tiled=True),
        lax.psum_scatter(loss_row, ("dp", "mp"), scatter_dimension=1, tiled=True),
    )
    loss = loss_cell[0, 0] / (valid_count * width)
    grad_qkv, grad_in, grad_out, grad_back, grad_qv_bias, grad_in_bias = (
        lax.psum_scatter(acc_qkv, "dp", scatter_dimension=0, tiled=True),
        lax.psum_scatter(acc_in, "dp", scatter_dimension=0, tiled=True),
        lax.psum_scatter(acc_out, "dp", scatter_dimension=1, tiled=True),
        lax.psum_scatter(acc_back, "dp", scatter_dimension=1, tiled=True),
        lax.psum_scatter(acc_qv, "dp", scatter_dimension=2, tiled=True),
        lax.psum_scatter(acc_in_bias.reshape(-1, 128), "dp", scatter_dimension=1, tiled=True),
    )
    y_out = jnp.stack(outs_y)
    grad_x = jnp.stack(outs_grad)
    return (
        y_out,
        loss,
        grad_x,
        grad_table,
        grad_norm_gains,
        grad_shifts,
        grad_qkv,
        grad_qv_bias,
        grad_out,
        grad_in,
        grad_in_bias,
        grad_back,
    )


MESH = pl.DeviceIdType.MESH
BF = jnp.bfloat16
F32 = jnp.float32
VM = pl.BlockSpec(memory_space=pltpu.VMEM)
DP = 8
ROWS = 96
VMEM_LIMIT = 64 * 1024 * 1024 - 65536


def place():
    dp, mp = lax.axis_index("dp"), lax.axis_index("mp")
    x, c = lax.div(mp, 2), lax.rem(mp, 2)
    return dp, mp, x, c


def remote(src, dst, send_sem, recv_sem, dp, mp):
    return pltpu.make_async_remote_copy(
        src_ref=src,
        dst_ref=dst,
        send_sem=send_sem,
        recv_sem=recv_sem,
        device_id=(dp, mp),
        device_id_type=MESH,
    )


def landed(dst, recv_sem, spare, dp, mp):
    remote(dst, dst, spare, recv_sem, dp, mp).wait_recv()


def greet_plane(dp, x, c):
    barrier = pltpu.get_barrier_semaphore()
    pl.semaphore_signal(barrier, inc=1, device_id=(dp, 2 * x + 1 - c), device_id_type=MESH)
    for k in range(DP):
        for xr in range(2):
            if k or xr:
                there = (lax.rem(dp + k, DP), 2 * lax.rem(x + xr, 2) + c)
                pl.semaphore_signal(barrier, inc=1, device_id=there, device_id_type=MESH)
    pl.semaphore_wait(barrier, 2 * DP)


def dot(a, b, dims):
    return lax.dot_general(a, b, (dims, ((), ())), preferred_element_type=F32)


T = 768
R = 256
LOG_SCALE = 0.125


def nn(a, b):
    return dot(a, b, ((1,), (0,)))


def nt(a, b):
    return dot(a, b, ((1,), (1,)))


def chunk(i):
    return pl.ds(pl.multiple_of(i * R, R), R)


def colsum(a):
    return jnp.sum(a, axis=0, keepdims=True)


def wide(column_tile, width):
    return jnp.concatenate([column_tile] * (width // 128), axis=1)


def gelu_pair(v):
    k = 0.7978845608028654
    v2 = v * v
    t = jnp.tanh(k * (v + 0.044715 * (v2 * v)))
    half = 0.5 * (1.0 + t)
    slope = half + 0.5 * v * ((1.0 - t * t) * (k * (1.0 + 0.134145 * v2)))
    return v * half, slope


def norm_back(g, normed, inverse):
    inner = jnp.mean(g * normed, axis=1, keepdims=True)
    return inverse * (g - jnp.mean(g, axis=1, keepdims=True) - normed * inner)


def step_kernel(
    xs, ts, wsh, small, mask, factor,
    gs, msgs, back,
    g, yg, sums, msg, s1, r1, r2, r3,
    tok, tea, w, smalls, vecs, vec, nin, q_s, kv, kvt, o_t, att, n2_s, act, gy, gm, gp, x3, recv, tr, dkx, dkr, lse,
    s_core, r_core, s_x, r_x,
    s_tok, r_tok, s_tea, r_tea, s_small, r_small, s_w, r_w, s_pair, r_pair,
    s_msg, r_msg, s_yg, r_yg, s_a, r_a, s_b, r_b, s_c, r_c,
):
    dp, mp, x, c = place()
    other, across = 2 * x + 1 - c, 2 * (1 - x) + c
    z, y = lax.div(dp, 2), lax.rem(dp, 2)
    mine = x * DP + dp
    half = pl.ds(pl.multiple_of(384 * c, 128), 384)
    beside = 2 * z + 1 - y
    greet_plane(dp, x, c)
    sent = []

    def go(copy):
        copy.start()
        sent.append(copy)

    def rows64(j):
        return pl.ds(pl.multiple_of(64 * j, 64), 64)

    def weights_z(p):
        pltpu.make_async_copy(wsh.at[p], w.at[p, mine], r_w.at[p, mine]).start()
        for k in range(1, 4):
            zz = lax.rem(z + k, 4)
            go(remote(wsh.at[p], w.at[p, mine], s_w.at[p, k - 1], r_w.at[p, mine], 2 * zz + y, mp))

    def weights_xy(p):
        go(remote(wsh.at[p], w.at[p, mine], s_w.at[p, 3], r_w.at[p, mine], dp, across))
        go(remote(wsh.at[p], w.at[p, mine], s_w.at[p, 4], r_w.at[p, mine], beside, mp))

    def spread(p):
        for k in (3, 2, 1):
            b = x * DP + 2 * lax.rem(z + k, 4) + y
            landed(w.at[p, b], r_w.at[p, b], s_w.at[p, 0], dp, mp)
            go(remote(w.at[p, b], w.at[p, b], s_w.at[p, 3 + 2 * k], r_w.at[p, b], dp, across))
            go(remote(w.at[p, b], w.at[p, b], s_w.at[p, 4 + 2 * k], r_w.at[p, b], beside, mp))

    def relay(p, steps=(3, 2, 1)):
        for n in steps:
            k = lax.rem(z + n, 4)
            bx, by = (1 - x) * DP + 2 * k + y, x * DP + 2 * k + 1 - y
            landed(w.at[p, bx], r_w.at[p, bx], s_w.at[p, 0], dp, mp)
            landed(w.at[p, by], r_w.at[p, by], s_w.at[p, 0], dp, mp)
            b = jnp.where(k < 2, bx, by)
            there = jnp.where(k < 2, beside, dp), jnp.where(k < 2, mp, across)
            go(remote(w.at[p, b], w.at[p, b], s_w.at[p, 11 + n], r_w.at[p, b], *there))

    def complete(p):
        landed(w.at[p, mine], r_w.at[p, mine], s_w.at[p, 0], dp, mp)
        for k in range(4):
            b = (1 - x) * DP + 2 * k + 1 - y
            landed(w.at[p, b], r_w.at[p, b], s_w.at[p, 0], dp, mp)

    weights_z(0)
    weights_xy(0)

    pltpu.make_async_copy(small, smalls.at[mp, dp], r_small.at[mine]).start()
    for k in range(DP):
        for xr in range(2):
            if k or xr:
                d, m = lax.rem(dp + k, DP), 2 * lax.rem(x + xr, 2) + c
                go(remote(small, smalls.at[mp, dp], s_small.at[2 * k + xr], r_small.at[mine], d, m))

    def token_copy(k, d, m_from, j):
        return remote(
            xs.at[m_from, d, :, half], tok.at[rows64(j), half], s_tok.at[k], r_tok.at[j], d, mp
        )

    weights_xy(1)
    weights_xy(2)
    pltpu.make_async_copy(xs.at[x, dp, :, half], tok.at[rows64(dp), half], r_tok.at[dp]).start()
    for k in range(1, DP):
        go(token_copy(k, lax.rem(dp + k, DP), x, dp))

    @pl.when(y == x)
    def _():
        pltpu.make_async_copy(
            xs.at[2, dp, :, half], tok.at[rows64(8 + z), half], r_tok.at[8 + z]
        ).start()
        for k in range(1, DP):
            token_copy(8 + k, lax.rem(dp + k, DP), 2, 8 + z).start()

    weights_z(1)
    weights_z(2)
    for p in range(3):
        relay(p, (0,))
    spread(0)

    for j in range(12):
        landed(tok.at[rows64(j), half], r_tok.at[j], s_tok.at[0], dp, mp)
    ours, theirs, whole = pl.ds(512, 256), pl.ds(768, 256), pl.ds(0, T)
    go(remote(tok.at[ours, half], tok.at[theirs, half], s_x.at[0], r_x.at[0], dp, across))
    go(remote(tok.at[whole, half], tok.at[whole, half], s_pair.at[0], r_pair.at[0], dp, other))
    for j in range(8):
        for xx in range(2):
            m = 2 * xx + c
            landed(smalls.at[m, j], r_small.at[xx * DP + j], s_small.at[0], dp, mp)
    go(remote(smalls.at[c], smalls.at[c], s_pair.at[1], r_pair.at[1], dp, other))
    go(remote(smalls.at[2 + c], smalls.at[2 + c], s_pair.at[2], r_pair.at[2], dp, other))
    relay(0)

    pltpu.make_async_copy(ts.at[x, dp], tea.at[mp, dp], r_tea.at[x, dp]).start()
    for k in range(DP):
        d = lax.rem(dp + k, DP)
        for xr in range(2):
            if k or xr:
                xx = lax.rem(x + xr, 2)
                go(remote(ts.at[xx, d], tea.at[mp, dp], s_tea.at[2 * k + xr], r_tea.at[x, dp], d, 2 * xx + c))
        if k:
            go(remote(ts.at[2, d], tea.at[mp, 8 + z], s_tea.at[16 + k], r_tea.at[x, 8 + z], d, 2 * y + c))

    @pl.when(y == x)
    def _():
        pltpu.make_async_copy(ts.at[2, dp], tea.at[mp, 8 + z], r_tea.at[x, 8 + z]).start()

    @pl.when(y != x)
    def _():
        remote(ts.at[2, dp], tea.at[mp, 8 + z], s_tea.at[16], r_tea.at[x, 8 + z], dp, 2 * y + c).start()

    o = 1 - c
    their_half = pl.ds(pl.multiple_of(384 * o, 128), 384)
    landed(tok.at[theirs, half], r_x.at[0], s_x.at[0], dp, mp)
    go(remote(tok.at[theirs, half], tok.at[theirs, half], s_pair.at[5], r_pair.at[5], dp, other))
    landed(tok.at[whole, their_half], r_pair.at[0], s_pair.at[0], dp, mp)
    landed(smalls.at[o], r_pair.at[1], s_pair.at[0], dp, mp)
    landed(smalls.at[2 + o], r_pair.at[2], s_pair.at[0], dp, mp)

    low, high = lax.broadcasted_iota(jnp.int32, (512, 128), 0), lax.broadcasted_iota(jnp.int32, (512, 128), 1)
    lane, quarter = low & 127, lax.shift_right_logical(low, 7)
    pick = jnp.where((high == 24 * quarter + lane) & (lane < 24), 1.0, 0.0).astype(BF)
    stacked = jnp.concatenate(
        [jnp.concatenate([smalls[m, d, 0:32] for m in range(4)], axis=1) for d in range(DP)], axis=0
    )
    picked = nn(stacked, pick)
    vecs[...] = jnp.concatenate([picked[32 * d : 32 * d + 32, 0:96] for d in range(DP)], axis=1)
    vec[0:1] = vecs[pl.ds(6 + x * DP + dp, 1)]
    vec[1:2] = vecs[pl.ds(6 + 2 * DP + dp, 1)]
    vec[2:8] = vecs[0:6]
    blank = jnp.zeros((1, 64), F32)
    for xi in range(2):
        biases = smalls[2 * xi + c, 0, 32:48].astype(F32)
        for d in range(1, DP):
            biases = biases + smalls[2 * xi + c, d, 32:48].astype(F32)
        vec[10 + xi : 11 + xi] = jnp.concatenate([biases[k : k + 1] for k in range(6)], axis=1)
        pieces = []
        for j in range(3):
            pieces += [biases[8 + j : 9 + j, 0:64], blank, biases[11 + j : 12 + j, 0:64]]
        vec[8 + xi : 9 + xi] = jnp.concatenate(pieces + [blank] * 3, axis=1)
    landed(tok.at[theirs, their_half], r_pair.at[5], s_pair.at[0], dp, mp)
    complete(0)
    smid = g.at[0, 0]

    def half_of(p, xi, low, high):
        return w[p, DP * xi : DP * xi + DP, :, low:high].reshape(768, high - low)

    sums[...] = jnp.zeros(sums.shape, F32)

    def core(k, buffer, i):
        rows = chunk(i)
        return remote(
            buffer.at[rows], recv.at[k % 2, rows], s_core.at[k, i], r_core.at[k, i], dp, other
        )

    def each(count, body):
        def run(i, carry):
            body(i)
            return carry

        lax.fori_loop(0, count, run, 0)

    def lanes(h):
        return pl.ds(pl.multiple_of(128 * h, 128), 128)

    def add(row, value):
        width = value.shape[1]
        sums[row : row + 1, 0:width] = sums[row : row + 1, 0:width] + value

    def stream(i):
        return tok[chunk(i)].astype(F32) + jnp.where(i < 2, vec[0:1], vec[1:2])

    def block(p, xi, d):
        return g.at[p, xi, pl.ds(pl.multiple_of(ROWS * d, ROWS), ROWS)]

    def first(p):
        for n in range(1, 5):
            k = lax.rem(z + n, 4)
            staged = s1 if p == 2 else w.at[p]
            staged[k] = block(p, 1 - x, 2 * k + 1 - y)[...].astype(BF)
            there = jnp.where(k < (1 if p == 1 else 2), dp, beside), jnp.where(k < (1 if p == 1 else 2), across, mp)
            go(remote(staged.at[k], r1.at[p, k], s_a.at[p, k], r_a.at[p, k], *there))

    def second(p):
        for n in range(1, 5):
            k = lax.rem(z + n, 4)
            landed(r1.at[p, k], r_a.at[p, k], s_a.at[p, k], dp, mp)
            extra = r1[p, k].astype(F32)
            gx, gy_ = block(p, 1 - x, 2 * k + y)[...], block(p, x, 2 * k + 1 - y)[...]
            w[p, 4 + k] = (gx + jnp.where(k < (1 if p == 1 else 2), 0.0, extra)).astype(BF)
            w[p, 8 + k] = (gy_ + jnp.where(k < (1 if p == 1 else 2), extra, 0.0)).astype(BF)
            go(remote(w.at[p, 4 + k], r2.at[p, 0, k], s_b.at[p, 0, k], r_b.at[p, 0, k], dp, across))
            go(remote(w.at[p, 8 + k], r2.at[p, 1, k], s_b.at[p, 1, k], r_b.at[p, 1, k], beside, mp))

    def third(p):
        for k in range(1, 5):
            zz = lax.rem(z + k, 4)
            for side in range(2):
                landed(r2.at[p, side, zz], r_b.at[p, side, zz], s_b.at[p, side, 0], dp, mp)
            total = block(p, x, 2 * zz + y)[...] + r2[p, 0, zz].astype(F32) + r2[p, 1, zz].astype(F32)
            if k < 4:
                w[p, 11 + k] = total.astype(BF)
                go(remote(w.at[p, 11 + k], r3.at[p, k - 1], s_c.at[p, k - 1], r_c.at[p, k - 1], 2 * zz + y, mp))
            else:
                gs[p] = total

    def last(p):
        for k in range(3):
            landed(r3.at[p, k], r_c.at[p, k], s_c.at[p, k], dp, mp)
        gs[p] = gs[p] + (r3[p, 0].astype(F32) + r3[p, 1].astype(F32) + r3[p, 2].astype(F32))

    def home_copy(n):
        return remote(
            yg.at[n, mp, 8 + z], back.at[n, 2, dp], s_yg.at[n, 16], r_yg.at[n, 2, dp], 2 * z + x, mp
        )

    def go_home(n):
        pltpu.make_async_copy(yg.at[n, mp, dp], back.at[n, x, dp], r_yg.at[n, x, dp]).start()
        for k in range(DP):
            s = lax.rem(dp + k, DP)
            for xr in range(2):
                if k or xr:
                    m = 2 * lax.rem(x + xr, 2) + c
                    go(remote(yg.at[n, m, s], back.at[n, x, dp], s_yg.at[n, 2 * k + xr], r_yg.at[n, x, dp], s, m))
        for k in range(4):
            j = lax.rem(z + k, 4)
            for xr in range(2):
                m = 2 * lax.rem(x + xr, 2) + c
                if k or xr:
                    go(remote(yg.at[n, m, 8 + j], back.at[n, 2, dp], s_yg.at[n, 16 + 2 * k + xr], r_yg.at[n, 2, dp], 2 * j + x, m))

        @pl.when(y == x)
        def _():
            pltpu.make_async_copy(yg.at[n, mp, 8 + z], back.at[n, 2, dp], r_yg.at[n, 2, dp]).start()

        @pl.when(y != x)
        def _():
            home_copy(n).start()

    def project(i):
        rows = chunk(i)
        normed, _ = normalize_rows(stream(i))
        nb = (normed * vec[2:3] + vec[4:5]).astype(BF)
        nin[rows] = nb
        for xi in range(2):
            pr = (nn(nb, half_of(0, xi, 0, 640)) + vec[8 + xi : 9 + xi, 0:640]).astype(BF)
            for j in range(3):
                head, a = 3 * xi + j, 192 * j
                q_s[head, rows] = jnp.concatenate([pr[:, a : a + 64], jnp.zeros((R, 64), BF)], axis=1)
                kv[head, rows] = pr[:, a + 64 : a + 192]

    each(3, project)

    normed, _ = normalize_rows(stream(3))
    nb = (normed * vec[2:3] + vec[4:5]).astype(BF)
    for xi in range(2):
        pr = (nn(nb, half_of(0, xi, 0, 640)) + vec[8 + xi : 9 + xi, 0:640]).astype(BF)
        for j in range(3):
            kv[3 * xi + j, theirs] = pr[:, 192 * j + 64 : 192 * j + 192]

    spread(1)

    def turn(part):
        def body(h):
            kvt[h, :, part * 512 : part * 512 + 512] = kv[h, part * 512 : part * 512 + 512].T

        each(6, body)

    def attend(h, block):
        part = block // 2
        keys, rows = slice(part * 512, part * 512 + 512), slice(block * R, block * R + R)
        st = nt(kv[h, keys], q_s[h, rows]) * LOG_SCALE + wide(mask[keys], R)
        top = jnp.max(st, axis=0, keepdims=True)
        e = jnp.exp(st - top)
        total = colsum(e)
        pt = (e * (1.0 / total)).astype(BF)
        ot = nn(kvt[h, 64:128, keys], pt)
        xi, j = lax.div(h, 3), lax.rem(h, 3)
        o_t[xi, pl.ds(pl.multiple_of(64 + 64 * j, 64), 64), rows] = ot.astype(BF)
        lse[h, :, rows] = top + jnp.log(total)

    o_t[:, 0:64] = jnp.zeros((2, 64, T), BF)
    turn(0)

    def attend_a(h):
        attend(h, 0)
        attend(h, 1)

    each(6, attend_a)
    relay(1)
    turn(1)
    each(6, lambda h: attend(h, 2))
    spread(2)

    def out_project(i):
        rows = chunk(i)
        part = None
        for xi in range(2):
            a = o_t[xi, :, rows].T
            att[xi, rows] = a
            piece = nt(a, half_of(0, xi, 512, 768))
            part = piece if part is None else part + piece
        smid[rows] = part
        core(0, smid, i).start()

    each(3, out_project)
    complete(1)

    def forward(i):
        rows = chunk(i)
        core(0, smid, i).wait()
        mid = stream(i) + (smid[rows] + recv[0, rows] + vec[6:7])
        smid[rows] = mid
        normed, _ = normalize_rows(mid)
        nb = (normed * vec[3:4] + vec[5:6]).astype(BF)
        n2_s[rows] = nb
        for xi in range(2):
            value, slope = gelu_pair(nn(nb, half_of(1, xi, 0, 768)) + vec[10 + xi : 11 + xi])
            act[xi, rows] = value.astype(BF)
            g[1, xi, rows] = slope

    each(3, forward)
    relay(2)
    for xx in range(2):
        for j in range(12):
            landed(tea.at[2 * xx + c, j], r_tea.at[xx, j], s_tea.at[0], dp, mp)
    go(remote(tea.at[c], tea.at[c], s_pair.at[3], r_pair.at[3], dp, other))
    go(remote(tea.at[2 + c], tea.at[2 + c], s_pair.at[4], r_pair.at[4], dp, other))
    complete(2)

    def forward_out(i):
        rows = chunk(i)
        gy[rows] = nt(act[0, rows], half_of(2, 0, 0, 768)) + nt(act[1, rows], half_of(2, 1, 0, 768))
        core(1, gy, i).start()

    each(3, forward_out)
    landed(tea.at[o], r_pair.at[3], s_pair.at[0], dp, mp)
    landed(tea.at[2 + o], r_pair.at[4], s_pair.at[0], dp, mp)

    def teacher_rows(j):
        pieces = []
        for m in range(4):
            low = tea[m, j, 64:96]
            pieces += [tea[m, j, 0:64], jnp.concatenate([low[:, 0:64], low[:, 64:128]], axis=0)]
        return jnp.concatenate(pieces, axis=1)

    def pack_out(n, i, value):
        for q in range(4):
            a = 64 * q
            for m in range(4):
                b = 192 * m
                yg[n, m, 4 * i + q, 0:64] = value[a : a + 64, b : b + 128]
                yg[n, m, 4 * i + q, 64:96] = jnp.concatenate(
                    [value[a : a + 32, b + 128 : b + 192], value[a + 32 : a + 64, b + 128 : b + 192]], axis=1
                )

    def take_loss(i):
        rows = chunk(i)
        core(1, gy, i).wait()
        out = smid[rows] + (gy[rows] + recv[1, rows] + vec[7:8])
        out_b = out.astype(BF)
        pack_out(0, i, out_b)
        target = jnp.concatenate([teacher_rows(4 * i + q) for q in range(4)], axis=0)
        residual = jnp.where(wide(mask[rows], T) == 0.0, out - target.astype(F32), 0.0)
        add(8, colsum(residual * residual))
        grad_y = residual * factor[0:1, 0:1]
        gy[rows] = grad_y
        gb = grad_y.astype(BF)
        gm[rows] = gb
        add(5, colsum(gb.astype(F32)))

    each(3, take_loss)

    def turn_rows(source):
        def body(i):
            tr[:, chunk(i)] = source[chunk(i)].T

        each(3, body)

    def weight_grad(p, values):
        def body(i):
            for xi in range(2):
                g[p, xi, chunk(i)] = nn(tr[chunk(i)], values[xi])

        each(3, body)

    turn_rows(gm)
    weight_grad(2, act)
    for copy in sent:
        copy.wait_send()
    sent.clear()
    first(2)
    go_home(0)

    def turn_back(i):
        rows = chunk(i)
        gb = gm[rows]
        part = None
        for xi in range(2):
            gpre = (nn(gb, half_of(2, xi, 0, 768)) * g[1, xi, rows]).astype(BF)
            gp[xi, rows] = gpre
            add(11 + xi, colsum(gpre.astype(F32)))
            piece = nt(gpre, half_of(1, xi, 0, 768))
            part = piece if part is None else part + piece
        x3[rows] = part
        core(2, x3, i).start()

    each(3, turn_back)

    turn_rows(n2_s)
    weight_grad(1, gp)
    first(1)
    second(2)

    def mid_back(i):
        rows = chunk(i)
        core(2, x3, i).wait()
        grad_h = x3[rows] + recv[0, rows]
        normed, inverse = normalize_rows(smid[rows])
        add(1, colsum(grad_h * normed))
        add(3, colsum(grad_h))
        grad_mid = gy[rows] + norm_back(grad_h * vec[3:4], normed, inverse)
        gy[rows] = grad_mid
        gb = grad_mid.astype(BF)
        gm[rows] = gb
        add(4, colsum(gb.astype(F32)))
        for xi in range(2):
            gatt = nn(gb, half_of(0, xi, 512, 768)).astype(BF)
            for j in range(3):
                piece = gatt[:, 64 + 64 * j : 128 + 64 * j]
                n2_s[rows, 384 * xi + 128 * j : 384 * xi + 128 * j + 128] = jnp.concatenate([jnp.zeros((R, 64), BF), piece], axis=1)

    each(3, mid_back)

    def attend_grad(h, block):
        part = block // 2
        keys, rows = slice(part * 512, part * 512 + 512), slice(block * R, block * R + R)
        kvs, q, go = kv[h, keys], q_s[h, rows], n2_s[rows, lanes(h)]
        st = nt(kvs, q) * LOG_SCALE + wide(mask[keys], R)
        pt = jnp.exp(st - lse[h, :, rows])
        dpt = nt(kvs, go)
        delta = colsum(pt * dpt)
        dst = (pt * (dpt - delta)).astype(BF)
        dqt = nn(kvt[h, 0:64, keys], dst) * LOG_SCALE
        q_s[h, rows, 0:64] = dqt.T.astype(BF)
        return nn(dst, q) * LOG_SCALE + nn(pt.astype(BF), go)

    def grad_c(h):
        both = attend_grad(h, 2)
        recv[0, 512:768, lanes(h)] = both[0:256]
        dkx[h] = both[256:512].astype(BF)

    def grad_a(h):
        recv[0, 0:512, lanes(h)] = attend_grad(h, 0) + attend_grad(h, 1)

    each(6, grad_c)
    dk_copy = remote(dkx, dkr, s_x.at[1], r_x.at[1], dp, across)
    dk_copy.start()
    second(1)
    third(2)
    each(6, grad_a)
    turn_rows(gm)

    def out_grad(i):
        for xi in range(2):
            g[0, xi, chunk(i), 512:768] = nn(tr[chunk(i)], att[xi])

    each(3, out_grad)
    third(1)
    dk_copy.wait()

    def join(h):
        recv[0, 512:768, lanes(h)] = recv[0, 512:768, lanes(h)] + dkr[h].astype(F32)

    each(6, join)

    def project_back(i):
        rows = chunk(i)
        part = None
        for xi in range(2):
            pieces = []
            for j in range(3):
                at = 384 * xi + 128 * j
                pieces += [q_s[3 * xi + j, rows, 0:64], recv[0, rows, at : at + 128].astype(BF)]
            gr = jnp.concatenate(pieces + [jnp.zeros((R, 64), BF)], axis=1)
            gp[xi, rows, 0:640] = gr
            add(9 + xi if xi == 0 else 13, colsum(gr.astype(F32)))
            piece = nt(gr, half_of(0, xi, 0, 640))
            part = piece if part is None else part + piece
        x3[rows] = part
        core(3, x3, i).start()

    each(3, project_back)
    turn_rows(nin)

    def qkv_grad(i):
        rows = chunk(i)
        for xi in range(2):
            h = nn(tr[rows], gp[xi, :, 0:640])
            g[0, xi, rows, 0:512] = h[:, 0:512]
            g[0, xi, rows, 512:640] = g[0, xi, rows, 512:640] + h[:, 512:640]

    each(3, qkv_grad)
    first(0)

    def in_back(i):
        rows = chunk(i)
        core(3, x3, i).wait()
        grad_h = x3[rows] + recv[1, rows]
        normed, inverse = normalize_rows(stream(i))
        add(0, colsum(grad_h * normed))
        add(2, colsum(grad_h))
        grad_in = gy[rows] + norm_back(grad_h * vec[2:3], normed, inverse)
        total = colsum(grad_in)
        add(6, jnp.where(i < 2, total, 0.0))
        add(7, jnp.where(i < 2, 0.0, total))
        out_b = grad_in.astype(BF)
        pack_out(1, i, out_b)

    each(3, in_back)
    second(0)

    msg[...] = jnp.zeros(msg.shape, F32)
    loss_row = sums[8:9, 0:128]
    for k in range(1, 6):
        loss_row = loss_row + sums[8:9, 128 * k : 128 * k + 128]
    for xi in range(2):
        bias_sums = sums[9:10] if xi == 0 else sums[13:14]
        hidden = sums[11 + xi : 12 + xi]
        for d in range(DP):
            at, owner = 96 * d + 48 * xi, 8 * xi + d
            msg[owner, 0:8, 0:24] = jnp.where(c == 0, sums[0:8, at : at + 24], sums[0:8, at + 24 : at + 48])
            msg[owner, 8:9] = loss_row
            for j in range(3):
                for kind in range(2):
                    low = 192 * j + 128 * kind
                    msg[owner, 9 + 3 * kind + j : 10 + 3 * kind + j, 0:64] = bias_sums[:, low : low + 64]
            for k in range(6):
                msg[owner, 16 + k : 17 + k] = hidden[:, 128 * k : 128 * k + 128]
    pltpu.make_async_copy(msg.at[mine], msgs.at[mine], r_msg.at[mine]).start()
    for k in range(DP):
        for xr in range(2):
            if k or xr:
                d, xx = lax.rem(dp + k, DP), lax.rem(x + xr, 2)
                go(remote(msg.at[xx * DP + d], msgs.at[mine], s_msg.at[2 * k + xr], r_msg.at[mine], d, 2 * xx + c))
    go_home(1)
    third(0)
    last(2)
    last(1)
    last(0)
    for j in range(16):
        landed(msgs.at[j], r_msg.at[j], s_msg.at[0], dp, mp)
    for n in range(2):
        for m in range(3):
            for j in range(DP):
                landed(back.at[n, m, j], r_yg.at[n, m, j], s_yg.at[n, 0], dp, mp)
    for copy in sent:
        copy.wait_send()

    @pl.when(y == x)
    def _():
        for k in range(1, DP):
            token_copy(8 + k, lax.rem(dp + k, DP), 2, 8 + z).wait_send()

    @pl.when(y != x)
    def _():
        remote(ts.at[2, dp], tea.at[mp, 8 + z], s_tea.at[16], r_tea.at[x, 8 + z], dp, 2 * y + c).wait_send()
        home_copy(0).wait_send()
        home_copy(1).wait_send()


def step(xs, ts, wsh, small, mask, factor):
    dma = pltpu.SemaphoreType.DMA
    vm = pltpu.VMEM
    block = (ROWS, 768)
    return pl.pallas_call(
        step_kernel,
        name="step",
        out_shape=(
            jax.ShapeDtypeStruct((3, ROWS, 768), F32),
            jax.ShapeDtypeStruct((16, 24, 128), F32),
            jax.ShapeDtypeStruct((2, 3, DP, 96, 128), BF),
        ),
        in_specs=[pl.BlockSpec(memory_space=pl.ANY)] * 4 + [VM] * 2,
        out_specs=(VM, VM, pl.BlockSpec(memory_space=pl.ANY)),
        scratch_shapes=[
            vm((3, 2, T, 768), F32), vm((2, 4, 12, 96, 128), BF), vm((16, 768), F32), vm((16, 24, 128), F32),
            vm((4,) + block, BF), vm((3, 4) + block, BF), vm((3, 2, 4) + block, BF), vm((3, 3) + block, BF),
            vm((1024, 768), BF), vm((4, 12, 96, 128), BF), vm((3, 16) + block, BF),
            vm((4, DP, 48, 128), BF), vm((32, 768), F32), vm((16, 768), F32),
            vm((T, 768), BF), vm((6, T, 128), BF), vm((6, 1024, 128), BF), vm((6, 128, 1024), BF),
            vm((2, R, T), BF), vm((2, T, R), BF), vm((T, 768), BF), vm((2, T, 768), BF),
            vm((T, 768), F32), vm((T, 768), BF), vm((2, T, 768), BF), vm((T, 768), F32),
            vm((2, T, 768), F32), vm((768, T), BF), vm((6, R, 128), BF), vm((6, R, 128), BF),
            vm((6, 1, T), F32),
            dma((4, 3)), dma((4, 3)), dma((2,)), dma((2,)),
            dma((16,)), dma((12,)), dma((24,)), dma((2, 12)), dma((16,)), dma((16,)),
            dma((3, 15)), dma((3, 16)), dma((6,)), dma((6,)),
            dma((16,)), dma((16,)), dma((2, 24)), dma((2, 3, DP)), dma((3, 4)), dma((3, 4)),
            dma((3, 2, 4)), dma((3, 2, 4)), dma((3, 3)), dma((3, 3)),
        ],
        compiler_params=pltpu.CompilerParams(
            collective_id=3, has_side_effects=True, vmem_limit_bytes=VMEM_LIMIT
        ),
    )(xs, ts, wsh, small, mask, factor)


def send_slot(perm, m, d, dp):
    index = 0
    for k in range(DP):
        v = perm[m, DP * d + k]
        index = index + jnp.where(lax.shift_right_logical(v, 3) == dp, v & 7, 0)
    return index


def one_hot(timestep):
    steps = lax.broadcasted_iota(jnp.int32, (1, 1000), 1)
    return jnp.concatenate(
        [jnp.where(steps == timestep[n], 1.0, 0.0).astype(F32) for n in range(24)], axis=0
    )


def valid_count(lengths):
    count = lengths[0]
    for n in range(1, 24):
        count = count + lengths[n]
    return count


def pack_kernel(
    perm, lengths, timestep, xin, tin, table, gains, shifts, qvb, inb, w_qkv, w_out, w_in, w_back,
    xs, ts, wsh, small, mask, factor,
    rows, lines, sem,
):
    dp, mp, x, c = place()
    slots = [[send_slot(perm, m, d, dp) for d in range(DP)] for m in range(3)]
    copies = []
    for m in range(3):
        for d in range(DP):
            source = xin.at[m, pl.ds(pl.multiple_of(64 * slots[m][d], 64), 64)]
            copies.append(pltpu.make_async_copy(source, xs.at[m, d], sem.at[m, d]))
            copies[-1].start()
    for m in range(3):
        rows[m] = tin[m].T
    for m in range(3):
        for d in range(DP):
            v = rows[m, pl.ds(pl.multiple_of(64 * slots[m][d], 64), 64)]
            ts[m, d, 0:64] = v[:, 0:128]
            ts[m, d, 64:96] = jnp.concatenate([v[0:32, 128:192], v[32:64, 128:192]], axis=1)
    wsh[0, :, 0:576] = w_qkv[...]
    wsh[0, :, 576:768] = w_out[...].T
    wsh[1] = w_in[...]
    wsh[2] = w_back[...]

    lane = lax.broadcasted_iota(jnp.int32, (8, 128), 1)
    lines[...] = jnp.zeros(lines.shape, F32)
    lines[0:2, 0:24] = gains[...].astype(F32)
    lines[2:6, 0:24] = shifts[...].astype(F32)
    lines[6:30, 0:24] = nt(one_hot(timestep).astype(BF), table[...])
    spread = jnp.concatenate([inb[...].astype(F32)] * 8, axis=1)
    lines[32:38] = jnp.where(lax.shift_right_logical(lane[0:6], 4) == dp, spread, 0.0)
    for j in range(3):
        both = jnp.concatenate([qvb[j].astype(F32)] * 8, axis=1)
        both = jnp.where(lax.shift_right_logical(lane[0:2, 0:64], 3) == dp, both, 0.0)
        lines[40 + j : 41 + j, 0:64] = both[0:1]
        lines[43 + j : 44 + j, 0:64] = both[1:2]
    small[...] = lines[...].astype(BF)

    inside = lax.broadcasted_iota(jnp.int32, (64, 128), 0)
    micro_lengths = lengths[x * DP + dp], lengths[2 * DP + dp]
    for j in range(16):
        own = j < 8
        m = x if own else 2
        wanted = j if own else 2 * (j % 4) + (x if j < 12 else 1 - x)
        at = 0
        for p in range(DP):
            v = perm[m, DP * dp + p]
            at = at + jnp.where(lax.shift_right_logical(v, 3) == wanted, p, 0)
        live = inside + 64 * at < micro_lengths[0 if own else 1]
        mask[64 * j : 64 * j + 64] = jnp.where(live, 0.0, -1e30).astype(F32)
    count = jnp.full((8, 128), valid_count(lengths), jnp.int32).astype(F32)
    factor[...] = (3.0 * DP * 512) / count
    for copy in copies:
        copy.wait()


def pack(*arguments):
    vm = pltpu.VMEM
    smem = pl.BlockSpec(memory_space=pltpu.SMEM)
    return pl.pallas_call(
        pack_kernel,
        name="pack",
        out_shape=(
            jax.ShapeDtypeStruct((3, DP, 64, 768), BF),
            jax.ShapeDtypeStruct((3, DP, 96, 128), BF),
            jax.ShapeDtypeStruct((3, ROWS, 768), BF),
            jax.ShapeDtypeStruct((48, 128), BF),
            jax.ShapeDtypeStruct((1024, 128), F32),
            jax.ShapeDtypeStruct((8, 128), F32),
        ),
        in_specs=[smem] * 3 + [pl.BlockSpec(memory_space=pl.ANY)] + [VM] * 10,
        out_specs=(VM,) * 6,
        scratch_shapes=[vm((3, 512, 192), BF), vm((48, 128), F32), pltpu.SemaphoreType.DMA((3, DP))],
        compiler_params=pltpu.CompilerParams(vmem_limit_bytes=VMEM_LIMIT),
    )(*arguments)


def unpack_kernel(
    perm, lengths, timestep, gs, msgs, home,
    y_out, loss, grad_x, table, gains, shifts, g_qkv, g_qvb, g_out, g_in, g_inb, g_back,
    rows,
):
    dp, mp, x, c = place()
    for m in range(3):
        slots = [send_slot(perm, m, d, dp) for d in range(DP)]
        for n, target in ((0, y_out), (1, grad_x)):
            for d in range(DP):
                low = home[n, m, d, 64:96]
                value = jnp.concatenate(
                    [home[n, m, d, 0:64], jnp.concatenate([low[:, 0:64], low[:, 64:128]], axis=0)], axis=1
                )
                rows[n, pl.ds(pl.multiple_of(64 * slots[d], 64), 64)] = value
            target[m] = rows[n].T
    total = msgs[0]
    for j in range(1, 16):
        total = total + msgs[j]
    count = jnp.full((1, 1), valid_count(lengths), jnp.int32).astype(F32)
    loss[...] = jnp.sum(total[8:9], axis=1, keepdims=True) / (count * 768.0)
    gains[...] = total[0:2, 0:24]
    shifts[...] = total[2:6, 0:24]
    turned = pltpu.roll(total, lax.rem(128 - 8 * dp, 128), 1)
    for j in range(3):
        for kind in range(2):
            at = 9 + 3 * kind + j
            g_qvb[j, kind : kind + 1] = turned[at : at + 1, 0:8]
    g_inb[...] = pltpu.roll(total, lax.rem(128 - 16 * dp, 128), 1)[16:22, 0:16]
    lines = [msgs[j, 6:7] for j in range(16)] + [msgs[d, 7:8] + msgs[DP + d, 7:8] for d in range(DP)]
    columns = jnp.concatenate(lines, axis=0).T[0:24]
    chosen = one_hot(timestep)
    result = columns[:, 0:1] * chosen[0:1]
    for n in range(1, 24):
        result = result + columns[:, n : n + 1] * chosen[n : n + 1]
    table[...] = result
    g_qkv[...] = gs[0, :, 0:576]
    g_out[...] = gs[0, :, 576:768].T
    g_in[...] = gs[1]
    g_back[...] = gs[2]


def unpack(*arguments):
    smem = pl.BlockSpec(memory_space=pltpu.SMEM)
    shapes = [
        ((3, 192, 512), BF), ((1, 1), F32), ((3, 192, 512), BF), ((24, 1000), F32), ((2, 24), F32),
        ((4, 24), F32), ((96, 576), F32), ((3, 2, 8), F32), ((192, 96), F32), ((96, 768), F32),
        ((6, 16), F32), ((96, 768), F32),
    ]
    return pl.pallas_call(
        unpack_kernel,
        name="unpack",
        out_shape=tuple(jax.ShapeDtypeStruct(*shape) for shape in shapes),
        in_specs=[smem] * 3 + [VM] * 3,
        out_specs=(VM,) * 12,
        scratch_shapes=[pltpu.VMEM((2, 512, 192), BF)],
        compiler_params=pltpu.CompilerParams(vmem_limit_bytes=VMEM_LIMIT),
    )(*arguments)


def per_device_compact(
    input_stream, teacher, timestep, lengths, block_perm, table, norm_gains, shifts,
    w_qkv, qv_bias, w_out, w_in, in_bias, w_back,
):
    packed = pack(
        block_perm, lengths, timestep, input_stream, teacher.transpose(0, 2, 1), table.T, norm_gains, shifts,
        qv_bias.transpose(1, 0, 2), in_bias, w_qkv, w_out, w_in, w_back.T,
    )
    outs = list(unpack(block_perm, lengths, timestep, *step(*packed)))
    outs[0], outs[2] = outs[0].transpose(0, 2, 1), outs[2].transpose(0, 2, 1)
    outs[1], outs[3] = outs[1].reshape(()), outs[3].T
    outs[7], outs[11] = outs[7].transpose(1, 0, 2), outs[11].T
    return tuple(outs)


def solution(mesh):
    compact = mesh.shape["dp"] == 8 and mesh.shape["mp"] == 4
    return jax.shard_map(
        per_device_compact if compact else per_device,
        mesh=mesh,
        in_specs=(
            P(None, "dp", None),
            P(None, "dp", "mp"),
            P(),
            P(),
            P(),
            P(None, ("dp", "mp")),
            P(None, ("dp", "mp")),
            P(None, ("dp", "mp")),
            P("dp", "mp"),
            P(None, "mp", "dp"),
            P("mp", "dp"),
            P("dp", "mp"),
            P("mp", "dp"),
            P("mp", "dp"),
        ),
        out_specs=(
            P(None, "dp", "mp"),
            P(),
            P(None, "dp", "mp"),
            P(None, ("dp", "mp")),
            P(None, ("dp", "mp")),
            P(None, ("dp", "mp")),
            P("dp", "mp"),
            P(None, "mp", "dp"),
            P("mp", "dp"),
            P("dp", "mp"),
            P("mp", "dp"),
            P("mp", "dp"),
        ),
        check_vma=False,
    )
```

```python
import functools
import math

import jax
import jax.numpy as jnp
from jax import lax
from jax.experimental import pallas as pl
from jax.experimental.pallas import tpu as pltpu
from jax.sharding import PartitionSpec as P

H = 12
DH = 64


epsilon = 1e-05


def normalize_rows(stream):
    centered = stream - jnp.mean(stream, axis=-1, keepdims=True)
    inverse = lax.rsqrt(jnp.mean(centered * centered, axis=-1, keepdims=True) + epsilon)
    return (centered * inverse, inverse)


def column_part(array, start, width):
    return lax.dynamic_slice_in_dim(array, start, width, array.ndim - 1)


def fetch_weights(w_qkv, w_in, w_out, w_back, qv_bias, in_bias):
    return (
        lax.all_gather(w_qkv, "dp", axis=0, tiled=True),
        lax.all_gather(w_in, "dp", axis=0, tiled=True),
        lax.all_gather(w_out, "dp", axis=1, tiled=True),
        lax.all_gather(w_back, "dp", axis=1, tiled=True),
        lax.all_gather(qv_bias, "dp", axis=2, tiled=True),
        lax.all_gather(in_bias, "dp", axis=1, tiled=True),
    )


def invert_map(targets, size):
    ranks = jnp.arange(size, dtype=jnp.int32)
    return jnp.sum(jnp.where(targets[None, :] == ranks[:, None], ranks[None, :], 0), axis=1)


def masked_scores(queries, keys_all, is_live, score_scale):
    scores = (
        jnp.einsum("qhe,khe->hqk", queries, keys_all, preferred_element_type=jnp.float32)
        * score_scale
    )
    return jnp.where(is_live[None, None, :], scores, -1e30)


def attend_rows(keys_all, values, is_live, score_scale, queries):
    scores = masked_scores(queries, keys_all, is_live, score_scale)
    row_top = jnp.max(scores, axis=-1, keepdims=True)
    exponent = jnp.exp(scores - row_top)
    row_total = jnp.sum(exponent, axis=-1, keepdims=True)
    weights_p = (exponent / row_total).astype(jnp.bfloat16)
    mixed = jnp.einsum("hqk,khe->qhe", weights_p, values, preferred_element_type=jnp.float32)
    return (mixed, (row_top + jnp.log(row_total))[..., 0])


def attend_back(keys_all, values, is_live, score_scale, carry, inputs):
    queries, grad_rows, log_total = inputs
    grad_keys, grad_values = carry
    scores = masked_scores(queries, keys_all, is_live, score_scale)
    probabilities = jnp.exp(scores - log_total[..., None])
    grad_probs = jnp.einsum("qhe,khe->hqk", grad_rows, values, preferred_element_type=jnp.float32)
    row_delta = jnp.sum(probabilities * grad_probs, axis=-1, keepdims=True)
    grad_scores = (probabilities * (grad_probs - row_delta)).astype(jnp.bfloat16)
    grad_queries = (
        jnp.einsum("hqk,khe->qhe", grad_scores, keys_all, preferred_element_type=jnp.float32)
        * score_scale
    )
    grad_keys = (
        grad_keys
        + jnp.einsum("hqk,qhe->khe", grad_scores, queries, preferred_element_type=jnp.float32)
        * score_scale
    )
    grad_values = grad_values + jnp.einsum(
        "hqk,qhe->khe",
        probabilities.astype(jnp.bfloat16),
        grad_rows,
        preferred_element_type=jnp.float32,
    )
    return ((grad_keys, grad_values), grad_queries)


def norm_sums(partial_value, normed, gain_full, mp_count):
    weighted = partial_value * gain_full
    sums = jnp.stack([jnp.sum(weighted, axis=1), jnp.sum(weighted * normed, axis=1)], axis=1)
    return jnp.tile(sums, (1, mp_count))


def norm_input_grad(grad_part, gain_part, normed_part, inverse, sums, width):
    scaled = grad_part * gain_part
    return inverse * (scaled - sums[:, 0:1] / width - normed_part * sums[:, 1:2] / width)


def per_device(
    input_stream,
    teacher,
    timestep,
    lengths,
    block_perm,
    table,
    norm_gains,
    shifts,
    w_qkv,
    qv_bias,
    w_out,
    w_in,
    in_bias,
    w_back,
):
    dp_count = lax.axis_size("dp")
    mp_count = lax.axis_size("mp")
    dp_rank = lax.axis_index("dp")
    mp_rank = lax.axis_index("mp")
    micro_count, seq_len, width = input_stream.shape
    part_width = teacher.shape[2]
    block_rows = seq_len // dp_count
    heads_here = H // mp_count
    score_scale = 1.0 / math.sqrt(DH)
    col_start = mp_rank * part_width
    row_block = min(512, seq_len)
    block_count = seq_len // row_block
    valid_count = jnp.sum(lengths).astype(jnp.float32)
    loss_factor = micro_count * dp_count * seq_len / valid_count
    chosen = jnp.take(table, timestep, axis=0)
    gains_full, shifts_full, table_rows = (
        lax.all_gather(norm_gains, ("dp", "mp"), axis=1, tiled=True),
        lax.all_gather(shifts, ("dp", "mp"), axis=1, tiled=True),
        lax.all_gather(chosen, ("dp", "mp"), axis=1, tiled=True),
    )
    gains_full = gains_full.astype(jnp.float32)
    shifts_full = shifts_full.astype(jnp.float32)
    gain_parts = column_part(gains_full, col_start, part_width)
    acc_qkv = jnp.zeros((width, heads_here * 3 * DH), jnp.float32)
    acc_in = jnp.zeros((width, w_in.shape[1]), jnp.float32)
    acc_out = jnp.zeros((heads_here * DH, width), jnp.float32)
    acc_back = jnp.zeros((w_back.shape[0], width), jnp.float32)
    acc_qv = jnp.zeros((2, heads_here, DH), jnp.float32)
    acc_in_bias = jnp.zeros((w_in.shape[1],), jnp.float32)
    acc_gains = jnp.zeros((2, part_width), jnp.float32)
    acc_shifts = jnp.zeros((4, part_width), jnp.float32)
    loss_part = jnp.zeros((), jnp.float32)
    table_sums = []
    outs_y = []
    outs_grad = []
    for micro_index in range(micro_count):
        forward_set = fetch_weights(w_qkv, w_in, w_out, w_back, qv_bias, in_bias)
        proj_qkv, proj_in, proj_out, proj_back, bias_qv, bias_in = forward_set
        bias_qv = bias_qv.astype(jnp.float32)
        bias_in = bias_in.reshape(-1).astype(jnp.float32)
        block_order = block_perm[micro_index].reshape(dp_count, dp_count)
        source = block_order // dp_count
        local_index = block_order % dp_count
        send_index = jnp.sum(jnp.where(source == dp_rank, local_index, 0), axis=1)
        x_blocks = input_stream[micro_index].reshape(dp_count, block_rows, width)
        t_blocks = teacher[micro_index].reshape(dp_count, block_rows, part_width)
        got_x, got_t = (
            lax.all_to_all(
                jnp.take(x_blocks, send_index, axis=0),
                "dp",
                split_axis=0,
                concat_axis=0,
                tiled=True,
            ),
            lax.all_to_all(
                jnp.take(t_blocks, send_index, axis=0),
                "dp",
                split_axis=0,
                concat_axis=0,
                tiled=True,
            ),
        )
        my_source = lax.dynamic_index_in_dim(source, dp_rank, 0, keepdims=False)
        tokens = jnp.take(got_x, my_source, axis=0).reshape(seq_len, width).astype(jnp.float32)
        target = jnp.take(got_t, my_source, axis=0).reshape(seq_len, part_width).astype(jnp.float32)
        seq_index = micro_index * dp_count + dp_rank
        length = lax.dynamic_index_in_dim(lengths, seq_index, 0, keepdims=False)
        table_row = lax.dynamic_index_in_dim(table_rows, seq_index, 0, keepdims=False).astype(
            jnp.float32
        )
        is_live = jnp.arange(seq_len, dtype=jnp.int32) < length
        stream_in = tokens + table_row[None, :]
        normed1, inverse1 = normalize_rows(stream_in)
        normed_in = (normed1 * gains_full[0] + shifts_full[0]).astype(jnp.bfloat16)
        projected = jnp.dot(normed_in, proj_qkv, preferred_element_type=jnp.float32).reshape(
            seq_len, heads_here, 3, DH
        )
        queries = (projected[:, :, 0] + bias_qv[0]).astype(jnp.bfloat16)
        keys_all = projected[:, :, 1].astype(jnp.bfloat16)
        values = (projected[:, :, 2] + bias_qv[1]).astype(jnp.bfloat16)
        query_blocks = queries.reshape(block_count, row_block, heads_here, DH)
        mixed, log_total = lax.map(
            functools.partial(attend_rows, keys_all, values, is_live, score_scale), query_blocks
        )
        attended = mixed.reshape(seq_len, heads_here * DH).astype(jnp.bfloat16)
        attn_part = jnp.dot(attended, proj_out, preferred_element_type=jnp.float32)
        branch_attn = lax.psum_scatter(
            attn_part, "mp", scatter_dimension=1, tiled=True
        ) + column_part(shifts_full[2], col_start, part_width)
        mid_part = column_part(stream_in, col_start, part_width) + branch_attn
        stream_mid = lax.all_gather(mid_part, "mp", axis=1, tiled=True)
        normed2, inverse2 = normalize_rows(stream_mid)
        normed_mid = (normed2 * gains_full[1] + shifts_full[1]).astype(jnp.bfloat16)
        pre_act = jnp.dot(normed_mid, proj_in, preferred_element_type=jnp.float32) + bias_in
        activation = jax.nn.gelu(pre_act, approximate=True).astype(jnp.bfloat16)
        mlp_part = jnp.dot(activation, proj_back, preferred_element_type=jnp.float32)
        mlp_out = lax.psum_scatter(mlp_part, "mp", scatter_dimension=1, tiled=True) + column_part(
            shifts_full[3], col_start, part_width
        )
        out_part = mid_part + mlp_out
        residual_err = jnp.where(is_live[:, None], out_part - target, 0.0)
        loss_part = loss_part + jnp.sum(residual_err * residual_err)
        grad_y = residual_err * loss_factor
        grad_mlp = grad_y.astype(jnp.bfloat16)
        acc_shifts = acc_shifts.at[3].add(jnp.sum(grad_mlp.astype(jnp.float32), axis=0))
        grad_mlp_full = lax.all_gather(grad_mlp, "mp", axis=1, tiled=True)
        back_set = fetch_weights(w_qkv, w_in, w_out, w_back, qv_bias, in_bias)
        back_qkv, back_in, back_out, back_back = (
            back_set[0],
            back_set[1],
            back_set[2],
            back_set[3],
        )
        acc_back = acc_back + jnp.einsum(
            "tf,td->fd", activation, grad_mlp_full, preferred_element_type=jnp.float32
        )
        grad_act = jnp.einsum(
            "td,fd->tf", grad_mlp_full, back_back, preferred_element_type=jnp.float32
        )
        gelu_value, gelu_pull = jax.vjp(lambda inner: jax.nn.gelu(inner, approximate=True), pre_act)
        grad_pre = gelu_pull(grad_act)[0].astype(jnp.bfloat16)
        acc_in_bias = acc_in_bias + jnp.sum(grad_pre.astype(jnp.float32), axis=0)
        acc_in = acc_in + jnp.einsum(
            "td,tf->df", normed_mid, grad_pre, preferred_element_type=jnp.float32
        )
        partial2 = jnp.einsum("tf,df->td", grad_pre, back_in, preferred_element_type=jnp.float32)
        grad_h2, sums2 = (
            lax.psum_scatter(partial2, "mp", scatter_dimension=1, tiled=True),
            lax.psum_scatter(
                norm_sums(partial2, normed2, gains_full[1], mp_count),
                "mp",
                scatter_dimension=1,
                tiled=True,
            ),
        )
        normed2_part = column_part(normed2, col_start, part_width)
        acc_gains = acc_gains.at[1].add(jnp.sum(grad_h2 * normed2_part, axis=0))
        acc_shifts = acc_shifts.at[1].add(jnp.sum(grad_h2, axis=0))
        grad_mid = grad_y + norm_input_grad(
            grad_h2, gain_parts[1], normed2_part, inverse2, sums2, width
        )
        grad_branch = grad_mid.astype(jnp.bfloat16)
        acc_shifts = acc_shifts.at[2].add(jnp.sum(grad_branch.astype(jnp.float32), axis=0))
        grad_branch_full = lax.all_gather(grad_branch, "mp", axis=1, tiled=True)
        acc_out = acc_out + jnp.einsum(
            "tc,td->cd", attended, grad_branch_full, preferred_element_type=jnp.float32
        )
        grad_att = jnp.einsum(
            "td,cd->tc", grad_branch_full, back_out, preferred_element_type=jnp.float32
        ).astype(jnp.bfloat16)
        grad_blocks = grad_att.reshape(block_count, row_block, heads_here, DH)
        zero_heads = jnp.zeros((seq_len, heads_here, DH), jnp.float32)
        (grad_keys, grad_values), grad_queries = lax.scan(
            functools.partial(attend_back, keys_all, values, is_live, score_scale),
            (zero_heads, zero_heads),
            (query_blocks, grad_blocks, log_total),
        )
        grad_queries = grad_queries.reshape(seq_len, heads_here, DH).astype(jnp.bfloat16)
        grad_keys = grad_keys.astype(jnp.bfloat16)
        grad_values = grad_values.astype(jnp.bfloat16)
        acc_qv = acc_qv + jnp.stack(
            [
                jnp.sum(grad_queries.astype(jnp.float32), axis=0),
                jnp.sum(grad_values.astype(jnp.float32), axis=0),
            ]
        )
        grad_qkv_rows = jnp.stack([grad_queries, grad_keys, grad_values], axis=2).reshape(
            seq_len, heads_here * 3 * DH
        )
        acc_qkv = acc_qkv + jnp.einsum(
            "td,tc->dc", normed_in, grad_qkv_rows, preferred_element_type=jnp.float32
        )
        partial1 = jnp.einsum(
            "tc,dc->td", grad_qkv_rows, back_qkv, preferred_element_type=jnp.float32
        )
        grad_h1, sums1 = (
            lax.psum_scatter(partial1, "mp", scatter_dimension=1, tiled=True),
            lax.psum_scatter(
                norm_sums(partial1, normed1, gains_full[0], mp_count),
                "mp",
                scatter_dimension=1,
                tiled=True,
            ),
        )
        normed1_part = column_part(normed1, col_start, part_width)
        acc_gains = acc_gains.at[0].add(jnp.sum(grad_h1 * normed1_part, axis=0))
        acc_shifts = acc_shifts.at[0].add(jnp.sum(grad_h1, axis=0))
        grad_in_stream = grad_mid + norm_input_grad(
            grad_h1, gain_parts[0], normed1_part, inverse1, sums1, width
        )
        table_sums.append(jnp.sum(grad_in_stream, axis=0))
        back_order = invert_map(my_source, dp_count)
        out_blocks = jnp.take(
            out_part.astype(jnp.bfloat16).reshape(dp_count, block_rows, part_width),
            back_order,
            axis=0,
        )
        grad_send = jnp.take(
            grad_in_stream.astype(jnp.bfloat16).reshape(dp_count, block_rows, part_width),
            back_order,
            axis=0,
        )
        home_out, home_grad = (
            lax.all_to_all(out_blocks, "dp", split_axis=0, concat_axis=0, tiled=True),
            lax.all_to_all(grad_send, "dp", split_axis=0, concat_axis=0, tiled=True),
        )
        home_place = invert_map(send_index, dp_count)
        outs_y.append(jnp.take(home_out, home_place, axis=0).reshape(seq_len, part_width))
        outs_grad.append(jnp.take(home_grad, home_place, axis=0).reshape(seq_len, part_width))
    row_sums = jnp.zeros((micro_count, width), jnp.float32)
    row_sums = lax.dynamic_update_slice_in_dim(row_sums, jnp.stack(table_sums), col_start, 1)
    my_steps = jnp.take(timestep, jnp.arange(micro_count, dtype=jnp.int32) * dp_count + dp_rank)
    step_onehot = (
        jnp.arange(table.shape[0], dtype=jnp.int32)[:, None] == my_steps[None, :]
    ).astype(jnp.float32)
    table_grad = jnp.dot(
        step_onehot, row_sums, precision=lax.Precision.HIGHEST, preferred_element_type=jnp.float32
    )
    gains_grad = lax.dynamic_update_slice_in_dim(
        jnp.zeros((2, width), jnp.float32), acc_gains, col_start, 1
    )
    shifts_grad = lax.dynamic_update_slice_in_dim(
        jnp.zeros((4, width), jnp.float32), acc_shifts, col_start, 1
    )
    loss_row = jnp.full((1, dp_count * mp_count), loss_part, jnp.float32)
    grad_table, grad_norm_gains, grad_shifts, loss_cell = (
        lax.psum_scatter(table_grad, ("dp", "mp"), scatter_dimension=1, tiled=True),
        lax.psum_scatter(gains_grad, ("dp", "mp"), scatter_dimension=1, tiled=True),
        lax.psum_scatter(shifts_grad, ("dp", "mp"), scatter_dimension=1, tiled=True),
        lax.psum_scatter(loss_row, ("dp", "mp"), scatter_dimension=1, tiled=True),
    )
    loss = loss_cell[0, 0] / (valid_count * width)
    grad_qkv, grad_in, grad_out, grad_back, grad_qv_bias, grad_in_bias = (
        lax.psum_scatter(acc_qkv, "dp", scatter_dimension=0, tiled=True),
        lax.psum_scatter(acc_in, "dp", scatter_dimension=0, tiled=True),
        lax.psum_scatter(acc_out, "dp", scatter_dimension=1, tiled=True),
        lax.psum_scatter(acc_back, "dp", scatter_dimension=1, tiled=True),
        lax.psum_scatter(acc_qv, "dp", scatter_dimension=2, tiled=True),
        lax.psum_scatter(acc_in_bias.reshape(-1, 128), "dp", scatter_dimension=1, tiled=True),
    )
    y_out = jnp.stack(outs_y)
    grad_x = jnp.stack(outs_grad)
    return (
        y_out,
        loss,
        grad_x,
        grad_table,
        grad_norm_gains,
        grad_shifts,
        grad_qkv,
        grad_qv_bias,
        grad_out,
        grad_in,
        grad_in_bias,
        grad_back,
    )


MESH = pl.DeviceIdType.MESH
BF = jnp.bfloat16
F32 = jnp.float32
VM = pl.BlockSpec(memory_space=pltpu.VMEM)
DP = 8
ROWS = 96
VMEM_LIMIT = 64 * 1024 * 1024 - 65536


def place():
    dp, mp = lax.axis_index("dp"), lax.axis_index("mp")
    x, c = lax.div(mp, 2), lax.rem(mp, 2)
    return dp, mp, x, c


def remote(src, dst, send_sem, recv_sem, dp, mp):
    return pltpu.make_async_remote_copy(
        src_ref=src,
        dst_ref=dst,
        send_sem=send_sem,
        recv_sem=recv_sem,
        device_id=(dp, mp),
        device_id_type=MESH,
    )


def landed(dst, recv_sem, spare, dp, mp):
    remote(dst, dst, spare, recv_sem, dp, mp).wait_recv()


def greet_plane(dp, x, c):
    barrier = pltpu.get_barrier_semaphore()
    pl.semaphore_signal(barrier, inc=1, device_id=(dp, 2 * x + 1 - c), device_id_type=MESH)
    for k in range(DP):
        for xr in range(2):
            if k or xr:
                there = (lax.rem(dp + k, DP), 2 * lax.rem(x + xr, 2) + c)
                pl.semaphore_signal(barrier, inc=1, device_id=there, device_id_type=MESH)
    pl.semaphore_wait(barrier, 2 * DP)


def dot(a, b, dims):
    return lax.dot_general(a, b, (dims, ((), ())), preferred_element_type=F32)


T = 768
R = 256
LOG_SCALE = 0.125


def nn(a, b):
    return dot(a, b, ((1,), (0,)))


def nt(a, b):
    return dot(a, b, ((1,), (1,)))


def chunk(i):
    return pl.ds(pl.multiple_of(i * R, R), R)


def colsum(a):
    return jnp.sum(a, axis=0, keepdims=True)


def wide(column_tile, width):
    return jnp.concatenate([column_tile] * (width // 128), axis=1)


def gelu_pair(v):
    k = 0.7978845608028654
    v2 = v * v
    t = jnp.tanh(k * (v + 0.044715 * (v2 * v)))
    half = 0.5 * (1.0 + t)
    slope = half + 0.5 * v * ((1.0 - t * t) * (k * (1.0 + 0.134145 * v2)))
    return v * half, slope


def norm_back(g, normed, inverse):
    inner = jnp.mean(g * normed, axis=1, keepdims=True)
    return inverse * (g - jnp.mean(g, axis=1, keepdims=True) - normed * inner)


def step_kernel(
    xs, ts, wsh, small, mask, factor,
    gs, msgs, back,
    g, yg, sums, msg, s1, r1, r2, r3,
    tok, tea, w, smalls, vecs, vec, nin, q_s, kv, kvt, o_t, att, n2_s, act, gy, gm, gp, x3, recv, tr, dkx, dkr, lse,
    s_core, r_core, s_x, r_x,
    s_tok, r_tok, s_tea, r_tea, s_small, r_small, s_w, r_w, s_pair, r_pair,
    s_msg, r_msg, s_yg, r_yg, s_a, r_a, s_b, r_b, s_c, r_c,
):
    dp, mp, x, c = place()
    other, across = 2 * x + 1 - c, 2 * (1 - x) + c
    z, y = lax.div(dp, 2), lax.rem(dp, 2)
    mine = x * DP + dp
    half = pl.ds(pl.multiple_of(384 * c, 128), 384)
    beside = 2 * z + 1 - y
    greet_plane(dp, x, c)
    sent = []

    def go(copy):
        copy.start()
        sent.append(copy)

    def rows64(j):
        return pl.ds(pl.multiple_of(64 * j, 64), 64)

    def weights_z(p):
        pltpu.make_async_copy(wsh.at[p], w.at[p, mine], r_w.at[p, mine]).start()
        for k in range(1, 4):
            zz = lax.rem(z + k, 4)
            go(remote(wsh.at[p], w.at[p, mine], s_w.at[p, k - 1], r_w.at[p, mine], 2 * zz + y, mp))

    def weights_xy(p):
        go(remote(wsh.at[p], w.at[p, mine], s_w.at[p, 3], r_w.at[p, mine], dp, across))
        go(remote(wsh.at[p], w.at[p, mine], s_w.at[p, 4], r_w.at[p, mine], beside, mp))

    def spread(p):
        for k in (3, 2, 1):
            b = x * DP + 2 * lax.rem(z + k, 4) + y
            landed(w.at[p, b], r_w.at[p, b], s_w.at[p, 0], dp, mp)
            go(remote(w.at[p, b], w.at[p, b], s_w.at[p, 3 + 2 * k], r_w.at[p, b], dp, across))
            go(remote(w.at[p, b], w.at[p, b], s_w.at[p, 4 + 2 * k], r_w.at[p, b], beside, mp))

    def relay(p, steps=(3, 2, 1)):
        for n in steps:
            k = lax.rem(z + n, 4)
            bx, by = (1 - x) * DP + 2 * k + y, x * DP + 2 * k + 1 - y
            landed(w.at[p, bx], r_w.at[p, bx], s_w.at[p, 0], dp, mp)
            landed(w.at[p, by], r_w.at[p, by], s_w.at[p, 0], dp, mp)
            b = jnp.where(k < 2, bx, by)
            there = jnp.where(k < 2, beside, dp), jnp.where(k < 2, mp, across)
            go(remote(w.at[p, b], w.at[p, b], s_w.at[p, 11 + n], r_w.at[p, b], *there))

    def complete(p):
        landed(w.at[p, mine], r_w.at[p, mine], s_w.at[p, 0], dp, mp)
        for k in range(4):
            b = (1 - x) * DP + 2 * k + 1 - y
            landed(w.at[p, b], r_w.at[p, b], s_w.at[p, 0], dp, mp)

    weights_z(0)
    weights_xy(0)

    pltpu.make_async_copy(small, smalls.at[mp, dp], r_small.at[mine]).start()
    for k in range(DP):
        for xr in range(2):
            if k or xr:
                d, m = lax.rem(dp + k, DP), 2 * lax.rem(x + xr, 2) + c
                go(remote(small, smalls.at[mp, dp], s_small.at[2 * k + xr], r_small.at[mine], d, m))

    def token_copy(k, d, m_from, j):
        return remote(
            xs.at[m_from, d, :, half], tok.at[rows64(j), half], s_tok.at[k], r_tok.at[j], d, mp
        )

    weights_xy(1)
    weights_xy(2)
    pltpu.make_async_copy(xs.at[x, dp, :, half], tok.at[rows64(dp), half], r_tok.at[dp]).start()
    for k in range(1, DP):
        go(token_copy(k, lax.rem(dp + k, DP), x, dp))

    @pl.when(y == x)
    def _():
        pltpu.make_async_copy(
            xs.at[2, dp, :, half], tok.at[rows64(8 + z), half], r_tok.at[8 + z]
        ).start()
        for k in range(1, DP):
            token_copy(8 + k, lax.rem(dp + k, DP), 2, 8 + z).start()

    weights_z(1)
    weights_z(2)
    for p in range(3):
        relay(p, (0,))
    spread(0)

    for j in range(12):
        landed(tok.at[rows64(j), half], r_tok.at[j], s_tok.at[0], dp, mp)
    ours, theirs, whole = pl.ds(512, 256), pl.ds(768, 256), pl.ds(0, T)
    go(remote(tok.at[ours, half], tok.at[theirs, half], s_x.at[0], r_x.at[0], dp, across))
    go(remote(tok.at[whole, half], tok.at[whole, half], s_pair.at[0], r_pair.at[0], dp, other))
    for j in range(8):
        for xx in range(2):
            m = 2 * xx + c
            landed(smalls.at[m, j], r_small.at[xx * DP + j], s_small.at[0], dp, mp)
    go(remote(smalls.at[c], smalls.at[c], s_pair.at[1], r_pair.at[1], dp, other))
    go(remote(smalls.at[2 + c], smalls.at[2 + c], s_pair.at[2], r_pair.at[2], dp, other))
    relay(0)

    pltpu.make_async_copy(ts.at[x, dp], tea.at[mp, dp], r_tea.at[x, dp]).start()
    for k in range(DP):
        d = lax.rem(dp + k, DP)
        for xr in range(2):
            if k or xr:
                xx = lax.rem(x + xr, 2)
                go(remote(ts.at[xx, d], tea.at[mp, dp], s_tea.at[2 * k + xr], r_tea.at[x, dp], d, 2 * xx + c))
        if k:
            go(remote(ts.at[2, d], tea.at[mp, 8 + z], s_tea.at[16 + k], r_tea.at[x, 8 + z], d, 2 * y + c))

    @pl.when(y == x)
    def _():
        pltpu.make_async_copy(ts.at[2, dp], tea.at[mp, 8 + z], r_tea.at[x, 8 + z]).start()

    @pl.when(y != x)
    def _():
        remote(ts.at[2, dp], tea.at[mp, 8 + z], s_tea.at[16], r_tea.at[x, 8 + z], dp, 2 * y + c).start()

    o = 1 - c
    their_half = pl.ds(pl.multiple_of(384 * o, 128), 384)
    landed(tok.at[theirs, half], r_x.at[0], s_x.at[0], dp, mp)
    go(remote(tok.at[theirs, half], tok.at[theirs, half], s_pair.at[5], r_pair.at[5], dp, other))
    landed(tok.at[whole, their_half], r_pair.at[0], s_pair.at[0], dp, mp)
    landed(smalls.at[o], r_pair.at[1], s_pair.at[0], dp, mp)
    landed(smalls.at[2 + o], r_pair.at[2], s_pair.at[0], dp, mp)

    low, high = lax.broadcasted_iota(jnp.int32, (512, 128), 0), lax.broadcasted_iota(jnp.int32, (512, 128), 1)
    lane, quarter = low & 127, lax.shift_right_logical(low, 7)
    pick = jnp.where((high == 24 * quarter + lane) & (lane < 24), 1.0, 0.0).astype(BF)
    stacked = jnp.concatenate(
        [jnp.concatenate([smalls[m, d, 0:32] for m in range(4)], axis=1) for d in range(DP)], axis=0
    )
    picked = nn(stacked, pick)
    vecs[...] = jnp.concatenate([picked[32 * d : 32 * d + 32, 0:96] for d in range(DP)], axis=1)
    vec[0:1] = vecs[pl.ds(6 + x * DP + dp, 1)]
    vec[1:2] = vecs[pl.ds(6 + 2 * DP + dp, 1)]
    vec[2:8] = vecs[0:6]
    blank = jnp.zeros((1, 64), F32)
    for xi in range(2):
        biases = smalls[2 * xi + c, 0, 32:48].astype(F32)
        for d in range(1, DP):
            biases = biases + smalls[2 * xi + c, d, 32:48].astype(F32)
        vec[10 + xi : 11 + xi] = jnp.concatenate([biases[k : k + 1] for k in range(6)], axis=1)
        pieces = []
        for j in range(3):
            pieces += [biases[8 + j : 9 + j, 0:64], blank, biases[11 + j : 12 + j, 0:64]]
        vec[8 + xi : 9 + xi] = jnp.concatenate(pieces + [blank] * 3, axis=1)
    landed(tok.at[theirs, their_half], r_pair.at[5], s_pair.at[0], dp, mp)
    complete(0)
    smid = g.at[0, 0]

    def half_of(p, xi, low, high):
        return w[p, DP * xi : DP * xi + DP, :, low:high].reshape(768, high - low)

    sums[...] = jnp.zeros(sums.shape, F32)

    def core(k, buffer, i):
        rows = chunk(i)
        return remote(
            buffer.at[rows], recv.at[k % 2, rows], s_core.at[k, i], r_core.at[k, i], dp, other
        )

    def each(count, body):
        def run(i, carry):
            body(i)
            return carry

        lax.fori_loop(0, count, run, 0)

    def lanes(h):
        return pl.ds(pl.multiple_of(128 * h, 128), 128)

    def add(row, value):
        width = value.shape[1]
        sums[row : row + 1, 0:width] = sums[row : row + 1, 0:width] + value

    def stream(i):
        return tok[chunk(i)].astype(F32) + jnp.where(i < 2, vec[0:1], vec[1:2])

    def block(p, xi, d):
        return g.at[p, xi, pl.ds(pl.multiple_of(ROWS * d, ROWS), ROWS)]

    def first(p):
        for n in range(1, 5):
            k = lax.rem(z + n, 4)
            staged = s1 if p == 2 else w.at[p]
            staged[k] = block(p, 1 - x, 2 * k + 1 - y)[...].astype(BF)
            there = jnp.where(k < (1 if p == 1 else 2), dp, beside), jnp.where(k < (1 if p == 1 else 2), across, mp)
            go(remote(staged.at[k], r1.at[p, k], s_a.at[p, k], r_a.at[p, k], *there))

    def second(p):
        for n in range(1, 5):
            k = lax.rem(z + n, 4)
            landed(r1.at[p, k], r_a.at[p, k], s_a.at[p, k], dp, mp)
            extra = r1[p, k].astype(F32)
            gx, gy_ = block(p, 1 - x, 2 * k + y)[...], block(p, x, 2 * k + 1 - y)[...]
            w[p, 4 + k] = (gx + jnp.where(k < (1 if p == 1 else 2), 0.0, extra)).astype(BF)
            w[p, 8 + k] = (gy_ + jnp.where(k < (1 if p == 1 else 2), extra, 0.0)).astype(BF)
            go(remote(w.at[p, 4 + k], r2.at[p, 0, k], s_b.at[p, 0, k], r_b.at[p, 0, k], dp, across))
            go(remote(w.at[p, 8 + k], r2.at[p, 1, k], s_b.at[p, 1, k], r_b.at[p, 1, k], beside, mp))

    def third(p):
        for k in range(1, 5):
            zz = lax.rem(z + k, 4)
            for side in range(2):
                landed(r2.at[p, side, zz], r_b.at[p, side, zz], s_b.at[p, side, 0], dp, mp)
            total = block(p, x, 2 * zz + y)[...] + r2[p, 0, zz].astype(F32) + r2[p, 1, zz].astype(F32)
            if k < 4:
                w[p, 11 + k] = total.astype(BF)
                go(remote(w.at[p, 11 + k], r3.at[p, k - 1], s_c.at[p, k - 1], r_c.at[p, k - 1], 2 * zz + y, mp))
            else:
                gs[p] = total

    def last(p):
        for k in range(3):
            landed(r3.at[p, k], r_c.at[p, k], s_c.at[p, k], dp, mp)
        gs[p] = gs[p] + (r3[p, 0].astype(F32) + r3[p, 1].astype(F32) + r3[p, 2].astype(F32))

    def home_copy(n):
        return remote(
            yg.at[n, mp, 8 + z], back.at[n, 2, dp], s_yg.at[n, 16], r_yg.at[n, 2, dp], 2 * z + x, mp
        )

    def go_home(n):
        pltpu.make_async_copy(yg.at[n, mp, dp], back.at[n, x, dp], r_yg.at[n, x, dp]).start()
        for k in range(DP):
            s = lax.rem(dp + k, DP)
            for xr in range(2):
                if k or xr:
                    m = 2 * lax.rem(x + xr, 2) + c
                    go(remote(yg.at[n, m, s], back.at[n, x, dp], s_yg.at[n, 2 * k + xr], r_yg.at[n, x, dp], s, m))
        for k in range(4):
            j = lax.rem(z + k, 4)
            for xr in range(2):
                m = 2 * lax.rem(x + xr, 2) + c
                if k or xr:
                    go(remote(yg.at[n, m, 8 + j], back.at[n, 2, dp], s_yg.at[n, 16 + 2 * k + xr], r_yg.at[n, 2, dp], 2 * j + x, m))

        @pl.when(y == x)
        def _():
            pltpu.make_async_copy(yg.at[n, mp, 8 + z], back.at[n, 2, dp], r_yg.at[n, 2, dp]).start()

        @pl.when(y != x)
        def _():
            home_copy(n).start()

    def project(i):
        rows = chunk(i)
        normed, _ = normalize_rows(stream(i))
        nb = (normed * vec[2:3] + vec[4:5]).astype(BF)
        nin[rows] = nb
        for xi in range(2):
            pr = (nn(nb, half_of(0, xi, 0, 640)) + vec[8 + xi : 9 + xi, 0:640]).astype(BF)
            for j in range(3):
                head, a = 3 * xi + j, 192 * j
                q_s[head, rows] = jnp.concatenate([pr[:, a : a + 64], jnp.zeros((R, 64), BF)], axis=1)
                kv[head, rows] = pr[:, a + 64 : a + 192]

    each(3, project)

    normed, _ = normalize_rows(stream(3))
    nb = (normed * vec[2:3] + vec[4:5]).astype(BF)
    for xi in range(2):
        pr = (nn(nb, half_of(0, xi, 0, 640)) + vec[8 + xi : 9 + xi, 0:640]).astype(BF)
        for j in range(3):
            kv[3 * xi + j, theirs] = pr[:, 192 * j + 64 : 192 * j + 192]

    spread(1)

    def turn(part):
        def body(h):
            kvt[h, :, part * 512 : part * 512 + 512] = kv[h, part * 512 : part * 512 + 512].T

        each(6, body)

    def attend(h, block):
        part = block // 2
        keys, rows = slice(part * 512, part * 512 + 512), slice(block * R, block * R + R)
        st = nt(kv[h, keys], q_s[h, rows]) * LOG_SCALE + wide(mask[keys], R)
        top = jnp.max(st, axis=0, keepdims=True)
        e = jnp.exp(st - top)
        total = colsum(e)
        pt = (e * (1.0 / total)).astype(BF)
        ot = nn(kvt[h, 64:128, keys], pt)
        xi, j = lax.div(h, 3), lax.rem(h, 3)
        o_t[xi, pl.ds(pl.multiple_of(64 + 64 * j, 64), 64), rows] = ot.astype(BF)
        lse[h, :, rows] = top + jnp.log(total)

    o_t[:, 0:64] = jnp.zeros((2, 64, T), BF)
    turn(0)

    def attend_a(h):
        attend(h, 0)
        attend(h, 1)

    each(6, attend_a)
    relay(1)
    turn(1)
    each(6, lambda h: attend(h, 2))
    spread(2)

    def out_project(i):
        rows = chunk(i)
        part = None
        for xi in range(2):
            a = o_t[xi, :, rows].T
            att[xi, rows] = a
            piece = nt(a, half_of(0, xi, 512, 768))
            part = piece if part is None else part + piece
        smid[rows] = part
        core(0, smid, i).start()

    each(3, out_project)
    complete(1)

    def forward(i):
        rows = chunk(i)
        core(0, smid, i).wait()
        mid = stream(i) + (smid[rows] + recv[0, rows] + vec[6:7])
        smid[rows] = mid
        normed, _ = normalize_rows(mid)
        nb = (normed * vec[3:4] + vec[5:6]).astype(BF)
        n2_s[rows] = nb
        for xi in range(2):
            value, slope = gelu_pair(nn(nb, half_of(1, xi, 0, 768)) + vec[10 + xi : 11 + xi])
            act[xi, rows] = value.astype(BF)
            g[1, xi, rows] = slope

    each(3, forward)
    relay(2)
    for xx in range(2):
        for j in range(12):
            landed(tea.at[2 * xx + c, j], r_tea.at[xx, j], s_tea.at[0], dp, mp)
    go(remote(tea.at[c], tea.at[c], s_pair.at[3], r_pair.at[3], dp, other))
    go(remote(tea.at[2 + c], tea.at[2 + c], s_pair.at[4], r_pair.at[4], dp, other))
    complete(2)

    def forward_out(i):
        rows = chunk(i)
        gy[rows] = nt(act[0, rows], half_of(2, 0, 0, 768)) + nt(act[1, rows], half_of(2, 1, 0, 768))
        core(1, gy, i).start()

    each(3, forward_out)
    landed(tea.at[o], r_pair.at[3], s_pair.at[0], dp, mp)
    landed(tea.at[2 + o], r_pair.at[4], s_pair.at[0], dp, mp)

    def teacher_rows(j):
        pieces = []
        for m in range(4):
            low = tea[m, j, 64:96]
            pieces += [tea[m, j, 0:64], jnp.concatenate([low[:, 0:64], low[:, 64:128]], axis=0)]
        return jnp.concatenate(pieces, axis=1)

    def pack_out(n, i, value):
        for q in range(4):
            a = 64 * q
            for m in range(4):
                b = 192 * m
                yg[n, m, 4 * i + q, 0:64] = value[a : a + 64, b : b + 128]
                yg[n, m, 4 * i + q, 64:96] = jnp.concatenate(
                    [value[a : a + 32, b + 128 : b + 192], value[a + 32 : a + 64, b + 128 : b + 192]], axis=1
                )

    def take_loss(i):
        rows = chunk(i)
        core(1, gy, i).wait()
        out = smid[rows] + (gy[rows] + recv[1, rows] + vec[7:8])
        out_b = out.astype(BF)
        pack_out(0, i, out_b)
        target = jnp.concatenate([teacher_rows(4 * i + q) for q in range(4)], axis=0)
        residual = jnp.where(wide(mask[rows], T) == 0.0, out - target.astype(F32), 0.0)
        add(8, colsum(residual * residual))
        grad_y = residual * factor[0:1, 0:1]
        gy[rows] = grad_y
        gb = grad_y.astype(BF)
        gm[rows] = gb
        add(5, colsum(gb.astype(F32)))

    each(3, take_loss)

    def turn_rows(source):
        def body(i):
            tr[:, chunk(i)] = source[chunk(i)].T

        each(3, body)

    def weight_grad(p, values):
        def body(i):
            for xi in range(2):
                g[p, xi, chunk(i)] = nn(tr[chunk(i)], values[xi])

        each(3, body)

    turn_rows(gm)
    weight_grad(2, act)
    for copy in sent:
        copy.wait_send()
    sent.clear()
    first(2)
    go_home(0)

    def turn_back(i):
        rows = chunk(i)
        gb = gm[rows]
        part = None
        for xi in range(2):
            gpre = (nn(gb, half_of(2, xi, 0, 768)) * g[1, xi, rows]).astype(BF)
            gp[xi, rows] = gpre
            add(11 + xi, colsum(gpre.astype(F32)))
            piece = nt(gpre, half_of(1, xi, 0, 768))
            part = piece if part is None else part + piece
        x3[rows] = part
        core(2, x3, i).start()

    each(3, turn_back)

    turn_rows(n2_s)
    weight_grad(1, gp)
    first(1)
    second(2)

    def mid_back(i):
        rows = chunk(i)
        core(2, x3, i).wait()
        grad_h = x3[rows] + recv[0, rows]
        normed, inverse = normalize_rows(smid[rows])
        add(1, colsum(grad_h * normed))
        add(3, colsum(grad_h))
        grad_mid = gy[rows] + norm_back(grad_h * vec[3:4], normed, inverse)
        gy[rows] = grad_mid
        gb = grad_mid.astype(BF)
        gm[rows] = gb
        add(4, colsum(gb.astype(F32)))
        for xi in range(2):
            gatt = nn(gb, half_of(0, xi, 512, 768)).astype(BF)
            for j in range(3):
                piece = gatt[:, 64 + 64 * j : 128 + 64 * j]
                n2_s[rows, 384 * xi + 128 * j : 384 * xi + 128 * j + 128] = jnp.concatenate([jnp.zeros((R, 64), BF), piece], axis=1)

    each(3, mid_back)

    def attend_grad(h, block):
        part = block // 2
        keys, rows = slice(part * 512, part * 512 + 512), slice(block * R, block * R + R)
        kvs, q, go = kv[h, keys], q_s[h, rows], n2_s[rows, lanes(h)]
        st = nt(kvs, q) * LOG_SCALE + wide(mask[keys], R)
        pt = jnp.exp(st - lse[h, :, rows])
        dpt = nt(kvs, go)
        delta = colsum(pt * dpt)
        dst = (pt * (dpt - delta)).astype(BF)
        dqt = nn(kvt[h, 0:64, keys], dst) * LOG_SCALE
        q_s[h, rows, 0:64] = dqt.T.astype(BF)
        return nn(dst, q) * LOG_SCALE + nn(pt.astype(BF), go)

    def grad_c(h):
        both = attend_grad(h, 2)
        recv[0, 512:768, lanes(h)] = both[0:256]
        dkx[h] = both[256:512].astype(BF)

    def grad_a(h):
        recv[0, 0:512, lanes(h)] = attend_grad(h, 0) + attend_grad(h, 1)

    each(6, grad_c)
    dk_copy = remote(dkx, dkr, s_x.at[1], r_x.at[1], dp, across)
    dk_copy.start()
    second(1)
    third(2)
    each(6, grad_a)
    turn_rows(gm)

    def out_grad(i):
        for xi in range(2):
            g[0, xi, chunk(i), 512:768] = nn(tr[chunk(i)], att[xi])

    each(3, out_grad)
    third(1)
    dk_copy.wait()

    def join(h):
        recv[0, 512:768, lanes(h)] = recv[0, 512:768, lanes(h)] + dkr[h].astype(F32)

    each(6, join)

    def project_back(i):
        rows = chunk(i)
        part = None
        for xi in range(2):
            pieces = []
            for j in range(3):
                at = 384 * xi + 128 * j
                pieces += [q_s[3 * xi + j, rows, 0:64], recv[0, rows, at : at + 128].astype(BF)]
            gr = jnp.concatenate(pieces + [jnp.zeros((R, 64), BF)], axis=1)
            gp[xi, rows, 0:640] = gr
            add(9 + xi if xi == 0 else 13, colsum(gr.astype(F32)))
            piece = nt(gr, half_of(0, xi, 0, 640))
            part = piece if part is None else part + piece
        x3[rows] = part
        core(3, x3, i).start()

    each(3, project_back)
    turn_rows(nin)

    def qkv_grad(i):
        rows = chunk(i)
        for xi in range(2):
            h = nn(tr[rows], gp[xi, :, 0:640])
            g[0, xi, rows, 0:512] = h[:, 0:512]
            g[0, xi, rows, 512:640] = g[0, xi, rows, 512:640] + h[:, 512:640]

    each(3, qkv_grad)
    first(0)

    def in_back(i):
        rows = chunk(i)
        core(3, x3, i).wait()
        grad_h = x3[rows] + recv[1, rows]
        normed, inverse = normalize_rows(stream(i))
        add(0, colsum(grad_h * normed))
        add(2, colsum(grad_h))
        grad_in = gy[rows] + norm_back(grad_h * vec[2:3], normed, inverse)
        total = colsum(grad_in)
        add(6, jnp.where(i < 2, total, 0.0))
        add(7, jnp.where(i < 2, 0.0, total))
        out_b = grad_in.astype(BF)
        pack_out(1, i, out_b)

    each(3, in_back)
    go_home(1)
    second(0)

    msg[...] = jnp.zeros(msg.shape, F32)
    loss_row = sums[8:9, 0:128]
    for k in range(1, 6):
        loss_row = loss_row + sums[8:9, 128 * k : 128 * k + 128]
    for xi in range(2):
        bias_sums = sums[9:10] if xi == 0 else sums[13:14]
        hidden = sums[11 + xi : 12 + xi]
        for d in range(DP):
            at, owner = 96 * d + 48 * xi, 8 * xi + d
            msg[owner, 0:8, 0:24] = jnp.where(c == 0, sums[0:8, at : at + 24], sums[0:8, at + 24 : at + 48])
            msg[owner, 8:9] = loss_row
            for j in range(3):
                for kind in range(2):
                    low = 192 * j + 128 * kind
                    msg[owner, 9 + 3 * kind + j : 10 + 3 * kind + j, 0:64] = bias_sums[:, low : low + 64]
            for k in range(6):
                msg[owner, 16 + k : 17 + k] = hidden[:, 128 * k : 128 * k + 128]
    pltpu.make_async_copy(msg.at[mine], msgs.at[mine], r_msg.at[mine]).start()
    for k in range(DP):
        for xr in range(2):
            if k or xr:
                d, xx = lax.rem(dp + k, DP), lax.rem(x + xr, 2)
                go(remote(msg.at[xx * DP + d], msgs.at[mine], s_msg.at[2 * k + xr], r_msg.at[mine], d, 2 * xx + c))
    third(0)
    last(2)
    last(1)
    last(0)
    for j in range(16):
        landed(msgs.at[j], r_msg.at[j], s_msg.at[0], dp, mp)
    for n in range(2):
        for m in range(3):
            for j in range(DP):
                landed(back.at[n, m, j], r_yg.at[n, m, j], s_yg.at[n, 0], dp, mp)
    for copy in sent:
        copy.wait_send()

    @pl.when(y == x)
    def _():
        for k in range(1, DP):
            token_copy(8 + k, lax.rem(dp + k, DP), 2, 8 + z).wait_send()

    @pl.when(y != x)
    def _():
        remote(ts.at[2, dp], tea.at[mp, 8 + z], s_tea.at[16], r_tea.at[x, 8 + z], dp, 2 * y + c).wait_send()
        home_copy(0).wait_send()
        home_copy(1).wait_send()


def step(xs, ts, wsh, small, mask, factor):
    dma = pltpu.SemaphoreType.DMA
    vm = pltpu.VMEM
    block = (ROWS, 768)
    return pl.pallas_call(
        step_kernel,
        name="step",
        out_shape=(
            jax.ShapeDtypeStruct((3, ROWS, 768), F32),
            jax.ShapeDtypeStruct((16, 24, 128), F32),
            jax.ShapeDtypeStruct((2, 3, DP, 96, 128), BF),
        ),
        in_specs=[pl.BlockSpec(memory_space=pl.ANY)] * 4 + [VM] * 2,
        out_specs=(VM, VM, pl.BlockSpec(memory_space=pl.ANY)),
        scratch_shapes=[
            vm((3, 2, T, 768), F32), vm((2, 4, 12, 96, 128), BF), vm((16, 768), F32), vm((16, 24, 128), F32),
            vm((4,) + block, BF), vm((3, 4) + block, BF), vm((3, 2, 4) + block, BF), vm((3, 3) + block, BF),
            vm((1024, 768), BF), vm((4, 12, 96, 128), BF), vm((3, 16) + block, BF),
            vm((4, DP, 48, 128), BF), vm((32, 768), F32), vm((16, 768), F32),
            vm((T, 768), BF), vm((6, T, 128), BF), vm((6, 1024, 128), BF), vm((6, 128, 1024), BF),
            vm((2, R, T), BF), vm((2, T, R), BF), vm((T, 768), BF), vm((2, T, 768), BF),
            vm((T, 768), F32), vm((T, 768), BF), vm((2, T, 768), BF), vm((T, 768), F32),
            vm((2, T, 768), F32), vm((768, T), BF), vm((6, R, 128), BF), vm((6, R, 128), BF),
            vm((6, 1, T), F32),
            dma((4, 3)), dma((4, 3)), dma((2,)), dma((2,)),
            dma((16,)), dma((12,)), dma((24,)), dma((2, 12)), dma((16,)), dma((16,)),
            dma((3, 15)), dma((3, 16)), dma((6,)), dma((6,)),
            dma((16,)), dma((16,)), dma((2, 24)), dma((2, 3, DP)), dma((3, 4)), dma((3, 4)),
            dma((3, 2, 4)), dma((3, 2, 4)), dma((3, 3)), dma((3, 3)),
        ],
        compiler_params=pltpu.CompilerParams(
            collective_id=3, has_side_effects=True, vmem_limit_bytes=VMEM_LIMIT
        ),
    )(xs, ts, wsh, small, mask, factor)


def send_slot(perm, m, d, dp):
    index = 0
    for k in range(DP):
        v = perm[m, DP * d + k]
        index = index + jnp.where(lax.shift_right_logical(v, 3) == dp, v & 7, 0)
    return index


def one_hot(timestep):
    steps = lax.broadcasted_iota(jnp.int32, (1, 1000), 1)
    return jnp.concatenate(
        [jnp.where(steps == timestep[n], 1.0, 0.0).astype(F32) for n in range(24)], axis=0
    )


def valid_count(lengths):
    count = lengths[0]
    for n in range(1, 24):
        count = count + lengths[n]
    return count


def pack_kernel(
    perm, lengths, timestep, xin, tin, table, gains, shifts, qvb, inb, w_qkv, w_out, w_in, w_back,
    xs, ts, wsh, small, mask, factor,
    rows, lines, sem,
):
    dp, mp, x, c = place()
    slots = [[send_slot(perm, m, d, dp) for d in range(DP)] for m in range(3)]
    copies = []
    for m in range(3):
        for d in range(DP):
            source = xin.at[m, pl.ds(pl.multiple_of(64 * slots[m][d], 64), 64)]
            copies.append(pltpu.make_async_copy(source, xs.at[m, d], sem.at[m, d]))
            copies[-1].start()
    for m in range(3):
        rows[m] = tin[m].T
    for m in range(3):
        for d in range(DP):
            v = rows[m, pl.ds(pl.multiple_of(64 * slots[m][d], 64), 64)]
            ts[m, d, 0:64] = v[:, 0:128]
            ts[m, d, 64:96] = jnp.concatenate([v[0:32, 128:192], v[32:64, 128:192]], axis=1)
    wsh[0, :, 0:576] = w_qkv[...]
    wsh[0, :, 576:768] = w_out[...].T
    wsh[1] = w_in[...]
    wsh[2] = w_back[...]

    lane = lax.broadcasted_iota(jnp.int32, (8, 128), 1)
    lines[...] = jnp.zeros(lines.shape, F32)
    lines[0:2, 0:24] = gains[...].astype(F32)
    lines[2:6, 0:24] = shifts[...].astype(F32)
    lines[6:30, 0:24] = nt(one_hot(timestep).astype(BF), table[...])
    spread = jnp.concatenate([inb[...].astype(F32)] * 8, axis=1)
    lines[32:38] = jnp.where(lax.shift_right_logical(lane[0:6], 4) == dp, spread, 0.0)
    for j in range(3):
        both = jnp.concatenate([qvb[j].astype(F32)] * 8, axis=1)
        both = jnp.where(lax.shift_right_logical(lane[0:2, 0:64], 3) == dp, both, 0.0)
        lines[40 + j : 41 + j, 0:64] = both[0:1]
        lines[43 + j : 44 + j, 0:64] = both[1:2]
    small[...] = lines[...].astype(BF)

    inside = lax.broadcasted_iota(jnp.int32, (64, 128), 0)
    micro_lengths = lengths[x * DP + dp], lengths[2 * DP + dp]
    for j in range(16):
        own = j < 8
        m = x if own else 2
        wanted = j if own else 2 * (j % 4) + (x if j < 12 else 1 - x)
        at = 0
        for p in range(DP):
            v = perm[m, DP * dp + p]
            at = at + jnp.where(lax.shift_right_logical(v, 3) == wanted, p, 0)
        live = inside + 64 * at < micro_lengths[0 if own else 1]
        mask[64 * j : 64 * j + 64] = jnp.where(live, 0.0, -1e30).astype(F32)
    count = jnp.full((8, 128), valid_count(lengths), jnp.int32).astype(F32)
    factor[...] = (3.0 * DP * 512) / count
    for copy in copies:
        copy.wait()


def pack(*arguments):
    vm = pltpu.VMEM
    smem = pl.BlockSpec(memory_space=pltpu.SMEM)
    return pl.pallas_call(
        pack_kernel,
        name="pack",
        out_shape=(
            jax.ShapeDtypeStruct((3, DP, 64, 768), BF),
            jax.ShapeDtypeStruct((3, DP, 96, 128), BF),
            jax.ShapeDtypeStruct((3, ROWS, 768), BF),
            jax.ShapeDtypeStruct((48, 128), BF),
            jax.ShapeDtypeStruct((1024, 128), F32),
            jax.ShapeDtypeStruct((8, 128), F32),
        ),
        in_specs=[smem] * 3 + [pl.BlockSpec(memory_space=pl.ANY)] + [VM] * 10,
        out_specs=(VM,) * 6,
        scratch_shapes=[vm((3, 512, 192), BF), vm((48, 128), F32), pltpu.SemaphoreType.DMA((3, DP))],
        compiler_params=pltpu.CompilerParams(vmem_limit_bytes=VMEM_LIMIT),
    )(*arguments)


def unpack_kernel(
    perm, lengths, timestep, gs, msgs, home,
    y_out, loss, grad_x, table, gains, shifts, g_qkv, g_qvb, g_out, g_in, g_inb, g_back,
    rows,
):
    dp, mp, x, c = place()
    for m in range(3):
        slots = [send_slot(perm, m, d, dp) for d in range(DP)]
        for n, target in ((0, y_out), (1, grad_x)):
            for d in range(DP):
                low = home[n, m, d, 64:96]
                value = jnp.concatenate(
                    [home[n, m, d, 0:64], jnp.concatenate([low[:, 0:64], low[:, 64:128]], axis=0)], axis=1
                )
                rows[n, pl.ds(pl.multiple_of(64 * slots[d], 64), 64)] = value
            target[m] = rows[n].T
    total = msgs[0]
    for j in range(1, 16):
        total = total + msgs[j]
    count = jnp.full((1, 1), valid_count(lengths), jnp.int32).astype(F32)
    loss[...] = jnp.sum(total[8:9], axis=1, keepdims=True) / (count * 768.0)
    gains[...] = total[0:2, 0:24]
    shifts[...] = total[2:6, 0:24]
    turned = pltpu.roll(total, lax.rem(128 - 8 * dp, 128), 1)
    for j in range(3):
        for kind in range(2):
            at = 9 + 3 * kind + j
            g_qvb[j, kind : kind + 1] = turned[at : at + 1, 0:8]
    g_inb[...] = pltpu.roll(total, lax.rem(128 - 16 * dp, 128), 1)[16:22, 0:16]
    lines = [msgs[j, 6:7] for j in range(16)] + [msgs[d, 7:8] + msgs[DP + d, 7:8] for d in range(DP)]
    columns = jnp.concatenate(lines, axis=0).T[0:24]
    chosen = one_hot(timestep)
    result = columns[:, 0:1] * chosen[0:1]
    for n in range(1, 24):
        result = result + columns[:, n : n + 1] * chosen[n : n + 1]
    table[...] = result
    g_qkv[...] = gs[0, :, 0:576]
    g_out[...] = gs[0, :, 576:768].T
    g_in[...] = gs[1]
    g_back[...] = gs[2]


def unpack(*arguments):
    smem = pl.BlockSpec(memory_space=pltpu.SMEM)
    shapes = [
        ((3, 192, 512), BF), ((1, 1), F32), ((3, 192, 512), BF), ((24, 1000), F32), ((2, 24), F32),
        ((4, 24), F32), ((96, 576), F32), ((3, 2, 8), F32), ((192, 96), F32), ((96, 768), F32),
        ((6, 16), F32), ((96, 768), F32),
    ]
    return pl.pallas_call(
        unpack_kernel,
        name="unpack",
        out_shape=tuple(jax.ShapeDtypeStruct(*shape) for shape in shapes),
        in_specs=[smem] * 3 + [VM] * 3,
        out_specs=(VM,) * 12,
        scratch_shapes=[pltpu.VMEM((2, 512, 192), BF)],
        compiler_params=pltpu.CompilerParams(vmem_limit_bytes=VMEM_LIMIT),
    )(*arguments)


def per_device_compact(
    input_stream, teacher, timestep, lengths, block_perm, table, norm_gains, shifts,
    w_qkv, qv_bias, w_out, w_in, in_bias, w_back,
):
    packed = pack(
        block_perm, lengths, timestep, input_stream, teacher.transpose(0, 2, 1), table.T, norm_gains, shifts,
        qv_bias.transpose(1, 0, 2), in_bias, w_qkv, w_out, w_in, w_back.T,
    )
    outs = list(unpack(block_perm, lengths, timestep, *step(*packed)))
    outs[0], outs[2] = outs[0].transpose(0, 2, 1), outs[2].transpose(0, 2, 1)
    outs[1], outs[3] = outs[1].reshape(()), outs[3].T
    outs[7], outs[11] = outs[7].transpose(1, 0, 2), outs[11].T
    return tuple(outs)


def solution(mesh):
    compact = mesh.shape["dp"] == 8 and mesh.shape["mp"] == 4
    return jax.shard_map(
        per_device_compact if compact else per_device,
        mesh=mesh,
        in_specs=(
            P(None, "dp", None),
            P(None, "dp", "mp"),
            P(),
            P(),
            P(),
            P(None, ("dp", "mp")),
            P(None, ("dp", "mp")),
            P(None, ("dp", "mp")),
            P("dp", "mp"),
            P(None, "mp", "dp"),
            P("mp", "dp"),
            P("dp", "mp"),
            P("mp", "dp"),
            P("mp", "dp"),
        ),
        out_specs=(
            P(None, "dp", "mp"),
            P(),
            P(None, "dp", "mp"),
            P(None, ("dp", "mp")),
            P(None, ("dp", "mp")),
            P(None, ("dp", "mp")),
            P("dp", "mp"),
            P(None, "mp", "dp"),
            P("mp", "dp"),
            P("dp", "mp"),
            P("mp", "dp"),
            P("mp", "dp"),
        ),
        check_vma=False,
    )
```

```python
import functools
import math

import jax
import jax.numpy as jnp
from jax import lax
from jax.experimental import pallas as pl
from jax.experimental.pallas import tpu as pltpu
from jax.sharding import PartitionSpec as P

H = 12
DH = 64


epsilon = 1e-05


def normalize_rows(stream):
    centered = stream - jnp.mean(stream, axis=-1, keepdims=True)
    inverse = lax.rsqrt(jnp.mean(centered * centered, axis=-1, keepdims=True) + epsilon)
    return (centered * inverse, inverse)


def column_part(array, start, width):
    return lax.dynamic_slice_in_dim(array, start, width, array.ndim - 1)


def fetch_weights(w_qkv, w_in, w_out, w_back, qv_bias, in_bias):
    return (
        lax.all_gather(w_qkv, "dp", axis=0, tiled=True),
        lax.all_gather(w_in, "dp", axis=0, tiled=True),
        lax.all_gather(w_out, "dp", axis=1, tiled=True),
        lax.all_gather(w_back, "dp", axis=1, tiled=True),
        lax.all_gather(qv_bias, "dp", axis=2, tiled=True),
        lax.all_gather(in_bias, "dp", axis=1, tiled=True),
    )


def invert_map(targets, size):
    ranks = jnp.arange(size, dtype=jnp.int32)
    return jnp.sum(jnp.where(targets[None, :] == ranks[:, None], ranks[None, :], 0), axis=1)


def masked_scores(queries, keys_all, is_live, score_scale):
    scores = (
        jnp.einsum("qhe,khe->hqk", queries, keys_all, preferred_element_type=jnp.float32)
        * score_scale
    )
    return jnp.where(is_live[None, None, :], scores, -1e30)


def attend_rows(keys_all, values, is_live, score_scale, queries):
    scores = masked_scores(queries, keys_all, is_live, score_scale)
    row_top = jnp.max(scores, axis=-1, keepdims=True)
    exponent = jnp.exp(scores - row_top)
    row_total = jnp.sum(exponent, axis=-1, keepdims=True)
    weights_p = (exponent / row_total).astype(jnp.bfloat16)
    mixed = jnp.einsum("hqk,khe->qhe", weights_p, values, preferred_element_type=jnp.float32)
    return (mixed, (row_top + jnp.log(row_total))[..., 0])


def attend_back(keys_all, values, is_live, score_scale, carry, inputs):
    queries, grad_rows, log_total = inputs
    grad_keys, grad_values = carry
    scores = masked_scores(queries, keys_all, is_live, score_scale)
    probabilities = jnp.exp(scores - log_total[..., None])
    grad_probs = jnp.einsum("qhe,khe->hqk", grad_rows, values, preferred_element_type=jnp.float32)
    row_delta = jnp.sum(probabilities * grad_probs, axis=-1, keepdims=True)
    grad_scores = (probabilities * (grad_probs - row_delta)).astype(jnp.bfloat16)
    grad_queries = (
        jnp.einsum("hqk,khe->qhe", grad_scores, keys_all, preferred_element_type=jnp.float32)
        * score_scale
    )
    grad_keys = (
        grad_keys
        + jnp.einsum("hqk,qhe->khe", grad_scores, queries, preferred_element_type=jnp.float32)
        * score_scale
    )
    grad_values = grad_values + jnp.einsum(
        "hqk,qhe->khe",
        probabilities.astype(jnp.bfloat16),
        grad_rows,
        preferred_element_type=jnp.float32,
    )
    return ((grad_keys, grad_values), grad_queries)


def norm_sums(partial_value, normed, gain_full, mp_count):
    weighted = partial_value * gain_full
    sums = jnp.stack([jnp.sum(weighted, axis=1), jnp.sum(weighted * normed, axis=1)], axis=1)
    return jnp.tile(sums, (1, mp_count))


def norm_input_grad(grad_part, gain_part, normed_part, inverse, sums, width):
    scaled = grad_part * gain_part
    return inverse * (scaled - sums[:, 0:1] / width - normed_part * sums[:, 1:2] / width)


def per_device(
    input_stream,
    teacher,
    timestep,
    lengths,
    block_perm,
    table,
    norm_gains,
    shifts,
    w_qkv,
    qv_bias,
    w_out,
    w_in,
    in_bias,
    w_back,
):
    dp_count = lax.axis_size("dp")
    mp_count = lax.axis_size("mp")
    dp_rank = lax.axis_index("dp")
    mp_rank = lax.axis_index("mp")
    micro_count, seq_len, width = input_stream.shape
    part_width = teacher.shape[2]
    block_rows = seq_len // dp_count
    heads_here = H // mp_count
    score_scale = 1.0 / math.sqrt(DH)
    col_start = mp_rank * part_width
    row_block = min(512, seq_len)
    block_count = seq_len // row_block
    valid_count = jnp.sum(lengths).astype(jnp.float32)
    loss_factor = micro_count * dp_count * seq_len / valid_count
    chosen = jnp.take(table, timestep, axis=0)
    gains_full, shifts_full, table_rows = (
        lax.all_gather(norm_gains, ("dp", "mp"), axis=1, tiled=True),
        lax.all_gather(shifts, ("dp", "mp"), axis=1, tiled=True),
        lax.all_gather(chosen, ("dp", "mp"), axis=1, tiled=True),
    )
    gains_full = gains_full.astype(jnp.float32)
    shifts_full = shifts_full.astype(jnp.float32)
    gain_parts = column_part(gains_full, col_start, part_width)
    acc_qkv = jnp.zeros((width, heads_here * 3 * DH), jnp.float32)
    acc_in = jnp.zeros((width, w_in.shape[1]), jnp.float32)
    acc_out = jnp.zeros((heads_here * DH, width), jnp.float32)
    acc_back = jnp.zeros((w_back.shape[0], width), jnp.float32)
    acc_qv = jnp.zeros((2, heads_here, DH), jnp.float32)
    acc_in_bias = jnp.zeros((w_in.shape[1],), jnp.float32)
    acc_gains = jnp.zeros((2, part_width), jnp.float32)
    acc_shifts = jnp.zeros((4, part_width), jnp.float32)
    loss_part = jnp.zeros((), jnp.float32)
    table_sums = []
    outs_y = []
    outs_grad = []
    for micro_index in range(micro_count):
        forward_set = fetch_weights(w_qkv, w_in, w_out, w_back, qv_bias, in_bias)
        proj_qkv, proj_in, proj_out, proj_back, bias_qv, bias_in = forward_set
        bias_qv = bias_qv.astype(jnp.float32)
        bias_in = bias_in.reshape(-1).astype(jnp.float32)
        block_order = block_perm[micro_index].reshape(dp_count, dp_count)
        source = block_order // dp_count
        local_index = block_order % dp_count
        send_index = jnp.sum(jnp.where(source == dp_rank, local_index, 0), axis=1)
        x_blocks = input_stream[micro_index].reshape(dp_count, block_rows, width)
        t_blocks = teacher[micro_index].reshape(dp_count, block_rows, part_width)
        got_x, got_t = (
            lax.all_to_all(
                jnp.take(x_blocks, send_index, axis=0),
                "dp",
                split_axis=0,
                concat_axis=0,
                tiled=True,
            ),
            lax.all_to_all(
                jnp.take(t_blocks, send_index, axis=0),
                "dp",
                split_axis=0,
                concat_axis=0,
                tiled=True,
            ),
        )
        my_source = lax.dynamic_index_in_dim(source, dp_rank, 0, keepdims=False)
        tokens = jnp.take(got_x, my_source, axis=0).reshape(seq_len, width).astype(jnp.float32)
        target = jnp.take(got_t, my_source, axis=0).reshape(seq_len, part_width).astype(jnp.float32)
        seq_index = micro_index * dp_count + dp_rank
        length = lax.dynamic_index_in_dim(lengths, seq_index, 0, keepdims=False)
        table_row = lax.dynamic_index_in_dim(table_rows, seq_index, 0, keepdims=False).astype(
            jnp.float32
        )
        is_live = jnp.arange(seq_len, dtype=jnp.int32) < length
        stream_in = tokens + table_row[None, :]
        normed1, inverse1 = normalize_rows(stream_in)
        normed_in = (normed1 * gains_full[0] + shifts_full[0]).astype(jnp.bfloat16)
        projected = jnp.dot(normed_in, proj_qkv, preferred_element_type=jnp.float32).reshape(
            seq_len, heads_here, 3, DH
        )
        queries = (projected[:, :, 0] + bias_qv[0]).astype(jnp.bfloat16)
        keys_all = projected[:, :, 1].astype(jnp.bfloat16)
        values = (projected[:, :, 2] + bias_qv[1]).astype(jnp.bfloat16)
        query_blocks = queries.reshape(block_count, row_block, heads_here, DH)
        mixed, log_total = lax.map(
            functools.partial(attend_rows, keys_all, values, is_live, score_scale), query_blocks
        )
        attended = mixed.reshape(seq_len, heads_here * DH).astype(jnp.bfloat16)
        attn_part = jnp.dot(attended, proj_out, preferred_element_type=jnp.float32)
        branch_attn = lax.psum_scatter(
            attn_part, "mp", scatter_dimension=1, tiled=True
        ) + column_part(shifts_full[2], col_start, part_width)
        mid_part = column_part(stream_in, col_start, part_width) + branch_attn
        stream_mid = lax.all_gather(mid_part, "mp", axis=1, tiled=True)
        normed2, inverse2 = normalize_rows(stream_mid)
        normed_mid = (normed2 * gains_full[1] + shifts_full[1]).astype(jnp.bfloat16)
        pre_act = jnp.dot(normed_mid, proj_in, preferred_element_type=jnp.float32) + bias_in
        activation = jax.nn.gelu(pre_act, approximate=True).astype(jnp.bfloat16)
        mlp_part = jnp.dot(activation, proj_back, preferred_element_type=jnp.float32)
        mlp_out = lax.psum_scatter(mlp_part, "mp", scatter_dimension=1, tiled=True) + column_part(
            shifts_full[3], col_start, part_width
        )
        out_part = mid_part + mlp_out
        residual_err = jnp.where(is_live[:, None], out_part - target, 0.0)
        loss_part = loss_part + jnp.sum(residual_err * residual_err)
        grad_y = residual_err * loss_factor
        grad_mlp = grad_y.astype(jnp.bfloat16)
        acc_shifts = acc_shifts.at[3].add(jnp.sum(grad_mlp.astype(jnp.float32), axis=0))
        grad_mlp_full = lax.all_gather(grad_mlp, "mp", axis=1, tiled=True)
        back_set = fetch_weights(w_qkv, w_in, w_out, w_back, qv_bias, in_bias)
        back_qkv, back_in, back_out, back_back = (
            back_set[0],
            back_set[1],
            back_set[2],
            back_set[3],
        )
        acc_back = acc_back + jnp.einsum(
            "tf,td->fd", activation, grad_mlp_full, preferred_element_type=jnp.float32
        )
        grad_act = jnp.einsum(
            "td,fd->tf", grad_mlp_full, back_back, preferred_element_type=jnp.float32
        )
        gelu_value, gelu_pull = jax.vjp(lambda inner: jax.nn.gelu(inner, approximate=True), pre_act)
        grad_pre = gelu_pull(grad_act)[0].astype(jnp.bfloat16)
        acc_in_bias = acc_in_bias + jnp.sum(grad_pre.astype(jnp.float32), axis=0)
        acc_in = acc_in + jnp.einsum(
            "td,tf->df", normed_mid, grad_pre, preferred_element_type=jnp.float32
        )
        partial2 = jnp.einsum("tf,df->td", grad_pre, back_in, preferred_element_type=jnp.float32)
        grad_h2, sums2 = (
            lax.psum_scatter(partial2, "mp", scatter_dimension=1, tiled=True),
            lax.psum_scatter(
                norm_sums(partial2, normed2, gains_full[1], mp_count),
                "mp",
                scatter_dimension=1,
                tiled=True,
            ),
        )
        normed2_part = column_part(normed2, col_start, part_width)
        acc_gains = acc_gains.at[1].add(jnp.sum(grad_h2 * normed2_part, axis=0))
        acc_shifts = acc_shifts.at[1].add(jnp.sum(grad_h2, axis=0))
        grad_mid = grad_y + norm_input_grad(
            grad_h2, gain_parts[1], normed2_part, inverse2, sums2, width
        )
        grad_branch = grad_mid.astype(jnp.bfloat16)
        acc_shifts = acc_shifts.at[2].add(jnp.sum(grad_branch.astype(jnp.float32), axis=0))
        grad_branch_full = lax.all_gather(grad_branch, "mp", axis=1, tiled=True)
        acc_out = acc_out + jnp.einsum(
            "tc,td->cd", attended, grad_branch_full, preferred_element_type=jnp.float32
        )
        grad_att = jnp.einsum(
            "td,cd->tc", grad_branch_full, back_out, preferred_element_type=jnp.float32
        ).astype(jnp.bfloat16)
        grad_blocks = grad_att.reshape(block_count, row_block, heads_here, DH)
        zero_heads = jnp.zeros((seq_len, heads_here, DH), jnp.float32)
        (grad_keys, grad_values), grad_queries = lax.scan(
            functools.partial(attend_back, keys_all, values, is_live, score_scale),
            (zero_heads, zero_heads),
            (query_blocks, grad_blocks, log_total),
        )
        grad_queries = grad_queries.reshape(seq_len, heads_here, DH).astype(jnp.bfloat16)
        grad_keys = grad_keys.astype(jnp.bfloat16)
        grad_values = grad_values.astype(jnp.bfloat16)
        acc_qv = acc_qv + jnp.stack(
            [
                jnp.sum(grad_queries.astype(jnp.float32), axis=0),
                jnp.sum(grad_values.astype(jnp.float32), axis=0),
            ]
        )
        grad_qkv_rows = jnp.stack([grad_queries, grad_keys, grad_values], axis=2).reshape(
            seq_len, heads_here * 3 * DH
        )
        acc_qkv = acc_qkv + jnp.einsum(
            "td,tc->dc", normed_in, grad_qkv_rows, preferred_element_type=jnp.float32
        )
        partial1 = jnp.einsum(
            "tc,dc->td", grad_qkv_rows, back_qkv, preferred_element_type=jnp.float32
        )
        grad_h1, sums1 = (
            lax.psum_scatter(partial1, "mp", scatter_dimension=1, tiled=True),
            lax.psum_scatter(
                norm_sums(partial1, normed1, gains_full[0], mp_count),
                "mp",
                scatter_dimension=1,
                tiled=True,
            ),
        )
        normed1_part = column_part(normed1, col_start, part_width)
        acc_gains = acc_gains.at[0].add(jnp.sum(grad_h1 * normed1_part, axis=0))
        acc_shifts = acc_shifts.at[0].add(jnp.sum(grad_h1, axis=0))
        grad_in_stream = grad_mid + norm_input_grad(
            grad_h1, gain_parts[0], normed1_part, inverse1, sums1, width
        )
        table_sums.append(jnp.sum(grad_in_stream, axis=0))
        back_order = invert_map(my_source, dp_count)
        out_blocks = jnp.take(
            out_part.astype(jnp.bfloat16).reshape(dp_count, block_rows, part_width),
            back_order,
            axis=0,
        )
        grad_send = jnp.take(
            grad_in_stream.astype(jnp.bfloat16).reshape(dp_count, block_rows, part_width),
            back_order,
            axis=0,
        )
        home_out, home_grad = (
            lax.all_to_all(out_blocks, "dp", split_axis=0, concat_axis=0, tiled=True),
            lax.all_to_all(grad_send, "dp", split_axis=0, concat_axis=0, tiled=True),
        )
        home_place = invert_map(send_index, dp_count)
        outs_y.append(jnp.take(home_out, home_place, axis=0).reshape(seq_len, part_width))
        outs_grad.append(jnp.take(home_grad, home_place, axis=0).reshape(seq_len, part_width))
    row_sums = jnp.zeros((micro_count, width), jnp.float32)
    row_sums = lax.dynamic_update_slice_in_dim(row_sums, jnp.stack(table_sums), col_start, 1)
    my_steps = jnp.take(timestep, jnp.arange(micro_count, dtype=jnp.int32) * dp_count + dp_rank)
    step_onehot = (
        jnp.arange(table.shape[0], dtype=jnp.int32)[:, None] == my_steps[None, :]
    ).astype(jnp.float32)
    table_grad = jnp.dot(
        step_onehot, row_sums, precision=lax.Precision.HIGHEST, preferred_element_type=jnp.float32
    )
    gains_grad = lax.dynamic_update_slice_in_dim(
        jnp.zeros((2, width), jnp.float32), acc_gains, col_start, 1
    )
    shifts_grad = lax.dynamic_update_slice_in_dim(
        jnp.zeros((4, width), jnp.float32), acc_shifts, col_start, 1
    )
    loss_row = jnp.full((1, dp_count * mp_count), loss_part, jnp.float32)
    grad_table, grad_norm_gains, grad_shifts, loss_cell = (
        lax.psum_scatter(table_grad, ("dp", "mp"), scatter_dimension=1, tiled=True),
        lax.psum_scatter(gains_grad, ("dp", "mp"), scatter_dimension=1, tiled=True),
        lax.psum_scatter(shifts_grad, ("dp", "mp"), scatter_dimension=1, tiled=True),
        lax.psum_scatter(loss_row, ("dp", "mp"), scatter_dimension=1, tiled=True),
    )
    loss = loss_cell[0, 0] / (valid_count * width)
    grad_qkv, grad_in, grad_out, grad_back, grad_qv_bias, grad_in_bias = (
        lax.psum_scatter(acc_qkv, "dp", scatter_dimension=0, tiled=True),
        lax.psum_scatter(acc_in, "dp", scatter_dimension=0, tiled=True),
        lax.psum_scatter(acc_out, "dp", scatter_dimension=1, tiled=True),
        lax.psum_scatter(acc_back, "dp", scatter_dimension=1, tiled=True),
        lax.psum_scatter(acc_qv, "dp", scatter_dimension=2, tiled=True),
        lax.psum_scatter(acc_in_bias.reshape(-1, 128), "dp", scatter_dimension=1, tiled=True),
    )
    y_out = jnp.stack(outs_y)
    grad_x = jnp.stack(outs_grad)
    return (
        y_out,
        loss,
        grad_x,
        grad_table,
        grad_norm_gains,
        grad_shifts,
        grad_qkv,
        grad_qv_bias,
        grad_out,
        grad_in,
        grad_in_bias,
        grad_back,
    )


MESH = pl.DeviceIdType.MESH
BF = jnp.bfloat16
F32 = jnp.float32
VM = pl.BlockSpec(memory_space=pltpu.VMEM)
DP = 8
ROWS = 96
VMEM_LIMIT = 64 * 1024 * 1024 - 65536


def place():
    dp, mp = lax.axis_index("dp"), lax.axis_index("mp")
    x, c = lax.div(mp, 2), lax.rem(mp, 2)
    return dp, mp, x, c


def remote(src, dst, send_sem, recv_sem, dp, mp):
    return pltpu.make_async_remote_copy(
        src_ref=src,
        dst_ref=dst,
        send_sem=send_sem,
        recv_sem=recv_sem,
        device_id=(dp, mp),
        device_id_type=MESH,
    )


def landed(dst, recv_sem, spare, dp, mp):
    remote(dst, dst, spare, recv_sem, dp, mp).wait_recv()


def greet_plane(dp, x, c):
    barrier = pltpu.get_barrier_semaphore()
    pl.semaphore_signal(barrier, inc=1, device_id=(dp, 2 * x + 1 - c), device_id_type=MESH)
    for k in range(DP):
        for xr in range(2):
            if k or xr:
                there = (lax.rem(dp + k, DP), 2 * lax.rem(x + xr, 2) + c)
                pl.semaphore_signal(barrier, inc=1, device_id=there, device_id_type=MESH)
    pl.semaphore_wait(barrier, 2 * DP)


def dot(a, b, dims):
    return lax.dot_general(a, b, (dims, ((), ())), preferred_element_type=F32)


T = 768
R = 256
LOG_SCALE = 0.125


def nn(a, b):
    return dot(a, b, ((1,), (0,)))


def nt(a, b):
    return dot(a, b, ((1,), (1,)))


def chunk(i):
    return pl.ds(pl.multiple_of(i * R, R), R)


def colsum(a):
    return jnp.sum(a, axis=0, keepdims=True)


def wide(column_tile, width):
    return jnp.concatenate([column_tile] * (width // 128), axis=1)


def gelu_pair(v):
    k = 0.7978845608028654
    v2 = v * v
    t = jnp.tanh(k * (v + 0.044715 * (v2 * v)))
    half = 0.5 * (1.0 + t)
    slope = half + 0.5 * v * ((1.0 - t * t) * (k * (1.0 + 0.134145 * v2)))
    return v * half, slope


def norm_back(g, normed, inverse):
    inner = jnp.mean(g * normed, axis=1, keepdims=True)
    return inverse * (g - jnp.mean(g, axis=1, keepdims=True) - normed * inner)


def step_kernel(
    xs, ts, wsh, small, mask, factor,
    gs, msgs, back,
    g, yg, sums, msg, s1, r1, r2, r3,
    tok, tea, w, smalls, vecs, vec, nin, q_s, kv, kvt, o_t, att, n2_s, act, gy, gm, gp, x3, recv, tr, dkx, dkr, lse,
    s_core, r_core, s_x, r_x,
    s_tok, r_tok, s_tea, r_tea, s_small, r_small, s_w, r_w, s_pair, r_pair,
    s_msg, r_msg, s_yg, r_yg, s_a, r_a, s_b, r_b, s_c, r_c,
):
    dp, mp, x, c = place()
    other, across = 2 * x + 1 - c, 2 * (1 - x) + c
    z, y = lax.div(dp, 2), lax.rem(dp, 2)
    mine = x * DP + dp
    half = pl.ds(pl.multiple_of(384 * c, 128), 384)
    beside = 2 * z + 1 - y
    greet_plane(dp, x, c)
    sent = []

    def go(copy):
        copy.start()
        sent.append(copy)

    def rows64(j):
        return pl.ds(pl.multiple_of(64 * j, 64), 64)

    def weights_z(p):
        pltpu.make_async_copy(wsh.at[p], w.at[p, mine], r_w.at[p, mine]).start()
        for k in range(1, 4):
            zz = lax.rem(z + k, 4)
            go(remote(wsh.at[p], w.at[p, mine], s_w.at[p, k - 1], r_w.at[p, mine], 2 * zz + y, mp))

    def weights_xy(p):
        go(remote(wsh.at[p], w.at[p, mine], s_w.at[p, 3], r_w.at[p, mine], dp, across))
        go(remote(wsh.at[p], w.at[p, mine], s_w.at[p, 4], r_w.at[p, mine], beside, mp))

    def spread(p):
        for k in (3, 2, 1):
            b = x * DP + 2 * lax.rem(z + k, 4) + y
            landed(w.at[p, b], r_w.at[p, b], s_w.at[p, 0], dp, mp)
            go(remote(w.at[p, b], w.at[p, b], s_w.at[p, 3 + 2 * k], r_w.at[p, b], dp, across))
            go(remote(w.at[p, b], w.at[p, b], s_w.at[p, 4 + 2 * k], r_w.at[p, b], beside, mp))

    def relay(p, steps=(3, 2, 1)):
        for n in steps:
            k = lax.rem(z + n, 4)
            bx, by = (1 - x) * DP + 2 * k + y, x * DP + 2 * k + 1 - y
            landed(w.at[p, bx], r_w.at[p, bx], s_w.at[p, 0], dp, mp)
            landed(w.at[p, by], r_w.at[p, by], s_w.at[p, 0], dp, mp)
            b = jnp.where(k < 2, bx, by)
            there = jnp.where(k < 2, beside, dp), jnp.where(k < 2, mp, across)
            go(remote(w.at[p, b], w.at[p, b], s_w.at[p, 11 + n], r_w.at[p, b], *there))

    def complete(p):
        landed(w.at[p, mine], r_w.at[p, mine], s_w.at[p, 0], dp, mp)
        for k in range(4):
            b = (1 - x) * DP + 2 * k + 1 - y
            landed(w.at[p, b], r_w.at[p, b], s_w.at[p, 0], dp, mp)

    weights_z(0)
    weights_xy(0)

    pltpu.make_async_copy(small, smalls.at[mp, dp], r_small.at[mine]).start()
    for k in range(DP):
        for xr in range(2):
            if k or xr:
                d, m = lax.rem(dp + k, DP), 2 * lax.rem(x + xr, 2) + c
                go(remote(small, smalls.at[mp, dp], s_small.at[2 * k + xr], r_small.at[mine], d, m))

    def token_copy(k, d, m_from, j):
        return remote(
            xs.at[m_from, d, :, half], tok.at[rows64(j), half], s_tok.at[k], r_tok.at[j], d, mp
        )

    weights_xy(1)
    weights_xy(2)
    pltpu.make_async_copy(xs.at[x, dp, :, half], tok.at[rows64(dp), half], r_tok.at[dp]).start()
    for k in range(1, DP):
        go(token_copy(k, lax.rem(dp + k, DP), x, dp))

    @pl.when(y == x)
    def _():
        pltpu.make_async_copy(
            xs.at[2, dp, :, half], tok.at[rows64(8 + z), half], r_tok.at[8 + z]
        ).start()
        for k in range(1, DP):
            token_copy(8 + k, lax.rem(dp + k, DP), 2, 8 + z).start()

    weights_z(1)
    weights_z(2)
    for p in range(3):
        relay(p, (0,))
    spread(0)

    for j in range(12):
        landed(tok.at[rows64(j), half], r_tok.at[j], s_tok.at[0], dp, mp)
    ours, theirs, whole = pl.ds(512, 256), pl.ds(768, 256), pl.ds(0, T)
    go(remote(tok.at[ours, half], tok.at[theirs, half], s_x.at[0], r_x.at[0], dp, across))
    go(remote(tok.at[whole, half], tok.at[whole, half], s_pair.at[0], r_pair.at[0], dp, other))
    for j in range(8):
        for xx in range(2):
            m = 2 * xx + c
            landed(smalls.at[m, j], r_small.at[xx * DP + j], s_small.at[0], dp, mp)
    go(remote(smalls.at[c], smalls.at[c], s_pair.at[1], r_pair.at[1], dp, other))
    go(remote(smalls.at[2 + c], smalls.at[2 + c], s_pair.at[2], r_pair.at[2], dp, other))
    relay(0)

    pltpu.make_async_copy(ts.at[x, dp], tea.at[mp, dp], r_tea.at[x, dp]).start()
    for k in range(DP):
        d = lax.rem(dp + k, DP)
        for xr in range(2):
            if k or xr:
                xx = lax.rem(x + xr, 2)
                go(remote(ts.at[xx, d], tea.at[mp, dp], s_tea.at[2 * k + xr], r_tea.at[x, dp], d, 2 * xx + c))
        if k:
            go(remote(ts.at[2, d], tea.at[mp, 8 + z], s_tea.at[16 + k], r_tea.at[x, 8 + z], d, 2 * y + c))

    @pl.when(y == x)
    def _():
        pltpu.make_async_copy(ts.at[2, dp], tea.at[mp, 8 + z], r_tea.at[x, 8 + z]).start()

    @pl.when(y != x)
    def _():
        remote(ts.at[2, dp], tea.at[mp, 8 + z], s_tea.at[16], r_tea.at[x, 8 + z], dp, 2 * y + c).start()

    o = 1 - c
    their_half = pl.ds(pl.multiple_of(384 * o, 128), 384)
    landed(tok.at[theirs, half], r_x.at[0], s_x.at[0], dp, mp)
    go(remote(tok.at[theirs, half], tok.at[theirs, half], s_pair.at[5], r_pair.at[5], dp, other))
    landed(tok.at[whole, their_half], r_pair.at[0], s_pair.at[0], dp, mp)
    landed(smalls.at[o], r_pair.at[1], s_pair.at[0], dp, mp)
    landed(smalls.at[2 + o], r_pair.at[2], s_pair.at[0], dp, mp)

    low, high = lax.broadcasted_iota(jnp.int32, (512, 128), 0), lax.broadcasted_iota(jnp.int32, (512, 128), 1)
    lane, quarter = low & 127, lax.shift_right_logical(low, 7)
    pick = jnp.where((high == 24 * quarter + lane) & (lane < 24), 1.0, 0.0).astype(BF)
    stacked = jnp.concatenate(
        [jnp.concatenate([smalls[m, d, 0:32] for m in range(4)], axis=1) for d in range(DP)], axis=0
    )
    picked = nn(stacked, pick)
    vecs[...] = jnp.concatenate([picked[32 * d : 32 * d + 32, 0:96] for d in range(DP)], axis=1)
    vec[0:1] = vecs[pl.ds(6 + x * DP + dp, 1)]
    vec[1:2] = vecs[pl.ds(6 + 2 * DP + dp, 1)]
    vec[2:8] = vecs[0:6]
    blank = jnp.zeros((1, 64), F32)
    for xi in range(2):
        biases = smalls[2 * xi + c, 0, 32:48].astype(F32)
        for d in range(1, DP):
            biases = biases + smalls[2 * xi + c, d, 32:48].astype(F32)
        vec[10 + xi : 11 + xi] = jnp.concatenate([biases[k : k + 1] for k in range(6)], axis=1)
        pieces = []
        for j in range(3):
            pieces += [biases[8 + j : 9 + j, 0:64], blank, biases[11 + j : 12 + j, 0:64]]
        vec[8 + xi : 9 + xi] = jnp.concatenate(pieces + [blank] * 3, axis=1)
    landed(tok.at[theirs, their_half], r_pair.at[5], s_pair.at[0], dp, mp)
    complete(0)
    smid = g.at[0, 0]

    def half_of(p, xi, low, high):
        return w[p, DP * xi : DP * xi + DP, :, low:high].reshape(768, high - low)

    sums[...] = jnp.zeros(sums.shape, F32)

    def core(k, buffer, i):
        rows = chunk(i)
        return remote(
            buffer.at[rows], recv.at[k % 2, rows], s_core.at[k, i], r_core.at[k, i], dp, other
        )

    def each(count, body):
        def run(i, carry):
            body(i)
            return carry

        lax.fori_loop(0, count, run, 0)

    def lanes(h):
        return pl.ds(pl.multiple_of(128 * h, 128), 128)

    def add(row, value):
        width = value.shape[1]
        sums[row : row + 1, 0:width] = sums[row : row + 1, 0:width] + value

    def stream(i):
        return tok[chunk(i)].astype(F32) + jnp.where(i < 2, vec[0:1], vec[1:2])

    def block(p, xi, d):
        return g.at[p, xi, pl.ds(pl.multiple_of(ROWS * d, ROWS), ROWS)]

    def first(p):
        for n in range(1, 5):
            k = lax.rem(z + n, 4)
            staged = s1 if p == 2 else w.at[p]
            staged[k] = block(p, 1 - x, 2 * k + 1 - y)[...].astype(BF)
            there = jnp.where(k < (1 if p == 1 else 2), dp, beside), jnp.where(k < (1 if p == 1 else 2), across, mp)
            go(remote(staged.at[k], r1.at[p, k], s_a.at[p, k], r_a.at[p, k], *there))

    def second(p):
        for n in range(1, 5):
            k = lax.rem(z + n, 4)
            landed(r1.at[p, k], r_a.at[p, k], s_a.at[p, k], dp, mp)
            extra = r1[p, k].astype(F32)
            gx, gy_ = block(p, 1 - x, 2 * k + y)[...], block(p, x, 2 * k + 1 - y)[...]
            w[p, 4 + k] = (gx + jnp.where(k < (1 if p == 1 else 2), 0.0, extra)).astype(BF)
            w[p, 8 + k] = (gy_ + jnp.where(k < (1 if p == 1 else 2), extra, 0.0)).astype(BF)
            go(remote(w.at[p, 4 + k], r2.at[p, 0, k], s_b.at[p, 0, k], r_b.at[p, 0, k], dp, across))
            go(remote(w.at[p, 8 + k], r2.at[p, 1, k], s_b.at[p, 1, k], r_b.at[p, 1, k], beside, mp))

    def third(p):
        for k in range(1, 5):
            zz = lax.rem(z + k, 4)
            for side in range(2):
                landed(r2.at[p, side, zz], r_b.at[p, side, zz], s_b.at[p, side, 0], dp, mp)
            total = block(p, x, 2 * zz + y)[...] + r2[p, 0, zz].astype(F32) + r2[p, 1, zz].astype(F32)
            if k < 4:
                w[p, 11 + k] = total.astype(BF)
                go(remote(w.at[p, 11 + k], r3.at[p, k - 1], s_c.at[p, k - 1], r_c.at[p, k - 1], 2 * zz + y, mp))
            else:
                gs[p] = total

    def last(p):
        for k in range(3):
            landed(r3.at[p, k], r_c.at[p, k], s_c.at[p, k], dp, mp)
        gs[p] = gs[p] + (r3[p, 0].astype(F32) + r3[p, 1].astype(F32) + r3[p, 2].astype(F32))

    def home_copy(n):
        return remote(
            yg.at[n, mp, 8 + z], back.at[n, 2, dp], s_yg.at[n, 16], r_yg.at[n, 2, dp], 2 * z + x, mp
        )

    def go_home(n):
        pltpu.make_async_copy(yg.at[n, mp, dp], back.at[n, x, dp], r_yg.at[n, x, dp]).start()
        for k in range(DP):
            s = lax.rem(dp + k, DP)
            for xr in range(2):
                if k or xr:
                    m = 2 * lax.rem(x + xr, 2) + c
                    go(remote(yg.at[n, m, s], back.at[n, x, dp], s_yg.at[n, 2 * k + xr], r_yg.at[n, x, dp], s, m))
        for k in range(4):
            j = lax.rem(z + k, 4)
            for xr in range(2):
                m = 2 * lax.rem(x + xr, 2) + c
                if k or xr:
                    go(remote(yg.at[n, m, 8 + j], back.at[n, 2, dp], s_yg.at[n, 16 + 2 * k + xr], r_yg.at[n, 2, dp], 2 * j + x, m))

        @pl.when(y == x)
        def _():
            pltpu.make_async_copy(yg.at[n, mp, 8 + z], back.at[n, 2, dp], r_yg.at[n, 2, dp]).start()

        @pl.when(y != x)
        def _():
            home_copy(n).start()

    def project(i):
        rows = chunk(i)
        normed, _ = normalize_rows(stream(i))
        nb = (normed * vec[2:3] + vec[4:5]).astype(BF)
        nin[rows] = nb
        for xi in range(2):
            pr = (nn(nb, half_of(0, xi, 0, 640)) + vec[8 + xi : 9 + xi, 0:640]).astype(BF)
            for j in range(3):
                head, a = 3 * xi + j, 192 * j
                q_s[head, rows] = jnp.concatenate([pr[:, a : a + 64], jnp.zeros((R, 64), BF)], axis=1)
                kv[head, rows] = pr[:, a + 64 : a + 192]

    each(3, project)

    normed, _ = normalize_rows(stream(3))
    nb = (normed * vec[2:3] + vec[4:5]).astype(BF)
    for xi in range(2):
        pr = (nn(nb, half_of(0, xi, 0, 640)) + vec[8 + xi : 9 + xi, 0:640]).astype(BF)
        for j in range(3):
            kv[3 * xi + j, theirs] = pr[:, 192 * j + 64 : 192 * j + 192]

    spread(1)

    def turn(part):
        def body(h):
            kvt[h, :, part * 512 : part * 512 + 512] = kv[h, part * 512 : part * 512 + 512].T

        each(6, body)

    def attend(h, block):
        part = block // 2
        keys, rows = slice(part * 512, part * 512 + 512), slice(block * R, block * R + R)
        st = nt(kv[h, keys], q_s[h, rows]) * LOG_SCALE + wide(mask[keys], R)
        top = jnp.max(st, axis=0, keepdims=True)
        e = jnp.exp(st - top)
        total = colsum(e)
        pt = (e * (1.0 / total)).astype(BF)
        ot = nn(kvt[h, 64:128, keys], pt)
        xi, j = lax.div(h, 3), lax.rem(h, 3)
        o_t[xi, pl.ds(pl.multiple_of(64 + 64 * j, 64), 64), rows] = ot.astype(BF)
        lse[h, :, rows] = top + jnp.log(total)

    o_t[:, 0:64] = jnp.zeros((2, 64, T), BF)
    turn(0)

    def attend_a(h):
        attend(h, 0)
        attend(h, 1)

    each(6, attend_a)
    relay(1)
    turn(1)
    each(6, lambda h: attend(h, 2))
    spread(2)

    def out_project(i):
        rows = chunk(i)
        part = None
        for xi in range(2):
            a = o_t[xi, :, rows].T
            att[xi, rows] = a
            piece = nt(a, half_of(0, xi, 512, 768))
            part = piece if part is None else part + piece
        smid[rows] = part
        core(0, smid, i).start()

    each(3, out_project)
    complete(1)

    def forward(i):
        rows = chunk(i)
        core(0, smid, i).wait()
        mid = stream(i) + (smid[rows] + recv[0, rows] + vec[6:7])
        smid[rows] = mid
        normed, _ = normalize_rows(mid)
        nb = (normed * vec[3:4] + vec[5:6]).astype(BF)
        n2_s[rows] = nb
        for xi in range(2):
            value, slope = gelu_pair(nn(nb, half_of(1, xi, 0, 768)) + vec[10 + xi : 11 + xi])
            act[xi, rows] = value.astype(BF)
            g[1, xi, rows] = slope

    each(3, forward)
    relay(2)
    for xx in range(2):
        for j in range(12):
            landed(tea.at[2 * xx + c, j], r_tea.at[xx, j], s_tea.at[0], dp, mp)
    go(remote(tea.at[c], tea.at[c], s_pair.at[3], r_pair.at[3], dp, other))
    go(remote(tea.at[2 + c], tea.at[2 + c], s_pair.at[4], r_pair.at[4], dp, other))
    complete(2)

    def forward_out(i):
        rows = chunk(i)
        gy[rows] = nt(act[0, rows], half_of(2, 0, 0, 768)) + nt(act[1, rows], half_of(2, 1, 0, 768))
        core(1, gy, i).start()

    each(3, forward_out)
    landed(tea.at[o], r_pair.at[3], s_pair.at[0], dp, mp)
    landed(tea.at[2 + o], r_pair.at[4], s_pair.at[0], dp, mp)

    def teacher_rows(j):
        pieces = []
        for m in range(4):
            low = tea[m, j, 64:96]
            pieces += [tea[m, j, 0:64], jnp.concatenate([low[:, 0:64], low[:, 64:128]], axis=0)]
        return jnp.concatenate(pieces, axis=1)

    def pack_out(n, i, value):
        for q in range(4):
            a = 64 * q
            for m in range(4):
                b = 192 * m
                yg[n, m, 4 * i + q, 0:64] = value[a : a + 64, b : b + 128]
                yg[n, m, 4 * i + q, 64:96] = jnp.concatenate(
                    [value[a : a + 32, b + 128 : b + 192], value[a + 32 : a + 64, b + 128 : b + 192]], axis=1
                )

    def take_loss(i):
        rows = chunk(i)
        core(1, gy, i).wait()
        out = smid[rows] + (gy[rows] + recv[1, rows] + vec[7:8])
        out_b = out.astype(BF)
        pack_out(0, i, out_b)
        target = jnp.concatenate([teacher_rows(4 * i + q) for q in range(4)], axis=0)
        residual = jnp.where(wide(mask[rows], T) == 0.0, out - target.astype(F32), 0.0)
        add(8, colsum(residual * residual))
        grad_y = residual * factor[0:1, 0:1]
        gy[rows] = grad_y
        gb = grad_y.astype(BF)
        gm[rows] = gb
        add(5, colsum(gb.astype(F32)))

    each(3, take_loss)

    def turn_rows(source):
        def body(i):
            tr[:, chunk(i)] = source[chunk(i)].T

        each(3, body)

    def weight_grad(p, values):
        def body(i):
            for xi in range(2):
                g[p, xi, chunk(i)] = nn(tr[chunk(i)], values[xi])

        each(3, body)

    turn_rows(gm)
    weight_grad(2, act)
    for copy in sent:
        copy.wait_send()
    sent.clear()
    first(2)
    go_home(0)

    def turn_back(i):
        rows = chunk(i)
        gb = gm[rows]
        part = None
        for xi in range(2):
            gpre = (nn(gb, half_of(2, xi, 0, 768)) * g[1, xi, rows]).astype(BF)
            gp[xi, rows] = gpre
            add(11 + xi, colsum(gpre.astype(F32)))
            piece = nt(gpre, half_of(1, xi, 0, 768))
            part = piece if part is None else part + piece
        x3[rows] = part
        core(2, x3, i).start()

    each(3, turn_back)

    turn_rows(n2_s)
    weight_grad(1, gp)
    first(1)
    second(2)

    def mid_back(i):
        rows = chunk(i)
        core(2, x3, i).wait()
        grad_h = x3[rows] + recv[0, rows]
        normed, inverse = normalize_rows(smid[rows])
        add(1, colsum(grad_h * normed))
        add(3, colsum(grad_h))
        grad_mid = gy[rows] + norm_back(grad_h * vec[3:4], normed, inverse)
        gy[rows] = grad_mid
        gb = grad_mid.astype(BF)
        gm[rows] = gb
        add(4, colsum(gb.astype(F32)))
        for xi in range(2):
            gatt = nn(gb, half_of(0, xi, 512, 768)).astype(BF)
            for j in range(3):
                piece = gatt[:, 64 + 64 * j : 128 + 64 * j]
                n2_s[rows, 384 * xi + 128 * j : 384 * xi + 128 * j + 128] = jnp.concatenate([jnp.zeros((R, 64), BF), piece], axis=1)

    each(3, mid_back)
    second(1)

    def attend_grad(h, block):
        part = block // 2
        keys, rows = slice(part * 512, part * 512 + 512), slice(block * R, block * R + R)
        kvs, q, go = kv[h, keys], q_s[h, rows], n2_s[rows, lanes(h)]
        st = nt(kvs, q) * LOG_SCALE + wide(mask[keys], R)
        pt = jnp.exp(st - lse[h, :, rows])
        dpt = nt(kvs, go)
        delta = colsum(pt * dpt)
        dst = (pt * (dpt - delta)).astype(BF)
        dqt = nn(kvt[h, 0:64, keys], dst) * LOG_SCALE
        q_s[h, rows, 0:64] = dqt.T.astype(BF)
        return nn(dst, q) * LOG_SCALE + nn(pt.astype(BF), go)

    def grad_c(h):
        both = attend_grad(h, 2)
        recv[0, 512:768, lanes(h)] = both[0:256]
        dkx[h] = both[256:512].astype(BF)

    def grad_a(h):
        recv[0, 0:512, lanes(h)] = attend_grad(h, 0) + attend_grad(h, 1)

    each(6, grad_c)
    dk_copy = remote(dkx, dkr, s_x.at[1], r_x.at[1], dp, across)
    dk_copy.start()
    third(2)
    each(6, grad_a)
    turn_rows(gm)

    def out_grad(i):
        for xi in range(2):
            g[0, xi, chunk(i), 512:768] = nn(tr[chunk(i)], att[xi])

    each(3, out_grad)
    third(1)
    dk_copy.wait()

    def join(h):
        recv[0, 512:768, lanes(h)] = recv[0, 512:768, lanes(h)] + dkr[h].astype(F32)

    each(6, join)

    def project_back(i):
        rows = chunk(i)
        part = None
        for xi in range(2):
            pieces = []
            for j in range(3):
                at = 384 * xi + 128 * j
                pieces += [q_s[3 * xi + j, rows, 0:64], recv[0, rows, at : at + 128].astype(BF)]
            gr = jnp.concatenate(pieces + [jnp.zeros((R, 64), BF)], axis=1)
            gp[xi, rows, 0:640] = gr
            add(9 + xi if xi == 0 else 13, colsum(gr.astype(F32)))
            piece = nt(gr, half_of(0, xi, 0, 640))
            part = piece if part is None else part + piece
        x3[rows] = part
        core(3, x3, i).start()

    each(3, project_back)
    turn_rows(nin)

    def qkv_grad(i):
        rows = chunk(i)
        for xi in range(2):
            h = nn(tr[rows], gp[xi, :, 0:640])
            g[0, xi, rows, 0:512] = h[:, 0:512]
            g[0, xi, rows, 512:640] = g[0, xi, rows, 512:640] + h[:, 512:640]

    each(3, qkv_grad)
    first(0)

    def in_back(i):
        rows = chunk(i)
        core(3, x3, i).wait()
        grad_h = x3[rows] + recv[1, rows]
        normed, inverse = normalize_rows(stream(i))
        add(0, colsum(grad_h * normed))
        add(2, colsum(grad_h))
        grad_in = gy[rows] + norm_back(grad_h * vec[2:3], normed, inverse)
        total = colsum(grad_in)
        add(6, jnp.where(i < 2, total, 0.0))
        add(7, jnp.where(i < 2, 0.0, total))
        out_b = grad_in.astype(BF)
        pack_out(1, i, out_b)

    each(3, in_back)
    go_home(1)
    second(0)

    msg[...] = jnp.zeros(msg.shape, F32)
    loss_row = sums[8:9, 0:128]
    for k in range(1, 6):
        loss_row = loss_row + sums[8:9, 128 * k : 128 * k + 128]
    for xi in range(2):
        bias_sums = sums[9:10] if xi == 0 else sums[13:14]
        hidden = sums[11 + xi : 12 + xi]
        for d in range(DP):
            at, owner = 96 * d + 48 * xi, 8 * xi + d
            msg[owner, 0:8, 0:24] = jnp.where(c == 0, sums[0:8, at : at + 24], sums[0:8, at + 24 : at + 48])
            msg[owner, 8:9] = loss_row
            for j in range(3):
                for kind in range(2):
                    low = 192 * j + 128 * kind
                    msg[owner, 9 + 3 * kind + j : 10 + 3 * kind + j, 0:64] = bias_sums[:, low : low + 64]
            for k in range(6):
                msg[owner, 16 + k : 17 + k] = hidden[:, 128 * k : 128 * k + 128]
    pltpu.make_async_copy(msg.at[mine], msgs.at[mine], r_msg.at[mine]).start()
    for k in range(DP):
        for xr in range(2):
            if k or xr:
                d, xx = lax.rem(dp + k, DP), lax.rem(x + xr, 2)
                go(remote(msg.at[xx * DP + d], msgs.at[mine], s_msg.at[2 * k + xr], r_msg.at[mine], d, 2 * xx + c))
    third(0)
    last(2)
    last(1)
    last(0)
    for j in range(16):
        landed(msgs.at[j], r_msg.at[j], s_msg.at[0], dp, mp)
    for n in range(2):
        for m in range(3):
            for j in range(DP):
                landed(back.at[n, m, j], r_yg.at[n, m, j], s_yg.at[n, 0], dp, mp)
    for copy in sent:
        copy.wait_send()

    @pl.when(y == x)
    def _():
        for k in range(1, DP):
            token_copy(8 + k, lax.rem(dp + k, DP), 2, 8 + z).wait_send()

    @pl.when(y != x)
    def _():
        remote(ts.at[2, dp], tea.at[mp, 8 + z], s_tea.at[16], r_tea.at[x, 8 + z], dp, 2 * y + c).wait_send()
        home_copy(0).wait_send()
        home_copy(1).wait_send()


def step(xs, ts, wsh, small, mask, factor):
    dma = pltpu.SemaphoreType.DMA
    vm = pltpu.VMEM
    block = (ROWS, 768)
    return pl.pallas_call(
        step_kernel,
        name="step",
        out_shape=(
            jax.ShapeDtypeStruct((3, ROWS, 768), F32),
            jax.ShapeDtypeStruct((16, 24, 128), F32),
            jax.ShapeDtypeStruct((2, 3, DP, 96, 128), BF),
        ),
        in_specs=[pl.BlockSpec(memory_space=pl.ANY)] * 4 + [VM] * 2,
        out_specs=(VM, VM, pl.BlockSpec(memory_space=pl.ANY)),
        scratch_shapes=[
            vm((3, 2, T, 768), F32), vm((2, 4, 12, 96, 128), BF), vm((16, 768), F32), vm((16, 24, 128), F32),
            vm((4,) + block, BF), vm((3, 4) + block, BF), vm((3, 2, 4) + block, BF), vm((3, 3) + block, BF),
            vm((1024, 768), BF), vm((4, 12, 96, 128), BF), vm((3, 16) + block, BF),
            vm((4, DP, 48, 128), BF), vm((32, 768), F32), vm((16, 768), F32),
            vm((T, 768), BF), vm((6, T, 128), BF), vm((6, 1024, 128), BF), vm((6, 128, 1024), BF),
            vm((2, R, T), BF), vm((2, T, R), BF), vm((T, 768), BF), vm((2, T, 768), BF),
            vm((T, 768), F32), vm((T, 768), BF), vm((2, T, 768), BF), vm((T, 768), F32),
            vm((2, T, 768), F32), vm((768, T), BF), vm((6, R, 128), BF), vm((6, R, 128), BF),
            vm((6, 1, T), F32),
            dma((4, 3)), dma((4, 3)), dma((2,)), dma((2,)),
            dma((16,)), dma((12,)), dma((24,)), dma((2, 12)), dma((16,)), dma((16,)),
            dma((3, 15)), dma((3, 16)), dma((6,)), dma((6,)),
            dma((16,)), dma((16,)), dma((2, 24)), dma((2, 3, DP)), dma((3, 4)), dma((3, 4)),
            dma((3, 2, 4)), dma((3, 2, 4)), dma((3, 3)), dma((3, 3)),
        ],
        compiler_params=pltpu.CompilerParams(
            collective_id=3, has_side_effects=True, vmem_limit_bytes=VMEM_LIMIT
        ),
    )(xs, ts, wsh, small, mask, factor)


def send_slot(perm, m, d, dp):
    index = 0
    for k in range(DP):
        v = perm[m, DP * d + k]
        index = index + jnp.where(lax.shift_right_logical(v, 3) == dp, v & 7, 0)
    return index


def one_hot(timestep):
    steps = lax.broadcasted_iota(jnp.int32, (1, 1000), 1)
    return jnp.concatenate(
        [jnp.where(steps == timestep[n], 1.0, 0.0).astype(F32) for n in range(24)], axis=0
    )


def valid_count(lengths):
    count = lengths[0]
    for n in range(1, 24):
        count = count + lengths[n]
    return count


def pack_kernel(
    perm, lengths, timestep, xin, tin, table, gains, shifts, qvb, inb, w_qkv, w_out, w_in, w_back,
    xs, ts, wsh, small, mask, factor,
    rows, lines, sem,
):
    dp, mp, x, c = place()
    slots = [[send_slot(perm, m, d, dp) for d in range(DP)] for m in range(3)]
    copies = []
    for m in range(3):
        for d in range(DP):
            source = xin.at[m, pl.ds(pl.multiple_of(64 * slots[m][d], 64), 64)]
            copies.append(pltpu.make_async_copy(source, xs.at[m, d], sem.at[m, d]))
            copies[-1].start()
    for m in range(3):
        rows[m] = tin[m].T
    for m in range(3):
        for d in range(DP):
            v = rows[m, pl.ds(pl.multiple_of(64 * slots[m][d], 64), 64)]
            ts[m, d, 0:64] = v[:, 0:128]
            ts[m, d, 64:96] = jnp.concatenate([v[0:32, 128:192], v[32:64, 128:192]], axis=1)
    wsh[0, :, 0:576] = w_qkv[...]
    wsh[0, :, 576:768] = w_out[...].T
    wsh[1] = w_in[...]
    wsh[2] = w_back[...]

    lane = lax.broadcasted_iota(jnp.int32, (8, 128), 1)
    lines[...] = jnp.zeros(lines.shape, F32)
    lines[0:2, 0:24] = gains[...].astype(F32)
    lines[2:6, 0:24] = shifts[...].astype(F32)
    lines[6:30, 0:24] = nt(one_hot(timestep).astype(BF), table[...])
    spread = jnp.concatenate([inb[...].astype(F32)] * 8, axis=1)
    lines[32:38] = jnp.where(lax.shift_right_logical(lane[0:6], 4) == dp, spread, 0.0)
    for j in range(3):
        both = jnp.concatenate([qvb[j].astype(F32)] * 8, axis=1)
        both = jnp.where(lax.shift_right_logical(lane[0:2, 0:64], 3) == dp, both, 0.0)
        lines[40 + j : 41 + j, 0:64] = both[0:1]
        lines[43 + j : 44 + j, 0:64] = both[1:2]
    small[...] = lines[...].astype(BF)

    inside = lax.broadcasted_iota(jnp.int32, (64, 128), 0)
    micro_lengths = lengths[x * DP + dp], lengths[2 * DP + dp]
    for j in range(16):
        own = j < 8
        m = x if own else 2
        wanted = j if own else 2 * (j % 4) + (x if j < 12 else 1 - x)
        at = 0
        for p in range(DP):
            v = perm[m, DP * dp + p]
            at = at + jnp.where(lax.shift_right_logical(v, 3) == wanted, p, 0)
        live = inside + 64 * at < micro_lengths[0 if own else 1]
        mask[64 * j : 64 * j + 64] = jnp.where(live, 0.0, -1e30).astype(F32)
    count = jnp.full((8, 128), valid_count(lengths), jnp.int32).astype(F32)
    factor[...] = (3.0 * DP * 512) / count
    for copy in copies:
        copy.wait()


def pack(*arguments):
    vm = pltpu.VMEM
    smem = pl.BlockSpec(memory_space=pltpu.SMEM)
    return pl.pallas_call(
        pack_kernel,
        name="pack",
        out_shape=(
            jax.ShapeDtypeStruct((3, DP, 64, 768), BF),
            jax.ShapeDtypeStruct((3, DP, 96, 128), BF),
            jax.ShapeDtypeStruct((3, ROWS, 768), BF),
            jax.ShapeDtypeStruct((48, 128), BF),
            jax.ShapeDtypeStruct((1024, 128), F32),
            jax.ShapeDtypeStruct((8, 128), F32),
        ),
        in_specs=[smem] * 3 + [pl.BlockSpec(memory_space=pl.ANY)] + [VM] * 10,
        out_specs=(VM,) * 6,
        scratch_shapes=[vm((3, 512, 192), BF), vm((48, 128), F32), pltpu.SemaphoreType.DMA((3, DP))],
        compiler_params=pltpu.CompilerParams(vmem_limit_bytes=VMEM_LIMIT),
    )(*arguments)


def unpack_kernel(
    perm, lengths, timestep, gs, msgs, home,
    y_out, loss, grad_x, table, gains, shifts, g_qkv, g_qvb, g_out, g_in, g_inb, g_back,
    rows,
):
    dp, mp, x, c = place()
    for m in range(3):
        slots = [send_slot(perm, m, d, dp) for d in range(DP)]
        for n, target in ((0, y_out), (1, grad_x)):
            for d in range(DP):
                low = home[n, m, d, 64:96]
                value = jnp.concatenate(
                    [home[n, m, d, 0:64], jnp.concatenate([low[:, 0:64], low[:, 64:128]], axis=0)], axis=1
                )
                rows[n, pl.ds(pl.multiple_of(64 * slots[d], 64), 64)] = value
            target[m] = rows[n].T
    total = msgs[0]
    for j in range(1, 16):
        total = total + msgs[j]
    count = jnp.full((1, 1), valid_count(lengths), jnp.int32).astype(F32)
    loss[...] = jnp.sum(total[8:9], axis=1, keepdims=True) / (count * 768.0)
    gains[...] = total[0:2, 0:24]
    shifts[...] = total[2:6, 0:24]
    turned = pltpu.roll(total, lax.rem(128 - 8 * dp, 128), 1)
    for j in range(3):
        for kind in range(2):
            at = 9 + 3 * kind + j
            g_qvb[j, kind : kind + 1] = turned[at : at + 1, 0:8]
    g_inb[...] = pltpu.roll(total, lax.rem(128 - 16 * dp, 128), 1)[16:22, 0:16]
    lines = [msgs[j, 6:7] for j in range(16)] + [msgs[d, 7:8] + msgs[DP + d, 7:8] for d in range(DP)]
    columns = jnp.concatenate(lines, axis=0).T[0:24]
    chosen = one_hot(timestep)
    result = columns[:, 0:1] * chosen[0:1]
    for n in range(1, 24):
        result = result + columns[:, n : n + 1] * chosen[n : n + 1]
    table[...] = result
    g_qkv[...] = gs[0, :, 0:576]
    g_out[...] = gs[0, :, 576:768].T
    g_in[...] = gs[1]
    g_back[...] = gs[2]


def unpack(*arguments):
    smem = pl.BlockSpec(memory_space=pltpu.SMEM)
    shapes = [
        ((3, 192, 512), BF), ((1, 1), F32), ((3, 192, 512), BF), ((24, 1000), F32), ((2, 24), F32),
        ((4, 24), F32), ((96, 576), F32), ((3, 2, 8), F32), ((192, 96), F32), ((96, 768), F32),
        ((6, 16), F32), ((96, 768), F32),
    ]
    return pl.pallas_call(
        unpack_kernel,
        name="unpack",
        out_shape=tuple(jax.ShapeDtypeStruct(*shape) for shape in shapes),
        in_specs=[smem] * 3 + [VM] * 3,
        out_specs=(VM,) * 12,
        scratch_shapes=[pltpu.VMEM((2, 512, 192), BF)],
        compiler_params=pltpu.CompilerParams(vmem_limit_bytes=VMEM_LIMIT),
    )(*arguments)


def per_device_compact(
    input_stream, teacher, timestep, lengths, block_perm, table, norm_gains, shifts,
    w_qkv, qv_bias, w_out, w_in, in_bias, w_back,
):
    packed = pack(
        block_perm, lengths, timestep, input_stream, teacher.transpose(0, 2, 1), table.T, norm_gains, shifts,
        qv_bias.transpose(1, 0, 2), in_bias, w_qkv, w_out, w_in, w_back.T,
    )
    outs = list(unpack(block_perm, lengths, timestep, *step(*packed)))
    outs[0], outs[2] = outs[0].transpose(0, 2, 1), outs[2].transpose(0, 2, 1)
    outs[1], outs[3] = outs[1].reshape(()), outs[3].T
    outs[7], outs[11] = outs[7].transpose(1, 0, 2), outs[11].T
    return tuple(outs)


def solution(mesh):
    compact = mesh.shape["dp"] == 8 and mesh.shape["mp"] == 4
    return jax.shard_map(
        per_device_compact if compact else per_device,
        mesh=mesh,
        in_specs=(
            P(None, "dp", None),
            P(None, "dp", "mp"),
            P(),
            P(),
            P(),
            P(None, ("dp", "mp")),
            P(None, ("dp", "mp")),
            P(None, ("dp", "mp")),
            P("dp", "mp"),
            P(None, "mp", "dp"),
            P("mp", "dp"),
            P("dp", "mp"),
            P("mp", "dp"),
            P("mp", "dp"),
        ),
        out_specs=(
            P(None, "dp", "mp"),
            P(),
            P(None, "dp", "mp"),
            P(None, ("dp", "mp")),
            P(None, ("dp", "mp")),
            P(None, ("dp", "mp")),
            P("dp", "mp"),
            P(None, "mp", "dp"),
            P("mp", "dp"),
            P("dp", "mp"),
            P("mp", "dp"),
            P("mp", "dp"),
        ),
        check_vma=False,
    )
```
